32 devices in a mesh: grp: 4 (over z), orb: 4 (over y, core), slab: 2 (over x).
Axes of the slice: x: 2, y: 2, z: 4, core: 2. Of those that a mesh axis runs over, the one named last changes fastest.
Arguments:
- orbitals: float32 [128, 64, 64, 64], P(('grp', 'orb'), 'slab'), may hold values from -6 to 6
- offsets: int32 [128, 2], replicated, may hold values from 0 to 15
- pairs: int32 [128, 2], P(('grp', 'orb')), may hold values from 0 to 127, as said below
- live: int32 [128], P(('grp', 'orb')), may hold values from 0 to 1, as said below
Outputs:
- exchange: float32 [128, 64, 64, 64], P(('grp', 'orb'), 'slab')
The draws below stay inside these ranges and needn't reach their ends.
Inputs may be any that keep to these rules, and one draw needn't show every extreme that they name: The 8 rows of one device of grp and orb (aligned blocks, in order) name as first orbital one of that device's 8 orbitals; the second orbital lies within 8 positions of the first on the cycle of 128 orbitals. In every block, row 0 pairs the device's lowest orbital with the orbital just below it on the cycle, and row 1 pairs the device's highest orbital with the orbital just above it. In each aligned block of 8 slots the live ones come first, at least two are live, and some block is all live.
All inputs are finite; a program needn't handle non-finite values.
Results may differ from the reference program's by a relative error of at most 0.0003.
Values sent between devices are 32-bit elements; how exact they have to be, the bound alone decides.
A program may use at most 192 MiB of HBM per device.

```python
import jax
import jax.numpy as jnp
from jax import lax

BOX = 64
MAXOFF = 16
PASSES = 8
ORB_DEV = 8
PAIR_DEV = 8
NORB = 128
PAIRS = 128


def draw_pairs(key, part):
    base = jax.random.fold_in(key, 7)
    key_one, key_two = jax.random.split(base)
    owner = jnp.arange(PAIRS, dtype=jnp.int32) // PAIR_DEV
    slot = jnp.arange(PAIRS, dtype=jnp.int32) % PAIR_DEV
    pick = jax.random.randint(key_one, (PAIRS,), 0, ORB_DEV, dtype=jnp.int32)
    pick = jnp.where(slot == 0, 0, jnp.where(slot == 1, ORB_DEV - 1, pick))
    first = owner * ORB_DEV + pick
    step = jax.random.randint(key_two, (PAIRS,), -ORB_DEV, ORB_DEV + 1, dtype=jnp.int32)
    step = jnp.where(slot == 0, -1, jnp.where(slot == 1, 1, step))
    second = jnp.mod(first + step, NORB)
    return jnp.stack([first, second], axis=1).astype(jnp.int32)


def draw_live(key, part):
    base = jax.random.fold_in(key, 11)
    key_one, key_two = jax.random.split(base)
    blocks = PAIRS // PAIR_DEV
    drawn = jax.random.randint(key_one, (blocks,), 0, PAIR_DEV, dtype=jnp.int32)
    counts = jnp.minimum(2 + drawn * drawn // PAIR_DEV, PAIR_DEV)
    fullest = jax.random.randint(key_two, (), 0, blocks, dtype=jnp.int32)
    counts = jnp.where(jnp.arange(blocks, dtype=jnp.int32) == fullest, PAIR_DEV, counts)
    slots = jnp.arange(PAIRS, dtype=jnp.int32) % PAIR_DEV
    return (slots < jnp.repeat(counts, PAIR_DEV)).astype(jnp.int32)


def set_ends(values, stream_key, smallest, largest):
    longest = values.shape.index(max(values.shape))
    spots = []
    for shift in (0, 1):
        where = [jax.random.randint(jax.random.fold_in(stream_key, axis), (), 0, length) for axis, length in enumerate(values.shape)]
        where[longest] = (where[longest] + shift) % values.shape[longest]
        spots.append(tuple(where))
    return values.at[spots[0]].set(smallest).at[spots[1]].set(largest)


def shard_levels(own_key, shape, pieces, low, largest):
    def one(position, blocks):
        heights = jax.random.uniform(jax.random.fold_in(jax.random.fold_in(own_key, 6), position), (blocks,), jnp.float32, low / len(pieces), largest / len(pieces))
        return jnp.repeat(jnp.exp(heights), shape[position] // blocks).reshape((-1,) + (1,) * (len(shape) - position - 1))

    level = one(*pieces[0])
    for cut in pieces[1:]:
        level = level * one(*cut)
    return level


def noise(rng, shape, width, most, pieces=(), kind=jnp.bfloat16):
    entries = width * jax.random.normal(rng, shape, jnp.float32)
    if pieces:
        entries = entries * shard_levels(rng, shape, pieces, -0.22, 0.18)
    return jnp.clip(entries, -most, most).astype(kind)


def setup_inputs(seed: int = 0) -> dict:
    splits = jax.random.split(jax.random.key(seed), 5)
    orbitals = noise(splits[0], (NORB, BOX, BOX, BOX), 1.0, 6.0, ((0, 16), (1, 2)), jnp.float32)
    offsets = set_ends(jax.random.randint(splits[1], (NORB, 2), 0, MAXOFF), jax.random.fold_in(splits[1], 1), 0, MAXOFF - 1).astype(jnp.int32)
    pairs = draw_pairs(jax.random.fold_in(splits[4], 71), 0)
    live = draw_live(jax.random.fold_in(splits[4], 71), 0)
    return {"orbitals": orbitals, "offsets": offsets, "pairs": pairs, "live": live}


DIAG = 6.25
THETA = 1.075
DELTA = 0.925


def place(field, shift_y, shift_z):
    lead = field.ndim - 2
    padded = jnp.pad(field, [(0, 0)] * lead + [(MAXOFF, MAXOFF), (MAXOFF, MAXOFF)])
    zero = jnp.zeros((), jnp.int32)
    starts = [zero] * lead + [(MAXOFF - shift_y).astype(jnp.int32), (MAXOFF - shift_z).astype(jnp.int32)]
    return lax.dynamic_slice(padded, starts, field.shape)


def apply_op(padded):
    core = padded[:, 1:-1]
    wider = jnp.pad(core, ((0, 0), (0, 0), (1, 1), (1, 1)))
    near = padded[:, 2:] + padded[:, :-2]
    near = near + wider[:, :, 2:, 1:-1] + wider[:, :, :-2, 1:-1]
    near = near + wider[:, :, 1:-1, 2:] + wider[:, :, 1:-1, :-2]
    return DIAG * core - near


def smooth(density, widen):
    sigma = THETA / DELTA
    resid = density
    value = jnp.zeros_like(density)
    step = resid / (DIAG * THETA)
    coef = 1.0 / sigma
    for turn in range(PASSES):
        value = value + step
        if turn < PASSES - 1:
            resid = resid - apply_op(widen(step))
            coef_new = 1.0 / (2.0 * sigma - coef)
            step = (coef_new * coef) * step + (2.0 * coef_new / DELTA) * (resid / DIAG)
            coef = coef_new
    return value


def pad_first(field):
    return jnp.pad(field, ((0, 0), (1, 1), (0, 0), (0, 0)))


def reference(orbitals, offsets, pairs, live):
    def one(total, row):
        pair_row, alive = row
        first = pair_row[0]
        second = pair_row[1]
        shift = offsets[second] - offsets[first]
        own = orbitals[first]
        partner = place(orbitals[second], shift[0], shift[1])
        density = (own * partner)[None]
        potential = smooth(density, pad_first)[0]
        weight = alive.astype(jnp.float32)
        to_first = weight * potential * partner
        to_second = weight * place(potential * own, -shift[0], -shift[1])
        total = total.at[first].add(to_first)
        total = total.at[second].add(to_second)
        return total, None

    start = jnp.zeros(orbitals.shape, jnp.float32)
    result, _ = lax.scan(one, start, (pairs, live))
    return result
```

```python
import cmath
import functools
import math

import jax
import jax.numpy as jnp
from jax import lax
from jax.experimental import pallas as pl
from jax.experimental.pallas import tpu as pltpu
from jax.sharding import PartitionSpec as P

PASSES = 8
DIAG = 6.25
THETA = 1.075
DELTA = 0.925
EDGE = PASSES - 1
PAD = 16
CYCLE = ("grp", "orb")
F32 = jnp.float32


def coefs():
    sigma = THETA / DELTA
    coef = 1.0 / sigma
    out = []
    for _ in range(PASSES - 1):
        new = 1.0 / (2.0 * sigma - coef)
        out.append((new * coef, 2.0 * new / (DELTA * DIAG)))
        coef = new
    return out


def lanes(shape):
    return lax.broadcasted_iota(jnp.int32, shape, len(shape) - 1)


def share_kernel(mine, every, send_sem, recv_sem):
    size, width = lax.axis_size(CYCLE), lax.axis_size("orb")
    me = lax.axis_index("grp") * width + lax.axis_index("orb")

    def peer(s):
        to = lax.rem(me + s, size)
        return {"grp": lax.div(to, width), "orb": lax.rem(to, width)}

    def greet(s, c):
        pl.semaphore_signal(
            barrier, inc=1, device_id=peer(s), device_id_type=pl.DeviceIdType.MESH
        )
        return c

    def copy(s, slot):
        return pltpu.make_async_remote_copy(
            src_ref=mine,
            dst_ref=every.at[slot],
            send_sem=send_sem.at[s],
            recv_sem=recv_sem.at[s],
            device_id=peer(s),
            device_id_type=pl.DeviceIdType.MESH,
        )

    def send(s, c):
        copy(s, me).start()
        return c

    def finish(s, c):
        copy(s, lax.rem(me + size - s, size)).wait()
        return c

    barrier = pltpu.get_barrier_semaphore()
    lax.fori_loop(1, size, greet, 0)
    pl.semaphore_wait(barrier, size - 1)
    lax.fori_loop(1, size, send, 0)
    every[me] = mine[...]
    lax.fori_loop(1, size, finish, 0)


def share(mine):
    size = lax.axis_size(CYCLE)
    vmem = pl.BlockSpec(memory_space=pltpu.VMEM)
    return pl.pallas_call(
        share_kernel,
        in_specs=[vmem],
        out_specs=vmem,
        out_shape=jax.ShapeDtypeStruct((size,) + mine.shape, mine.dtype),
        scratch_shapes=[pltpu.SemaphoreType.DMA((size,)), pltpu.SemaphoreType.DMA((size,))],
        compiler_params=pltpu.CompilerParams(collective_id=0, has_side_effects=True),
        name="share",
    )(mine)


def pack_kernel(src, dst):
    half = dst.shape[1]
    dst[0] = jnp.concatenate([src[0, :half], src[0, half:]], axis=-1)


def pack(orbitals):
    n, x, y, z = orbitals.shape
    return pl.pallas_call(
        pack_kernel,
        grid=(n,),
        in_specs=[pl.BlockSpec((1, x, y, z), lambda i: (i, 0, 0, 0))],
        out_specs=pl.BlockSpec((1, x // 2, y, 2 * z), lambda i: (i, 0, 0, 0)),
        out_shape=jax.ShapeDtypeStruct((n, x // 2, y, 2 * z), F32),
        name="pack",
    )(orbitals)


def copy_kernel(idx, src_a, src_b, dst_a, dst_b):
    dst_a[...] = src_a[...]
    dst_b[...] = src_b[...]


def gather(packed, lists, m):
    _, h, y, w = packed.shape
    blk = (1, h, y, w)
    out = jax.ShapeDtypeStruct((m, h, y, w), F32)
    return pl.pallas_call(
        copy_kernel,
        grid_spec=pltpu.PrefetchScalarGridSpec(
            num_scalar_prefetch=1,
            grid=(m,),
            in_specs=[
                pl.BlockSpec(blk, lambda i, idx: (idx[0, i], 0, 0, 0)),
                pl.BlockSpec(blk, lambda i, idx: (idx[1, i], 0, 0, 0)),
            ],
            out_specs=[pl.BlockSpec(blk, lambda i, idx: (i, 0, 0, 0))] * 2,
        ),
        out_shape=[out, out],
        name="gather",
    )(lists, packed, packed)


def place(value, room, a, b):
    y, w = value.shape[1:]
    z = w // 2
    room[:, PAD : PAD + y, :] = value
    moved = room[:, pl.ds(PAD - a, y), :]
    moved = pltpu.roll(moved, lax.rem(b + w, w), axis=2)
    pos = lanes(moved.shape) % z - b
    return jnp.where((pos >= 0) & (pos < z), moved, 0.0)


def clear_room(room):
    y = room.shape[1] - 2 * PAD
    room[:, :PAD, :] = jnp.zeros((room.shape[0], PAD, room.shape[2]), F32)
    room[:, PAD + y :, :] = jnp.zeros((room.shape[0], PAD, room.shape[2]), F32)


def density_kernel(plan, own, mine, prior, nxt, partner, density, low, high, room):
    p = pl.program_id(0)
    kind = plan[4, p]
    a, b = plan[5, p], plan[6, p]

    @pl.when(p == 0)
    def _():
        clear_room(room)

    on = plan[7, p] > 0

    def go(src):
        part = place(src[0], room, a, b)
        partner[0] = part
        dens = own[0] * part
        density[0] = dens
        h, y, w = dens.shape
        flat = jnp.concatenate([dens[..., : w // 2], dens[..., w // 2 :]], axis=0)
        top, bot = flat[:EDGE], flat[2 * h - EDGE :]
        low[0] = jnp.concatenate([top[:, : y // 2], top[:, y // 2 :]], axis=-1)
        high[0] = jnp.concatenate([bot[:, : y // 2], bot[:, y // 2 :]], axis=-1)

    for value, src in enumerate((mine, prior, nxt)):
        pl.when(on & (kind == value))(functools.partial(go, src))


def densities(plan, packed, prior, nxt):
    slots = plan.shape[1]
    _, h, y, w = packed.shape
    blk = (1, h, y, w)
    eblk = (1, EDGE, y // 2, w)

    def at(row):
        return pl.BlockSpec(
            blk, lambda i, plan: (plan[row, jnp.minimum(i, plan[8, 1] - 1)], 0, 0, 0)
        )

    full = jax.ShapeDtypeStruct((slots, h, y, w), F32)
    edge = jax.ShapeDtypeStruct((slots,) + eblk[1:], F32)
    here = lambda i, plan: (jnp.minimum(i, plan[8, 1] - 1), 0, 0, 0)
    return pl.pallas_call(
        density_kernel,
        grid_spec=pltpu.PrefetchScalarGridSpec(
            num_scalar_prefetch=1,
            grid=(slots,),
            in_specs=[at(0), at(1), at(2), at(3)],
            out_specs=[
                pl.BlockSpec(blk, here),
                pl.BlockSpec(blk, here),
                pl.BlockSpec(eblk, here),
                pl.BlockSpec(eblk, here),
            ],
            scratch_shapes=[pltpu.VMEM((h, y + 2 * PAD, w), F32)],
        ),
        out_shape=[full, full, edge, edge],
        name="density",
    )(plan, packed, packed, prior, nxt)


def solve_kernel(remote, plan, ends, density, partner, own, below, above, *refs):
    accs, (resid, step_a, step_b, total, mask, room) = refs[:-6], refs[-6:]
    acc = accs[0]
    p = pl.program_id(0)
    h, y, w = density.shape[1:]
    z = w // 2
    rows = h + 2 * EDGE
    group = 4 if h % 4 == 0 else 1

    @pl.when(p == 0)
    def _():
        clear_room(room)
        for ref in accs:
            ref[...] = jnp.zeros(ref.shape, F32)
        for ref in (step_a, step_b):
            ref[:, :8, :] = jnp.zeros((rows, 8, w), F32)
            ref[:, 8 + y :, :] = jnp.zeros((rows, 8, w), F32)
        lane = lanes((1, w))
        first = ends[0] == 0
        last = ends[0] == ends[1] - 1
        for t in range(rows):
            plane = jnp.where(lane < z, t - EDGE, t - EDGE + h)
            outside = ((plane < 0) & first) | ((plane >= 2 * h) & last)
            mask[t] = jnp.where(outside, 0.0, 1.0)

    chosen = (plan[4, p] > 0) if remote else (plan[4, p] == 0)

    @pl.when((plan[7, p] > 0) & chosen)
    def _():
        def unfold(part):
            return jnp.concatenate([part[..., :z], part[..., z:]], axis=1)

        dens = density[0]
        line = jnp.concatenate(
            [unfold(below[0]), dens[..., :z], dens[..., z:], unfold(above[0])], axis=0
        )
        resid[...] = jnp.concatenate([line[:rows], line[h:]], axis=-1)
        step_a[:, 8 : 8 + y, :] = resid[...] * (1.0 / (DIAG * THETA))
        total[...] = step_a[EDGE : EDGE + h, 8 : 8 + y, :]
        lane = lanes((y, w)) % z
        not_low = lane > 0
        not_high = lane < z - 1
        bufs = [step_a, step_b]
        for turn, (keep, gain) in enumerate(coefs()):
            now, then = bufs[turn % 2], bufs[1 - turn % 2]
            core_only = turn == PASSES - 2

            def row(t, now=now, then=then, keep=keep, gain=gain):
                core = now[t, 8 : 8 + y, :]
                near = now[t - 1, 8 : 8 + y, :] + now[t + 1, 8 : 8 + y, :]
                near = near + (now[t, 7 : 7 + y, :] + now[t, 9 : 9 + y, :])
                side = jnp.where(not_low, pltpu.roll(core, 1, axis=1), 0.0)
                side = side + jnp.where(not_high, pltpu.roll(core, w - 1, axis=1), 0.0)
                left = (resid[t] - DIAG * core) + (near + side)
                return left, keep * core + gain * left

            def outer(k, c, row=row, then=then):
                for t in (EDGE - 1 - k, EDGE + h + k):
                    left, fresh = row(t)
                    resid[t] = left
                    then[t, 8 : 8 + y, :] = fresh * mask[t]
                return c

            def inner(k, c, row=row, then=then, last=core_only):
                for g in range(group):
                    t = EDGE + k * group + g
                    left, fresh = row(t)
                    if not last:
                        resid[t] = left
                        then[t, 8 : 8 + y, :] = fresh
                    total[t - EDGE] += fresh
                return c

            if turn + 1 < EDGE:
                lax.fori_loop(0, EDGE - turn - 1, outer, 0)
            lax.fori_loop(0, h // group, inner, 0)

        pot = total[...]
        acc[plan[0, p]] += pot * partner[0]
        back = place(pot * own[0], room, -plan[5, p], -plan[6, p])
        if not remote:
            acc[plan[1, p]] += back
        else:
            for value in (1, 2):

                @pl.when(plan[4, p] == value)
                def _(ref=accs[value], value=value):
                    ref[plan[1 + value, p]] += back


def solve(remote, plan, ends, density, partner, packed, below, above, m):
    slots = plan.shape[1]
    n, h, y, w = packed.shape
    blk = (1, h, y, w)
    eblk = (1, EDGE, y // 2, w)
    rows = h + 2 * EDGE

    def spot(i, plan):
        far = plan[8, 0]
        if remote:
            return jnp.minimum(i, jnp.maximum(far - 1, 0))
        return jnp.clip(i, jnp.minimum(far, plan[8, 1] - 1), plan[8, 1] - 1)

    here = lambda i, plan, ends: (spot(i, plan), 0, 0, 0)
    fixed = lambda i, plan, ends: (0, 0, 0, 0)
    shapes = [(n, h, y, w)] + [(m, h, y, w)] * (2 if remote else 0)
    return pl.pallas_call(
        functools.partial(solve_kernel, remote),
        grid_spec=pltpu.PrefetchScalarGridSpec(
            num_scalar_prefetch=2,
            grid=(slots,),
            in_specs=[
                pl.BlockSpec(blk, here),
                pl.BlockSpec(blk, here),
                pl.BlockSpec(blk, lambda i, plan, ends: (plan[0, spot(i, plan)], 0, 0, 0)),
                pl.BlockSpec(eblk, here),
                pl.BlockSpec(eblk, here),
            ],
            out_specs=[pl.BlockSpec(s, fixed) for s in shapes],
            scratch_shapes=[
                pltpu.VMEM((rows, y, w), F32),
                pltpu.VMEM((rows, y + 16, w), F32),
                pltpu.VMEM((rows, y + 16, w), F32),
                pltpu.VMEM((h, y, w), F32),
                pltpu.VMEM((rows, 1, w), F32),
                pltpu.VMEM((h, y + 2 * PAD, w), F32),
            ],
        ),
        out_shape=[jax.ShapeDtypeStruct(s, F32) for s in shapes],
        compiler_params=pltpu.CompilerParams(vmem_limit_bytes=56 * 1024 * 1024),
        cost_estimate=pl.CostEstimate(
            flops=slots * rows * y * w * 100, bytes_accessed=24 << 20, transcendentals=0
        ),
        name="solve_far" if remote else "solve_near",
    )(plan, ends, density, partner, packed, below, above)


def combine_kernel(back, acc, acc_near, from_next, from_prior, out):
    k = pl.program_id(0)
    h = acc.shape[1]
    z = acc.shape[3] // 2
    value = acc[0] + acc_near[0]
    value = value + jnp.where(back[1, k] > 0, from_next[0], 0.0)
    value = value + jnp.where(back[3, k] > 0, from_prior[0], 0.0)
    out[0, :h] = value[:, :, :z]
    out[0, h:] = value[:, :, z:]


def combine(back, acc, acc_near, from_next, from_prior):
    n, h, y, w = acc.shape
    blk = (1, h, y, w)
    return pl.pallas_call(
        combine_kernel,
        grid_spec=pltpu.PrefetchScalarGridSpec(
            num_scalar_prefetch=1,
            grid=(n,),
            in_specs=[
                pl.BlockSpec(blk, lambda i, back: (i, 0, 0, 0)),
                pl.BlockSpec(blk, lambda i, back: (i, 0, 0, 0)),
                pl.BlockSpec(blk, lambda i, back: (back[0, i], 0, 0, 0)),
                pl.BlockSpec(blk, lambda i, back: (back[2, i], 0, 0, 0)),
            ],
            out_specs=pl.BlockSpec((1, 2 * h, y, w // 2), lambda i, back: (i, 0, 0, 0)),
        ),
        out_shape=jax.ShapeDtypeStruct((n, 2 * h, y, w // 2), F32),
        name="combine",
    )(back, acc, acc_near, from_next, from_prior)


def cycle(field, by):
    size = lax.axis_size(CYCLE)
    return lax.ppermute(field, CYCLE, [(i, (i + by) % size) for i in range(size)])


TASK = 8
LISTS = 256
INFO = 320
PLAN = 384


def factors():
    ratio = THETA / DELTA
    tall = math.acosh(ratio)
    points = [cmath.cosh(complex(tall, k * math.pi / 4)) for k in range(8)]
    marks = [DIAG * (1.0 - (THETA - DELTA * x)) for x in points]
    quads = [(-2.0 * marks[k].real, abs(marks[k]) ** 2) for k in (1, 2, 3)]
    line = -marks[4].real
    coef, resid, value, step = 1.0 / ratio, 1.0, 0.0, 1.0 / (DIAG * THETA)
    value += step
    for keep, gain in coefs():
        resid -= DIAG * step
        step = keep * step + gain * resid
        value += step
    product = line
    for _, c in quads:
        product *= c
    return quads, line, value / product


def front_kernel(
    orbs, pairs, live, fields, every, stage, own, far, edge, table,
    in_sem, out_sem, tab_send, tab_recv, edge_send, edge_recv, far_send, far_recv,
):
    n, h = orbs.shape[0], orbs.shape[1]
    half = h // 2
    halo = edge.shape[1]
    size, width = lax.axis_size(CYCLE), lax.axis_size("orb")
    me = lax.axis_index("grp") * width + lax.axis_index("orb")
    slab = lax.axis_index("slab")

    def peer(s):
        to = lax.rem(me + s, size)
        return {"grp": lax.div(to, width), "orb": lax.rem(to, width)}

    def load(k):
        return pltpu.make_async_copy(orbs.at[k], stage.at[k], in_sem.at[k])

    def order(q):
        return jnp.where(q == 0, 0, jnp.where(q == 1, n - 1, q - 1))

    def begin(q, c):
        load(order(q)).start()
        return c

    lax.fori_loop(0, n, begin, 0)

    barrier = pltpu.get_barrier_semaphore()

    def greet(s, c):
        pl.semaphore_signal(
            barrier, inc=1, device_id=peer(s), device_id_type=pl.DeviceIdType.MESH
        )
        return c

    lax.fori_loop(1, size, greet, 0)
    pl.semaphore_signal(
        barrier, inc=1, device_id={"slab": 1 - slab}, device_id_type=pl.DeviceIdType.MESH
    )
    table[:, 0:2] = pairs[...]
    table[:, 2:3] = live[...]
    pl.semaphore_wait(barrier, size)

    def share_copy(s, slot):
        return pltpu.make_async_remote_copy(
            src_ref=table, dst_ref=every.at[slot],
            send_sem=tab_send.at[s], recv_sem=tab_recv.at[s],
            device_id=peer(s), device_id_type=pl.DeviceIdType.MESH,
        )

    def share_send(s, c):
        share_copy(s, me).start()
        return c

    lax.fori_loop(1, size, share_send, 0)
    every[me] = table[...]

    def edge_copy(f, dst):
        return pltpu.make_async_remote_copy(
            src_ref=edge.at[f], dst_ref=dst,
            send_sem=edge_send.at[f], recv_sem=edge_recv.at[f],
            device_id={"slab": 1 - slab}, device_id_type=pl.DeviceIdType.MESH,
        )

    def own_edge(k):
        return edge_copy(k, own.at[k, pl.ds(half, halo)])

    def far_copy(k, f, s):
        return pltpu.make_async_remote_copy(
            src_ref=own.at[k, pl.ds(0, half)], dst_ref=far.at[f, pl.ds(0, half)],
            send_sem=far_send.at[f], recv_sem=far_recv.at[f],
            device_id=peer(s), device_id_type=pl.DeviceIdType.MESH,
        )

    def spot(t):
        return jnp.where(slab == 0, t, h - 1 - t)

    def pack(k):
        def row(r, c):
            own[k, r] = jnp.concatenate(
                [stage[k, spot(r)], stage[k, spot(r + half)]], axis=-1
            )
            return c

        lax.fori_loop(0, half, row, 0)

    def make_edge(k):
        for m in range(halo):
            edge[k, m] = jnp.concatenate(
                [stage[k, spot(h - 1 - m)], stage[k, spot(h - 1 - halo - m)]], axis=-1
            )

    up, down = far_copy(n - 1, 0, 1), far_copy(0, 1, size - 1)
    load(0).wait()
    pack(0)
    down.start()
    make_edge(0)
    own_edge(0).start()
    load(n - 1).wait()
    pack(n - 1)
    up.start()
    make_edge(n - 1)
    own_edge(n - 1).start()

    def rest(k, c):
        load(k).wait()
        make_edge(k)
        own_edge(k).start()
        pack(k)
        return c

    lax.fori_loop(1, n - 1, rest, 0)

    def share_done(s, c):
        share_copy(s, lax.rem(me + size - s, size)).wait()
        return c

    lax.fori_loop(1, size, share_done, 0)

    low = lanes((1, own.shape[-1])) < own.shape[-1] // 2
    for f, copy in ((1, down), (0, up)):
        copy.wait()
        for m in range(halo):
            a, b = far[f, half - 1 - m], far[f, half - 1 - halo - m]
            edge[n + f, m] = jnp.where(low, pltpu.roll(a, a.shape[-1] // 2, axis=1), b)
        edge_copy(n + f, far.at[f, pl.ds(half, halo)]).start()

    def own_done(k, c):
        own_edge(k).wait()
        pltpu.make_async_copy(own.at[k], fields.at[k], out_sem.at[k]).start()
        return c

    lax.fori_loop(0, n, own_done, 0)
    for f in (1, 0):
        edge_copy(n + f, far.at[f, pl.ds(half, halo)]).wait()
        pltpu.make_async_copy(far.at[f], fields.at[n + f], out_sem.at[n + f]).start()

    def out_done(k, c):
        pltpu.make_async_copy(own.at[k], fields.at[k], out_sem.at[k]).wait()
        return c

    lax.fori_loop(0, n, out_done, 0)
    for f in (1, 0):
        pltpu.make_async_copy(far.at[f], fields.at[n + f], out_sem.at[n + f]).wait()


def front(orbitals, pairs, live):
    n, h, y, z = orbitals.shape
    half, halo, w = h // 2, (EDGE + 1) // 2, 2 * z
    size = lax.axis_size(CYCLE)
    vmem = pl.BlockSpec(memory_space=pltpu.VMEM)
    hbm = pl.BlockSpec(memory_space=pl.ANY)
    dma = pltpu.SemaphoreType.DMA
    return pl.pallas_call(
        front_kernel,
        in_specs=[hbm, vmem, vmem],
        out_specs=[hbm, vmem],
        out_shape=[
            jax.ShapeDtypeStruct((n + 2, half + halo, y, w), F32),
            jax.ShapeDtypeStruct((size, n, 128), jnp.int32),
        ],
        scratch_shapes=[
            pltpu.VMEM((n, h, y, z), F32),
            pltpu.VMEM((n, half + halo, y, w), F32),
            pltpu.VMEM((2, half + halo, y, w), F32),
            pltpu.VMEM((n + 2, halo, y, w), F32),
            pltpu.VMEM((n, 128), jnp.int32),
            dma((n,)), dma((n + 2,)), dma((size,)), dma((size,)),
            dma((n + 2,)), dma((n + 2,)), dma((2,)), dma((2,)),
        ],
        compiler_params=pltpu.CompilerParams(collective_id=1, has_side_effects=True),
        name="front",
    )(orbitals, pairs, live[:, None])


def plan_kernel(every, offsets, plan, ups, downs, nups, ndowns):
    size, n = every.shape[0], every.shape[1]
    width = lax.axis_size("orb")
    me = lax.axis_index("grp") * width + lax.axis_index("orb")
    before, after = lax.rem(me + size - 1, size), lax.rem(me + 1, size)

    def clear(e, c):
        ups[e] = 0
        downs[e] = 0
        nups[e] = 0
        ndowns[e] = 0
        return c

    lax.fori_loop(0, size, clear, 0)

    def read(blk, r):
        i, j = every[blk, r, 0], every[blk, r, 1]
        bj = lax.div(j, n)
        is_up = bj == lax.rem(blk + 1, size)
        cross = bj != blk
        u = jnp.where(is_up, lax.rem(i, n), lax.rem(j, n))
        v = jnp.where(is_up, lax.rem(j, n), lax.rem(i, n))
        edge = jnp.where(is_up, blk, bj)
        return i, j, is_up, cross, u, v, edge, every[blk, r, 2] > 0

    def mark(p, c):
        blk, r = lax.div(p, n), lax.rem(p, n)
        i, j, is_up, cross, u, v, edge, on = read(blk, r)

        @pl.when(on & cross)
        def _():
            def put(bits, counts, x, free):
                bit = jnp.where(x == free, 0, lax.shift_left(1, x))
                had = bits[edge]
                bits[edge] = had | bit
                counts[edge] = counts[edge] + ((bit != 0) & ((had & bit) == 0)).astype(jnp.int32)

            put(ups, nups, u, n - 1)
            put(downs, ndowns, v, 0)

        return c

    lax.fori_loop(0, size * n, mark, 0)

    def widest(kind):
        def step(e, m):
            o = lax.rem(e, width)
            mine = jnp.where(o % 2 == 0, 2, jnp.where(o == width - 1, 1, 0))
            most = jnp.maximum(nups[e], ndowns[e])
            return jnp.maximum(m, jnp.where(mine == kind, most, 0))

        return lax.fori_loop(0, size, step, jnp.int32(0))

    for kind in range(3):
        plan[INFO + kind] = widest(kind)

    def listing(bits, base):
        def step(q, s):
            has = (lax.shift_right_logical(bits, q) & 1) > 0
            plan[base + jnp.where(has, s, n)] = q
            return s + has.astype(jnp.int32)

        return lax.fori_loop(0, n, step, jnp.int32(0))

    def wipe(s, c):
        plan[LISTS + s] = 0
        return c

    lax.fori_loop(0, 4 * n, wipe, 0)
    listing(ups[me], LISTS)
    listing(downs[before], LISTS + 2 * n)
    plan[INFO + 3] = nups[before]
    plan[INFO + 4] = ndowns[me]

    def blank(s, c):
        plan[s * TASK] = 0
        plan[s * TASK + 1] = 0
        plan[s * TASK + 2] = 0
        plan[s * TASK + 3] = 0
        plan[s * TASK + 4] = n
        plan[s * TASK + 5] = n
        return c

    lax.fori_loop(0, LISTS // TASK, blank, 0)

    def rank(bits, x):
        def step(q, s):
            return s + jnp.where(q < x, lax.shift_right_logical(bits, q) & 1, 0)

        return lax.fori_loop(0, n, step, jnp.int32(0))

    def place_of(x):
        blk, loc = lax.div(x, n), lax.rem(x, n)
        from_before = jnp.where(loc == n - 1, n, n + 2 + rank(ups[before], loc))
        from_after = jnp.where(loc == 0, n + 1, n + 2 + n - 1 + rank(downs[me], loc))
        return jnp.where(blk == me, loc, jnp.where(blk == before, from_before, from_after))

    def sweep(ready, blk, first, last, count):
        def step(r, s):
            i, j, is_up, cross, u, v, edge, on = read(blk, r)
            above = edge == me
            touch = on & (jnp.logical_not(cross) | above | (edge == before))
            free = jnp.logical_not(cross) | jnp.where(above, v == 0, u == n - 1)
            want = touch & (free == ready)

            @pl.when(want)
            def _():
                plan[s * TASK] = place_of(i)
                plan[s * TASK + 1] = place_of(j)
                plan[s * TASK + 2] = offsets[j, 0] - offsets[i, 0]
                plan[s * TASK + 3] = offsets[j, 1] - offsets[i, 1]
                plan[s * TASK + 4] = jnp.where(lax.div(i, n) == me, lax.rem(i, n), n)
                plan[s * TASK + 5] = jnp.where(lax.div(j, n) == me, lax.rem(j, n), n)

            return s + want.astype(jnp.int32)

        return lax.fori_loop(first, last, step, count)

    def around(ready, blk, first, last, count):
        def step(r, s):
            return sweep(ready, blk, r, r + 1, s)

        def maybe(r, s):
            j = every[blk, r, 1]
            return lax.cond(lax.div(j, n) == me, lambda: step(r, s), lambda: s)

        return lax.fori_loop(first, last, maybe, count)

    count = jnp.int32(0)
    for ready in (True, False):
        count = sweep(ready, me, 0, n, count)
        count = around(ready, before, 0, n, count)
        count = around(ready, after, 0, n, count)
        plan[INFO + (5 if ready else 6)] = count


def make_plan(every, offsets):
    size = every.shape[0]
    smem = pl.BlockSpec(memory_space=pltpu.SMEM)
    return pl.pallas_call(
        plan_kernel,
        in_specs=[smem, smem],
        out_specs=smem,
        out_shape=jax.ShapeDtypeStruct((PLAN,), jnp.int32),
        scratch_shapes=[pltpu.SMEM((size,), jnp.int32)] * 4,
        name="plan",
    )(every, offsets)


def pick_kernel(plan, src_a, src_b, dst_a, dst_b):
    dst_a[...] = src_a[...]
    dst_b[...] = src_b[...]


def pick(plan, fields, n, m):
    _, rows, y, w = fields.shape
    blk = (1, rows, y, w)
    out = jax.ShapeDtypeStruct((m, rows, y, w), F32)
    return pl.pallas_call(
        pick_kernel,
        grid_spec=pltpu.PrefetchScalarGridSpec(
            num_scalar_prefetch=1,
            grid=(m,),
            in_specs=[
                pl.BlockSpec(blk, lambda i, plan: (plan[LISTS + i], 0, 0, 0)),
                pl.BlockSpec(blk, lambda i, plan: (plan[LISTS + 2 * n + i], 0, 0, 0)),
            ],
            out_specs=[pl.BlockSpec(blk, lambda i, plan: (i, 0, 0, 0))] * 2,
        ),
        out_shape=[out, out],
        name="pick",
    )(plan, fields, fields)


def swap_kernel(counts, up, down, prior, nxt, send, recv):
    size, width = lax.axis_size(CYCLE), lax.axis_size("orb")
    o = lax.axis_index("orb")
    me = lax.axis_index("grp") * width + o

    def peer(s):
        to = lax.rem(me + s, size)
        return {"grp": lax.div(to, width), "orb": lax.rem(to, width)}

    def kind(q):
        return jnp.where(q % 2 == 0, 2, jnp.where(q == width - 1, 1, 0))

    above, under = kind(o), kind(lax.rem(o + width - 1, width))
    barrier = pltpu.get_barrier_semaphore()
    for s in (1, size - 1):
        pl.semaphore_signal(
            barrier, inc=1, device_id=peer(s), device_id_type=pl.DeviceIdType.MESH
        )
    pl.semaphore_wait(barrier, 2)

    def copy(way, r):
        src, dst, s = ((up, prior, 1), (down, nxt, size - 1))[way]
        return pltpu.make_async_remote_copy(
            src_ref=src.at[r], dst_ref=dst.at[r],
            send_sem=send.at[way, r], recv_sem=recv.at[way, r],
            device_id=peer(s), device_id_type=pl.DeviceIdType.MESH,
        )

    for r in range(up.shape[0]):
        for way, mine in ((0, above), (1, under)):
            for c in range(3):
                if r < counts[c]:
                    pl.when(mine == c)(lambda way=way, r=r: copy(way, r).start())
    for r in range(up.shape[0]):
        for way, out, into in ((0, above, under), (1, under, above)):
            for c in range(3):
                if r < counts[c]:
                    pl.when(out == c)(lambda way=way, r=r: copy(way, r).wait_send())
                    pl.when(into == c)(lambda way=way, r=r: copy(way, r).wait_recv())


def swap(counts, up, down, most, cid):
    hbm = pl.BlockSpec(memory_space=pl.ANY)
    out = jax.ShapeDtypeStruct((most,) + up.shape[1:], F32)
    m = up.shape[0]
    return pl.pallas_call(
        functools.partial(swap_kernel, counts),
        in_specs=[hbm, hbm],
        out_specs=[hbm, hbm],
        out_shape=[out, out],
        scratch_shapes=[pltpu.SemaphoreType.DMA((2, m)), pltpu.SemaphoreType.DMA((2, m))],
        compiler_params=pltpu.CompilerParams(collective_id=cid, has_side_effects=True),
        name="swap%d%d%d" % counts,
    )(up, down)


def pairs_kernel(
    plan, fields, prior, nxt, out, room, one, two, own2, par2, prod, acc, stage, sem, out_sem
):
    n, h, y, z = out.shape
    w = 2 * z
    half, each = h // 2, fields.shape[1]
    rows = each // y
    halo = rows - half
    most = prior.shape[0]
    slab = lax.axis_index("slab")
    quads, line, scale = factors()

    def field(src, s, f):
        return pltpu.make_async_copy(
            src.at[s], room.at[pl.ds(PAD + f * each, each)], sem.at[f]
        )

    def each_field(do):
        for f in range(n + 2):
            do(field(fields, f, f))
        for src, base, count in ((prior, n + 2, plan[INFO + 3]), (nxt, n + 2 + most, plan[INFO + 4])):
            for s in range(most):
                pl.when(s < count)(lambda src=src, s=s, base=base: do(field(src, s, base + s)))

    each_field(lambda c: c.start())
    acc[...] = jnp.zeros(acc.shape, F32)
    prod[0:PAD, :] = jnp.zeros((PAD, w), F32)
    prod[PAD + h * y :, :] = jnp.zeros((PAD, w), F32)
    for ref in (one, two):
        planes = ref.shape[0]
        ref[0] = jnp.zeros(ref.shape[1:], F32)
        ref[:, 0:8, :] = jnp.zeros((planes, 8, w), F32)
        ref[:, 8 + y :, :] = jnp.zeros((planes, 8, w), F32)
    each_field(lambda c: c.wait())

    lane = lanes((y, w))
    low = lane < z
    pos = lane % z
    line_y = lax.broadcasted_iota(jnp.int32, (y, w), 0)
    not_low, not_high = pos > 0, pos < z - 1

    def sweep(src, count, emit):
        def step(g, carry):
            prev, cur = carry
            for q in range(2):
                t = g * 2 + q
                nxt_ = src[t + 2, 8 : 8 + y, :]
                near = (prev + nxt_) + (src[t + 1, 7 : 7 + y, :] + src[t + 1, 9 : 9 + y, :])
                side = jnp.where(not_low, pltpu.roll(cur, 1, axis=1), 0.0)
                side = side + jnp.where(not_high, pltpu.roll(cur, w - 1, axis=1), 0.0)
                emit(t, cur, near + side)
                prev, cur = cur, nxt_
            return prev, cur

        lax.fori_loop(0, count // 2, step, (jnp.zeros((y, w), F32), src[1, 8 : 8 + y, :]))

    def group(g, c):
        p, q = g * 2 * TASK, (g * 2 + 1) * TASK
        rp, rq = plan[p] * each + PAD, plan[q] * each + PAD
        ap, aq, bp, bq = plan[p + 2], plan[q + 2], plan[p + 3], plan[q + 3]
        sp, sq = plan[p + 1] * each + PAD - ap, plan[q + 1] * each + PAD - aq
        fit_y = line_y - jnp.where(low, ap, aq)
        fit_z = pos - jnp.where(low, bp, bq)
        fits = (fit_y >= 0) & (fit_y < y) & (fit_z >= 0) & (fit_z < z)
        turn_p, turn_q = lax.rem(bp + w, w), lax.rem(bq + w, w)

        def dense(r, c):
            own_p, own_q = room[pl.ds(rp + r * y, y), :], room[pl.ds(rq + r * y, y), :]
            par_p, par_q = room[pl.ds(sp + r * y, y), :], room[pl.ds(sq + r * y, y), :]
            par_p, par_q = pltpu.roll(par_p, turn_p, axis=1), pltpu.roll(par_q, turn_q, axis=1)
            own_a = jnp.where(low, own_p, pltpu.roll(own_q, z, axis=1))
            own_b = jnp.where(low, pltpu.roll(own_p, z, axis=1), own_q)
            par_a = jnp.where(fits, jnp.where(low, par_p, pltpu.roll(par_q, z, axis=1)), 0.0)
            par_b = jnp.where(fits, jnp.where(low, pltpu.roll(par_p, z, axis=1), par_q), 0.0)
            ta = jnp.where(r < half, r, r + half)
            tb = jnp.where(r < half, r + half, r + half + halo)
            one[ta + 1, 8 : 8 + y, :] = own_a * par_a * scale
            one[tb + 1, 8 : 8 + y, :] = own_b * par_b * scale
            own2[ta] = own_a
            own2[tb] = own_b
            par2[ta] = par_a
            par2[tb] = par_b
            return c

        lax.fori_loop(0, rows, dense, 0)

        count = h + EDGE - 1
        for b, c2 in quads:
            def first(t, cur, near, b=b):
                two[t + 1, 8 : 8 + y, :] = near + b * cur

            def second(t, cur, near, c2=c2):
                one[t + 1, 8 : 8 + y, :] = near + c2 * one[t + 1, 8 : 8 + y, :]

            sweep(one, count, first)
            sweep(two, count, second)
            count -= 2

        kp, kq, mp, mq = plan[p + 4], plan[q + 4], plan[p + 5], plan[q + 5]

        def finish(t, cur, near):
            pot = near + line * cur
            gain = pot * par2[t]
            acc[kp, t] += jnp.where(low, gain, 0.0)
            acc[kq, t] += jnp.where(low, 0.0, gain)
            prod[pl.ds(PAD + t * y, y), :] = pot * own2[t]

        sweep(one, h, finish)

        for m, a, b, side in ((mp, ap, bp, low), (mq, aq, bq, jnp.logical_not(low))):
            @pl.when(m < n)
            def _(m=m, a=a, b=b, side=side):
                back_y, back_z = line_y + a, pos + b
                good = side & (back_y >= 0) & (back_y < y) & (back_z >= 0) & (back_z < z)
                turn = lax.rem(w - b, w)

                def plane(t, c):
                    moved = pltpu.roll(prod[pl.ds(PAD + t * y + a, y), :], turn, axis=1)
                    acc[m, t] += jnp.where(good, moved, 0.0)
                    return c

                lax.fori_loop(0, h, plane, 0)

        return c

    tasks = plan[INFO + 6]
    lax.fori_loop(0, lax.div(tasks + 1, 2), group, 0)

    def leave(k, slot):
        return pltpu.make_async_copy(stage.at[slot], out.at[k], out_sem.at[slot])

    def write(k, c):
        slot = lax.rem(k, 2)
        pl.when(k >= 2)(lambda: leave(k - 2, slot).wait())

        def plane(t, c):
            value = acc[k, t]
            value = value + pltpu.roll(value, z, axis=1)
            stage[slot, jnp.where(slab == 0, t, h - 1 - t)] = value[:, :z]
            return c

        lax.fori_loop(0, h, plane, 0)
        leave(k, slot).start()
        return c

    lax.fori_loop(0, n, write, 0)
    for k in (n - 2, n - 1):
        leave(k, k % 2).wait()


def solve_pairs(plan, fields, prior, nxt, shape):
    n, h, y, z = shape
    w, rows = 2 * z, fields.shape[1]
    most = prior.shape[0]
    flat = lambda f: f.reshape(f.shape[0], rows * y, w)
    hbm = pl.BlockSpec(memory_space=pl.ANY)
    total = n + 2 + 2 * most
    planes = 2 * rows
    return pl.pallas_call(
        pairs_kernel,
        grid_spec=pltpu.PrefetchScalarGridSpec(
            num_scalar_prefetch=1,
            grid=(1,),
            in_specs=[hbm, hbm, hbm],
            out_specs=hbm,
            scratch_shapes=[
                pltpu.VMEM((total * rows * y + 2 * PAD, w), F32),
                pltpu.VMEM((planes + 2, y + 16, w), F32),
                pltpu.VMEM((planes + 2, y + 16, w), F32),
                pltpu.VMEM((planes, y, w), F32),
                pltpu.VMEM((planes, y, w), F32),
                pltpu.VMEM((h * y + 2 * PAD, w), F32),
                pltpu.VMEM((n + 1, h, y, w), F32),
                pltpu.VMEM((2, h, y, z), F32),
                pltpu.SemaphoreType.DMA((total,)),
                pltpu.SemaphoreType.DMA((2,)),
            ],
        ),
        out_shape=jax.ShapeDtypeStruct(shape, F32),
        compiler_params=pltpu.CompilerParams(vmem_limit_bytes=56 * 1024 * 1024),
        name="pairs",
    )(plan, flat(fields), flat(prior), flat(nxt))


def fast_body(orbitals, offsets, pairs, live):
    n = orbitals.shape[0]
    most = n - 1
    fields, every = front(orbitals, pairs, live)
    plan = make_plan(every, offsets)

    combos = [(a, b, 4) for a in range(5) for b in range(5)] + [(most, most, most)]

    def branch(counts, cid):
        def run(_):
            m = max(counts)
            up, down = pick(plan, fields, n, m)
            return swap(counts, up, down, most, cid)

        return run

    ka, kb, kc = plan[INFO], plan[INFO + 1], plan[INFO + 2]
    big = jnp.maximum(jnp.maximum(ka, kb), kc) > 4
    which = jnp.where(big, len(combos) - 1, ka * 5 + kb)
    prior, nxt = lax.switch(which, [branch(c, 2 + i) for i, c in enumerate(combos)], 0)
    return solve_pairs(plan, fields, prior, nxt, orbitals.shape)


def body(orbitals, offsets, pairs, live):
    n = orbitals.shape[0]
    slots = pairs.shape[0]
    total = offsets.shape[0]
    blocks = total // n
    slabs = lax.axis_size("slab")
    me = lax.axis_index(CYCLE)
    packed = pack(orbitals)

    mine = jnp.concatenate([pairs, live[:, None]], axis=1)
    every = share(jnp.pad(mine, ((0, 0), (0, 128 - mine.shape[1]))))
    ids = jnp.arange(blocks, dtype=jnp.int32)
    second = every[:, :, 1]
    alive = every[:, :, 2] > 0
    orb = jnp.arange(n, dtype=jnp.int32)
    sides = jnp.stack([(ids - 1) % blocks, (ids + 1) % blocks])
    hit = alive[None] & (second[None] // n == sides[:, :, None])
    need = jnp.any(
        hit[..., None] & (second[None, :, :, None] % n == orb), axis=2
    )
    count = jnp.sum(need.astype(jnp.int32), axis=2)
    most = jnp.max(count)

    after, before = (me + 1) % blocks, (me - 1) % blocks
    flags = jnp.stack(
        [need[0, me], need[1, me], need[0, after], need[1, before]]
    ).astype(jnp.int32)
    spot = jnp.sum(
        flags[:, None, :] * (orb[None, :] < orb[:, None]).astype(jnp.int32)[None], axis=2
    )
    lists = jnp.sum(
        (flags[:, None, :] * (spot[:, None, :] == orb[None, :, None])) * orb, axis=2
    )
    back = jnp.stack(
        [spot[2] * flags[2], flags[2], spot[3] * flags[3], flags[3]]
    )

    i, j, on = pairs[:, 0], pairs[:, 1], live > 0
    owner, local = j // n, j % n
    pick_j = (local[:, None] == orb[None, :]).astype(jnp.int32)
    from_prior = (owner == before) & on
    from_next = (owner == after) & on
    kind = jnp.where(from_prior, 1, jnp.where(from_next, 2, 0))
    where_prior = jnp.sum(pick_j * spot[0][None, :], axis=1) * from_prior
    where_next = jnp.sum(pick_j * spot[1][None, :], axis=1) * from_next
    ids_all = jnp.arange(total, dtype=jnp.int32)
    diff = (j[:, None] == ids_all).astype(jnp.int32) - (i[:, None] == ids_all).astype(jnp.int32)
    shift = jnp.sum(diff[:, :, None] * offsets[None], axis=1)
    plan = jnp.stack(
        [i % n, local, where_prior, where_next, kind, shift[:, 0], shift[:, 1], live]
    ).astype(jnp.int32)
    order = jnp.where(on, jnp.where(kind > 0, 0, 1), 2) * slots + jnp.arange(slots)
    rank = jnp.sum((order[None, :] < order[:, None]).astype(jnp.int32), axis=1)
    move = (rank[:, None] == jnp.arange(slots)[None, :]).astype(jnp.int32)
    plan = jnp.sum(plan[:, :, None] * move[None], axis=1)
    far, lively = jnp.sum((kind > 0).astype(jnp.int32)), jnp.sum(on.astype(jnp.int32))
    tail = jnp.where(jnp.arange(slots) == 0, far, lively)
    plan = jnp.concatenate([plan, tail[None]], axis=0)
    ends = jnp.stack([lax.axis_index("slab"), slabs]).astype(jnp.int32)

    up = [(s, s + 1) for s in range(slabs - 1)]
    down = [(s + 1, s) for s in range(slabs - 1)]

    def branch(m):
        def run(_):
            to_next, to_prior = gather(packed, lists[2:], m)
            prior = cycle(to_next, 1)
            nxt = cycle(to_prior, -1)
            partner, density, low, high = densities(plan, packed, prior, nxt)
            below = lax.ppermute(high, "slab", up)
            above = lax.ppermute(low, "slab", down)
            given = (plan, ends, density, partner, packed, below, above, m)
            acc, acc_prior, acc_next = solve(True, *given)
            from_next, from_prior = cycle(acc_prior, -1), cycle(acc_next, 1)
            (acc_near,) = solve(False, *given)
            return combine(back, acc, acc_near, from_next, from_prior)

        return run

    sizes = sorted({min(s, slots - 1) for s in (3, 4, 5)} | {slots - 1})
    which = sum((most > s).astype(jnp.int32) for s in sizes[:-1])
    return lax.switch(which, [branch(s) for s in sizes], 0)


def solution(mesh):
    placed = (
        P(CYCLE, "slab", None, None),
        P(),
        P(CYCLE, None),
        P(CYCLE),
    )
    return jax.shard_map(
        fast_body if mesh.shape["slab"] == 2 else body,
        mesh=mesh,
        in_specs=placed,
        out_specs=P(CYCLE, "slab", None, None),
        check_vma=False,
    )
```

```python
import cmath
import functools
import math

import jax
import jax.numpy as jnp
import numpy as np
from jax import lax
from jax.experimental import pallas as pl
from jax.experimental.pallas import tpu as pltpu
from jax.sharding import PartitionSpec as P

PASSES = 8
DIAG = 6.25
THETA = 1.075
DELTA = 0.925
EDGE = PASSES - 1
PAD = 16
CYCLE = ("grp", "orb")
F32 = jnp.float32


def coefs():
    sigma = THETA / DELTA
    coef = 1.0 / sigma
    out = []
    for _ in range(PASSES - 1):
        new = 1.0 / (2.0 * sigma - coef)
        out.append((new * coef, 2.0 * new / (DELTA * DIAG)))
        coef = new
    return out


def lanes(shape):
    return lax.broadcasted_iota(jnp.int32, shape, len(shape) - 1)


def share_kernel(mine, every, send_sem, recv_sem):
    size, width = lax.axis_size(CYCLE), lax.axis_size("orb")
    me = lax.axis_index("grp") * width + lax.axis_index("orb")

    def peer(s):
        to = lax.rem(me + s, size)
        return {"grp": lax.div(to, width), "orb": lax.rem(to, width)}

    def greet(s, c):
        pl.semaphore_signal(
            barrier, inc=1, device_id=peer(s), device_id_type=pl.DeviceIdType.MESH
        )
        return c

    def copy(s, slot):
        return pltpu.make_async_remote_copy(
            src_ref=mine,
            dst_ref=every.at[slot],
            send_sem=send_sem.at[s],
            recv_sem=recv_sem.at[s],
            device_id=peer(s),
            device_id_type=pl.DeviceIdType.MESH,
        )

    def send(s, c):
        copy(s, me).start()
        return c

    def finish(s, c):
        copy(s, lax.rem(me + size - s, size)).wait()
        return c

    barrier = pltpu.get_barrier_semaphore()
    lax.fori_loop(1, size, greet, 0)
    pl.semaphore_wait(barrier, size - 1)
    lax.fori_loop(1, size, send, 0)
    every[me] = mine[...]
    lax.fori_loop(1, size, finish, 0)


def share(mine):
    size = lax.axis_size(CYCLE)
    vmem = pl.BlockSpec(memory_space=pltpu.VMEM)
    return pl.pallas_call(
        share_kernel,
        in_specs=[vmem],
        out_specs=vmem,
        out_shape=jax.ShapeDtypeStruct((size,) + mine.shape, mine.dtype),
        scratch_shapes=[pltpu.SemaphoreType.DMA((size,)), pltpu.SemaphoreType.DMA((size,))],
        compiler_params=pltpu.CompilerParams(collective_id=0, has_side_effects=True),
        name="share",
    )(mine)


def pack_kernel(src, dst):
    half = dst.shape[1]
    dst[0] = jnp.concatenate([src[0, :half], src[0, half:]], axis=-1)


def pack(orbitals):
    n, x, y, z = orbitals.shape
    return pl.pallas_call(
        pack_kernel,
        grid=(n,),
        in_specs=[pl.BlockSpec((1, x, y, z), lambda i: (i, 0, 0, 0))],
        out_specs=pl.BlockSpec((1, x // 2, y, 2 * z), lambda i: (i, 0, 0, 0)),
        out_shape=jax.ShapeDtypeStruct((n, x // 2, y, 2 * z), F32),
        name="pack",
    )(orbitals)


def copy_kernel(idx, src_a, src_b, dst_a, dst_b):
    dst_a[...] = src_a[...]
    dst_b[...] = src_b[...]


def gather(packed, lists, m):
    _, h, y, w = packed.shape
    blk = (1, h, y, w)
    out = jax.ShapeDtypeStruct((m, h, y, w), F32)
    return pl.pallas_call(
        copy_kernel,
        grid_spec=pltpu.PrefetchScalarGridSpec(
            num_scalar_prefetch=1,
            grid=(m,),
            in_specs=[
                pl.BlockSpec(blk, lambda i, idx: (idx[0, i], 0, 0, 0)),
                pl.BlockSpec(blk, lambda i, idx: (idx[1, i], 0, 0, 0)),
            ],
            out_specs=[pl.BlockSpec(blk, lambda i, idx: (i, 0, 0, 0))] * 2,
        ),
        out_shape=[out, out],
        name="gather",
    )(lists, packed, packed)


def place(value, room, a, b):
    y, w = value.shape[1:]
    z = w // 2
    room[:, PAD : PAD + y, :] = value
    moved = room[:, pl.ds(PAD - a, y), :]
    moved = pltpu.roll(moved, lax.rem(b + w, w), axis=2)
    pos = lanes(moved.shape) % z - b
    return jnp.where((pos >= 0) & (pos < z), moved, 0.0)


def clear_room(room):
    y = room.shape[1] - 2 * PAD
    room[:, :PAD, :] = jnp.zeros((room.shape[0], PAD, room.shape[2]), F32)
    room[:, PAD + y :, :] = jnp.zeros((room.shape[0], PAD, room.shape[2]), F32)


def density_kernel(plan, own, mine, prior, nxt, partner, density, low, high, room):
    p = pl.program_id(0)
    kind = plan[4, p]
    a, b = plan[5, p], plan[6, p]

    @pl.when(p == 0)
    def _():
        clear_room(room)

    on = plan[7, p] > 0

    def go(src):
        part = place(src[0], room, a, b)
        partner[0] = part
        dens = own[0] * part
        density[0] = dens
        h, y, w = dens.shape
        flat = jnp.concatenate([dens[..., : w // 2], dens[..., w // 2 :]], axis=0)
        top, bot = flat[:EDGE], flat[2 * h - EDGE :]
        low[0] = jnp.concatenate([top[:, : y // 2], top[:, y // 2 :]], axis=-1)
        high[0] = jnp.concatenate([bot[:, : y // 2], bot[:, y // 2 :]], axis=-1)

    for value, src in enumerate((mine, prior, nxt)):
        pl.when(on & (kind == value))(functools.partial(go, src))


def densities(plan, packed, prior, nxt):
    slots = plan.shape[1]
    _, h, y, w = packed.shape
    blk = (1, h, y, w)
    eblk = (1, EDGE, y // 2, w)

    def at(row):
        return pl.BlockSpec(
            blk, lambda i, plan: (plan[row, jnp.minimum(i, plan[8, 1] - 1)], 0, 0, 0)
        )

    full = jax.ShapeDtypeStruct((slots, h, y, w), F32)
    edge = jax.ShapeDtypeStruct((slots,) + eblk[1:], F32)
    here = lambda i, plan: (jnp.minimum(i, plan[8, 1] - 1), 0, 0, 0)
    return pl.pallas_call(
        density_kernel,
        grid_spec=pltpu.PrefetchScalarGridSpec(
            num_scalar_prefetch=1,
            grid=(slots,),
            in_specs=[at(0), at(1), at(2), at(3)],
            out_specs=[
                pl.BlockSpec(blk, here),
                pl.BlockSpec(blk, here),
                pl.BlockSpec(eblk, here),
                pl.BlockSpec(eblk, here),
            ],
            scratch_shapes=[pltpu.VMEM((h, y + 2 * PAD, w), F32)],
        ),
        out_shape=[full, full, edge, edge],
        name="density",
    )(plan, packed, packed, prior, nxt)


def solve_kernel(remote, plan, ends, density, partner, own, below, above, *refs):
    accs, (resid, step_a, step_b, total, mask, room) = refs[:-6], refs[-6:]
    acc = accs[0]
    p = pl.program_id(0)
    h, y, w = density.shape[1:]
    z = w // 2
    rows = h + 2 * EDGE
    group = 4 if h % 4 == 0 else 1

    @pl.when(p == 0)
    def _():
        clear_room(room)
        for ref in accs:
            ref[...] = jnp.zeros(ref.shape, F32)
        for ref in (step_a, step_b):
            ref[:, :8, :] = jnp.zeros((rows, 8, w), F32)
            ref[:, 8 + y :, :] = jnp.zeros((rows, 8, w), F32)
        lane = lanes((1, w))
        first = ends[0] == 0
        last = ends[0] == ends[1] - 1
        for t in range(rows):
            plane = jnp.where(lane < z, t - EDGE, t - EDGE + h)
            outside = ((plane < 0) & first) | ((plane >= 2 * h) & last)
            mask[t] = jnp.where(outside, 0.0, 1.0)

    chosen = (plan[4, p] > 0) if remote else (plan[4, p] == 0)

    @pl.when((plan[7, p] > 0) & chosen)
    def _():
        def unfold(part):
            return jnp.concatenate([part[..., :z], part[..., z:]], axis=1)

        dens = density[0]
        line = jnp.concatenate(
            [unfold(below[0]), dens[..., :z], dens[..., z:], unfold(above[0])], axis=0
        )
        resid[...] = jnp.concatenate([line[:rows], line[h:]], axis=-1)
        step_a[:, 8 : 8 + y, :] = resid[...] * (1.0 / (DIAG * THETA))
        total[...] = step_a[EDGE : EDGE + h, 8 : 8 + y, :]
        lane = lanes((y, w)) % z
        not_low = lane > 0
        not_high = lane < z - 1
        bufs = [step_a, step_b]
        for turn, (keep, gain) in enumerate(coefs()):
            now, then = bufs[turn % 2], bufs[1 - turn % 2]
            core_only = turn == PASSES - 2

            def row(t, now=now, then=then, keep=keep, gain=gain):
                core = now[t, 8 : 8 + y, :]
                near = now[t - 1, 8 : 8 + y, :] + now[t + 1, 8 : 8 + y, :]
                near = near + (now[t, 7 : 7 + y, :] + now[t, 9 : 9 + y, :])
                side = jnp.where(not_low, pltpu.roll(core, 1, axis=1), 0.0)
                side = side + jnp.where(not_high, pltpu.roll(core, w - 1, axis=1), 0.0)
                left = (resid[t] - DIAG * core) + (near + side)
                return left, keep * core + gain * left

            def outer(k, c, row=row, then=then):
                for t in (EDGE - 1 - k, EDGE + h + k):
                    left, fresh = row(t)
                    resid[t] = left
                    then[t, 8 : 8 + y, :] = fresh * mask[t]
                return c

            def inner(k, c, row=row, then=then, last=core_only):
                for g in range(group):
                    t = EDGE + k * group + g
                    left, fresh = row(t)
                    if not last:
                        resid[t] = left
                        then[t, 8 : 8 + y, :] = fresh
                    total[t - EDGE] += fresh
                return c

            if turn + 1 < EDGE:
                lax.fori_loop(0, EDGE - turn - 1, outer, 0)
            lax.fori_loop(0, h // group, inner, 0)

        pot = total[...]
        acc[plan[0, p]] += pot * partner[0]
        back = place(pot * own[0], room, -plan[5, p], -plan[6, p])
        if not remote:
            acc[plan[1, p]] += back
        else:
            for value in (1, 2):

                @pl.when(plan[4, p] == value)
                def _(ref=accs[value], value=value):
                    ref[plan[1 + value, p]] += back


def solve(remote, plan, ends, density, partner, packed, below, above, m):
    slots = plan.shape[1]
    n, h, y, w = packed.shape
    blk = (1, h, y, w)
    eblk = (1, EDGE, y // 2, w)
    rows = h + 2 * EDGE

    def spot(i, plan):
        far = plan[8, 0]
        if remote:
            return jnp.minimum(i, jnp.maximum(far - 1, 0))
        return jnp.clip(i, jnp.minimum(far, plan[8, 1] - 1), plan[8, 1] - 1)

    here = lambda i, plan, ends: (spot(i, plan), 0, 0, 0)
    fixed = lambda i, plan, ends: (0, 0, 0, 0)
    shapes = [(n, h, y, w)] + [(m, h, y, w)] * (2 if remote else 0)
    return pl.pallas_call(
        functools.partial(solve_kernel, remote),
        grid_spec=pltpu.PrefetchScalarGridSpec(
            num_scalar_prefetch=2,
            grid=(slots,),
            in_specs=[
                pl.BlockSpec(blk, here),
                pl.BlockSpec(blk, here),
                pl.BlockSpec(blk, lambda i, plan, ends: (plan[0, spot(i, plan)], 0, 0, 0)),
                pl.BlockSpec(eblk, here),
                pl.BlockSpec(eblk, here),
            ],
            out_specs=[pl.BlockSpec(s, fixed) for s in shapes],
            scratch_shapes=[
                pltpu.VMEM((rows, y, w), F32),
                pltpu.VMEM((rows, y + 16, w), F32),
                pltpu.VMEM((rows, y + 16, w), F32),
                pltpu.VMEM((h, y, w), F32),
                pltpu.VMEM((rows, 1, w), F32),
                pltpu.VMEM((h, y + 2 * PAD, w), F32),
            ],
        ),
        out_shape=[jax.ShapeDtypeStruct(s, F32) for s in shapes],
        compiler_params=pltpu.CompilerParams(vmem_limit_bytes=56 * 1024 * 1024),
        cost_estimate=pl.CostEstimate(
            flops=slots * rows * y * w * 100, bytes_accessed=24 << 20, transcendentals=0
        ),
        name="solve_far" if remote else "solve_near",
    )(plan, ends, density, partner, packed, below, above)


def combine_kernel(back, acc, acc_near, from_next, from_prior, out):
    k = pl.program_id(0)
    h = acc.shape[1]
    z = acc.shape[3] // 2
    value = acc[0] + acc_near[0]
    value = value + jnp.where(back[1, k] > 0, from_next[0], 0.0)
    value = value + jnp.where(back[3, k] > 0, from_prior[0], 0.0)
    out[0, :h] = value[:, :, :z]
    out[0, h:] = value[:, :, z:]


def combine(back, acc, acc_near, from_next, from_prior):
    n, h, y, w = acc.shape
    blk = (1, h, y, w)
    return pl.pallas_call(
        combine_kernel,
        grid_spec=pltpu.PrefetchScalarGridSpec(
            num_scalar_prefetch=1,
            grid=(n,),
            in_specs=[
                pl.BlockSpec(blk, lambda i, back: (i, 0, 0, 0)),
                pl.BlockSpec(blk, lambda i, back: (i, 0, 0, 0)),
                pl.BlockSpec(blk, lambda i, back: (back[0, i], 0, 0, 0)),
                pl.BlockSpec(blk, lambda i, back: (back[2, i], 0, 0, 0)),
            ],
            out_specs=pl.BlockSpec((1, 2 * h, y, w // 2), lambda i, back: (i, 0, 0, 0)),
        ),
        out_shape=jax.ShapeDtypeStruct((n, 2 * h, y, w // 2), F32),
        name="combine",
    )(back, acc, acc_near, from_next, from_prior)


def cycle(field, by):
    size = lax.axis_size(CYCLE)
    return lax.ppermute(field, CYCLE, [(i, (i + by) % size) for i in range(size)])


TASK = 8
LISTS = 256
INFO = 320
PLAN = 384
UNROLL = 4
DEPTH = 5
STRIP = 8


def factors():
    ratio = THETA / DELTA
    tall = math.acosh(ratio)
    points = [cmath.cosh(complex(tall, k * math.pi / 4)) for k in range(8)]
    marks = [DIAG * (1.0 - (THETA - DELTA * x)) for x in points]
    quads = [(-2.0 * marks[k].real, abs(marks[k]) ** 2) for k in (1, 2, 3)]
    line = -marks[4].real
    coef, resid, value, step = 1.0 / ratio, 1.0, 0.0, 1.0 / (DIAG * THETA)
    value += step
    for keep, gain in coefs():
        resid -= DIAG * step
        step = keep * step + gain * resid
        value += step
    product = line
    for _, c in quads:
        product *= c
    return quads, line, value / product


def front_kernel(
    orbs, pairs, live, fields, every, stage, own, far, edge, table,
    in_sem, out_sem, tab_send, tab_recv, edge_send, edge_recv, far_send, far_recv,
):
    n, h = orbs.shape[0], orbs.shape[1]
    half = h // 2
    halo = edge.shape[1]
    size, width = lax.axis_size(CYCLE), lax.axis_size("orb")
    me = lax.axis_index("grp") * width + lax.axis_index("orb")
    slab = lax.axis_index("slab")

    def peer(s):
        to = lax.rem(me + s, size)
        return {"grp": lax.div(to, width), "orb": lax.rem(to, width)}

    def load(k):
        return pltpu.make_async_copy(orbs.at[k], stage.at[k], in_sem.at[k])

    def order(q):
        return jnp.where(q == 0, 0, jnp.where(q == 1, n - 1, q - 1))

    def begin(q, c):
        load(order(q)).start()
        return c

    lax.fori_loop(0, n, begin, 0)

    barrier = pltpu.get_barrier_semaphore()

    def greet(s, c):
        pl.semaphore_signal(
            barrier, inc=1, device_id=peer(s), device_id_type=pl.DeviceIdType.MESH
        )
        return c

    lax.fori_loop(1, size, greet, 0)
    pl.semaphore_signal(
        barrier, inc=1, device_id={"slab": 1 - slab}, device_id_type=pl.DeviceIdType.MESH
    )
    table[:, 0:2] = pairs[...]
    table[:, 2:3] = live[...]
    pl.semaphore_wait(barrier, size)

    def share_copy(s, slot):
        return pltpu.make_async_remote_copy(
            src_ref=table, dst_ref=every.at[slot],
            send_sem=tab_send.at[s], recv_sem=tab_recv.at[s],
            device_id=peer(s), device_id_type=pl.DeviceIdType.MESH,
        )

    def share_send(s, c):
        share_copy(s, me).start()
        return c

    lax.fori_loop(1, size, share_send, 0)
    every[me] = table[...]

    def edge_copy(f, dst):
        return pltpu.make_async_remote_copy(
            src_ref=edge.at[f], dst_ref=dst,
            send_sem=edge_send.at[f], recv_sem=edge_recv.at[f],
            device_id={"slab": 1 - slab}, device_id_type=pl.DeviceIdType.MESH,
        )

    def own_edge(k):
        return edge_copy(k, own.at[k, pl.ds(half, halo)])

    def far_copy(k, f, s):
        return pltpu.make_async_remote_copy(
            src_ref=own.at[k, pl.ds(0, half)], dst_ref=far.at[f, pl.ds(0, half)],
            send_sem=far_send.at[f], recv_sem=far_recv.at[f],
            device_id=peer(s), device_id_type=pl.DeviceIdType.MESH,
        )

    def spot(t):
        return jnp.where(slab == 0, t, h - 1 - t)

    def pack(k):
        def row(r, c):
            own[k, r] = jnp.concatenate(
                [stage[k, spot(r)], stage[k, spot(r + half)]], axis=-1
            )
            return c

        lax.fori_loop(0, half, row, 0)

    def make_edge(k):
        for m in range(halo):
            edge[k, m] = jnp.concatenate(
                [stage[k, spot(h - 1 - m)], stage[k, spot(h - 1 - halo - m)]], axis=-1
            )

    up, down = far_copy(n - 1, 0, 1), far_copy(0, 1, size - 1)
    load(0).wait()
    pack(0)
    down.start()
    make_edge(0)
    own_edge(0).start()
    load(n - 1).wait()
    pack(n - 1)
    up.start()
    make_edge(n - 1)
    own_edge(n - 1).start()

    def rest(k, c):
        load(k).wait()
        make_edge(k)
        own_edge(k).start()
        pack(k)
        return c

    lax.fori_loop(1, n - 1, rest, 0)

    def share_done(s, c):
        share_copy(s, lax.rem(me + size - s, size)).wait()
        return c

    lax.fori_loop(1, size, share_done, 0)

    low = lanes((1, own.shape[-1])) < own.shape[-1] // 2
    for f, copy in ((1, down), (0, up)):
        copy.wait()
        for m in range(halo):
            a, b = far[f, half - 1 - m], far[f, half - 1 - halo - m]
            edge[n + f, m] = jnp.where(low, pltpu.roll(a, a.shape[-1] // 2, axis=1), b)
        edge_copy(n + f, far.at[f, pl.ds(half, halo)]).start()

    def own_done(k, c):
        own_edge(k).wait()
        pltpu.make_async_copy(own.at[k], fields.at[k], out_sem.at[k]).start()
        return c

    lax.fori_loop(0, n, own_done, 0)
    for f in (1, 0):
        edge_copy(n + f, far.at[f, pl.ds(half, halo)]).wait()
        pltpu.make_async_copy(far.at[f], fields.at[n + f], out_sem.at[n + f]).start()

    def out_done(k, c):
        pltpu.make_async_copy(own.at[k], fields.at[k], out_sem.at[k]).wait()
        return c

    lax.fori_loop(0, n, out_done, 0)
    for f in (1, 0):
        pltpu.make_async_copy(far.at[f], fields.at[n + f], out_sem.at[n + f]).wait()


def front(orbitals, pairs, live):
    n, h, y, z = orbitals.shape
    half, halo, w = h // 2, (EDGE + 1) // 2, 2 * z
    size = lax.axis_size(CYCLE)
    vmem = pl.BlockSpec(memory_space=pltpu.VMEM)
    hbm = pl.BlockSpec(memory_space=pl.ANY)
    dma = pltpu.SemaphoreType.DMA
    return pl.pallas_call(
        front_kernel,
        in_specs=[hbm, vmem, vmem],
        out_specs=[hbm, vmem],
        out_shape=[
            jax.ShapeDtypeStruct((n + 2, half + halo, y, w), F32),
            jax.ShapeDtypeStruct((size, n, 128), jnp.int32),
        ],
        scratch_shapes=[
            pltpu.VMEM((n, h, y, z), F32),
            pltpu.VMEM((n, half + halo, y, w), F32),
            pltpu.VMEM((2, half + halo, y, w), F32),
            pltpu.VMEM((n + 2, halo, y, w), F32),
            pltpu.VMEM((n, 128), jnp.int32),
            dma((n,)), dma((n + 2,)), dma((size,)), dma((size,)),
            dma((n + 2,)), dma((n + 2,)), dma((2,)), dma((2,)),
        ],
        compiler_params=pltpu.CompilerParams(collective_id=1, has_side_effects=True),
        name="front",
    )(orbitals, pairs, live[:, None])


def plan_kernel(every, offsets, plan, ups, downs, nups, ndowns):
    size, n = every.shape[0], every.shape[1]
    width = lax.axis_size("orb")
    me = lax.axis_index("grp") * width + lax.axis_index("orb")
    before, after = lax.rem(me + size - 1, size), lax.rem(me + 1, size)

    def clear(e, c):
        ups[e] = 0
        downs[e] = 0
        nups[e] = 0
        ndowns[e] = 0
        return c

    lax.fori_loop(0, size, clear, 0)

    def read(blk, r):
        i, j = every[blk, r, 0], every[blk, r, 1]
        bj = lax.div(j, n)
        is_up = bj == lax.rem(blk + 1, size)
        cross = bj != blk
        u = jnp.where(is_up, lax.rem(i, n), lax.rem(j, n))
        v = jnp.where(is_up, lax.rem(j, n), lax.rem(i, n))
        edge = jnp.where(is_up, blk, bj)
        return i, j, is_up, cross, u, v, edge, every[blk, r, 2] > 0

    def mark(p, c):
        blk, r = lax.div(p, n), lax.rem(p, n)
        i, j, is_up, cross, u, v, edge, on = read(blk, r)

        @pl.when(on & cross)
        def _():
            def put(bits, counts, x, free):
                bit = jnp.where(x == free, 0, lax.shift_left(1, x))
                had = bits[edge]
                bits[edge] = had | bit
                counts[edge] = counts[edge] + ((bit != 0) & ((had & bit) == 0)).astype(jnp.int32)

            put(ups, nups, u, n - 1)
            put(downs, ndowns, v, 0)

        return c

    lax.fori_loop(0, size * n, mark, 0)

    def widest(kind):
        def step(e, m):
            o = lax.rem(e, width)
            mine = jnp.where(o % 2 == 0, 2, jnp.where(o == width - 1, 1, 0))
            most = jnp.maximum(nups[e], ndowns[e])
            return jnp.maximum(m, jnp.where(mine == kind, most, 0))

        return lax.fori_loop(0, size, step, jnp.int32(0))

    for kind in range(3):
        plan[INFO + kind] = widest(kind)

    def listing(bits, base):
        def step(q, s):
            has = (lax.shift_right_logical(bits, q) & 1) > 0
            plan[base + jnp.where(has, s, n)] = q
            return s + has.astype(jnp.int32)

        return lax.fori_loop(0, n, step, jnp.int32(0))

    def wipe(s, c):
        plan[LISTS + s] = 0
        return c

    lax.fori_loop(0, 4 * n, wipe, 0)
    listing(ups[me], LISTS)
    listing(downs[before], LISTS + 2 * n)
    plan[INFO + 3] = nups[before]
    plan[INFO + 4] = ndowns[me]

    def blank(s, c):
        plan[s * TASK] = 0
        plan[s * TASK + 1] = 0
        plan[s * TASK + 2] = 0
        plan[s * TASK + 3] = 0
        plan[s * TASK + 4] = n
        plan[s * TASK + 5] = n
        return c

    lax.fori_loop(0, LISTS // TASK, blank, 0)

    def rank(bits, x):
        def step(q, s):
            return s + jnp.where(q < x, lax.shift_right_logical(bits, q) & 1, 0)

        return lax.fori_loop(0, n, step, jnp.int32(0))

    def place_of(x):
        blk, loc = lax.div(x, n), lax.rem(x, n)
        from_before = jnp.where(loc == n - 1, n, n + 2 + rank(ups[before], loc))
        from_after = jnp.where(loc == 0, n + 1, n + 2 + n - 1 + rank(downs[me], loc))
        return jnp.where(blk == me, loc, jnp.where(blk == before, from_before, from_after))

    def sweep(ready, blk, first, last, count):
        def step(r, s):
            i, j, is_up, cross, u, v, edge, on = read(blk, r)
            above = edge == me
            touch = on & (jnp.logical_not(cross) | above | (edge == before))
            free = jnp.logical_not(cross) | jnp.where(above, v == 0, u == n - 1)
            want = touch & (free == ready)

            @pl.when(want)
            def _():
                plan[s * TASK] = place_of(i)
                plan[s * TASK + 1] = place_of(j)
                plan[s * TASK + 2] = offsets[j, 0] - offsets[i, 0]
                plan[s * TASK + 3] = offsets[j, 1] - offsets[i, 1]
                plan[s * TASK + 4] = jnp.where(lax.div(i, n) == me, lax.rem(i, n), n)
                plan[s * TASK + 5] = jnp.where(lax.div(j, n) == me, lax.rem(j, n), n)

            return s + want.astype(jnp.int32)

        return lax.fori_loop(first, last, step, count)

    def around(ready, blk, first, last, count):
        def step(r, s):
            return sweep(ready, blk, r, r + 1, s)

        def maybe(r, s):
            j = every[blk, r, 1]
            return lax.cond(lax.div(j, n) == me, lambda: step(r, s), lambda: s)

        return lax.fori_loop(first, last, maybe, count)

    count = jnp.int32(0)
    for ready in (True, False):
        count = sweep(ready, me, 0, n, count)
        count = around(ready, before, 0, n, count)
        count = around(ready, after, 0, n, count)
        plan[INFO + (5 if ready else 6)] = count


def make_plan(every, offsets):
    size = every.shape[0]
    smem = pl.BlockSpec(memory_space=pltpu.SMEM)
    return pl.pallas_call(
        plan_kernel,
        in_specs=[smem, smem],
        out_specs=smem,
        out_shape=jax.ShapeDtypeStruct((PLAN,), jnp.int32),
        scratch_shapes=[pltpu.SMEM((size,), jnp.int32)] * 4,
        name="plan",
    )(every, offsets)


def pick_kernel(plan, src_a, src_b, dst_a, dst_b):
    dst_a[...] = src_a[...]
    dst_b[...] = src_b[...]


def pick(plan, fields, n, m):
    _, rows, y, w = fields.shape
    blk = (1, rows, y, w)
    out = jax.ShapeDtypeStruct((m, rows, y, w), F32)
    return pl.pallas_call(
        pick_kernel,
        grid_spec=pltpu.PrefetchScalarGridSpec(
            num_scalar_prefetch=1,
            grid=(m,),
            in_specs=[
                pl.BlockSpec(blk, lambda i, plan: (plan[LISTS + i], 0, 0, 0)),
                pl.BlockSpec(blk, lambda i, plan: (plan[LISTS + 2 * n + i], 0, 0, 0)),
            ],
            out_specs=[pl.BlockSpec(blk, lambda i, plan: (i, 0, 0, 0))] * 2,
        ),
        out_shape=[out, out],
        name="pick",
    )(plan, fields, fields)


def swap_kernel(counts, up, down, prior, nxt, send, recv):
    size, width = lax.axis_size(CYCLE), lax.axis_size("orb")
    o = lax.axis_index("orb")
    me = lax.axis_index("grp") * width + o

    def peer(s):
        to = lax.rem(me + s, size)
        return {"grp": lax.div(to, width), "orb": lax.rem(to, width)}

    def kind(q):
        return jnp.where(q % 2 == 0, 2, jnp.where(q == width - 1, 1, 0))

    above, under = kind(o), kind(lax.rem(o + width - 1, width))
    barrier = pltpu.get_barrier_semaphore()
    for s in (1, size - 1):
        pl.semaphore_signal(
            barrier, inc=1, device_id=peer(s), device_id_type=pl.DeviceIdType.MESH
        )
    pl.semaphore_wait(barrier, 2)

    def copy(way, r):
        src, dst, s = ((up, prior, 1), (down, nxt, size - 1))[way]
        return pltpu.make_async_remote_copy(
            src_ref=src.at[r], dst_ref=dst.at[r],
            send_sem=send.at[way, r], recv_sem=recv.at[way, r],
            device_id=peer(s), device_id_type=pl.DeviceIdType.MESH,
        )

    for r in range(up.shape[0]):
        for way, mine in ((0, above), (1, under)):
            for c in range(3):
                if r < counts[c]:
                    pl.when(mine == c)(lambda way=way, r=r: copy(way, r).start())
    for r in range(up.shape[0]):
        for way, out, into in ((0, above, under), (1, under, above)):
            for c in range(3):
                if r < counts[c]:
                    pl.when(out == c)(lambda way=way, r=r: copy(way, r).wait_send())
                    pl.when(into == c)(lambda way=way, r=r: copy(way, r).wait_recv())


def swap(counts, up, down, most, cid):
    hbm = pl.BlockSpec(memory_space=pl.ANY)
    out = jax.ShapeDtypeStruct((most,) + up.shape[1:], F32)
    m = up.shape[0]
    return pl.pallas_call(
        functools.partial(swap_kernel, counts),
        in_specs=[hbm, hbm],
        out_specs=[hbm, hbm],
        out_shape=[out, out],
        scratch_shapes=[pltpu.SemaphoreType.DMA((2, m)), pltpu.SemaphoreType.DMA((2, m))],
        compiler_params=pltpu.CompilerParams(collective_id=cid, has_side_effects=True),
        name="swap%d%d%d" % counts,
    )(up, down)


def pairs_kernel(
    plan, fields, prior, nxt, basis, basis_back, levels, out,
    room, one, two, own2, par2, prod, acc, stage, wheel, moves, sem, out_sem
):
    n, h, y, z = out.shape
    w = 2 * z
    half, rows = h // 2, fields.shape[1]
    halo = rows - half
    tall = y + PAD
    each = rows * tall
    most = prior.shape[0]
    slab = lax.axis_index("slab")
    quads, line, _ = factors()

    def field(src, s, f):
        return pltpu.make_async_copy(src.at[s], room.at[f + 1, :, pl.ds(0, y)], sem.at[f])

    def each_field(do):
        for f in range(n + 2):
            do(field(fields, f, f))
        for src, base, count in ((prior, n + 2, plan[INFO + 3]), (nxt, n + 2 + most, plan[INFO + 4])):
            for s in range(most):
                pl.when(s < count)(lambda src=src, s=s, base=base: do(field(src, s, base + s)))

    each_field(lambda c: c.start())
    acc[...] = jnp.zeros(acc.shape, F32)
    prod[0] = jnp.zeros((tall, w), F32)
    prod[:, y:, :] = jnp.zeros((h + 1, PAD, w), F32)
    room[0, rows - 1, y:, :] = jnp.zeros((PAD, w), F32)

    def blank(f):
        room[f + 1, :, y:, :] = jnp.zeros((rows, PAD, w), F32)

    def wipe(f, c):
        blank(f)
        return c

    lax.fori_loop(0, room.shape[0] - 1, wipe, 0)
    flat_room = room.reshape(room.shape[0] * each, w)
    flat_prod = prod.reshape((h + 1) * tall, w)

    k_at = lax.broadcasted_iota(jnp.int32, (2 * w, 2 * w), 0)
    c_at = lax.broadcasted_iota(jnp.int32, (2 * w, 2 * w), 1)
    task_k, half_k, task_c, half_c = k_at // w, k_at % w // z, c_at % w // z, c_at // w
    gap = k_at % z - c_at % z
    wheel[...] = jnp.where((task_k == task_c) & (half_k == half_c), gap, 4 * z)
    for ref in (one, two):
        planes = ref.shape[0]
        ref[0] = jnp.zeros(ref.shape[1:], F32)
        ref[:, 0:8, :] = jnp.zeros((planes, 8, w), F32)
        ref[:, 8 + y :, :] = jnp.zeros((planes, 8, w), F32)
    each_field(lambda c: c.wait())

    lane = lanes((y, w))
    low = lane < z
    pos = lane % z
    mu = jnp.broadcast_to(levels[...], (STRIP, w))

    def sweep(src, count, emit):
        def step(g, c):
            for r in range(0, y, STRIP):
                at = pl.ds(8 + r, STRIP)
                col = [src[g * UNROLL + q, at, :] for q in range(UNROLL + 2)]
                for q in range(UNROLL):
                    t = g * UNROLL + q
                    sides = src[t + 1, pl.ds(7 + r, STRIP), :] + src[t + 1, pl.ds(9 + r, STRIP), :]
                    emit(t, r, col[q + 1], (col[q] + col[q + 2]) + sides)
            return c

        lax.fori_loop(0, pl.cdiv(count, UNROLL), step, 0)

    def split(values):
        coarse = values.astype(jnp.bfloat16)
        return coarse, (values - coarse.astype(F32)).astype(jnp.bfloat16)

    def turn_z(values, wave):
        both = jnp.dot(
            jnp.concatenate(split(values), axis=1), wave[...], preferred_element_type=F32
        )
        return both[:, :w] + both[:, w:]

    def repeat(count, unroll, do):
        def step(g, c):
            for q in range(unroll):
                do(g * unroll + q)
            return c

        lax.fori_loop(0, count // unroll, step, 0)

    def group(g, c):
        p, q = g * 2 * TASK, (g * 2 + 1) * TASK
        rp, rq = (plan[p] + 1) * each, (plan[q] + 1) * each
        ap, aq, bp, bq = plan[p + 2], plan[q + 2], plan[p + 3], plan[q + 3]
        sp, sq = (plan[p + 1] + 1) * each - ap, (plan[q + 1] + 1) * each - aq
        col = lanes((1, 2 * w)) % w < z
        moves[...] = jnp.where(wheel[...] == jnp.where(col, -bp, -bq), 1.0, 0.0).astype(jnp.bfloat16)

        def planes(r):
            return jnp.where(r < half, r, r + half), jnp.where(r < half, r + half, r + half + halo)

        def dense(g, c):
            raw = []
            for q in range(DEPTH):
                for t in planes(jnp.maximum((g - 1) * DEPTH + q, 0)):
                    raw.append(two[t + 1, 8 : 8 + y, :])
            waves = turn_z(jnp.concatenate(raw, axis=0), basis)
            rs = [jnp.minimum(g * DEPTH + q, rows - 1) for q in range(DEPTH)]
            par = [
                jnp.concatenate(
                    [flat_room[pl.ds(sp + r * tall, y), :], flat_room[pl.ds(sq + r * tall, y), :]],
                    axis=1,
                )
                for r in rs
            ]
            par = jnp.concatenate(split(jnp.concatenate(par, axis=0)), axis=0)
            par = jnp.dot(par, moves[...], preferred_element_type=F32)
            par = par[: DEPTH * y] + par[DEPTH * y :]
            for q in range(DEPTH):
                old = planes(jnp.maximum((g - 1) * DEPTH + q, 0))
                for side in range(2):
                    at = (2 * q + side) * y
                    one[old[side] + 1, 8 : 8 + y, :] = waves[at : at + y]
            for q, r in enumerate(rs):
                own_p = flat_room[pl.ds(rp + r * tall, y), :]
                own_q = flat_room[pl.ds(rq + r * tall, y), :]
                own_a = jnp.where(low, own_p, pltpu.roll(own_q, z, axis=1))
                own_b = jnp.where(low, pltpu.roll(own_p, z, axis=1), own_q)
                for t, own, half_par in zip(
                    planes(r), (own_a, own_b), jnp.split(par[q * y : (q + 1) * y], 2, axis=1)
                ):
                    two[t + 1, 8 : 8 + y, :] = own * half_par
                    own2[t] = own
                    par2[t] = half_par
            return c

        lax.fori_loop(0, rows // DEPTH + 1, dense, 0)

        count = h + EDGE - 1
        for b, c2 in quads:
            def first(t, r, cur, near, b=b):
                two[t + 1, pl.ds(8 + r, STRIP), :] = near + (mu + b) * cur

            def second(t, r, cur, near, c2=c2):
                at = pl.ds(8 + r, STRIP)
                one[t + 1, at, :] = (near + mu * cur) + c2 * one[t + 1, at, :]

            sweep(one, count, first)
            sweep(two, count - 1, second)
            count -= 2

        kp, kq, mp, mq = plan[p + 4], plan[q + 4], plan[p + 5], plan[q + 5]

        def last(t, r, cur, near):
            two[t + 1, pl.ds(8 + r, STRIP), :] = near + (mu + line) * cur

        sweep(one, h, last)

        def finish(g, c):
            both = [two[g * 4 + q + 1, 8 : 8 + y, :] for q in range(4)]
            both = turn_z(jnp.concatenate(both, axis=0), basis_back)
            for q in range(4):
                t = g * 4 + q
                pot = both[q * y : (q + 1) * y]
                par2[t] = pot * par2[t]
                prod[t + 1, 0:y, :] = pot * own2[t]
            return c

        lax.fori_loop(0, h // 4, finish, 0)

        for k, m, a, b, side in ((kp, mp, ap, bp, low), (kq, mq, aq, bq, jnp.logical_not(low))):
            @pl.when(k < n)
            def _(k=k, side=side):
                def plane(t):
                    acc[k, t] += jnp.where(side, par2[t], 0.0)

                repeat(h, 4, plane)

            @pl.when(m < n)
            def _(m=m, a=a, b=b, side=side):
                back_z = pos + b
                good = side & (back_z >= 0) & (back_z < z)
                turn = lax.rem(w - b, w)

                def plane(t):
                    moved = pltpu.roll(flat_prod[pl.ds((t + 1) * tall + a, y), :], turn, axis=1)
                    acc[m, t] += jnp.where(good, moved, 0.0)

                repeat(h, 4, plane)

        return c

    tasks = plan[INFO + 6]
    lax.fori_loop(0, lax.div(tasks + 1, 2), group, 0)

    def leave(k, slot):
        return pltpu.make_async_copy(stage.at[slot], out.at[k], out_sem.at[slot])

    def write(k, c):
        slot = lax.rem(k, 2)
        pl.when(k >= 2)(lambda: leave(k - 2, slot).wait())

        def plane(t, c):
            value = acc[k, t]
            value = value + pltpu.roll(value, z, axis=1)
            stage[slot, jnp.where(slab == 0, t, h - 1 - t)] = value[:, :z]
            return c

        lax.fori_loop(0, h, plane, 0)
        leave(k, slot).start()
        return c

    lax.fori_loop(0, n, write, 0)
    for k in (n - 2, n - 1):
        leave(k, k % 2).wait()


def sines(z):
    k = np.arange(1, z + 1)
    wave = np.sqrt(2.0 / (z + 1)) * np.sin(np.pi * np.outer(k, k) / (z + 1))
    wave = np.kron(np.eye(2), wave).astype(np.float32)
    levels = np.tile(2.0 * np.cos(np.pi * k / (z + 1)), 2).astype(np.float32)[None]

    def parts(values):
        coarse = jnp.asarray(values).astype(jnp.bfloat16)
        fine = (jnp.asarray(values) - coarse.astype(F32)).astype(jnp.bfloat16)
        top = jnp.concatenate([coarse, fine], axis=1)
        bottom = jnp.concatenate([coarse, jnp.zeros_like(fine)], axis=1)
        return jnp.concatenate([top, bottom], axis=0)

    return parts(wave), parts(wave * np.float32(factors()[2])), jnp.asarray(levels)


def solve_pairs(plan, fields, prior, nxt, shape):
    n, h, y, z = shape
    w, rows = 2 * z, fields.shape[1]
    most = prior.shape[0]
    hbm = pl.BlockSpec(memory_space=pl.ANY)
    vmem = pl.BlockSpec(memory_space=pltpu.VMEM)
    total = n + 2 + 2 * most
    planes = 2 * rows
    return pl.pallas_call(
        pairs_kernel,
        grid_spec=pltpu.PrefetchScalarGridSpec(
            num_scalar_prefetch=1,
            grid=(1,),
            in_specs=[hbm, hbm, hbm, vmem, vmem, vmem],
            out_specs=hbm,
            scratch_shapes=[
                pltpu.VMEM((total + 1, rows, y + PAD, w), F32),
                pltpu.VMEM((planes + 6, y + 16, w), F32),
                pltpu.VMEM((planes + 6, y + 16, w), F32),
                pltpu.VMEM((planes, y, w), F32),
                pltpu.VMEM((planes, y, w), F32),
                pltpu.VMEM((h + 1, y + PAD, w), F32),
                pltpu.VMEM((n, h, y, w), F32),
                pltpu.VMEM((2, h, y, z), F32),
                pltpu.VMEM((2 * w, 2 * w), jnp.int32),
                pltpu.VMEM((2 * w, 2 * w), jnp.bfloat16),
                pltpu.SemaphoreType.DMA((total,)),
                pltpu.SemaphoreType.DMA((2,)),
            ],
        ),
        out_shape=jax.ShapeDtypeStruct(shape, F32),
        compiler_params=pltpu.CompilerParams(vmem_limit_bytes=56 * 1024 * 1024),
        name="pairs",
    )(plan, fields, prior, nxt, *sines(z))


def fast_body(orbitals, offsets, pairs, live):
    n = orbitals.shape[0]
    most = n - 1
    fields, every = front(orbitals, pairs, live)
    plan = make_plan(every, offsets)

    combos = [(a, b, 4) for a in range(5) for b in range(5)] + [(most, most, most)]

    def branch(counts, cid):
        def run(_):
            m = max(counts)
            up, down = pick(plan, fields, n, m)
            return swap(counts, up, down, most, cid)

        return run

    ka, kb, kc = plan[INFO], plan[INFO + 1], plan[INFO + 2]
    big = jnp.maximum(jnp.maximum(ka, kb), kc) > 4
    which = jnp.where(big, len(combos) - 1, ka * 5 + kb)
    prior, nxt = lax.switch(which, [branch(c, 2 + i) for i, c in enumerate(combos)], 0)
    return solve_pairs(plan, fields, prior, nxt, orbitals.shape)


def body(orbitals, offsets, pairs, live):
    n = orbitals.shape[0]
    slots = pairs.shape[0]
    total = offsets.shape[0]
    blocks = total // n
    slabs = lax.axis_size("slab")
    me = lax.axis_index(CYCLE)
    packed = pack(orbitals)

    mine = jnp.concatenate([pairs, live[:, None]], axis=1)
    every = share(jnp.pad(mine, ((0, 0), (0, 128 - mine.shape[1]))))
    ids = jnp.arange(blocks, dtype=jnp.int32)
    second = every[:, :, 1]
    alive = every[:, :, 2] > 0
    orb = jnp.arange(n, dtype=jnp.int32)
    sides = jnp.stack([(ids - 1) % blocks, (ids + 1) % blocks])
    hit = alive[None] & (second[None] // n == sides[:, :, None])
    need = jnp.any(
        hit[..., None] & (second[None, :, :, None] % n == orb), axis=2
    )
    count = jnp.sum(need.astype(jnp.int32), axis=2)
    most = jnp.max(count)

    after, before = (me + 1) % blocks, (me - 1) % blocks
    flags = jnp.stack(
        [need[0, me], need[1, me], need[0, after], need[1, before]]
    ).astype(jnp.int32)
    spot = jnp.sum(
        flags[:, None, :] * (orb[None, :] < orb[:, None]).astype(jnp.int32)[None], axis=2
    )
    lists = jnp.sum(
        (flags[:, None, :] * (spot[:, None, :] == orb[None, :, None])) * orb, axis=2
    )
    back = jnp.stack(
        [spot[2] * flags[2], flags[2], spot[3] * flags[3], flags[3]]
    )

    i, j, on = pairs[:, 0], pairs[:, 1], live > 0
    owner, local = j // n, j % n
    pick_j = (local[:, None] == orb[None, :]).astype(jnp.int32)
    from_prior = (owner == before) & on
    from_next = (owner == after) & on
    kind = jnp.where(from_prior, 1, jnp.where(from_next, 2, 0))
    where_prior = jnp.sum(pick_j * spot[0][None, :], axis=1) * from_prior
    where_next = jnp.sum(pick_j * spot[1][None, :], axis=1) * from_next
    ids_all = jnp.arange(total, dtype=jnp.int32)
    diff = (j[:, None] == ids_all).astype(jnp.int32) - (i[:, None] == ids_all).astype(jnp.int32)
    shift = jnp.sum(diff[:, :, None] * offsets[None], axis=1)
    plan = jnp.stack(
        [i % n, local, where_prior, where_next, kind, shift[:, 0], shift[:, 1], live]
    ).astype(jnp.int32)
    order = jnp.where(on, jnp.where(kind > 0, 0, 1), 2) * slots + jnp.arange(slots)
    rank = jnp.sum((order[None, :] < order[:, None]).astype(jnp.int32), axis=1)
    move = (rank[:, None] == jnp.arange(slots)[None, :]).astype(jnp.int32)
    plan = jnp.sum(plan[:, :, None] * move[None], axis=1)
    far, lively = jnp.sum((kind > 0).astype(jnp.int32)), jnp.sum(on.astype(jnp.int32))
    tail = jnp.where(jnp.arange(slots) == 0, far, lively)
    plan = jnp.concatenate([plan, tail[None]], axis=0)
    ends = jnp.stack([lax.axis_index("slab"), slabs]).astype(jnp.int32)

    up = [(s, s + 1) for s in range(slabs - 1)]
    down = [(s + 1, s) for s in range(slabs - 1)]

    def branch(m):
        def run(_):
            to_next, to_prior = gather(packed, lists[2:], m)
            prior = cycle(to_next, 1)
            nxt = cycle(to_prior, -1)
            partner, density, low, high = densities(plan, packed, prior, nxt)
            below = lax.ppermute(high, "slab", up)
            above = lax.ppermute(low, "slab", down)
            given = (plan, ends, density, partner, packed, below, above, m)
            acc, acc_prior, acc_next = solve(True, *given)
            from_next, from_prior = cycle(acc_prior, -1), cycle(acc_next, 1)
            (acc_near,) = solve(False, *given)
            return combine(back, acc, acc_near, from_next, from_prior)

        return run

    sizes = sorted({min(s, slots - 1) for s in (3, 4, 5)} | {slots - 1})
    which = sum((most > s).astype(jnp.int32) for s in sizes[:-1])
    return lax.switch(which, [branch(s) for s in sizes], 0)


def solution(mesh):
    placed = (
        P(CYCLE, "slab", None, None),
        P(),
        P(CYCLE, None),
        P(CYCLE),
    )
    return jax.shard_map(
        fast_body if mesh.shape["slab"] == 2 else body,
        mesh=mesh,
        in_specs=placed,
        out_specs=P(CYCLE, "slab", None, None),
        check_vma=False,
    )
```

```python
import cmath
import functools
import math

import jax
import jax.numpy as jnp
import numpy as np
from jax import lax
from jax.experimental import pallas as pl
from jax.experimental.pallas import tpu as pltpu
from jax.sharding import PartitionSpec as P

PASSES = 8
DIAG = 6.25
THETA = 1.075
DELTA = 0.925
EDGE = PASSES - 1
PAD = 16
CYCLE = ("grp", "orb")
F32 = jnp.float32


def coefs():
    sigma = THETA / DELTA
    coef = 1.0 / sigma
    out = []
    for _ in range(PASSES - 1):
        new = 1.0 / (2.0 * sigma - coef)
        out.append((new * coef, 2.0 * new / (DELTA * DIAG)))
        coef = new
    return out


def lanes(shape):
    return lax.broadcasted_iota(jnp.int32, shape, len(shape) - 1)


def share_kernel(mine, every, send_sem, recv_sem):
    size, width = lax.axis_size(CYCLE), lax.axis_size("orb")
    me = lax.axis_index("grp") * width + lax.axis_index("orb")

    def peer(s):
        to = lax.rem(me + s, size)
        return {"grp": lax.div(to, width), "orb": lax.rem(to, width)}

    def greet(s, c):
        pl.semaphore_signal(
            barrier, inc=1, device_id=peer(s), device_id_type=pl.DeviceIdType.MESH
        )
        return c

    def copy(s, slot):
        return pltpu.make_async_remote_copy(
            src_ref=mine,
            dst_ref=every.at[slot],
            send_sem=send_sem.at[s],
            recv_sem=recv_sem.at[s],
            device_id=peer(s),
            device_id_type=pl.DeviceIdType.MESH,
        )

    def send(s, c):
        copy(s, me).start()
        return c

    def finish(s, c):
        copy(s, lax.rem(me + size - s, size)).wait()
        return c

    barrier = pltpu.get_barrier_semaphore()
    lax.fori_loop(1, size, greet, 0)
    pl.semaphore_wait(barrier, size - 1)
    lax.fori_loop(1, size, send, 0)
    every[me] = mine[...]
    lax.fori_loop(1, size, finish, 0)


def share(mine):
    size = lax.axis_size(CYCLE)
    vmem = pl.BlockSpec(memory_space=pltpu.VMEM)
    return pl.pallas_call(
        share_kernel,
        in_specs=[vmem],
        out_specs=vmem,
        out_shape=jax.ShapeDtypeStruct((size,) + mine.shape, mine.dtype),
        scratch_shapes=[pltpu.SemaphoreType.DMA((size,)), pltpu.SemaphoreType.DMA((size,))],
        compiler_params=pltpu.CompilerParams(collective_id=0, has_side_effects=True),
        name="share",
    )(mine)


def pack_kernel(src, dst):
    half = dst.shape[1]
    dst[0] = jnp.concatenate([src[0, :half], src[0, half:]], axis=-1)


def pack(orbitals):
    n, x, y, z = orbitals.shape
    return pl.pallas_call(
        pack_kernel,
        grid=(n,),
        in_specs=[pl.BlockSpec((1, x, y, z), lambda i: (i, 0, 0, 0))],
        out_specs=pl.BlockSpec((1, x // 2, y, 2 * z), lambda i: (i, 0, 0, 0)),
        out_shape=jax.ShapeDtypeStruct((n, x // 2, y, 2 * z), F32),
        name="pack",
    )(orbitals)


def copy_kernel(idx, src_a, src_b, dst_a, dst_b):
    dst_a[...] = src_a[...]
    dst_b[...] = src_b[...]


def gather(packed, lists, m):
    _, h, y, w = packed.shape
    blk = (1, h, y, w)
    out = jax.ShapeDtypeStruct((m, h, y, w), F32)
    return pl.pallas_call(
        copy_kernel,
        grid_spec=pltpu.PrefetchScalarGridSpec(
            num_scalar_prefetch=1,
            grid=(m,),
            in_specs=[
                pl.BlockSpec(blk, lambda i, idx: (idx[0, i], 0, 0, 0)),
                pl.BlockSpec(blk, lambda i, idx: (idx[1, i], 0, 0, 0)),
            ],
            out_specs=[pl.BlockSpec(blk, lambda i, idx: (i, 0, 0, 0))] * 2,
        ),
        out_shape=[out, out],
        name="gather",
    )(lists, packed, packed)


def place(value, room, a, b):
    y, w = value.shape[1:]
    z = w // 2
    room[:, PAD : PAD + y, :] = value
    moved = room[:, pl.ds(PAD - a, y), :]
    moved = pltpu.roll(moved, lax.rem(b + w, w), axis=2)
    pos = lanes(moved.shape) % z - b
    return jnp.where((pos >= 0) & (pos < z), moved, 0.0)


def clear_room(room):
    y = room.shape[1] - 2 * PAD
    room[:, :PAD, :] = jnp.zeros((room.shape[0], PAD, room.shape[2]), F32)
    room[:, PAD + y :, :] = jnp.zeros((room.shape[0], PAD, room.shape[2]), F32)


def density_kernel(plan, own, mine, prior, nxt, partner, density, low, high, room):
    p = pl.program_id(0)
    kind = plan[4, p]
    a, b = plan[5, p], plan[6, p]

    @pl.when(p == 0)
    def _():
        clear_room(room)

    on = plan[7, p] > 0

    def go(src):
        part = place(src[0], room, a, b)
        partner[0] = part
        dens = own[0] * part
        density[0] = dens
        h, y, w = dens.shape
        flat = jnp.concatenate([dens[..., : w // 2], dens[..., w // 2 :]], axis=0)
        top, bot = flat[:EDGE], flat[2 * h - EDGE :]
        low[0] = jnp.concatenate([top[:, : y // 2], top[:, y // 2 :]], axis=-1)
        high[0] = jnp.concatenate([bot[:, : y // 2], bot[:, y // 2 :]], axis=-1)

    for value, src in enumerate((mine, prior, nxt)):
        pl.when(on & (kind == value))(functools.partial(go, src))


def densities(plan, packed, prior, nxt):
    slots = plan.shape[1]
    _, h, y, w = packed.shape
    blk = (1, h, y, w)
    eblk = (1, EDGE, y // 2, w)

    def at(row):
        return pl.BlockSpec(
            blk, lambda i, plan: (plan[row, jnp.minimum(i, plan[8, 1] - 1)], 0, 0, 0)
        )

    full = jax.ShapeDtypeStruct((slots, h, y, w), F32)
    edge = jax.ShapeDtypeStruct((slots,) + eblk[1:], F32)
    here = lambda i, plan: (jnp.minimum(i, plan[8, 1] - 1), 0, 0, 0)
    return pl.pallas_call(
        density_kernel,
        grid_spec=pltpu.PrefetchScalarGridSpec(
            num_scalar_prefetch=1,
            grid=(slots,),
            in_specs=[at(0), at(1), at(2), at(3)],
            out_specs=[
                pl.BlockSpec(blk, here),
                pl.BlockSpec(blk, here),
                pl.BlockSpec(eblk, here),
                pl.BlockSpec(eblk, here),
            ],
            scratch_shapes=[pltpu.VMEM((h, y + 2 * PAD, w), F32)],
        ),
        out_shape=[full, full, edge, edge],
        name="density",
    )(plan, packed, packed, prior, nxt)


def solve_kernel(remote, plan, ends, density, partner, own, below, above, *refs):
    accs, (resid, step_a, step_b, total, mask, room) = refs[:-6], refs[-6:]
    acc = accs[0]
    p = pl.program_id(0)
    h, y, w = density.shape[1:]
    z = w // 2
    rows = h + 2 * EDGE
    group = 4 if h % 4 == 0 else 1

    @pl.when(p == 0)
    def _():
        clear_room(room)
        for ref in accs:
            ref[...] = jnp.zeros(ref.shape, F32)
        for ref in (step_a, step_b):
            ref[:, :8, :] = jnp.zeros((rows, 8, w), F32)
            ref[:, 8 + y :, :] = jnp.zeros((rows, 8, w), F32)
        lane = lanes((1, w))
        first = ends[0] == 0
        last = ends[0] == ends[1] - 1
        for t in range(rows):
            plane = jnp.where(lane < z, t - EDGE, t - EDGE + h)
            outside = ((plane < 0) & first) | ((plane >= 2 * h) & last)
            mask[t] = jnp.where(outside, 0.0, 1.0)

    chosen = (plan[4, p] > 0) if remote else (plan[4, p] == 0)

    @pl.when((plan[7, p] > 0) & chosen)
    def _():
        def unfold(part):
            return jnp.concatenate([part[..., :z], part[..., z:]], axis=1)

        dens = density[0]
        line = jnp.concatenate(
            [unfold(below[0]), dens[..., :z], dens[..., z:], unfold(above[0])], axis=0
        )
        resid[...] = jnp.concatenate([line[:rows], line[h:]], axis=-1)
        step_a[:, 8 : 8 + y, :] = resid[...] * (1.0 / (DIAG * THETA))
        total[...] = step_a[EDGE : EDGE + h, 8 : 8 + y, :]
        lane = lanes((y, w)) % z
        not_low = lane > 0
        not_high = lane < z - 1
        bufs = [step_a, step_b]
        for turn, (keep, gain) in enumerate(coefs()):
            now, then = bufs[turn % 2], bufs[1 - turn % 2]
            core_only = turn == PASSES - 2

            def row(t, now=now, then=then, keep=keep, gain=gain):
                core = now[t, 8 : 8 + y, :]
                near = now[t - 1, 8 : 8 + y, :] + now[t + 1, 8 : 8 + y, :]
                near = near + (now[t, 7 : 7 + y, :] + now[t, 9 : 9 + y, :])
                side = jnp.where(not_low, pltpu.roll(core, 1, axis=1), 0.0)
                side = side + jnp.where(not_high, pltpu.roll(core, w - 1, axis=1), 0.0)
                left = (resid[t] - DIAG * core) + (near + side)
                return left, keep * core + gain * left

            def outer(k, c, row=row, then=then):
                for t in (EDGE - 1 - k, EDGE + h + k):
                    left, fresh = row(t)
                    resid[t] = left
                    then[t, 8 : 8 + y, :] = fresh * mask[t]
                return c

            def inner(k, c, row=row, then=then, last=core_only):
                for g in range(group):
                    t = EDGE + k * group + g
                    left, fresh = row(t)
                    if not last:
                        resid[t] = left
                        then[t, 8 : 8 + y, :] = fresh
                    total[t - EDGE] += fresh
                return c

            if turn + 1 < EDGE:
                lax.fori_loop(0, EDGE - turn - 1, outer, 0)
            lax.fori_loop(0, h // group, inner, 0)

        pot = total[...]
        acc[plan[0, p]] += pot * partner[0]
        back = place(pot * own[0], room, -plan[5, p], -plan[6, p])
        if not remote:
            acc[plan[1, p]] += back
        else:
            for value in (1, 2):

                @pl.when(plan[4, p] == value)
                def _(ref=accs[value], value=value):
                    ref[plan[1 + value, p]] += back


def solve(remote, plan, ends, density, partner, packed, below, above, m):
    slots = plan.shape[1]
    n, h, y, w = packed.shape
    blk = (1, h, y, w)
    eblk = (1, EDGE, y // 2, w)
    rows = h + 2 * EDGE

    def spot(i, plan):
        far = plan[8, 0]
        if remote:
            return jnp.minimum(i, jnp.maximum(far - 1, 0))
        return jnp.clip(i, jnp.minimum(far, plan[8, 1] - 1), plan[8, 1] - 1)

    here = lambda i, plan, ends: (spot(i, plan), 0, 0, 0)
    fixed = lambda i, plan, ends: (0, 0, 0, 0)
    shapes = [(n, h, y, w)] + [(m, h, y, w)] * (2 if remote else 0)
    return pl.pallas_call(
        functools.partial(solve_kernel, remote),
        grid_spec=pltpu.PrefetchScalarGridSpec(
            num_scalar_prefetch=2,
            grid=(slots,),
            in_specs=[
                pl.BlockSpec(blk, here),
                pl.BlockSpec(blk, here),
                pl.BlockSpec(blk, lambda i, plan, ends: (plan[0, spot(i, plan)], 0, 0, 0)),
                pl.BlockSpec(eblk, here),
                pl.BlockSpec(eblk, here),
            ],
            out_specs=[pl.BlockSpec(s, fixed) for s in shapes],
            scratch_shapes=[
                pltpu.VMEM((rows, y, w), F32),
                pltpu.VMEM((rows, y + 16, w), F32),
                pltpu.VMEM((rows, y + 16, w), F32),
                pltpu.VMEM((h, y, w), F32),
                pltpu.VMEM((rows, 1, w), F32),
                pltpu.VMEM((h, y + 2 * PAD, w), F32),
            ],
        ),
        out_shape=[jax.ShapeDtypeStruct(s, F32) for s in shapes],
        compiler_params=pltpu.CompilerParams(vmem_limit_bytes=56 * 1024 * 1024),
        cost_estimate=pl.CostEstimate(
            flops=slots * rows * y * w * 100, bytes_accessed=24 << 20, transcendentals=0
        ),
        name="solve_far" if remote else "solve_near",
    )(plan, ends, density, partner, packed, below, above)


def combine_kernel(back, acc, acc_near, from_next, from_prior, out):
    k = pl.program_id(0)
    h = acc.shape[1]
    z = acc.shape[3] // 2
    value = acc[0] + acc_near[0]
    value = value + jnp.where(back[1, k] > 0, from_next[0], 0.0)
    value = value + jnp.where(back[3, k] > 0, from_prior[0], 0.0)
    out[0, :h] = value[:, :, :z]
    out[0, h:] = value[:, :, z:]


def combine(back, acc, acc_near, from_next, from_prior):
    n, h, y, w = acc.shape
    blk = (1, h, y, w)
    return pl.pallas_call(
        combine_kernel,
        grid_spec=pltpu.PrefetchScalarGridSpec(
            num_scalar_prefetch=1,
            grid=(n,),
            in_specs=[
                pl.BlockSpec(blk, lambda i, back: (i, 0, 0, 0)),
                pl.BlockSpec(blk, lambda i, back: (i, 0, 0, 0)),
                pl.BlockSpec(blk, lambda i, back: (back[0, i], 0, 0, 0)),
                pl.BlockSpec(blk, lambda i, back: (back[2, i], 0, 0, 0)),
            ],
            out_specs=pl.BlockSpec((1, 2 * h, y, w // 2), lambda i, back: (i, 0, 0, 0)),
        ),
        out_shape=jax.ShapeDtypeStruct((n, 2 * h, y, w // 2), F32),
        name="combine",
    )(back, acc, acc_near, from_next, from_prior)


def cycle(field, by):
    size = lax.axis_size(CYCLE)
    return lax.ppermute(field, CYCLE, [(i, (i + by) % size) for i in range(size)])


TASK = 8
LISTS = 256
INFO = 320
PLAN = 384
UNROLL = 4
DEPTH = 5
STRIP = 8


def factors():
    ratio = THETA / DELTA
    tall = math.acosh(ratio)
    points = [cmath.cosh(complex(tall, k * math.pi / 4)) for k in range(8)]
    marks = [DIAG * (1.0 - (THETA - DELTA * x)) for x in points]
    quads = [(-2.0 * marks[k].real, abs(marks[k]) ** 2) for k in (1, 2, 3)]
    line = -marks[4].real
    coef, resid, value, step = 1.0 / ratio, 1.0, 0.0, 1.0 / (DIAG * THETA)
    value += step
    for keep, gain in coefs():
        resid -= DIAG * step
        step = keep * step + gain * resid
        value += step
    product = line
    for _, c in quads:
        product *= c
    return quads, line, value / product


def front_kernel(
    orbs, pairs, live, fields, every, edges, stage, own, far, edge, table,
    in_sem, out_sem, rim_sem, tab_send, tab_recv, edge_send, edge_recv, far_send, far_recv,
):
    n, h = orbs.shape[0], orbs.shape[1]
    half = h // 2
    halo = edge.shape[1]
    size, width = lax.axis_size(CYCLE), lax.axis_size("orb")
    me = lax.axis_index("grp") * width + lax.axis_index("orb")
    slab = lax.axis_index("slab")

    def peer(s):
        to = lax.rem(me + s, size)
        return {"grp": lax.div(to, width), "orb": lax.rem(to, width)}

    def load(k):
        return pltpu.make_async_copy(orbs.at[k], stage.at[k], in_sem.at[k])

    def order(q):
        return jnp.where(q == 0, 0, jnp.where(q == 1, n - 1, q - 1))

    def begin(q, c):
        load(order(q)).start()
        return c

    lax.fori_loop(0, n, begin, 0)

    barrier = pltpu.get_barrier_semaphore()

    def greet(s, c):
        pl.semaphore_signal(
            barrier, inc=1, device_id=peer(s), device_id_type=pl.DeviceIdType.MESH
        )
        return c

    lax.fori_loop(1, size, greet, 0)
    pl.semaphore_signal(
        barrier, inc=1, device_id={"slab": 1 - slab}, device_id_type=pl.DeviceIdType.MESH
    )
    table[0:2, 0:n] = pairs[...]
    table[2:3, 0:n] = live[...]
    pl.semaphore_wait(barrier, size)

    def share_copy(s, slot):
        return pltpu.make_async_remote_copy(
            src_ref=table, dst_ref=every.at[slot],
            send_sem=tab_send.at[s], recv_sem=tab_recv.at[s],
            device_id=peer(s), device_id_type=pl.DeviceIdType.MESH,
        )

    def share_send(s, c):
        share_copy(s, me).start()
        return c

    lax.fori_loop(1, size, share_send, 0)
    every[me] = table[...]

    def edge_copy(e, f, dst):
        return pltpu.make_async_remote_copy(
            src_ref=edge.at[f], dst_ref=dst,
            send_sem=edge_send.at[e], recv_sem=edge_recv.at[e],
            device_id={"slab": 1 - slab}, device_id_type=pl.DeviceIdType.MESH,
        )

    def own_edge(k, e):
        return edge_copy(e, k, own.at[k, pl.ds(half, halo)])

    def far_copy(k, f, s):
        return pltpu.make_async_remote_copy(
            src_ref=own.at[k, pl.ds(0, half)], dst_ref=far.at[f, pl.ds(0, half)],
            send_sem=far_send.at[f], recv_sem=far_recv.at[f],
            device_id=peer(s), device_id_type=pl.DeviceIdType.MESH,
        )

    def spot(t):
        return jnp.where(slab == 0, t, h - 1 - t)

    def pack(k):
        def row(r, c):
            own[k, r] = jnp.concatenate(
                [stage[k, spot(r)], stage[k, spot(r + half)]], axis=-1
            )
            return c

        lax.fori_loop(0, half, row, 0)

    def make_edge(k):
        for m in range(halo):
            edge[k, m] = jnp.concatenate(
                [stage[k, spot(h - 1 - m)], stage[k, spot(h - 1 - halo - m)]], axis=-1
            )

    def save(k):
        return pltpu.make_async_copy(
            own.at[k, pl.ds(0, half)], fields.at[k, pl.ds(0, half)], out_sem.at[k]
        )

    def rim(k, f, src):
        return pltpu.make_async_copy(
            src.at[k, pl.ds(half, halo)], fields.at[f, pl.ds(half, halo)], rim_sem.at[f]
        )

    def keep_edge(k):
        return pltpu.make_async_copy(edge.at[k], edges.at[k], rim_sem.at[k])

    up, down = far_copy(n - 1, 0, 1), far_copy(0, 1, size - 1)
    for k, send, e in ((0, down, 0), (n - 1, up, 1)):
        load(k).wait()
        pack(k)
        send.start()
        make_edge(k)
        own_edge(k, e).start()
        save(k).start()

    def rest(k, c):
        load(k).wait()
        pack(k)
        save(k).start()
        make_edge(k)
        keep_edge(k).start()
        return c

    lax.fori_loop(1, n - 1, rest, 0)

    def share_done(s, c):
        share_copy(s, lax.rem(me + size - s, size)).wait()
        return c

    lax.fori_loop(1, size, share_done, 0)

    low = lanes((1, own.shape[-1])) < own.shape[-1] // 2
    for f, copy in ((1, down), (0, up)):
        copy.wait()
        for m in range(halo):
            a, b = far[f, half - 1 - m], far[f, half - 1 - halo - m]
            edge[n + f, m] = jnp.where(low, pltpu.roll(a, a.shape[-1] // 2, axis=1), b)
        edge_copy(2 + f, n + f, far.at[f, pl.ds(half, halo)]).start()
        pltpu.make_async_copy(
            far.at[f, pl.ds(0, half)], fields.at[n + f, pl.ds(0, half)], out_sem.at[n + f]
        ).start()

    for k, e in ((0, 0), (n - 1, 1)):
        own_edge(k, e).wait()
        rim(k, k, own).start()
    for f in (1, 0):
        edge_copy(2 + f, n + f, far.at[f, pl.ds(half, halo)]).wait()
        rim(f, n + f, far).start()

    def out_done(k, c):
        save(k).wait()
        return c

    def edge_done(k, c):
        keep_edge(k).wait()
        return c

    lax.fori_loop(0, n, out_done, 0)
    lax.fori_loop(1, n - 1, edge_done, 0)
    for k in (0, n - 1):
        rim(k, k, own).wait()
    for f in (1, 0):
        rim(f, n + f, far).wait()
        pltpu.make_async_copy(
            far.at[f, pl.ds(0, half)], fields.at[n + f, pl.ds(0, half)], out_sem.at[n + f]
        ).wait()


def front(orbitals, pairs, live):
    n, h, y, z = orbitals.shape
    half, halo, w = h // 2, (EDGE + 1) // 2, 2 * z
    size = lax.axis_size(CYCLE)
    vmem = pl.BlockSpec(memory_space=pltpu.VMEM)
    hbm = pl.BlockSpec(memory_space=pl.ANY)
    dma = pltpu.SemaphoreType.DMA
    return pl.pallas_call(
        front_kernel,
        in_specs=[hbm, vmem, vmem],
        out_specs=[hbm, vmem, hbm],
        out_shape=[
            jax.ShapeDtypeStruct((n + 2, half + halo, y, w), F32),
            jax.ShapeDtypeStruct((size, 8, 128), jnp.int32),
            jax.ShapeDtypeStruct((n, halo, y, w), F32),
        ],
        scratch_shapes=[
            pltpu.VMEM((n, h, y, z), F32),
            pltpu.VMEM((n, half + halo, y, w), F32),
            pltpu.VMEM((2, half + halo, y, w), F32),
            pltpu.VMEM((n + 2, halo, y, w), F32),
            pltpu.VMEM((8, 128), jnp.int32),
            dma((n,)), dma((n + 2,)), dma((n + 2,)), dma((size,)), dma((size,)),
            dma((4,)), dma((4,)), dma((2,)), dma((2,)),
        ],
        compiler_params=pltpu.CompilerParams(collective_id=1, has_side_effects=True),
        name="front",
    )(orbitals, pairs.T, live[None])


def plan_kernel(n, combos, every, offsets, plan, which, ups, downs, nups, ndowns, alive):
    size = every.shape[0]
    width = lax.axis_size("orb")
    me = lax.axis_index("grp") * width + lax.axis_index("orb")
    before, after = lax.rem(me + size - 1, size), lax.rem(me + 1, size)

    def clear(e, c):
        ups[e] = 0
        downs[e] = 0
        nups[e] = 0
        ndowns[e] = 0
        alive[e] = sum(every[e, 2, r] for r in range(n))
        return c

    lax.fori_loop(0, size, clear, 0)

    def read(blk, r):
        i, j = every[blk, 0, r], every[blk, 1, r]
        bj = lax.div(j, n)
        is_up = bj == lax.rem(blk + 1, size)
        li, lj = lax.rem(i, n), lax.rem(j, n)
        u, v = jnp.where(is_up, li, lj), jnp.where(is_up, lj, li)
        return i, j, bj, u, v, jnp.where(is_up, blk, bj)

    def mark(blk, c):
        def row(r, c):
            i, j, bj, u, v, edge = read(blk, r)

            @pl.when(bj != blk)
            def _():
                for bits, counts, x, free in ((ups, nups, u, n - 1), (downs, ndowns, v, 0)):
                    bit = jnp.where(x == free, 0, lax.shift_left(1, x))
                    had = bits[edge]
                    bits[edge] = had | bit
                    counts[edge] = counts[edge] + jnp.where((had | bit) != had, 1, 0)

            return c

        return lax.fori_loop(2, alive[blk], row, c)

    lax.fori_loop(0, size, mark, 0)

    def widest(e, most):
        o = lax.rem(e, width)
        mine = jnp.where(o % 2 == 0, 2, jnp.where(o == width - 1, 1, 0))
        here = jnp.maximum(nups[e], ndowns[e])
        return tuple(jnp.maximum(m, jnp.where(mine == c, here, 0)) for c, m in enumerate(most))

    most = lax.fori_loop(0, size, widest, (jnp.int32(0),) * 3)
    pick = jnp.int32(len(combos) - 1)
    for c in range(len(combos) - 2, -1, -1):
        fit = functools.reduce(lambda p, q: p & q, [m <= k for m, k in zip(most, combos[c])])
        pick = jnp.where(fit, c, pick)
    which[0] = pick

    def listing(bits, base):
        def step(q, s):
            plan[base + s] = q
            return s + (lax.shift_right_logical(bits, q) & 1)

        for q in range(n):
            plan[base + q] = 0
        return lax.fori_loop(0, n, step, jnp.int32(0))

    listing(ups[me], LISTS)
    listing(downs[before], LISTS + 2 * n)
    plan[INFO + 3] = nups[before]
    plan[INFO + 4] = ndowns[me]

    def rank(bits, x):
        return sum(
            jnp.where(q < x, lax.shift_right_logical(bits, q) & 1, 0) for q in range(n)
        )

    def place_of(x):
        blk, loc = lax.div(x, n), lax.rem(x, n)
        from_before = jnp.where(loc == n - 1, n, n + 2 + rank(ups[before], loc))
        from_after = jnp.where(loc == 0, n + 1, n + 2 + n - 1 + rank(downs[me], loc))
        return jnp.where(blk == me, loc, jnp.where(blk == before, from_before, from_after))

    def sweep(ready, blk, start, skip, count):
        def step(r, s):
            i, j, bj, u, v, edge = read(blk, r)
            free = (bj == blk) | jnp.where(edge == me, v == 0, u == n - 1)
            want = ((blk == me) | (bj == me)) & (free == ready) & (r != skip)

            @pl.when(want)
            def _():
                plan[s * TASK] = place_of(i)
                plan[s * TASK + 1] = place_of(j)
                plan[s * TASK + 2] = offsets[0, j] - offsets[0, i]
                plan[s * TASK + 3] = offsets[1, j] - offsets[1, i]
                plan[s * TASK + 4] = jnp.where(lax.div(i, n) == me, lax.rem(i, n), n)
                plan[s * TASK + 5] = jnp.where(bj == me, lax.rem(j, n), n)

            return s + jnp.where(want, 1, 0)

        return lax.fori_loop(start, alive[blk], step, count)

    count = jnp.int32(0)
    for ready in (True, False):
        count = sweep(ready, me, 0, n, count)
        count = sweep(ready, before, 0, n, count)
        count = sweep(ready, after, 0, n, count)
    plan[INFO + 6] = count
    for c, value in enumerate((0, 0, 0, 0, n, n)):
        plan[count * TASK + c] = value


def make_plan(every, offsets, n, combos):
    size = every.shape[0]
    smem = pl.BlockSpec(memory_space=pltpu.SMEM)
    return pl.pallas_call(
        functools.partial(plan_kernel, n, combos),
        in_specs=[smem, smem],
        out_specs=[smem, smem],
        out_shape=[
            jax.ShapeDtypeStruct((PLAN,), jnp.int32),
            jax.ShapeDtypeStruct((1,), jnp.int32),
        ],
        scratch_shapes=[pltpu.SMEM((size,), jnp.int32)] * 5,
        name="plan",
    )(every, offsets.T)


def swap_kernel(
    counts, plan, fields, edges, prior, nxt, halos, own, sends, got, trim,
    in_sem, send, recv, edge_send, edge_recv, trim_send, trim_recv, main_sem, rim_sem,
):
    n, halo = edges.shape[0], edges.shape[1]
    half, w = own.shape[1], own.shape[-1]
    m = sends.shape[1]
    size, width = lax.axis_size(CYCLE), lax.axis_size("orb")
    o = lax.axis_index("orb")
    me = lax.axis_index("grp") * width + o
    slab = lax.axis_index("slab")
    other = {"slab": 1 - slab}

    def peer(s):
        to = lax.rem(me + s, size)
        return {"grp": lax.div(to, width), "orb": lax.rem(to, width)}

    def limit(q):
        return jnp.where(q % 2 == 0, counts[2], jnp.where(q == width - 1, counts[1], counts[0]))

    above, under = limit(o), limit(lax.rem(o + width - 1, width))
    ways = ((0, above, under, prior), (1, under, above, nxt))

    def load(k):
        return pltpu.make_async_copy(fields.at[k, pl.ds(0, half)], own.at[k], in_sem.at[k])

    def edge_copy(k):
        return pltpu.make_async_remote_copy(
            src_ref=edges.at[k], dst_ref=halos.at[k],
            send_sem=edge_send.at[k], recv_sem=edge_recv.at[k],
            device_id=other, device_id_type=pl.DeviceIdType.MESH,
        )

    def copy(way, r):
        return pltpu.make_async_remote_copy(
            src_ref=sends.at[way, r], dst_ref=got.at[way, r, pl.ds(0, half)],
            send_sem=send.at[way, r], recv_sem=recv.at[way, r],
            device_id=peer((1, size - 1)[way]), device_id_type=pl.DeviceIdType.MESH,
        )

    def trim_copy(way, r):
        return pltpu.make_async_remote_copy(
            src_ref=trim.at[way, r], dst_ref=got.at[way, r, pl.ds(half, halo)],
            send_sem=trim_send.at[way, r], recv_sem=trim_recv.at[way, r],
            device_id=other, device_id_type=pl.DeviceIdType.MESH,
        )

    def main_out(way, r, dst):
        part = pl.ds(0, half)
        return pltpu.make_async_copy(got.at[way, r, part], dst.at[r, part], main_sem.at[way, r])

    def rim_out(way, r, dst):
        part = pl.ds(half, halo)
        return pltpu.make_async_copy(got.at[way, r, part], dst.at[r, part], rim_sem.at[way, r])

    for k in range(n):
        load(k).start()
    barrier = pltpu.get_barrier_semaphore()
    for to in (peer(1), peer(size - 1), other):
        pl.semaphore_signal(barrier, inc=1, device_id=to, device_id_type=pl.DeviceIdType.MESH)
    pl.semaphore_wait(barrier, 3)

    def each(start, stop, do):
        def step(k, c):
            do(k)
            return c

        lax.fori_loop(start, stop, step, 0)

    each(1, n - 1, lambda k: edge_copy(k).start())
    for k in range(n):
        load(k).wait()

    def launch(r):
        for way, out, _, _ in ways:
            @pl.when(r < out)
            def _(way=way):
                k = plan[LISTS + way * 2 * n + r]

                def row(t):
                    sends[way, r, t] = own[k, t]

                each(0, half, row)
                copy(way, r).start()

    each(0, m, launch)
    low = lanes((1, w)) < w // 2

    def land(r):
        for way, _, into, dst in ways:
            @pl.when(r < into)
            def _(way=way, dst=dst):
                copy(way, r).wait_recv()
                main_out(way, r, dst).start()
                for e in range(halo):
                    a, b = got[way, r, half - 1 - e], got[way, r, half - 1 - halo - e]
                    trim[way, r, e] = jnp.where(low, pltpu.roll(a, w // 2, axis=1), b)
                trim_copy(way, r).start()

    each(0, m, land)
    each(1, n - 1, lambda k: edge_copy(k).wait())

    def settle(r):
        for way, out, into, dst in ways:
            @pl.when(r < into)
            def _(way=way, dst=dst):
                trim_copy(way, r).wait()
                rim_out(way, r, dst).start()

            @pl.when(r < out)
            def _(way=way):
                copy(way, r).wait_send()

    each(0, m, settle)

    def close(r):
        for way, _, into, dst in ways:
            @pl.when(r < into)
            def _(way=way, dst=dst):
                main_out(way, r, dst).wait()
                rim_out(way, r, dst).wait()

    each(0, m, close)


def swap(counts, plan, fields, edges, cid):
    n, halo, y, w = edges.shape
    rows = fields.shape[1]
    half, m = rows - halo, max(counts)
    hbm = pl.BlockSpec(memory_space=pl.ANY)
    smem = pl.BlockSpec(memory_space=pltpu.SMEM)
    dma = pltpu.SemaphoreType.DMA
    out = jax.ShapeDtypeStruct((n - 1, rows, y, w), F32)
    return pl.pallas_call(
        functools.partial(swap_kernel, counts),
        in_specs=[smem, hbm, hbm],
        out_specs=[hbm, hbm, hbm],
        out_shape=[out, out, jax.ShapeDtypeStruct((n, halo, y, w), F32)],
        scratch_shapes=[
            pltpu.VMEM((n, half, y, w), F32),
            pltpu.VMEM((2, m, half, y, w), F32),
            pltpu.VMEM((2, m, rows, y, w), F32),
            pltpu.VMEM((2, m, halo, y, w), F32),
            dma((n,)), dma((2, m)), dma((2, m)), dma((n,)), dma((n,)),
            dma((2, m)), dma((2, m)), dma((2, m)), dma((2, m)),
        ],
        compiler_params=pltpu.CompilerParams(collective_id=cid, has_side_effects=True),
        name="swap%d%d%d" % counts,
    )(plan, fields, edges)


def pairs_kernel(
    plan, fields, prior, nxt, halos, basis, basis_back, levels, out,
    room, one, two, own2, par2, prod, acc, stage, wheel, moves, sem, rim_sem, out_sem
):
    n, h, y, z = out.shape
    w = 2 * z
    half, rows = h // 2, fields.shape[1]
    halo = rows - half
    tall = y + PAD
    each = rows * tall
    most = prior.shape[0]
    slab = lax.axis_index("slab")
    quads, line, _ = factors()

    def field(src, s, f, first, count, sem):
        return pltpu.make_async_copy(
            src.at[s, pl.ds(first, count)],
            room.at[f + 1, pl.ds(rows - count if src is halos else first, count), pl.ds(0, y)],
            sem.at[f],
        )

    def each_field(do):
        for f in (0, n - 1, n, n + 1):
            do(field(fields, f, f, 0, rows, sem))
        for f in range(1, n - 1):
            do(field(fields, f, f, 0, half, sem))
            do(field(halos, f, f, 0, halo, rim_sem))
        for src, base, count in ((prior, n + 2, plan[INFO + 3]), (nxt, n + 2 + most, plan[INFO + 4])):
            for s in range(most):
                pl.when(s < count)(
                    lambda src=src, s=s, base=base: do(field(src, s, base + s, 0, rows, sem))
                )

    each_field(lambda c: c.start())
    acc[...] = jnp.zeros(acc.shape, F32)
    prod[0] = jnp.zeros((tall, w), F32)
    prod[:, y:, :] = jnp.zeros((h + 1, PAD, w), F32)
    room[0, rows - 1, y:, :] = jnp.zeros((PAD, w), F32)

    def blank(f):
        room[f + 1, :, y:, :] = jnp.zeros((rows, PAD, w), F32)

    def wipe(f, c):
        blank(f)
        return c

    lax.fori_loop(0, room.shape[0] - 1, wipe, 0)
    flat_room = room.reshape(room.shape[0] * each, w)
    flat_prod = prod.reshape((h + 1) * tall, w)

    k_at = lax.broadcasted_iota(jnp.int32, (2 * w, 2 * w), 0)
    c_at = lax.broadcasted_iota(jnp.int32, (2 * w, 2 * w), 1)
    task_k, half_k, task_c, half_c = k_at // w, k_at % w // z, c_at % w // z, c_at // w
    gap = k_at % z - c_at % z
    wheel[...] = jnp.where((task_k == task_c) & (half_k == half_c), gap, 4 * z)
    for ref in (one, two):
        planes = ref.shape[0]
        ref[0] = jnp.zeros(ref.shape[1:], F32)
        ref[:, 0:8, :] = jnp.zeros((planes, 8, w), F32)
        ref[:, 8 + y :, :] = jnp.zeros((planes, 8, w), F32)
    each_field(lambda c: c.wait())

    lane = lanes((y, w))
    low = lane < z
    pos = lane % z
    mu = jnp.broadcast_to(levels[...], (STRIP, w))

    def sweep(src, count, emit):
        def step(g, c):
            for r in range(0, y, STRIP):
                at = pl.ds(8 + r, STRIP)
                col = [src[g * UNROLL + q, at, :] for q in range(UNROLL + 2)]
                for q in range(UNROLL):
                    t = g * UNROLL + q
                    sides = src[t + 1, pl.ds(7 + r, STRIP), :] + src[t + 1, pl.ds(9 + r, STRIP), :]
                    emit(t, r, col[q + 1], (col[q] + col[q + 2]) + sides)
            return c

        lax.fori_loop(0, pl.cdiv(count, UNROLL), step, 0)

    def split(values):
        coarse = values.astype(jnp.bfloat16)
        return coarse, (values - coarse.astype(F32)).astype(jnp.bfloat16)

    def turn_z(values, wave):
        both = jnp.dot(
            jnp.concatenate(split(values), axis=1), wave[...], preferred_element_type=F32
        )
        return both[:, :w] + both[:, w:]

    def repeat(count, unroll, do):
        def step(g, c):
            for q in range(unroll):
                do(g * unroll + q)
            return c

        lax.fori_loop(0, count // unroll, step, 0)

    def group(g, c):
        p, q = g * 2 * TASK, (g * 2 + 1) * TASK
        rp, rq = (plan[p] + 1) * each, (plan[q] + 1) * each
        ap, aq, bp, bq = plan[p + 2], plan[q + 2], plan[p + 3], plan[q + 3]
        sp, sq = (plan[p + 1] + 1) * each - ap, (plan[q + 1] + 1) * each - aq
        col = lanes((1, 2 * w)) % w < z
        moves[...] = jnp.where(wheel[...] == jnp.where(col, -bp, -bq), 1.0, 0.0).astype(jnp.bfloat16)

        def planes(r):
            return jnp.where(r < half, r, r + half), jnp.where(r < half, r + half, r + half + halo)

        def dense(g, c):
            raw = []
            for q in range(DEPTH):
                for t in planes(jnp.maximum((g - 1) * DEPTH + q, 0)):
                    raw.append(two[t + 1, 8 : 8 + y, :])
            waves = turn_z(jnp.concatenate(raw, axis=0), basis)
            rs = [jnp.minimum(g * DEPTH + q, rows - 1) for q in range(DEPTH)]
            par = [
                jnp.concatenate(
                    [flat_room[pl.ds(sp + r * tall, y), :], flat_room[pl.ds(sq + r * tall, y), :]],
                    axis=1,
                )
                for r in rs
            ]
            par = jnp.concatenate(split(jnp.concatenate(par, axis=0)), axis=0)
            par = jnp.dot(par, moves[...], preferred_element_type=F32)
            par = par[: DEPTH * y] + par[DEPTH * y :]
            for q in range(DEPTH):
                old = planes(jnp.maximum((g - 1) * DEPTH + q, 0))
                for side in range(2):
                    at = (2 * q + side) * y
                    one[old[side] + 1, 8 : 8 + y, :] = waves[at : at + y]
            for q, r in enumerate(rs):
                own_p = flat_room[pl.ds(rp + r * tall, y), :]
                own_q = flat_room[pl.ds(rq + r * tall, y), :]
                own_a = jnp.where(low, own_p, pltpu.roll(own_q, z, axis=1))
                own_b = jnp.where(low, pltpu.roll(own_p, z, axis=1), own_q)
                for t, own, half_par in zip(
                    planes(r), (own_a, own_b), jnp.split(par[q * y : (q + 1) * y], 2, axis=1)
                ):
                    two[t + 1, 8 : 8 + y, :] = own * half_par
                    own2[t] = own
                    par2[t] = half_par
            return c

        lax.fori_loop(0, rows // DEPTH + 1, dense, 0)

        count = h + EDGE - 1
        for b, c2 in quads:
            def first(t, r, cur, near, b=b):
                two[t + 1, pl.ds(8 + r, STRIP), :] = near + (mu + b) * cur

            def second(t, r, cur, near, c2=c2):
                at = pl.ds(8 + r, STRIP)
                one[t + 1, at, :] = (near + mu * cur) + c2 * one[t + 1, at, :]

            sweep(one, count, first)
            sweep(two, count - 1, second)
            count -= 2

        kp, kq, mp, mq = plan[p + 4], plan[q + 4], plan[p + 5], plan[q + 5]

        def last(t, r, cur, near):
            two[t + 1, pl.ds(8 + r, STRIP), :] = near + (mu + line) * cur

        sweep(one, h, last)

        def finish(g, c):
            both = [two[g * 4 + q + 1, 8 : 8 + y, :] for q in range(4)]
            both = turn_z(jnp.concatenate(both, axis=0), basis_back)
            for q in range(4):
                t = g * 4 + q
                pot = both[q * y : (q + 1) * y]
                par2[t] = pot * par2[t]
                prod[t + 1, 0:y, :] = pot * own2[t]
            return c

        lax.fori_loop(0, h // 4, finish, 0)

        for k, m, a, b, side in ((kp, mp, ap, bp, low), (kq, mq, aq, bq, jnp.logical_not(low))):
            @pl.when(k < n)
            def _(k=k, side=side):
                def plane(t):
                    acc[k, t] += jnp.where(side, par2[t], 0.0)

                repeat(h, 4, plane)

            @pl.when(m < n)
            def _(m=m, a=a, b=b, side=side):
                back_z = pos + b
                good = side & (back_z >= 0) & (back_z < z)
                turn = lax.rem(w - b, w)

                def plane(t):
                    moved = pltpu.roll(flat_prod[pl.ds((t + 1) * tall + a, y), :], turn, axis=1)
                    acc[m, t] += jnp.where(good, moved, 0.0)

                repeat(h, 4, plane)

        return c

    tasks = plan[INFO + 6]
    lax.fori_loop(0, lax.div(tasks + 1, 2), group, 0)

    def leave(k, slot):
        return pltpu.make_async_copy(stage.at[slot], out.at[k], out_sem.at[slot])

    def write(k, c):
        slot = lax.rem(k, 2)
        pl.when(k >= 2)(lambda: leave(k - 2, slot).wait())

        def plane(t):
            value = acc[k, t]
            value = value + pltpu.roll(value, z, axis=1)
            stage[slot, jnp.where(slab == 0, t, h - 1 - t)] = value[:, :z]

        repeat(h, 4, plane)
        leave(k, slot).start()
        return c

    lax.fori_loop(0, n, write, 0)
    for k in (n - 2, n - 1):
        leave(k, k % 2).wait()


def sines(z):
    k = np.arange(1, z + 1)
    wave = np.sqrt(2.0 / (z + 1)) * np.sin(np.pi * np.outer(k, k) / (z + 1))
    wave = np.kron(np.eye(2), wave).astype(np.float32)
    levels = np.tile(2.0 * np.cos(np.pi * k / (z + 1)), 2).astype(np.float32)[None]

    def parts(values):
        coarse = jnp.asarray(values).astype(jnp.bfloat16)
        fine = (jnp.asarray(values) - coarse.astype(F32)).astype(jnp.bfloat16)
        top = jnp.concatenate([coarse, fine], axis=1)
        bottom = jnp.concatenate([coarse, jnp.zeros_like(fine)], axis=1)
        return jnp.concatenate([top, bottom], axis=0)

    return parts(wave), parts(wave * np.float32(factors()[2])), jnp.asarray(levels)


def solve_pairs(plan, fields, prior, nxt, halos, shape):
    n, h, y, z = shape
    w, rows = 2 * z, fields.shape[1]
    most = prior.shape[0]
    hbm = pl.BlockSpec(memory_space=pl.ANY)
    vmem = pl.BlockSpec(memory_space=pltpu.VMEM)
    total = n + 2 + 2 * most
    planes = 2 * rows
    return pl.pallas_call(
        pairs_kernel,
        grid_spec=pltpu.PrefetchScalarGridSpec(
            num_scalar_prefetch=1,
            grid=(1,),
            in_specs=[hbm, hbm, hbm, hbm, vmem, vmem, vmem],
            out_specs=hbm,
            scratch_shapes=[
                pltpu.VMEM((total + 1, rows, y + PAD, w), F32),
                pltpu.VMEM((planes + 6, y + 16, w), F32),
                pltpu.VMEM((planes + 6, y + 16, w), F32),
                pltpu.VMEM((planes, y, w), F32),
                pltpu.VMEM((planes, y, w), F32),
                pltpu.VMEM((h + 1, y + PAD, w), F32),
                pltpu.VMEM((n, h, y, w), F32),
                pltpu.VMEM((2, h, y, z), F32),
                pltpu.VMEM((2 * w, 2 * w), jnp.int32),
                pltpu.VMEM((2 * w, 2 * w), jnp.bfloat16),
                pltpu.SemaphoreType.DMA((total,)),
                pltpu.SemaphoreType.DMA((n,)),
                pltpu.SemaphoreType.DMA((2,)),
            ],
        ),
        out_shape=jax.ShapeDtypeStruct(shape, F32),
        compiler_params=pltpu.CompilerParams(vmem_limit_bytes=56 * 1024 * 1024),
        name="pairs",
    )(plan, fields, prior, nxt, halos, *sines(z))


def fast_body(orbitals, offsets, pairs, live):
    n = orbitals.shape[0]
    few = min(4, n - 1)
    combos = [(a, b, few) for a in range(1, few) for b in range(1, few)]
    combos += [(few, few, few), (n - 1, n - 1, n - 1)]
    fields, every, edges = front(orbitals, pairs, live)
    plan, which = make_plan(every, offsets, n, combos)

    def branch(counts, cid):
        return lambda _: swap(counts, plan, fields, edges, cid)

    prior, nxt, halos = lax.switch(
        which[0], [branch(c, 2 + i) for i, c in enumerate(combos)], 0
    )
    return solve_pairs(plan, fields, prior, nxt, halos, orbitals.shape)


def body(orbitals, offsets, pairs, live):
    n = orbitals.shape[0]
    slots = pairs.shape[0]
    total = offsets.shape[0]
    blocks = total // n
    slabs = lax.axis_size("slab")
    me = lax.axis_index(CYCLE)
    packed = pack(orbitals)

    mine = jnp.concatenate([pairs, live[:, None]], axis=1)
    every = share(jnp.pad(mine, ((0, 0), (0, 128 - mine.shape[1]))))
    ids = jnp.arange(blocks, dtype=jnp.int32)
    second = every[:, :, 1]
    alive = every[:, :, 2] > 0
    orb = jnp.arange(n, dtype=jnp.int32)
    sides = jnp.stack([(ids - 1) % blocks, (ids + 1) % blocks])
    hit = alive[None] & (second[None] // n == sides[:, :, None])
    need = jnp.any(
        hit[..., None] & (second[None, :, :, None] % n == orb), axis=2
    )
    count = jnp.sum(need.astype(jnp.int32), axis=2)
    most = jnp.max(count)

    after, before = (me + 1) % blocks, (me - 1) % blocks
    flags = jnp.stack(
        [need[0, me], need[1, me], need[0, after], need[1, before]]
    ).astype(jnp.int32)
    spot = jnp.sum(
        flags[:, None, :] * (orb[None, :] < orb[:, None]).astype(jnp.int32)[None], axis=2
    )
    lists = jnp.sum(
        (flags[:, None, :] * (spot[:, None, :] == orb[None, :, None])) * orb, axis=2
    )
    back = jnp.stack(
        [spot[2] * flags[2], flags[2], spot[3] * flags[3], flags[3]]
    )

    i, j, on = pairs[:, 0], pairs[:, 1], live > 0
    owner, local = j // n, j % n
    pick_j = (local[:, None] == orb[None, :]).astype(jnp.int32)
    from_prior = (owner == before) & on
    from_next = (owner == after) & on
    kind = jnp.where(from_prior, 1, jnp.where(from_next, 2, 0))
    where_prior = jnp.sum(pick_j * spot[0][None, :], axis=1) * from_prior
    where_next = jnp.sum(pick_j * spot[1][None, :], axis=1) * from_next
    ids_all = jnp.arange(total, dtype=jnp.int32)
    diff = (j[:, None] == ids_all).astype(jnp.int32) - (i[:, None] == ids_all).astype(jnp.int32)
    shift = jnp.sum(diff[:, :, None] * offsets[None], axis=1)
    plan = jnp.stack(
        [i % n, local, where_prior, where_next, kind, shift[:, 0], shift[:, 1], live]
    ).astype(jnp.int32)
    order = jnp.where(on, jnp.where(kind > 0, 0, 1), 2) * slots + jnp.arange(slots)
    rank = jnp.sum((order[None, :] < order[:, None]).astype(jnp.int32), axis=1)
    move = (rank[:, None] == jnp.arange(slots)[None, :]).astype(jnp.int32)
    plan = jnp.sum(plan[:, :, None] * move[None], axis=1)
    far, lively = jnp.sum((kind > 0).astype(jnp.int32)), jnp.sum(on.astype(jnp.int32))
    tail = jnp.where(jnp.arange(slots) == 0, far, lively)
    plan = jnp.concatenate([plan, tail[None]], axis=0)
    ends = jnp.stack([lax.axis_index("slab"), slabs]).astype(jnp.int32)

    up = [(s, s + 1) for s in range(slabs - 1)]
    down = [(s + 1, s) for s in range(slabs - 1)]

    def branch(m):
        def run(_):
            to_next, to_prior = gather(packed, lists[2:], m)
            prior = cycle(to_next, 1)
            nxt = cycle(to_prior, -1)
            partner, density, low, high = densities(plan, packed, prior, nxt)
            below = lax.ppermute(high, "slab", up)
            above = lax.ppermute(low, "slab", down)
            given = (plan, ends, density, partner, packed, below, above, m)
            acc, acc_prior, acc_next = solve(True, *given)
            from_next, from_prior = cycle(acc_prior, -1), cycle(acc_next, 1)
            (acc_near,) = solve(False, *given)
            return combine(back, acc, acc_near, from_next, from_prior)

        return run

    sizes = sorted({min(s, slots - 1) for s in (3, 4, 5)} | {slots - 1})
    which = sum((most > s).astype(jnp.int32) for s in sizes[:-1])
    return lax.switch(which, [branch(s) for s in sizes], 0)


def solution(mesh):
    placed = (
        P(CYCLE, "slab", None, None),
        P(),
        P(CYCLE, None),
        P(CYCLE),
    )
    return jax.shard_map(
        fast_body if mesh.shape["slab"] == 2 else body,
        mesh=mesh,
        in_specs=placed,
        out_specs=P(CYCLE, "slab", None, None),
        check_vma=False,
    )
```

```python
import cmath
import functools
import math

import jax
import jax.numpy as jnp
import numpy as np
from jax import lax
from jax.experimental import pallas as pl
from jax.experimental.pallas import tpu as pltpu
from jax.sharding import PartitionSpec as P

PASSES = 8
DIAG = 6.25
THETA = 1.075
DELTA = 0.925
EDGE = PASSES - 1
PAD = 16
CYCLE = ("grp", "orb")
F32 = jnp.float32


def coefs():
    sigma = THETA / DELTA
    coef = 1.0 / sigma
    out = []
    for _ in range(PASSES - 1):
        new = 1.0 / (2.0 * sigma - coef)
        out.append((new * coef, 2.0 * new / (DELTA * DIAG)))
        coef = new
    return out


def lanes(shape):
    return lax.broadcasted_iota(jnp.int32, shape, len(shape) - 1)


def share_kernel(mine, every, send_sem, recv_sem):
    size, width = lax.axis_size(CYCLE), lax.axis_size("orb")
    me = lax.axis_index("grp") * width + lax.axis_index("orb")

    def peer(s):
        to = lax.rem(me + s, size)
        return {"grp": lax.div(to, width), "orb": lax.rem(to, width)}

    def greet(s, c):
        pl.semaphore_signal(
            barrier, inc=1, device_id=peer(s), device_id_type=pl.DeviceIdType.MESH
        )
        return c

    def copy(s, slot):
        return pltpu.make_async_remote_copy(
            src_ref=mine,
            dst_ref=every.at[slot],
            send_sem=send_sem.at[s],
            recv_sem=recv_sem.at[s],
            device_id=peer(s),
            device_id_type=pl.DeviceIdType.MESH,
        )

    def send(s, c):
        copy(s, me).start()
        return c

    def finish(s, c):
        copy(s, lax.rem(me + size - s, size)).wait()
        return c

    barrier = pltpu.get_barrier_semaphore()
    lax.fori_loop(1, size, greet, 0)
    pl.semaphore_wait(barrier, size - 1)
    lax.fori_loop(1, size, send, 0)
    every[me] = mine[...]
    lax.fori_loop(1, size, finish, 0)


def share(mine):
    size = lax.axis_size(CYCLE)
    vmem = pl.BlockSpec(memory_space=pltpu.VMEM)
    return pl.pallas_call(
        share_kernel,
        in_specs=[vmem],
        out_specs=vmem,
        out_shape=jax.ShapeDtypeStruct((size,) + mine.shape, mine.dtype),
        scratch_shapes=[pltpu.SemaphoreType.DMA((size,)), pltpu.SemaphoreType.DMA((size,))],
        compiler_params=pltpu.CompilerParams(collective_id=0, has_side_effects=True),
        name="share",
    )(mine)


def pack_kernel(src, dst):
    half = dst.shape[1]
    dst[0] = jnp.concatenate([src[0, :half], src[0, half:]], axis=-1)


def pack(orbitals):
    n, x, y, z = orbitals.shape
    return pl.pallas_call(
        pack_kernel,
        grid=(n,),
        in_specs=[pl.BlockSpec((1, x, y, z), lambda i: (i, 0, 0, 0))],
        out_specs=pl.BlockSpec((1, x // 2, y, 2 * z), lambda i: (i, 0, 0, 0)),
        out_shape=jax.ShapeDtypeStruct((n, x // 2, y, 2 * z), F32),
        name="pack",
    )(orbitals)


def copy_kernel(idx, src_a, src_b, dst_a, dst_b):
    dst_a[...] = src_a[...]
    dst_b[...] = src_b[...]


def gather(packed, lists, m):
    _, h, y, w = packed.shape
    blk = (1, h, y, w)
    out = jax.ShapeDtypeStruct((m, h, y, w), F32)
    return pl.pallas_call(
        copy_kernel,
        grid_spec=pltpu.PrefetchScalarGridSpec(
            num_scalar_prefetch=1,
            grid=(m,),
            in_specs=[
                pl.BlockSpec(blk, lambda i, idx: (idx[0, i], 0, 0, 0)),
                pl.BlockSpec(blk, lambda i, idx: (idx[1, i], 0, 0, 0)),
            ],
            out_specs=[pl.BlockSpec(blk, lambda i, idx: (i, 0, 0, 0))] * 2,
        ),
        out_shape=[out, out],
        name="gather",
    )(lists, packed, packed)


def place(value, room, a, b):
    y, w = value.shape[1:]
    z = w // 2
    room[:, PAD : PAD + y, :] = value
    moved = room[:, pl.ds(PAD - a, y), :]
    moved = pltpu.roll(moved, lax.rem(b + w, w), axis=2)
    pos = lanes(moved.shape) % z - b
    return jnp.where((pos >= 0) & (pos < z), moved, 0.0)


def clear_room(room):
    y = room.shape[1] - 2 * PAD
    room[:, :PAD, :] = jnp.zeros((room.shape[0], PAD, room.shape[2]), F32)
    room[:, PAD + y :, :] = jnp.zeros((room.shape[0], PAD, room.shape[2]), F32)


def density_kernel(plan, own, mine, prior, nxt, partner, density, low, high, room):
    p = pl.program_id(0)
    kind = plan[4, p]
    a, b = plan[5, p], plan[6, p]

    @pl.when(p == 0)
    def _():
        clear_room(room)

    on = plan[7, p] > 0

    def go(src):
        part = place(src[0], room, a, b)
        partner[0] = part
        dens = own[0] * part
        density[0] = dens
        h, y, w = dens.shape
        flat = jnp.concatenate([dens[..., : w // 2], dens[..., w // 2 :]], axis=0)
        top, bot = flat[:EDGE], flat[2 * h - EDGE :]
        low[0] = jnp.concatenate([top[:, : y // 2], top[:, y // 2 :]], axis=-1)
        high[0] = jnp.concatenate([bot[:, : y // 2], bot[:, y // 2 :]], axis=-1)

    for value, src in enumerate((mine, prior, nxt)):
        pl.when(on & (kind == value))(functools.partial(go, src))


def densities(plan, packed, prior, nxt):
    slots = plan.shape[1]
    _, h, y, w = packed.shape
    blk = (1, h, y, w)
    eblk = (1, EDGE, y // 2, w)

    def at(row):
        return pl.BlockSpec(
            blk, lambda i, plan: (plan[row, jnp.minimum(i, plan[8, 1] - 1)], 0, 0, 0)
        )

    full = jax.ShapeDtypeStruct((slots, h, y, w), F32)
    edge = jax.ShapeDtypeStruct((slots,) + eblk[1:], F32)
    here = lambda i, plan: (jnp.minimum(i, plan[8, 1] - 1), 0, 0, 0)
    return pl.pallas_call(
        density_kernel,
        grid_spec=pltpu.PrefetchScalarGridSpec(
            num_scalar_prefetch=1,
            grid=(slots,),
            in_specs=[at(0), at(1), at(2), at(3)],
            out_specs=[
                pl.BlockSpec(blk, here),
                pl.BlockSpec(blk, here),
                pl.BlockSpec(eblk, here),
                pl.BlockSpec(eblk, here),
            ],
            scratch_shapes=[pltpu.VMEM((h, y + 2 * PAD, w), F32)],
        ),
        out_shape=[full, full, edge, edge],
        name="density",
    )(plan, packed, packed, prior, nxt)


def solve_kernel(remote, plan, ends, density, partner, own, below, above, *refs):
    accs, (resid, step_a, step_b, total, mask, room) = refs[:-6], refs[-6:]
    acc = accs[0]
    p = pl.program_id(0)
    h, y, w = density.shape[1:]
    z = w // 2
    rows = h + 2 * EDGE
    group = 4 if h % 4 == 0 else 1

    @pl.when(p == 0)
    def _():
        clear_room(room)
        for ref in accs:
            ref[...] = jnp.zeros(ref.shape, F32)
        for ref in (step_a, step_b):
            ref[:, :8, :] = jnp.zeros((rows, 8, w), F32)
            ref[:, 8 + y :, :] = jnp.zeros((rows, 8, w), F32)
        lane = lanes((1, w))
        first = ends[0] == 0
        last = ends[0] == ends[1] - 1
        for t in range(rows):
            plane = jnp.where(lane < z, t - EDGE, t - EDGE + h)
            outside = ((plane < 0) & first) | ((plane >= 2 * h) & last)
            mask[t] = jnp.where(outside, 0.0, 1.0)

    chosen = (plan[4, p] > 0) if remote else (plan[4, p] == 0)

    @pl.when((plan[7, p] > 0) & chosen)
    def _():
        def unfold(part):
            return jnp.concatenate([part[..., :z], part[..., z:]], axis=1)

        dens = density[0]
        line = jnp.concatenate(
            [unfold(below[0]), dens[..., :z], dens[..., z:], unfold(above[0])], axis=0
        )
        resid[...] = jnp.concatenate([line[:rows], line[h:]], axis=-1)
        step_a[:, 8 : 8 + y, :] = resid[...] * (1.0 / (DIAG * THETA))
        total[...] = step_a[EDGE : EDGE + h, 8 : 8 + y, :]
        lane = lanes((y, w)) % z
        not_low = lane > 0
        not_high = lane < z - 1
        bufs = [step_a, step_b]
        for turn, (keep, gain) in enumerate(coefs()):
            now, then = bufs[turn % 2], bufs[1 - turn % 2]
            core_only = turn == PASSES - 2

            def row(t, now=now, then=then, keep=keep, gain=gain):
                core = now[t, 8 : 8 + y, :]
                near = now[t - 1, 8 : 8 + y, :] + now[t + 1, 8 : 8 + y, :]
                near = near + (now[t, 7 : 7 + y, :] + now[t, 9 : 9 + y, :])
                side = jnp.where(not_low, pltpu.roll(core, 1, axis=1), 0.0)
                side = side + jnp.where(not_high, pltpu.roll(core, w - 1, axis=1), 0.0)
                left = (resid[t] - DIAG * core) + (near + side)
                return left, keep * core + gain * left

            def outer(k, c, row=row, then=then):
                for t in (EDGE - 1 - k, EDGE + h + k):
                    left, fresh = row(t)
                    resid[t] = left
                    then[t, 8 : 8 + y, :] = fresh * mask[t]
                return c

            def inner(k, c, row=row, then=then, last=core_only):
                for g in range(group):
                    t = EDGE + k * group + g
                    left, fresh = row(t)
                    if not last:
                        resid[t] = left
                        then[t, 8 : 8 + y, :] = fresh
                    total[t - EDGE] += fresh
                return c

            if turn + 1 < EDGE:
                lax.fori_loop(0, EDGE - turn - 1, outer, 0)
            lax.fori_loop(0, h // group, inner, 0)

        pot = total[...]
        acc[plan[0, p]] += pot * partner[0]
        back = place(pot * own[0], room, -plan[5, p], -plan[6, p])
        if not remote:
            acc[plan[1, p]] += back
        else:
            for value in (1, 2):

                @pl.when(plan[4, p] == value)
                def _(ref=accs[value], value=value):
                    ref[plan[1 + value, p]] += back


def solve(remote, plan, ends, density, partner, packed, below, above, m):
    slots = plan.shape[1]
    n, h, y, w = packed.shape
    blk = (1, h, y, w)
    eblk = (1, EDGE, y // 2, w)
    rows = h + 2 * EDGE

    def spot(i, plan):
        far = plan[8, 0]
        if remote:
            return jnp.minimum(i, jnp.maximum(far - 1, 0))
        return jnp.clip(i, jnp.minimum(far, plan[8, 1] - 1), plan[8, 1] - 1)

    here = lambda i, plan, ends: (spot(i, plan), 0, 0, 0)
    fixed = lambda i, plan, ends: (0, 0, 0, 0)
    shapes = [(n, h, y, w)] + [(m, h, y, w)] * (2 if remote else 0)
    return pl.pallas_call(
        functools.partial(solve_kernel, remote),
        grid_spec=pltpu.PrefetchScalarGridSpec(
            num_scalar_prefetch=2,
            grid=(slots,),
            in_specs=[
                pl.BlockSpec(blk, here),
                pl.BlockSpec(blk, here),
                pl.BlockSpec(blk, lambda i, plan, ends: (plan[0, spot(i, plan)], 0, 0, 0)),
                pl.BlockSpec(eblk, here),
                pl.BlockSpec(eblk, here),
            ],
            out_specs=[pl.BlockSpec(s, fixed) for s in shapes],
            scratch_shapes=[
                pltpu.VMEM((rows, y, w), F32),
                pltpu.VMEM((rows, y + 16, w), F32),
                pltpu.VMEM((rows, y + 16, w), F32),
                pltpu.VMEM((h, y, w), F32),
                pltpu.VMEM((rows, 1, w), F32),
                pltpu.VMEM((h, y + 2 * PAD, w), F32),
            ],
        ),
        out_shape=[jax.ShapeDtypeStruct(s, F32) for s in shapes],
        compiler_params=pltpu.CompilerParams(vmem_limit_bytes=56 * 1024 * 1024),
        cost_estimate=pl.CostEstimate(
            flops=slots * rows * y * w * 100, bytes_accessed=24 << 20, transcendentals=0
        ),
        name="solve_far" if remote else "solve_near",
    )(plan, ends, density, partner, packed, below, above)


def combine_kernel(back, acc, acc_near, from_next, from_prior, out):
    k = pl.program_id(0)
    h = acc.shape[1]
    z = acc.shape[3] // 2
    value = acc[0] + acc_near[0]
    value = value + jnp.where(back[1, k] > 0, from_next[0], 0.0)
    value = value + jnp.where(back[3, k] > 0, from_prior[0], 0.0)
    out[0, :h] = value[:, :, :z]
    out[0, h:] = value[:, :, z:]


def combine(back, acc, acc_near, from_next, from_prior):
    n, h, y, w = acc.shape
    blk = (1, h, y, w)
    return pl.pallas_call(
        combine_kernel,
        grid_spec=pltpu.PrefetchScalarGridSpec(
            num_scalar_prefetch=1,
            grid=(n,),
            in_specs=[
                pl.BlockSpec(blk, lambda i, back: (i, 0, 0, 0)),
                pl.BlockSpec(blk, lambda i, back: (i, 0, 0, 0)),
                pl.BlockSpec(blk, lambda i, back: (back[0, i], 0, 0, 0)),
                pl.BlockSpec(blk, lambda i, back: (back[2, i], 0, 0, 0)),
            ],
            out_specs=pl.BlockSpec((1, 2 * h, y, w // 2), lambda i, back: (i, 0, 0, 0)),
        ),
        out_shape=jax.ShapeDtypeStruct((n, 2 * h, y, w // 2), F32),
        name="combine",
    )(back, acc, acc_near, from_next, from_prior)


def cycle(field, by):
    size = lax.axis_size(CYCLE)
    return lax.ppermute(field, CYCLE, [(i, (i + by) % size) for i in range(size)])


TASK = 8
LISTS = 256
INFO = 320
PLAN = 384
EARLY = 3
AHEAD = 4
UNROLL = 4
DEPTH = 5
STRIP = 8


def factors():
    ratio = THETA / DELTA
    tall = math.acosh(ratio)
    points = [cmath.cosh(complex(tall, k * math.pi / 4)) for k in range(8)]
    marks = [DIAG * (1.0 - (THETA - DELTA * x)) for x in points]
    quads = [(-2.0 * marks[k].real, abs(marks[k]) ** 2) for k in (1, 2, 3)]
    line = -marks[4].real
    coef, resid, value, step = 1.0 / ratio, 1.0, 0.0, 1.0 / (DIAG * THETA)
    value += step
    for keep, gain in coefs():
        resid -= DIAG * step
        step = keep * step + gain * resid
        value += step
    product = line
    for _, c in quads:
        product *= c
    return quads, line, value / product


def front_kernel(
    orbs, pairs, live, fields, every, edges, stage, own, far, edge, table,
    in_sem, out_sem, rim_sem, tab_send, tab_recv, edge_send, edge_recv, far_send, far_recv,
):
    n, h = orbs.shape[0], orbs.shape[1]
    half = h // 2
    halo = edge.shape[1]
    size, width = lax.axis_size(CYCLE), lax.axis_size("orb")
    me = lax.axis_index("grp") * width + lax.axis_index("orb")
    slab = lax.axis_index("slab")

    def peer(s):
        to = lax.rem(me + s, size)
        return {"grp": lax.div(to, width), "orb": lax.rem(to, width)}

    def load(k):
        return pltpu.make_async_copy(orbs.at[k], stage.at[k], in_sem.at[k])

    def order(q):
        return jnp.where(q == 0, 0, jnp.where(q == 1, n - 1, q - 1))

    def begin(q, c):
        load(order(q)).start()
        return c

    lax.fori_loop(0, n, begin, 0)

    barrier = pltpu.get_barrier_semaphore()

    def greet(s, c):
        pl.semaphore_signal(
            barrier, inc=1, device_id=peer(s), device_id_type=pl.DeviceIdType.MESH
        )
        return c

    lax.fori_loop(1, size, greet, 0)
    pl.semaphore_signal(
        barrier, inc=1, device_id={"slab": 1 - slab}, device_id_type=pl.DeviceIdType.MESH
    )
    table[0:2, 0:n] = pairs[...]
    table[2:3, 0:n] = live[...]
    pl.semaphore_wait(barrier, size)

    def share_copy(s, slot):
        return pltpu.make_async_remote_copy(
            src_ref=table, dst_ref=every.at[slot],
            send_sem=tab_send.at[s], recv_sem=tab_recv.at[s],
            device_id=peer(s), device_id_type=pl.DeviceIdType.MESH,
        )

    def share_send(s, c):
        share_copy(s, me).start()
        return c

    lax.fori_loop(1, size, share_send, 0)
    every[me] = table[...]

    def edge_copy(e, f, dst):
        return pltpu.make_async_remote_copy(
            src_ref=edge.at[f], dst_ref=dst,
            send_sem=edge_send.at[e], recv_sem=edge_recv.at[e],
            device_id={"slab": 1 - slab}, device_id_type=pl.DeviceIdType.MESH,
        )

    def own_edge(k, e):
        return edge_copy(e, k, own.at[k, pl.ds(half, halo)])

    def far_copy(k, f, s):
        return pltpu.make_async_remote_copy(
            src_ref=own.at[k, pl.ds(0, half)], dst_ref=far.at[f, pl.ds(0, half)],
            send_sem=far_send.at[f], recv_sem=far_recv.at[f],
            device_id=peer(s), device_id_type=pl.DeviceIdType.MESH,
        )

    def spot(t):
        return jnp.where(slab == 0, t, h - 1 - t)

    def pack(k):
        def row(r, c):
            own[k, r] = jnp.concatenate(
                [stage[k, spot(r)], stage[k, spot(r + half)]], axis=-1
            )
            return c

        lax.fori_loop(0, half, row, 0)

    def make_edge(k):
        for m in range(halo):
            edge[k, m] = jnp.concatenate(
                [stage[k, spot(h - 1 - m)], stage[k, spot(h - 1 - halo - m)]], axis=-1
            )

    def save(k):
        return pltpu.make_async_copy(
            own.at[k, pl.ds(0, half)], fields.at[k, pl.ds(0, half)], out_sem.at[k]
        )

    def rim(k, f, src):
        return pltpu.make_async_copy(
            src.at[k, pl.ds(half, halo)], fields.at[f, pl.ds(half, halo)], rim_sem.at[f]
        )

    def keep_edge(k):
        return pltpu.make_async_copy(edge.at[k], edges.at[k], rim_sem.at[k])

    early = edge_send.shape[0] - 4

    up, down = far_copy(n - 1, 0, 1), far_copy(0, 1, size - 1)
    for k, send, e in ((0, down, 0), (n - 1, up, 1)):
        load(k).wait()
        pack(k)
        send.start()
        make_edge(k)
        own_edge(k, e).start()
        save(k).start()

    def rest(k, c):
        load(k).wait()
        pack(k)
        save(k).start()
        make_edge(k)
        pl.when(k <= early)(lambda: own_edge(k, 3 + k).start())
        pl.when(k > early)(lambda: keep_edge(k).start())
        return c

    lax.fori_loop(1, n - 1, rest, 0)

    def share_done(s, c):
        share_copy(s, lax.rem(me + size - s, size)).wait()
        return c

    lax.fori_loop(1, size, share_done, 0)

    low = lanes((1, own.shape[-1])) < own.shape[-1] // 2
    for f, copy in ((1, down), (0, up)):
        copy.wait()
        for m in range(halo):
            a, b = far[f, half - 1 - m], far[f, half - 1 - halo - m]
            edge[n + f, m] = jnp.where(low, pltpu.roll(a, a.shape[-1] // 2, axis=1), b)
        edge_copy(2 + f, n + f, far.at[f, pl.ds(half, halo)]).start()
        pltpu.make_async_copy(
            far.at[f, pl.ds(0, half)], fields.at[n + f, pl.ds(0, half)], out_sem.at[n + f]
        ).start()

    own_rims = [(0, 0), (n - 1, 1)] + [(k, 3 + k) for k in range(1, early + 1)]
    for k, e in own_rims:
        own_edge(k, e).wait()
        rim(k, k, own).start()
    for f in (1, 0):
        edge_copy(2 + f, n + f, far.at[f, pl.ds(half, halo)]).wait()
        rim(f, n + f, far).start()

    def out_done(k, c):
        save(k).wait()
        return c

    def edge_done(k, c):
        keep_edge(k).wait()
        return c

    lax.fori_loop(0, n, out_done, 0)
    lax.fori_loop(early + 1, n - 1, edge_done, 0)
    for k, _ in own_rims:
        rim(k, k, own).wait()
    for f in (1, 0):
        rim(f, n + f, far).wait()
        pltpu.make_async_copy(
            far.at[f, pl.ds(0, half)], fields.at[n + f, pl.ds(0, half)], out_sem.at[n + f]
        ).wait()


def front(orbitals, pairs, live):
    n, h, y, z = orbitals.shape
    half, halo, w = h // 2, (EDGE + 1) // 2, 2 * z
    size = lax.axis_size(CYCLE)
    vmem = pl.BlockSpec(memory_space=pltpu.VMEM)
    hbm = pl.BlockSpec(memory_space=pl.ANY)
    dma = pltpu.SemaphoreType.DMA
    return pl.pallas_call(
        front_kernel,
        in_specs=[hbm, vmem, vmem],
        out_specs=[hbm, vmem, hbm],
        out_shape=[
            jax.ShapeDtypeStruct((n + 2, half + halo, y, w), F32),
            jax.ShapeDtypeStruct((size, 8, 128), jnp.int32),
            jax.ShapeDtypeStruct((n, halo, y, w), F32),
        ],
        scratch_shapes=[
            pltpu.VMEM((n, h, y, z), F32),
            pltpu.VMEM((n, half + halo, y, w), F32),
            pltpu.VMEM((2, half + halo, y, w), F32),
            pltpu.VMEM((n + 2, halo, y, w), F32),
            pltpu.VMEM((8, 128), jnp.int32),
            dma((n,)), dma((n + 2,)), dma((n + 2,)), dma((size,)), dma((size,)),
            dma((4 + EARLY,)), dma((4 + EARLY,)), dma((2,)), dma((2,)),
        ],
        compiler_params=pltpu.CompilerParams(collective_id=1, has_side_effects=True),
        name="front",
    )(orbitals, pairs.T, live[None])


def plan_kernel(n, combos, every, offsets, plan, which, ups, downs, nups, ndowns, alive):
    size = every.shape[0]
    width = lax.axis_size("orb")
    me = lax.axis_index("grp") * width + lax.axis_index("orb")
    before, after = lax.rem(me + size - 1, size), lax.rem(me + 1, size)

    def clear(e, c):
        ups[e] = 0
        downs[e] = 0
        nups[e] = 0
        ndowns[e] = 0
        alive[e] = sum(every[e, 2, r] for r in range(n))
        return c

    lax.fori_loop(0, size, clear, 0)

    def read(blk, r):
        i, j = every[blk, 0, r], every[blk, 1, r]
        bj = lax.div(j, n)
        is_up = bj == lax.rem(blk + 1, size)
        li, lj = lax.rem(i, n), lax.rem(j, n)
        u, v = jnp.where(is_up, li, lj), jnp.where(is_up, lj, li)
        return i, j, bj, u, v, jnp.where(is_up, blk, bj)

    def mark(blk, c):
        def row(r, c):
            i, j, bj, u, v, edge = read(blk, r)

            @pl.when(bj != blk)
            def _():
                for bits, counts, x, free in ((ups, nups, u, n - 1), (downs, ndowns, v, 0)):
                    bit = jnp.where(x == free, 0, lax.shift_left(1, x))
                    had = bits[edge]
                    bits[edge] = had | bit
                    counts[edge] = counts[edge] + jnp.where((had | bit) != had, 1, 0)

            return c

        return lax.fori_loop(2, alive[blk], row, c)

    lax.fori_loop(0, size, mark, 0)

    def widest(e, most):
        o = lax.rem(e, width)
        mine = jnp.where(o % 2 == 0, 2, jnp.where(o == width - 1, 1, 0))
        here = jnp.maximum(nups[e], ndowns[e])
        return tuple(jnp.maximum(m, jnp.where(mine == c, here, 0)) for c, m in enumerate(most))

    most = lax.fori_loop(0, size, widest, (jnp.int32(0),) * 3)
    pick = jnp.int32(len(combos) - 1)
    for c in range(len(combos) - 2, -1, -1):
        fit = functools.reduce(lambda p, q: p & q, [m <= k for m, k in zip(most, combos[c])])
        pick = jnp.where(fit, c, pick)
    which[0] = pick

    def listing(bits, base):
        def step(q, s):
            plan[base + s] = q
            return s + (lax.shift_right_logical(bits, q) & 1)

        for q in range(n):
            plan[base + q] = 0
        return lax.fori_loop(0, n, step, jnp.int32(0))

    listing(ups[me], LISTS)
    listing(downs[before], LISTS + 2 * n)
    plan[INFO + 3] = nups[before]
    plan[INFO + 4] = ndowns[me]

    def rank(bits, x):
        return sum(
            jnp.where(q < x, lax.shift_right_logical(bits, q) & 1, 0) for q in range(n)
        )

    def place_of(x):
        blk, loc = lax.div(x, n), lax.rem(x, n)
        from_before = jnp.where(loc == n - 1, n, n + 2 + rank(ups[before], loc))
        from_after = jnp.where(loc == 0, n + 1, n + 2 + n - 1 + rank(downs[me], loc))
        return jnp.where(blk == me, loc, jnp.where(blk == before, from_before, from_after))

    def sweep(ready, blk, start, skip, count):
        def step(r, s):
            i, j, bj, u, v, edge = read(blk, r)
            free = (bj == blk) | jnp.where(edge == me, v == 0, u == n - 1)
            want = ((blk == me) | (bj == me)) & (free == ready) & (r != skip)

            @pl.when(want)
            def _():
                write(s * TASK, i, j)

            return s + jnp.where(want, 1, 0)

        return lax.fori_loop(start, alive[blk], step, count)

    def write(at, i, j):
        plan[at] = place_of(i)
        plan[at + 1] = place_of(j)
        plan[at + 2] = offsets[0, j] - offsets[0, i]
        plan[at + 3] = offsets[1, j] - offsets[1, i]
        plan[at + 4] = jnp.where(lax.div(i, n) == me, lax.rem(i, n), n)
        plan[at + 5] = jnp.where(lax.div(j, n) == me, lax.rem(j, n), n)

    def blank(s):
        for c, value in enumerate((0, 0, 0, 0, n, n)):
            plan[s * TASK + c] = value

    for s, (blk, r) in enumerate(((me, 1), (after, 0), (me, 0), (before, 1))):
        write(s * TASK, every[blk, 0, r], every[blk, 1, r])
    for s in range(4, 2 * AHEAD):
        blank(s)
    count = jnp.int32(4)
    for ready in (True, False):
        count = sweep(ready, me, 2, n, count)
        count = sweep(ready, before, 0, 1, count)
        count = sweep(ready, after, 1, n, count)
        if ready:
            count = jnp.maximum(count, 2 * AHEAD)
    plan[INFO + 6] = count
    blank(count)


def make_plan(every, offsets, n, combos):
    size = every.shape[0]
    smem = pl.BlockSpec(memory_space=pltpu.SMEM)
    return pl.pallas_call(
        functools.partial(plan_kernel, n, combos),
        in_specs=[smem, smem],
        out_specs=[smem, smem],
        out_shape=[
            jax.ShapeDtypeStruct((PLAN,), jnp.int32),
            jax.ShapeDtypeStruct((1,), jnp.int32),
        ],
        scratch_shapes=[pltpu.SMEM((size,), jnp.int32)] * 5,
        name="plan",
    )(every, offsets.T)


def wipe_room(room, y):
    def step(f, c):
        room[f, :, y:, :] = jnp.zeros((room.shape[1], PAD, room.shape[3]), F32)
        return c

    lax.fori_loop(0, room.shape[0], step, 0)


def repeat(count, unroll, do):
    def step(g, c):
        for q in range(unroll):
            do(g * unroll + q)
        return c

    lax.fori_loop(0, count // unroll, step, 0)


def solver(plan, room, one, two, own2, par2, prod, wheel, moves, basis, basis_back, levels, h):
    rows, tall, w = room.shape[1:]
    y, z = tall - PAD, w // 2
    half = h // 2
    halo = rows - half
    each = rows * tall
    quads, line, _ = factors()

    prod[0] = jnp.zeros((tall, w), F32)
    prod[:, y:, :] = jnp.zeros((h + 1, PAD, w), F32)
    for ref in (one, two):
        planes = ref.shape[0]
        ref[0] = jnp.zeros(ref.shape[1:], F32)
        ref[:, 0:8, :] = jnp.zeros((planes, 8, w), F32)
        ref[:, 8 + y :, :] = jnp.zeros((planes, 8, w), F32)
    flat_room = room.reshape(room.shape[0] * each, w)
    flat_prod = prod.reshape((h + 1) * tall, w)

    k_at = lax.broadcasted_iota(jnp.int32, (2 * w, 2 * w), 0)
    c_at = lax.broadcasted_iota(jnp.int32, (2 * w, 2 * w), 1)
    task_k, half_k, task_c, half_c = k_at // w, k_at % w // z, c_at % w // z, c_at // w
    gap = k_at % z - c_at % z
    wheel[...] = jnp.where((task_k == task_c) & (half_k == half_c), gap, 4 * z)

    lane = lanes((y, w))
    low = lane < z
    pos = lane % z
    mu = jnp.broadcast_to(levels[...], (STRIP, w))

    def sweep(src, count, emit):
        def step(g, c):
            for r in range(0, y, STRIP):
                at = pl.ds(8 + r, STRIP)
                col = [src[g * UNROLL + q, at, :] for q in range(UNROLL + 2)]
                for q in range(UNROLL):
                    t = g * UNROLL + q
                    sides = src[t + 1, pl.ds(7 + r, STRIP), :] + src[t + 1, pl.ds(9 + r, STRIP), :]
                    emit(t, r, col[q + 1], (col[q] + col[q + 2]) + sides)
            return c

        lax.fori_loop(0, (count + UNROLL - 1) // UNROLL, step, 0)

    def split(values):
        coarse = values.astype(jnp.bfloat16)
        return coarse, (values - coarse.astype(F32)).astype(jnp.bfloat16)

    def turn_z(values, wave):
        both = jnp.dot(
            jnp.concatenate(split(values), axis=1), wave[...], preferred_element_type=F32
        )
        return both[:, :w] + both[:, w:]

    def planes(r):
        return jnp.where(r < half, r, r + half), jnp.where(r < half, r + half, r + half + halo)

    def run(g, gains, backs):
        p, q = g * 2 * TASK, (g * 2 + 1) * TASK
        rp, rq = (plan[p] + 1) * each, (plan[q] + 1) * each
        ap, aq, bp, bq = plan[p + 2], plan[q + 2], plan[p + 3], plan[q + 3]
        sp, sq = (plan[p + 1] + 1) * each - ap, (plan[q + 1] + 1) * each - aq
        col = lanes((1, 2 * w)) % w < z
        moves[...] = jnp.where(wheel[...] == jnp.where(col, -bp, -bq), 1.0, 0.0).astype(jnp.bfloat16)

        def dense(g, c):
            raw = []
            for q in range(DEPTH):
                for t in planes(jnp.maximum((g - 1) * DEPTH + q, 0)):
                    raw.append(two[t + 1, 8 : 8 + y, :])
            waves = turn_z(jnp.concatenate(raw, axis=0), basis)
            rs = [jnp.minimum(g * DEPTH + q, rows - 1) for q in range(DEPTH)]
            par = [
                jnp.concatenate(
                    [flat_room[pl.ds(sp + r * tall, y), :], flat_room[pl.ds(sq + r * tall, y), :]],
                    axis=1,
                )
                for r in rs
            ]
            par = jnp.concatenate(split(jnp.concatenate(par, axis=0)), axis=0)
            par = jnp.dot(par, moves[...], preferred_element_type=F32)
            par = par[: DEPTH * y] + par[DEPTH * y :]
            for q in range(DEPTH):
                old = planes(jnp.maximum((g - 1) * DEPTH + q, 0))
                for side in range(2):
                    at = (2 * q + side) * y
                    one[old[side] + 1, 8 : 8 + y, :] = waves[at : at + y]
            for q, r in enumerate(rs):
                own_p = flat_room[pl.ds(rp + r * tall, y), :]
                own_q = flat_room[pl.ds(rq + r * tall, y), :]
                own_a = jnp.where(low, own_p, pltpu.roll(own_q, z, axis=1))
                own_b = jnp.where(low, pltpu.roll(own_p, z, axis=1), own_q)
                for t, own, half_par in zip(
                    planes(r), (own_a, own_b), jnp.split(par[q * y : (q + 1) * y], 2, axis=1)
                ):
                    two[t + 1, 8 : 8 + y, :] = own * half_par
                    own2[t] = own
                    par2[t] = half_par
            return c

        lax.fori_loop(0, rows // DEPTH + 1, dense, 0)

        def quad(k, c):
            b, c2 = jnp.float32(quads[0][0]), jnp.float32(quads[0][1])
            for m in range(1, len(quads)):
                b = jnp.where(k == m, jnp.float32(quads[m][0]), b)
                c2 = jnp.where(k == m, jnp.float32(quads[m][1]), c2)
            mu_b = mu + b

            def first(t, r, cur, near):
                two[t + 1, pl.ds(8 + r, STRIP), :] = near + mu_b * cur

            def second(t, r, cur, near):
                at = pl.ds(8 + r, STRIP)
                one[t + 1, at, :] = (near + mu * cur) + c2 * one[t + 1, at, :]

            count = h + EDGE - 1 - 2 * k
            sweep(one, count, first)
            sweep(two, count - 1, second)
            return c

        lax.fori_loop(0, len(quads), quad, 0)
        mu_line = mu + line

        def last(t, r, cur, near):
            two[t + 1, pl.ds(8 + r, STRIP), :] = near + mu_line * cur

        sweep(one, h, last)

        def finish(g, c):
            both = [two[g * 4 + q + 1, 8 : 8 + y, :] for q in range(4)]
            both = turn_z(jnp.concatenate(both, axis=0), basis_back)
            for q in range(4):
                t = g * 4 + q
                pot = both[q * y : (q + 1) * y]
                gains[t] = pot * par2[t]
                prod[t + 1, 0:y, :] = pot * own2[t]
            return c

        lax.fori_loop(0, h // 4, finish, 0)

        back = pos + jnp.where(low, bp, bq)
        good = (back >= 0) & (back < z)
        turn_p, turn_q = lax.rem(w - bp, w), lax.rem(w - bq, w)

        def plane(t):
            at = (t + 1) * tall
            moved_p = pltpu.roll(flat_prod[pl.ds(at + ap, y), :], turn_p, axis=1)
            moved_q = pltpu.roll(flat_prod[pl.ds(at + aq, y), :], turn_q, axis=1)
            backs[t] = jnp.where(good, jnp.where(low, moved_p, moved_q), 0.0)

        repeat(h, 4, plane)

    return run


def solver_scratch(fields, h, y, w, rows):
    planes = 2 * rows
    return [
        pltpu.VMEM((fields + 1, rows, y + PAD, w), F32),
        pltpu.VMEM((planes + 6, y + 16, w), F32),
        pltpu.VMEM((planes + 6, y + 16, w), F32),
        pltpu.VMEM((planes, y, w), F32),
        pltpu.VMEM((planes, y, w), F32),
        pltpu.VMEM((h + 1, y + PAD, w), F32),
        pltpu.VMEM((2 * w, 2 * w), jnp.int32),
        pltpu.VMEM((2 * w, 2 * w), jnp.bfloat16),
    ]


def swap_kernel(
    counts, plan, fields, edges, basis, basis_back, levels, prior, nxt, halos, results,
    room, one, two, own2, par2, prod, wheel, moves, sends, got, trim, hal, parts,
    in_sem, send, recv, edge_send, edge_recv, trim_send, trim_recv, main_sem, rim_sem,
    hal_sem, part_sem,
):
    n, halo, y, w = edges.shape
    rows = fields.shape[1]
    half = rows - halo
    m = sends.shape[1]
    late = hal.shape[0]
    size, width = lax.axis_size(CYCLE), lax.axis_size("orb")
    o = lax.axis_index("orb")
    me = lax.axis_index("grp") * width + o
    slab = lax.axis_index("slab")
    other = {"slab": 1 - slab}

    def peer(s):
        to = lax.rem(me + s, size)
        return {"grp": lax.div(to, width), "orb": lax.rem(to, width)}

    def limit(q):
        return jnp.where(q % 2 == 0, counts[2], jnp.where(q == width - 1, counts[1], counts[0]))

    above, under = limit(o), limit(lax.rem(o + width - 1, width))
    ways = ((0, above, under, prior), (1, under, above, nxt))

    def load(f):
        return pltpu.make_async_copy(fields.at[f], room.at[f + 1, :, pl.ds(0, y)], in_sem.at[f])

    def edge_copy(k):
        return pltpu.make_async_remote_copy(
            src_ref=edges.at[n - 1 - late + k], dst_ref=hal.at[k],
            send_sem=edge_send.at[k], recv_sem=edge_recv.at[k],
            device_id=other, device_id_type=pl.DeviceIdType.MESH,
        )

    def keep_hal(k):
        return pltpu.make_async_copy(hal.at[k], halos.at[k], hal_sem.at[k])

    def copy(way, r):
        return pltpu.make_async_remote_copy(
            src_ref=sends.at[way, r], dst_ref=got.at[way, r, pl.ds(0, half)],
            send_sem=send.at[way, r], recv_sem=recv.at[way, r],
            device_id=peer((1, size - 1)[way]), device_id_type=pl.DeviceIdType.MESH,
        )

    def trim_copy(way, r):
        return pltpu.make_async_remote_copy(
            src_ref=trim.at[way, r], dst_ref=got.at[way, r, pl.ds(half, halo)],
            send_sem=trim_send.at[way, r], recv_sem=trim_recv.at[way, r],
            device_id=other, device_id_type=pl.DeviceIdType.MESH,
        )

    def main_out(way, r, dst):
        part = pl.ds(0, half)
        return pltpu.make_async_copy(got.at[way, r, part], dst.at[r, part], main_sem.at[way, r])

    def rim_out(way, r, dst):
        part = pl.ds(half, halo)
        return pltpu.make_async_copy(got.at[way, r, part], dst.at[r, part], rim_sem.at[way, r])

    def part_out(g):
        return pltpu.make_async_copy(parts.at[g % 2], results.at[g], part_sem.at[g % 2])

    def each(start, stop, do):
        def step(k, c):
            do(k)
            return c

        lax.fori_loop(start, stop, step, 0)

    each(0, n + 2, lambda f: load(f).start())
    barrier = pltpu.get_barrier_semaphore()
    for to in (peer(1), peer(size - 1), other):
        pl.semaphore_signal(barrier, inc=1, device_id=to, device_id_type=pl.DeviceIdType.MESH)
    wipe_room(room, y)
    run = solver(
        plan, room, one, two, own2, par2, prod, wheel, moves, basis, basis_back, levels, 2 * half
    )
    pl.semaphore_wait(barrier, 3)
    each(0, late, lambda k: edge_copy(k).start())
    each(0, n + 2, lambda f: load(f).wait())

    def launch(r):
        for way, out, _, _ in ways:
            @pl.when(r < out)
            def _(way=way):
                k = plan[LISTS + way * 2 * n + r]

                def row(t):
                    sends[way, r, t] = room[k + 1, t, 0:y, :]

                each(0, half, row)
                copy(way, r).start()

    each(0, m, launch)
    low = lanes((1, w)) < w // 2

    def land(r):
        for way, _, into, dst in ways:
            @pl.when(r < into)
            def _(way=way, dst=dst):
                copy(way, r).wait_recv()
                main_out(way, r, dst).start()
                for e in range(halo):
                    a, b = got[way, r, half - 1 - e], got[way, r, half - 1 - halo - e]
                    trim[way, r, e] = jnp.where(low, pltpu.roll(a, w // 2, axis=1), b)
                trim_copy(way, r).start()

    def work(g):
        pl.when(g >= 2)(lambda: part_out(g - 2).wait())

        @pl.when(g == 2)
        def _():
            for k in range(late):
                edge_copy(k).wait()
                keep_hal(k).start()
                room[n - late + k, half:, 0:y, :] = hal[k]

        run(g, parts.at[g % 2, 0], parts.at[g % 2, 1])
        part_out(g).start()
        pl.when((g >= 1) & (g - 1 < m))(lambda: land(g - 1))

    each(0, AHEAD, work)
    each(min(AHEAD - 1, m), m, land)
    for k in range(late):
        keep_hal(k).wait()
    for g in range(AHEAD - 2, AHEAD):
        part_out(g).wait()

    def settle(r):
        for way, out, into, dst in ways:
            @pl.when(r < into)
            def _(way=way, dst=dst):
                trim_copy(way, r).wait()
                rim_out(way, r, dst).start()

            @pl.when(r < out)
            def _(way=way):
                copy(way, r).wait_send()

    each(0, m, settle)

    def close(r):
        for way, _, into, dst in ways:
            @pl.when(r < into)
            def _(way=way, dst=dst):
                main_out(way, r, dst).wait()
                rim_out(way, r, dst).wait()

    each(0, m, close)


def swap(counts, plan, fields, edges, waves, cid):
    n, halo, y, w = edges.shape
    rows = fields.shape[1]
    half, m = rows - halo, max(counts)
    late = n - 2 - EARLY
    hbm = pl.BlockSpec(memory_space=pl.ANY)
    smem = pl.BlockSpec(memory_space=pltpu.SMEM)
    vmem = pl.BlockSpec(memory_space=pltpu.VMEM)
    dma = pltpu.SemaphoreType.DMA
    out = jax.ShapeDtypeStruct((n - 1, rows, y, w), F32)
    return pl.pallas_call(
        functools.partial(swap_kernel, counts),
        in_specs=[smem, hbm, hbm, vmem, vmem, vmem],
        out_specs=[hbm, hbm, hbm, hbm],
        out_shape=[
            out,
            out,
            jax.ShapeDtypeStruct((late, halo, y, w), F32),
            jax.ShapeDtypeStruct((AHEAD, 2, 2 * half, y, w), F32),
        ],
        scratch_shapes=solver_scratch(n + 2, 2 * half, y, w, rows)
        + [
            pltpu.VMEM((2, m, half, y, w), F32),
            pltpu.VMEM((2, m, rows, y, w), F32),
            pltpu.VMEM((2, m, halo, y, w), F32),
            pltpu.VMEM((late, halo, y, w), F32),
            pltpu.VMEM((2, 2, 2 * half, y, w), F32),
            dma((n + 2,)), dma((2, m)), dma((2, m)), dma((late,)), dma((late,)),
            dma((2, m)), dma((2, m)), dma((2, m)), dma((2, m)), dma((late,)), dma((2,)),
        ],
        compiler_params=pltpu.CompilerParams(
            collective_id=cid, has_side_effects=True, vmem_limit_bytes=58 * 1024 * 1024
        ),
        name="swap%d%d%d" % counts,
    )(plan, fields, edges, *waves)


def pairs_kernel(
    plan, fields, prior, nxt, halos, results, basis, basis_back, levels, out,
    room, one, two, own2, par2, prod, wheel, moves, acc, stage, parts, sem, rim_sem, out_sem, part_sem,
):
    n, h, y, z = out.shape
    w = 2 * z
    half, rows = h // 2, fields.shape[1]
    halo = rows - half
    most = prior.shape[0]
    late = halos.shape[0]
    slab = lax.axis_index("slab")

    def part(g):
        return pltpu.make_async_copy(results.at[g], parts.at[g % 2], part_sem.at[g % 2])

    def field(src, s, f, first, count, sem):
        return pltpu.make_async_copy(
            src.at[s, pl.ds(first, count)],
            room.at[f + 1, pl.ds(rows - count if src is halos else first, count), pl.ds(0, y)],
            sem.at[f],
        )

    def each_field(do):
        for f in range(n + 2):
            if n - 1 - late <= f < n - 1:
                do(field(fields, f, f, 0, half, sem))
                do(field(halos, f - (n - 1 - late), f, 0, halo, rim_sem))
            else:
                do(field(fields, f, f, 0, rows, sem))
        for src, base, count in ((prior, n + 2, plan[INFO + 3]), (nxt, n + 2 + most, plan[INFO + 4])):
            for s in range(most):
                pl.when(s < count)(
                    lambda src=src, s=s, base=base: do(field(src, s, base + s, 0, rows, sem))
                )

    part(0).start()
    part(1).start()
    each_field(lambda c: c.start())
    acc[...] = jnp.zeros(acc.shape, F32)
    wipe_room(room, y)
    run = solver(plan, room, one, two, own2, par2, prod, wheel, moves, basis, basis_back, levels, h)
    low = lanes((y, w)) < w // 2

    def collect(g, gains, backs):
        p, q = g * 2 * TASK, (g * 2 + 1) * TASK
        for k, src, side in (
            (plan[p + 4], gains, low),
            (plan[q + 4], gains, jnp.logical_not(low)),
            (plan[p + 5], backs, low),
            (plan[q + 5], backs, jnp.logical_not(low)),
        ):
            @pl.when(k < n)
            def _(k=k, src=src, side=side):
                def plane(t):
                    acc[k, t] += jnp.where(side, src[t], 0.0)

                repeat(h, 4, plane)

    def gather(g, c):
        part(g).wait()
        collect(g, parts.at[g % 2, 0], parts.at[g % 2, 1])
        pl.when(g + 2 < AHEAD)(lambda: part(g + 2).start())
        return c

    lax.fori_loop(0, AHEAD, gather, 0)
    each_field(lambda c: c.wait())

    def group(g, c):
        run(g, parts.at[0, 0], parts.at[0, 1])
        collect(g, parts.at[0, 0], parts.at[0, 1])
        return c

    lax.fori_loop(AHEAD, lax.div(plan[INFO + 6] + 1, 2), group, 0)

    def leave(k, slot):
        return pltpu.make_async_copy(stage.at[slot], out.at[k], out_sem.at[slot])

    def write(k, c):
        slot = lax.rem(k, 2)
        pl.when(k >= 2)(lambda: leave(k - 2, slot).wait())

        def plane(t):
            value = acc[k, t]
            value = value + pltpu.roll(value, z, axis=1)
            stage[slot, jnp.where(slab == 0, t, h - 1 - t)] = value[:, :z]

        repeat(h, 4, plane)
        leave(k, slot).start()
        return c

    lax.fori_loop(0, n, write, 0)
    for k in (n - 2, n - 1):
        leave(k, k % 2).wait()


def sines(z):
    k = np.arange(1, z + 1)
    wave = np.sqrt(2.0 / (z + 1)) * np.sin(np.pi * np.outer(k, k) / (z + 1))
    wave = np.kron(np.eye(2), wave).astype(np.float32)
    levels = np.tile(2.0 * np.cos(np.pi * k / (z + 1)), 2).astype(np.float32)[None]

    def parts(values):
        coarse = jnp.asarray(values).astype(jnp.bfloat16)
        fine = (jnp.asarray(values) - coarse.astype(F32)).astype(jnp.bfloat16)
        top = jnp.concatenate([coarse, fine], axis=1)
        bottom = jnp.concatenate([coarse, jnp.zeros_like(fine)], axis=1)
        return jnp.concatenate([top, bottom], axis=0)

    return parts(wave), parts(wave * np.float32(factors()[2])), jnp.asarray(levels)


def solve_pairs(plan, fields, prior, nxt, halos, results, waves, shape):
    n, h, y, z = shape
    w, rows = 2 * z, fields.shape[1]
    most = prior.shape[0]
    hbm = pl.BlockSpec(memory_space=pl.ANY)
    vmem = pl.BlockSpec(memory_space=pltpu.VMEM)
    dma = pltpu.SemaphoreType.DMA
    total = n + 2 + 2 * most
    return pl.pallas_call(
        pairs_kernel,
        grid_spec=pltpu.PrefetchScalarGridSpec(
            num_scalar_prefetch=1,
            grid=(1,),
            in_specs=[hbm] * 5 + [vmem] * 3,
            out_specs=hbm,
            scratch_shapes=solver_scratch(total, h, y, w, rows)
            + [
                pltpu.VMEM((n, h, y, w), F32),
                pltpu.VMEM((2, h, y, z), F32),
                pltpu.VMEM((2, 2, h, y, w), F32),
                dma((total,)), dma((n,)), dma((2,)), dma((2,)),
            ],
        ),
        out_shape=jax.ShapeDtypeStruct(shape, F32),
        compiler_params=pltpu.CompilerParams(vmem_limit_bytes=58 * 1024 * 1024),
        name="pairs",
    )(plan, fields, prior, nxt, halos, results, *waves)


def fast_body(orbitals, offsets, pairs, live):
    n = orbitals.shape[0]
    combos = [(1, 1, 2), (1, 2, 2), (2, 1, 2), (2, 2, 2), (2, 2, 3), (2, 3, 3), (3, 2, 3), (3, 3, 3)]
    combos += [(4, 4, 4), (n - 1, n - 1, n - 1)]
    fields, every, edges = front(orbitals, pairs, live)
    plan, which = make_plan(every, offsets, n, combos)
    waves = sines(orbitals.shape[-1])

    def branch(counts, cid):
        return lambda _: swap(counts, plan, fields, edges, waves, cid)

    prior, nxt, halos, results = lax.switch(
        which[0], [branch(c, 2 + i) for i, c in enumerate(combos)], 0
    )
    return solve_pairs(plan, fields, prior, nxt, halos, results, waves, orbitals.shape)


def body(orbitals, offsets, pairs, live):
    n = orbitals.shape[0]
    slots = pairs.shape[0]
    total = offsets.shape[0]
    blocks = total // n
    slabs = lax.axis_size("slab")
    me = lax.axis_index(CYCLE)
    packed = pack(orbitals)

    mine = jnp.concatenate([pairs, live[:, None]], axis=1)
    every = share(jnp.pad(mine, ((0, 0), (0, 128 - mine.shape[1]))))
    ids = jnp.arange(blocks, dtype=jnp.int32)
    second = every[:, :, 1]
    alive = every[:, :, 2] > 0
    orb = jnp.arange(n, dtype=jnp.int32)
    sides = jnp.stack([(ids - 1) % blocks, (ids + 1) % blocks])
    hit = alive[None] & (second[None] // n == sides[:, :, None])
    need = jnp.any(
        hit[..., None] & (second[None, :, :, None] % n == orb), axis=2
    )
    count = jnp.sum(need.astype(jnp.int32), axis=2)
    most = jnp.max(count)

    after, before = (me + 1) % blocks, (me - 1) % blocks
    flags = jnp.stack(
        [need[0, me], need[1, me], need[0, after], need[1, before]]
    ).astype(jnp.int32)
    spot = jnp.sum(
        flags[:, None, :] * (orb[None, :] < orb[:, None]).astype(jnp.int32)[None], axis=2
    )
    lists = jnp.sum(
        (flags[:, None, :] * (spot[:, None, :] == orb[None, :, None])) * orb, axis=2
    )
    back = jnp.stack(
        [spot[2] * flags[2], flags[2], spot[3] * flags[3], flags[3]]
    )

    i, j, on = pairs[:, 0], pairs[:, 1], live > 0
    owner, local = j // n, j % n
    pick_j = (local[:, None] == orb[None, :]).astype(jnp.int32)
    from_prior = (owner == before) & on
    from_next = (owner == after) & on
    kind = jnp.where(from_prior, 1, jnp.where(from_next, 2, 0))
    where_prior = jnp.sum(pick_j * spot[0][None, :], axis=1) * from_prior
    where_next = jnp.sum(pick_j * spot[1][None, :], axis=1) * from_next
    ids_all = jnp.arange(total, dtype=jnp.int32)
    diff = (j[:, None] == ids_all).astype(jnp.int32) - (i[:, None] == ids_all).astype(jnp.int32)
    shift = jnp.sum(diff[:, :, None] * offsets[None], axis=1)
    plan = jnp.stack(
        [i % n, local, where_prior, where_next, kind, shift[:, 0], shift[:, 1], live]
    ).astype(jnp.int32)
    order = jnp.where(on, jnp.where(kind > 0, 0, 1), 2) * slots + jnp.arange(slots)
    rank = jnp.sum((order[None, :] < order[:, None]).astype(jnp.int32), axis=1)
    move = (rank[:, None] == jnp.arange(slots)[None, :]).astype(jnp.int32)
    plan = jnp.sum(plan[:, :, None] * move[None], axis=1)
    far, lively = jnp.sum((kind > 0).astype(jnp.int32)), jnp.sum(on.astype(jnp.int32))
    tail = jnp.where(jnp.arange(slots) == 0, far, lively)
    plan = jnp.concatenate([plan, tail[None]], axis=0)
    ends = jnp.stack([lax.axis_index("slab"), slabs]).astype(jnp.int32)

    up = [(s, s + 1) for s in range(slabs - 1)]
    down = [(s + 1, s) for s in range(slabs - 1)]

    def branch(m):
        def run(_):
            to_next, to_prior = gather(packed, lists[2:], m)
            prior = cycle(to_next, 1)
            nxt = cycle(to_prior, -1)
            partner, density, low, high = densities(plan, packed, prior, nxt)
            below = lax.ppermute(high, "slab", up)
            above = lax.ppermute(low, "slab", down)
            given = (plan, ends, density, partner, packed, below, above, m)
            acc, acc_prior, acc_next = solve(True, *given)
            from_next, from_prior = cycle(acc_prior, -1), cycle(acc_next, 1)
            (acc_near,) = solve(False, *given)
            return combine(back, acc, acc_near, from_next, from_prior)

        return run

    sizes = sorted({min(s, slots - 1) for s in (3, 4, 5)} | {slots - 1})
    which = sum((most > s).astype(jnp.int32) for s in sizes[:-1])
    return lax.switch(which, [branch(s) for s in sizes], 0)


def solution(mesh):
    placed = (
        P(CYCLE, "slab", None, None),
        P(),
        P(CYCLE, None),
        P(CYCLE),
    )
    return jax.shard_map(
        fast_body if mesh.shape["slab"] == 2 else body,
        mesh=mesh,
        in_specs=placed,
        out_specs=P(CYCLE, "slab", None, None),
        check_vma=False,
    )
```

```python
import cmath
import functools
import math

import jax
import jax.numpy as jnp
import numpy as np
from jax import lax
from jax.experimental import pallas as pl
from jax.experimental.pallas import tpu as pltpu
from jax.sharding import PartitionSpec as P

PASSES = 8
DIAG = 6.25
THETA = 1.075
DELTA = 0.925
EDGE = PASSES - 1
PAD = 16
CYCLE = ("grp", "orb")
F32 = jnp.float32


def coefs():
    sigma = THETA / DELTA
    coef = 1.0 / sigma
    out = []
    for _ in range(PASSES - 1):
        new = 1.0 / (2.0 * sigma - coef)
        out.append((new * coef, 2.0 * new / (DELTA * DIAG)))
        coef = new
    return out


def lanes(shape):
    return lax.broadcasted_iota(jnp.int32, shape, len(shape) - 1)


def share_kernel(mine, every, send_sem, recv_sem):
    size, width = lax.axis_size(CYCLE), lax.axis_size("orb")
    me = lax.axis_index("grp") * width + lax.axis_index("orb")

    def peer(s):
        to = lax.rem(me + s, size)
        return {"grp": lax.div(to, width), "orb": lax.rem(to, width)}

    def greet(s, c):
        pl.semaphore_signal(
            barrier, inc=1, device_id=peer(s), device_id_type=pl.DeviceIdType.MESH
        )
        return c

    def copy(s, slot):
        return pltpu.make_async_remote_copy(
            src_ref=mine,
            dst_ref=every.at[slot],
            send_sem=send_sem.at[s],
            recv_sem=recv_sem.at[s],
            device_id=peer(s),
            device_id_type=pl.DeviceIdType.MESH,
        )

    def send(s, c):
        copy(s, me).start()
        return c

    def finish(s, c):
        copy(s, lax.rem(me + size - s, size)).wait()
        return c

    barrier = pltpu.get_barrier_semaphore()
    lax.fori_loop(1, size, greet, 0)
    pl.semaphore_wait(barrier, size - 1)
    lax.fori_loop(1, size, send, 0)
    every[me] = mine[...]
    lax.fori_loop(1, size, finish, 0)


def share(mine):
    size = lax.axis_size(CYCLE)
    vmem = pl.BlockSpec(memory_space=pltpu.VMEM)
    return pl.pallas_call(
        share_kernel,
        in_specs=[vmem],
        out_specs=vmem,
        out_shape=jax.ShapeDtypeStruct((size,) + mine.shape, mine.dtype),
        scratch_shapes=[pltpu.SemaphoreType.DMA((size,)), pltpu.SemaphoreType.DMA((size,))],
        compiler_params=pltpu.CompilerParams(collective_id=0, has_side_effects=True),
        name="share",
    )(mine)


def pack_kernel(src, dst):
    half = dst.shape[1]
    dst[0] = jnp.concatenate([src[0, :half], src[0, half:]], axis=-1)


def pack(orbitals):
    n, x, y, z = orbitals.shape
    return pl.pallas_call(
        pack_kernel,
        grid=(n,),
        in_specs=[pl.BlockSpec((1, x, y, z), lambda i: (i, 0, 0, 0))],
        out_specs=pl.BlockSpec((1, x // 2, y, 2 * z), lambda i: (i, 0, 0, 0)),
        out_shape=jax.ShapeDtypeStruct((n, x // 2, y, 2 * z), F32),
        name="pack",
    )(orbitals)


def copy_kernel(idx, src_a, src_b, dst_a, dst_b):
    dst_a[...] = src_a[...]
    dst_b[...] = src_b[...]


def gather(packed, lists, m):
    _, h, y, w = packed.shape
    blk = (1, h, y, w)
    out = jax.ShapeDtypeStruct((m, h, y, w), F32)
    return pl.pallas_call(
        copy_kernel,
        grid_spec=pltpu.PrefetchScalarGridSpec(
            num_scalar_prefetch=1,
            grid=(m,),
            in_specs=[
                pl.BlockSpec(blk, lambda i, idx: (idx[0, i], 0, 0, 0)),
                pl.BlockSpec(blk, lambda i, idx: (idx[1, i], 0, 0, 0)),
            ],
            out_specs=[pl.BlockSpec(blk, lambda i, idx: (i, 0, 0, 0))] * 2,
        ),
        out_shape=[out, out],
        name="gather",
    )(lists, packed, packed)


def place(value, room, a, b):
    y, w = value.shape[1:]
    z = w // 2
    room[:, PAD : PAD + y, :] = value
    moved = room[:, pl.ds(PAD - a, y), :]
    moved = pltpu.roll(moved, lax.rem(b + w, w), axis=2)
    pos = lanes(moved.shape) % z - b
    return jnp.where((pos >= 0) & (pos < z), moved, 0.0)


def clear_room(room):
    y = room.shape[1] - 2 * PAD
    room[:, :PAD, :] = jnp.zeros((room.shape[0], PAD, room.shape[2]), F32)
    room[:, PAD + y :, :] = jnp.zeros((room.shape[0], PAD, room.shape[2]), F32)


def density_kernel(plan, own, mine, prior, nxt, partner, density, low, high, room):
    p = pl.program_id(0)
    kind = plan[4, p]
    a, b = plan[5, p], plan[6, p]

    @pl.when(p == 0)
    def _():
        clear_room(room)

    on = plan[7, p] > 0

    def go(src):
        part = place(src[0], room, a, b)
        partner[0] = part
        dens = own[0] * part
        density[0] = dens
        h, y, w = dens.shape
        flat = jnp.concatenate([dens[..., : w // 2], dens[..., w // 2 :]], axis=0)
        top, bot = flat[:EDGE], flat[2 * h - EDGE :]
        low[0] = jnp.concatenate([top[:, : y // 2], top[:, y // 2 :]], axis=-1)
        high[0] = jnp.concatenate([bot[:, : y // 2], bot[:, y // 2 :]], axis=-1)

    for value, src in enumerate((mine, prior, nxt)):
        pl.when(on & (kind == value))(functools.partial(go, src))


def densities(plan, packed, prior, nxt):
    slots = plan.shape[1]
    _, h, y, w = packed.shape
    blk = (1, h, y, w)
    eblk = (1, EDGE, y // 2, w)

    def at(row):
        return pl.BlockSpec(
            blk, lambda i, plan: (plan[row, jnp.minimum(i, plan[8, 1] - 1)], 0, 0, 0)
        )

    full = jax.ShapeDtypeStruct((slots, h, y, w), F32)
    edge = jax.ShapeDtypeStruct((slots,) + eblk[1:], F32)
    here = lambda i, plan: (jnp.minimum(i, plan[8, 1] - 1), 0, 0, 0)
    return pl.pallas_call(
        density_kernel,
        grid_spec=pltpu.PrefetchScalarGridSpec(
            num_scalar_prefetch=1,
            grid=(slots,),
            in_specs=[at(0), at(1), at(2), at(3)],
            out_specs=[
                pl.BlockSpec(blk, here),
                pl.BlockSpec(blk, here),
                pl.BlockSpec(eblk, here),
                pl.BlockSpec(eblk, here),
            ],
            scratch_shapes=[pltpu.VMEM((h, y + 2 * PAD, w), F32)],
        ),
        out_shape=[full, full, edge, edge],
        name="density",
    )(plan, packed, packed, prior, nxt)


def solve_kernel(remote, plan, ends, density, partner, own, below, above, *refs):
    accs, (resid, step_a, step_b, total, mask, room) = refs[:-6], refs[-6:]
    acc = accs[0]
    p = pl.program_id(0)
    h, y, w = density.shape[1:]
    z = w // 2
    rows = h + 2 * EDGE
    group = 4 if h % 4 == 0 else 1

    @pl.when(p == 0)
    def _():
        clear_room(room)
        for ref in accs:
            ref[...] = jnp.zeros(ref.shape, F32)
        for ref in (step_a, step_b):
            ref[:, :8, :] = jnp.zeros((rows, 8, w), F32)
            ref[:, 8 + y :, :] = jnp.zeros((rows, 8, w), F32)
        lane = lanes((1, w))
        first = ends[0] == 0
        last = ends[0] == ends[1] - 1
        for t in range(rows):
            plane = jnp.where(lane < z, t - EDGE, t - EDGE + h)
            outside = ((plane < 0) & first) | ((plane >= 2 * h) & last)
            mask[t] = jnp.where(outside, 0.0, 1.0)

    chosen = (plan[4, p] > 0) if remote else (plan[4, p] == 0)

    @pl.when((plan[7, p] > 0) & chosen)
    def _():
        def unfold(part):
            return jnp.concatenate([part[..., :z], part[..., z:]], axis=1)

        dens = density[0]
        line = jnp.concatenate(
            [unfold(below[0]), dens[..., :z], dens[..., z:], unfold(above[0])], axis=0
        )
        resid[...] = jnp.concatenate([line[:rows], line[h:]], axis=-1)
        step_a[:, 8 : 8 + y, :] = resid[...] * (1.0 / (DIAG * THETA))
        total[...] = step_a[EDGE : EDGE + h, 8 : 8 + y, :]
        lane = lanes((y, w)) % z
        not_low = lane > 0
        not_high = lane < z - 1
        bufs = [step_a, step_b]
        for turn, (keep, gain) in enumerate(coefs()):
            now, then = bufs[turn % 2], bufs[1 - turn % 2]
            core_only = turn == PASSES - 2

            def row(t, now=now, then=then, keep=keep, gain=gain):
                core = now[t, 8 : 8 + y, :]
                near = now[t - 1, 8 : 8 + y, :] + now[t + 1, 8 : 8 + y, :]
                near = near + (now[t, 7 : 7 + y, :] + now[t, 9 : 9 + y, :])
                side = jnp.where(not_low, pltpu.roll(core, 1, axis=1), 0.0)
                side = side + jnp.where(not_high, pltpu.roll(core, w - 1, axis=1), 0.0)
                left = (resid[t] - DIAG * core) + (near + side)
                return left, keep * core + gain * left

            def outer(k, c, row=row, then=then):
                for t in (EDGE - 1 - k, EDGE + h + k):
                    left, fresh = row(t)
                    resid[t] = left
                    then[t, 8 : 8 + y, :] = fresh * mask[t]
                return c

            def inner(k, c, row=row, then=then, last=core_only):
                for g in range(group):
                    t = EDGE + k * group + g
                    left, fresh = row(t)
                    if not last:
                        resid[t] = left
                        then[t, 8 : 8 + y, :] = fresh
                    total[t - EDGE] += fresh
                return c

            if turn + 1 < EDGE:
                lax.fori_loop(0, EDGE - turn - 1, outer, 0)
            lax.fori_loop(0, h // group, inner, 0)

        pot = total[...]
        acc[plan[0, p]] += pot * partner[0]
        back = place(pot * own[0], room, -plan[5, p], -plan[6, p])
        if not remote:
            acc[plan[1, p]] += back
        else:
            for value in (1, 2):

                @pl.when(plan[4, p] == value)
                def _(ref=accs[value], value=value):
                    ref[plan[1 + value, p]] += back


def solve(remote, plan, ends, density, partner, packed, below, above, m):
    slots = plan.shape[1]
    n, h, y, w = packed.shape
    blk = (1, h, y, w)
    eblk = (1, EDGE, y // 2, w)
    rows = h + 2 * EDGE

    def spot(i, plan):
        far = plan[8, 0]
        if remote:
            return jnp.minimum(i, jnp.maximum(far - 1, 0))
        return jnp.clip(i, jnp.minimum(far, plan[8, 1] - 1), plan[8, 1] - 1)

    here = lambda i, plan, ends: (spot(i, plan), 0, 0, 0)
    fixed = lambda i, plan, ends: (0, 0, 0, 0)
    shapes = [(n, h, y, w)] + [(m, h, y, w)] * (2 if remote else 0)
    return pl.pallas_call(
        functools.partial(solve_kernel, remote),
        grid_spec=pltpu.PrefetchScalarGridSpec(
            num_scalar_prefetch=2,
            grid=(slots,),
            in_specs=[
                pl.BlockSpec(blk, here),
                pl.BlockSpec(blk, here),
                pl.BlockSpec(blk, lambda i, plan, ends: (plan[0, spot(i, plan)], 0, 0, 0)),
                pl.BlockSpec(eblk, here),
                pl.BlockSpec(eblk, here),
            ],
            out_specs=[pl.BlockSpec(s, fixed) for s in shapes],
            scratch_shapes=[
                pltpu.VMEM((rows, y, w), F32),
                pltpu.VMEM((rows, y + 16, w), F32),
                pltpu.VMEM((rows, y + 16, w), F32),
                pltpu.VMEM((h, y, w), F32),
                pltpu.VMEM((rows, 1, w), F32),
                pltpu.VMEM((h, y + 2 * PAD, w), F32),
            ],
        ),
        out_shape=[jax.ShapeDtypeStruct(s, F32) for s in shapes],
        compiler_params=pltpu.CompilerParams(vmem_limit_bytes=56 * 1024 * 1024),
        cost_estimate=pl.CostEstimate(
            flops=slots * rows * y * w * 100, bytes_accessed=24 << 20, transcendentals=0
        ),
        name="solve_far" if remote else "solve_near",
    )(plan, ends, density, partner, packed, below, above)


def combine_kernel(back, acc, acc_near, from_next, from_prior, out):
    k = pl.program_id(0)
    h = acc.shape[1]
    z = acc.shape[3] // 2
    value = acc[0] + acc_near[0]
    value = value + jnp.where(back[1, k] > 0, from_next[0], 0.0)
    value = value + jnp.where(back[3, k] > 0, from_prior[0], 0.0)
    out[0, :h] = value[:, :, :z]
    out[0, h:] = value[:, :, z:]


def combine(back, acc, acc_near, from_next, from_prior):
    n, h, y, w = acc.shape
    blk = (1, h, y, w)
    return pl.pallas_call(
        combine_kernel,
        grid_spec=pltpu.PrefetchScalarGridSpec(
            num_scalar_prefetch=1,
            grid=(n,),
            in_specs=[
                pl.BlockSpec(blk, lambda i, back: (i, 0, 0, 0)),
                pl.BlockSpec(blk, lambda i, back: (i, 0, 0, 0)),
                pl.BlockSpec(blk, lambda i, back: (back[0, i], 0, 0, 0)),
                pl.BlockSpec(blk, lambda i, back: (back[2, i], 0, 0, 0)),
            ],
            out_specs=pl.BlockSpec((1, 2 * h, y, w // 2), lambda i, back: (i, 0, 0, 0)),
        ),
        out_shape=jax.ShapeDtypeStruct((n, 2 * h, y, w // 2), F32),
        name="combine",
    )(back, acc, acc_near, from_next, from_prior)


def cycle(field, by):
    size = lax.axis_size(CYCLE)
    return lax.ppermute(field, CYCLE, [(i, (i + by) % size) for i in range(size)])


TASK = 8
LISTS = 256
INFO = 320
PLAN = 384
EARLY = 3
AHEAD = 4
UNROLL = 4
DEPTH = 5
STRIP = 8


def factors():
    ratio = THETA / DELTA
    tall = math.acosh(ratio)
    points = [cmath.cosh(complex(tall, k * math.pi / 4)) for k in range(8)]
    marks = [DIAG * (1.0 - (THETA - DELTA * x)) for x in points]
    quads = [(-2.0 * marks[k].real, abs(marks[k]) ** 2) for k in (1, 2, 3)]
    line = -marks[4].real
    coef, resid, value, step = 1.0 / ratio, 1.0, 0.0, 1.0 / (DIAG * THETA)
    value += step
    for keep, gain in coefs():
        resid -= DIAG * step
        step = keep * step + gain * resid
        value += step
    product = line
    for _, c in quads:
        product *= c
    return quads, line, value / product


def front_kernel(
    orbs, pairs, live, fields, every, edges, stage, own, rims, far, edge, table, first,
    in_sem, out_sem, rim_sem, tab_send, tab_recv, edge_send, edge_recv, far_send, far_recv,
):
    n, h = orbs.shape[0], orbs.shape[1]
    half = h // 2
    halo = edge.shape[1]
    size, width = lax.axis_size(CYCLE), lax.axis_size("orb")
    me = lax.axis_index("grp") * width + lax.axis_index("orb")
    slab = lax.axis_index("slab")

    def peer(s):
        to = lax.rem(me + s, size)
        return {"grp": lax.div(to, width), "orb": lax.rem(to, width)}

    def load(k):
        return pltpu.make_async_copy(orbs.at[k], stage.at[k], in_sem.at[k])

    def order(q):
        return jnp.where(q == 0, 0, jnp.where(q == 1, n - 1, q - 1))

    def begin(q, c):
        load(order(q)).start()
        return c

    lax.fori_loop(0, n, begin, 0)

    barrier = pltpu.get_barrier_semaphore()

    def greet(s, c):
        pl.semaphore_signal(
            barrier, inc=1, device_id=peer(s), device_id_type=pl.DeviceIdType.MESH
        )
        return c

    lax.fori_loop(1, size, greet, 0)
    pl.semaphore_signal(
        barrier, inc=1, device_id={"slab": 1 - slab}, device_id_type=pl.DeviceIdType.MESH
    )
    table[...] = jnp.zeros(table.shape, jnp.int32)
    table[0:2, 0:n] = pairs[...]
    table[2:3, 0:n] = live[...]
    pl.semaphore_wait(barrier, size)

    def share_copy(s, slot):
        return pltpu.make_async_remote_copy(
            src_ref=table, dst_ref=every.at[slot],
            send_sem=tab_send.at[s], recv_sem=tab_recv.at[s],
            device_id=peer(s), device_id_type=pl.DeviceIdType.MESH,
        )

    def share_send(s, c):
        share_copy(s, me).start()
        return c

    lax.fori_loop(1, size, share_send, 0)
    every[me] = table[...]

    def edge_copy(e, f, dst):
        return pltpu.make_async_remote_copy(
            src_ref=edge.at[f], dst_ref=dst,
            send_sem=edge_send.at[e], recv_sem=edge_recv.at[e],
            device_id={"slab": 1 - slab}, device_id_type=pl.DeviceIdType.MESH,
        )

    def own_edge(k, e):
        return edge_copy(e, k, rims.at[k])

    def far_copy(src, f, s):
        return pltpu.make_async_remote_copy(
            src_ref=src, dst_ref=far.at[f, pl.ds(0, half)],
            send_sem=far_send.at[f], recv_sem=far_recv.at[f],
            device_id=peer(s), device_id_type=pl.DeviceIdType.MESH,
        )

    def spot(t):
        return jnp.where(slab == 0, t, h - 1 - t)

    def pack(k):
        def row(r, c):
            own[k, r] = jnp.concatenate(
                [stage[k, spot(r)], stage[k, spot(r + half)]], axis=-1
            )
            return c

        lax.fori_loop(0, half, row, 0)

    def make_edge(k):
        for m in range(halo):
            edge[k, m] = jnp.concatenate(
                [stage[k, spot(h - 1 - m)], stage[k, spot(h - 1 - halo - m)]], axis=-1
            )

    def save(k):
        return pltpu.make_async_copy(
            own.at[k], fields.at[k, pl.ds(0, half)], out_sem.at[k]
        )

    def save_far(f):
        return pltpu.make_async_copy(
            far.at[f, pl.ds(0, half)], fields.at[n + f, pl.ds(0, half)], out_sem.at[n + f]
        )

    def rim(f, src):
        return pltpu.make_async_copy(src, fields.at[f, pl.ds(half, halo)], rim_sem.at[f])

    def keep_edge(k):
        return pltpu.make_async_copy(edge.at[k], edges.at[k], rim_sem.at[k])

    early = edge_send.shape[0] - 4

    up, down = far_copy(own.at[n - 1], 0, 1), far_copy(own.at[0], 1, size - 1)
    for k, send, e in ((0, down, 0), (n - 1, up, 1)):
        load(k).wait()
        pack(k)
        send.start()
        make_edge(k)
        own_edge(k, e).start()
        save(k).start()

    def rest(k, c):
        load(k).wait()
        pack(k)
        save(k).start()
        make_edge(k)
        pl.when(k <= early)(lambda: own_edge(k, 3 + k).start())
        pl.when(k > early)(lambda: keep_edge(k).start())
        return c

    lax.fori_loop(1, n - 1, rest, 0)

    def share_done(s, c):
        share_copy(s, lax.rem(me + size - s, size)).wait()
        return c

    lax.fori_loop(1, size, share_done, 0)

    bits = n.bit_length() - 1
    here, under, above = every[me], every[lax.rem(me + size - 1, size)], every[lax.rem(me + 1, size)]
    slot = lanes((1, here.shape[1])) < n

    def lowest(tile, source, target, row, free):
        to = lax.shift_right_logical(tile[1:2], bits)
        value = tile[row : row + 1] & (n - 1)
        fit = slot & (tile[2:3] > 0) & (to == target) & (value != free)
        return jnp.min(jnp.where(fit, value, n))

    before, after = lax.rem(me + size - 1, size), lax.rem(me + 1, size)
    up_first = jnp.minimum(
        lowest(here, me, after, 0, n - 1), lowest(above, after, me, 1, n - 1)
    )
    down_first = jnp.minimum(lowest(here, me, before, 0, 0), lowest(under, before, me, 1, 0))
    more = []
    for f, (k, s) in enumerate(((up_first, 1), (down_first, size - 1))):
        k = jnp.where(k == n, 0, k)

        def row(r, c, f=f, k=k):
            first[f, r] = own[k, r]
            return c

        lax.fori_loop(0, half, row, 0)
        more.append(far_copy(first.at[f], 2 + f, s))
        more[f].start()

    low = lanes((1, own.shape[-1])) < own.shape[-1] // 2
    for f, copy in ((1, down), (0, up)):
        copy.wait()
        for m in range(halo):
            a, b = far[f, half - 1 - m], far[f, half - 1 - halo - m]
            edge[n + f, m] = jnp.where(low, pltpu.roll(a, a.shape[-1] // 2, axis=1), b)
        edge_copy(2 + f, n + f, far.at[f, pl.ds(half, halo)]).start()
        save_far(f).start()

    own_rims = [(0, 0), (n - 1, 1)] + [(k, 3 + k) for k in range(1, early + 1)]
    for k, e in own_rims:
        own_edge(k, e).wait()
        rim(k, rims.at[k]).start()
    for f in (1, 0):
        edge_copy(2 + f, n + f, far.at[f, pl.ds(half, halo)]).wait()
        rim(n + f, far.at[f, pl.ds(half, halo)]).start()
    for f in range(2):
        more[f].wait()
        save_far(2 + f).start()

    def out_done(k, c):
        save(k).wait()
        return c

    def edge_done(k, c):
        keep_edge(k).wait()
        return c

    lax.fori_loop(0, n, out_done, 0)
    lax.fori_loop(early + 1, n - 1, edge_done, 0)
    for k, _ in own_rims:
        rim(k, rims.at[k]).wait()
    for f in (1, 0):
        rim(n + f, far.at[f, pl.ds(half, halo)]).wait()
    for f in range(4):
        save_far(f).wait()


def front(orbitals, pairs, live):
    n, h, y, z = orbitals.shape
    half, halo, w = h // 2, (EDGE + 1) // 2, 2 * z
    size = lax.axis_size(CYCLE)
    vmem = pl.BlockSpec(memory_space=pltpu.VMEM)
    hbm = pl.BlockSpec(memory_space=pl.ANY)
    dma = pltpu.SemaphoreType.DMA
    return pl.pallas_call(
        front_kernel,
        in_specs=[hbm, vmem, vmem],
        out_specs=[hbm, vmem, hbm],
        out_shape=[
            jax.ShapeDtypeStruct((n + 4, half + halo, y, w), F32),
            jax.ShapeDtypeStruct((size, 8, 128), jnp.int32),
            jax.ShapeDtypeStruct((n, halo, y, w), F32),
        ],
        scratch_shapes=[
            pltpu.VMEM((n, h, y, z), F32),
            pltpu.VMEM((n, half, y, w), F32),
            pltpu.VMEM((n, halo, y, w), F32),
            pltpu.VMEM((4, half + halo, y, w), F32),
            pltpu.VMEM((n + 2, halo, y, w), F32),
            pltpu.VMEM((8, 128), jnp.int32),
            pltpu.VMEM((2, half, y, w), F32),
            dma((n,)), dma((n + 4,)), dma((n + 2,)), dma((size,)), dma((size,)),
            dma((4 + EARLY,)), dma((4 + EARLY,)), dma((4,)), dma((4,)),
        ],
        compiler_params=pltpu.CompilerParams(collective_id=1, has_side_effects=True),
        name="front",
    )(orbitals, pairs.T, live[None])


def plan_kernel(n, combos, every, offsets, plan, which, ups, downs, nups, ndowns, alive):
    size = every.shape[0]
    width = lax.axis_size("orb")
    me = lax.axis_index("grp") * width + lax.axis_index("orb")
    before, after = lax.rem(me + size - 1, size), lax.rem(me + 1, size)
    block = lambda x: lax.shift_right_logical(x, n.bit_length() - 1)

    def clear(e, c):
        ups[e] = 0
        downs[e] = 0
        nups[e] = 0
        ndowns[e] = 0
        alive[e] = sum(every[e, 2, r] for r in range(n))
        return c

    lax.fori_loop(0, size, clear, 0)

    def read(blk, r):
        i, j = every[blk, 0, r], every[blk, 1, r]
        bj = block(j)
        is_up = bj == jnp.where(blk + 1 == size, 0, blk + 1)
        li, lj = i & (n - 1), j & (n - 1)
        u, v = jnp.where(is_up, li, lj), jnp.where(is_up, lj, li)
        return i, j, bj, u, v, jnp.where(is_up, blk, bj)

    def mark(blk, c):
        def row(r, c):
            i, j, bj, u, v, edge = read(blk, r)

            @pl.when(bj != blk)
            def _():
                for bits, counts, x, free in ((ups, nups, u, n - 1), (downs, ndowns, v, 0)):
                    bit = jnp.where(x == free, 0, lax.shift_left(1, x))
                    had = bits[edge]
                    bits[edge] = had | bit
                    counts[edge] = counts[edge] + jnp.where((had | bit) != had, 1, 0)

            return c

        return lax.fori_loop(2, alive[blk], row, c)

    lax.fori_loop(0, size, mark, 0)

    def widest(e, most):
        o = lax.rem(e, width)
        mine = jnp.where(o % 2 == 0, 2, jnp.where(o == width - 1, 1, 0))
        here = jnp.maximum(nups[e], ndowns[e])
        return tuple(jnp.maximum(m, jnp.where(mine == c, here, 0)) for c, m in enumerate(most))

    most = lax.fori_loop(0, size, widest, (jnp.int32(0),) * 3)
    pick = jnp.int32(len(combos) - 1)
    for c in range(len(combos) - 2, -1, -1):
        fit = functools.reduce(lambda p, q: p & q, [m <= k for m, k in zip(most, combos[c])])
        pick = jnp.where(fit, c, pick)
    which[0] = pick

    def listing(bits, base):
        def step(q, s):
            plan[base + s] = q
            return s + (lax.shift_right_logical(bits, q) & 1)

        for q in range(n):
            plan[base + q] = 0
        return lax.fori_loop(0, n, step, jnp.int32(0))

    listing(ups[me], LISTS)
    listing(downs[before], LISTS + 2 * n)
    plan[INFO + 3] = nups[before]
    plan[INFO + 4] = ndowns[me]

    def rank(bits, x):
        return sum(
            jnp.where(q < x, lax.shift_right_logical(bits, q) & 1, 0) for q in range(n)
        )

    def place_of(x):
        blk, loc = block(x), x & (n - 1)
        from_before = jnp.where(loc == n - 1, n, n + 2 + rank(ups[before], loc))
        from_after = jnp.where(loc == 0, n + 1, n + 2 + n - 1 + rank(downs[me], loc))
        return jnp.where(blk == me, loc, jnp.where(blk == before, from_before, from_after))

    def sweep(ready, blk, start, skip, count):
        def step(r, s):
            i, j, bj, u, v, edge = read(blk, r)
            free = (bj == blk) | jnp.where(edge == me, v == 0, u == n - 1)
            want = ((blk == me) | (bj == me)) & (free == ready) & (r != skip)

            @pl.when(want)
            def _():
                write(s * TASK, i, j)

            return s + jnp.where(want, 1, 0)

        return lax.fori_loop(start, alive[blk], step, count)

    def write(at, i, j):
        plan[at] = place_of(i)
        plan[at + 1] = place_of(j)
        plan[at + 2] = offsets[0, j] - offsets[0, i]
        plan[at + 3] = offsets[1, j] - offsets[1, i]
        plan[at + 4] = jnp.where(block(i) == me, i & (n - 1), n)
        plan[at + 5] = jnp.where(block(j) == me, j & (n - 1), n)

    def blank(s):
        for c, value in enumerate((0, 0, 0, 0, n, n)):
            plan[s * TASK + c] = value

    for s, (blk, r) in enumerate(((me, 1), (after, 0), (me, 0), (before, 1))):
        write(s * TASK, every[blk, 0, r], every[blk, 1, r])
    for s in range(4, 2 * AHEAD):
        blank(s)
    count = jnp.int32(4)
    for ready in (True, False):
        count = sweep(ready, me, 2, n, count)
        count = sweep(ready, before, 0, 1, count)
        count = sweep(ready, after, 1, n, count)
        if ready:
            count = jnp.maximum(count, 2 * AHEAD)
    plan[INFO + 6] = count
    blank(count)


def make_plan(every, offsets, n, combos):
    size = every.shape[0]
    smem = pl.BlockSpec(memory_space=pltpu.SMEM)
    return pl.pallas_call(
        functools.partial(plan_kernel, n, combos),
        in_specs=[smem, smem],
        out_specs=[smem, smem],
        out_shape=[
            jax.ShapeDtypeStruct((PLAN,), jnp.int32),
            jax.ShapeDtypeStruct((1,), jnp.int32),
        ],
        scratch_shapes=[pltpu.SMEM((size,), jnp.int32)] * 5,
        name="plan",
    )(every, offsets.T)


def wipe_room(room, y):
    def step(f, c):
        room[f, :, y:, :] = jnp.zeros((room.shape[1], PAD, room.shape[3]), F32)
        return c

    lax.fori_loop(0, room.shape[0], step, 0)


def repeat(count, unroll, do):
    def step(g, c):
        for q in range(unroll):
            do(g * unroll + q)
        return c

    lax.fori_loop(0, count // unroll, step, 0)


def solver(plan, room, one, two, own2, par2, prod, wheel, moves, basis, basis_back, levels, h):
    rows, tall, w = room.shape[1:]
    y, z = tall - PAD, w // 2
    half = h // 2
    halo = rows - half
    each = rows * tall
    quads, line, _ = factors()

    prod[0] = jnp.zeros((tall, w), F32)
    prod[:, y:, :] = jnp.zeros((h + 1, PAD, w), F32)
    for ref in (one, two):
        planes = ref.shape[0]
        ref[0] = jnp.zeros(ref.shape[1:], F32)
        ref[:, 0:8, :] = jnp.zeros((planes, 8, w), F32)
        ref[:, 8 + y :, :] = jnp.zeros((planes, 8, w), F32)
    flat_room = room.reshape(room.shape[0] * each, w)
    flat_prod = prod.reshape((h + 1) * tall, w)

    k_at = lax.broadcasted_iota(jnp.int32, (2 * w, 2 * w), 0)
    c_at = lax.broadcasted_iota(jnp.int32, (2 * w, 2 * w), 1)
    task_k, half_k, task_c, half_c = k_at // w, k_at % w // z, c_at % w // z, c_at // w
    gap = k_at % z - c_at % z
    wheel[...] = jnp.where((task_k == task_c) & (half_k == half_c), gap, 4 * z)

    lane = lanes((y, w))
    low = lane < z
    pos = lane % z
    mu = jnp.broadcast_to(levels[...], (STRIP, w))

    def sweep(src, count, emit):
        def step(g, c):
            for r in range(0, y, STRIP):
                at = pl.ds(8 + r, STRIP)
                col = [src[g * UNROLL + q, at, :] for q in range(UNROLL + 2)]
                for q in range(UNROLL):
                    t = g * UNROLL + q
                    sides = src[t + 1, pl.ds(7 + r, STRIP), :] + src[t + 1, pl.ds(9 + r, STRIP), :]
                    emit(t, r, col[q + 1], (col[q] + col[q + 2]) + sides)
            return c

        lax.fori_loop(0, (count + UNROLL - 1) // UNROLL, step, 0)

    def split(values):
        coarse = values.astype(jnp.bfloat16)
        return coarse, (values - coarse.astype(F32)).astype(jnp.bfloat16)

    def turn_z(values, wave):
        both = jnp.dot(
            jnp.concatenate(split(values), axis=1), wave[...], preferred_element_type=F32
        )
        return both[:, :w] + both[:, w:]

    def planes(r):
        return jnp.where(r < half, r, r + half), jnp.where(r < half, r + half, r + half + halo)

    def run(g, gains, backs):
        p, q = g * 2 * TASK, (g * 2 + 1) * TASK
        rp, rq = (plan[p] + 1) * each, (plan[q] + 1) * each
        ap, aq, bp, bq = plan[p + 2], plan[q + 2], plan[p + 3], plan[q + 3]
        sp, sq = (plan[p + 1] + 1) * each - ap, (plan[q + 1] + 1) * each - aq
        col = lanes((1, 2 * w)) % w < z
        moves[...] = jnp.where(wheel[...] == jnp.where(col, -bp, -bq), 1.0, 0.0).astype(jnp.bfloat16)

        def waves_of(g):
            raw = []
            for q in range(DEPTH):
                for t in planes(g * DEPTH + q):
                    raw.append(two[t + 1, 8 : 8 + y, :])
            return turn_z(jnp.concatenate(raw, axis=0), basis)

        def keep_waves(g, waves):
            for q in range(DEPTH):
                for side, t in enumerate(planes(g * DEPTH + q)):
                    at = (2 * q + side) * y
                    one[t + 1, 8 : 8 + y, :] = waves[at : at + y]

        def partners(g):
            par = [
                jnp.concatenate(
                    [flat_room[pl.ds(sp + r * tall, y), :], flat_room[pl.ds(sq + r * tall, y), :]],
                    axis=1,
                )
                for r in [g * DEPTH + q for q in range(DEPTH)]
            ]
            par = jnp.concatenate(split(jnp.concatenate(par, axis=0)), axis=0)
            par = jnp.dot(par, moves[...], preferred_element_type=F32)
            return par[: DEPTH * y] + par[DEPTH * y :]

        def keep_partners(g, par):
            for q in range(DEPTH):
                r = g * DEPTH + q
                own_p = flat_room[pl.ds(rp + r * tall, y), :]
                own_q = flat_room[pl.ds(rq + r * tall, y), :]
                own_a = jnp.where(low, own_p, pltpu.roll(own_q, z, axis=1))
                own_b = jnp.where(low, pltpu.roll(own_p, z, axis=1), own_q)
                for t, own, half_par in zip(
                    planes(r), (own_a, own_b), jnp.split(par[q * y : (q + 1) * y], 2, axis=1)
                ):
                    two[t + 1, 8 : 8 + y, :] = own * half_par
                    own2[t] = own
                    par2[t] = half_par

        def dense(g, c):
            waves, par = waves_of(g - 1), partners(g)
            keep_waves(g - 1, waves)
            keep_partners(g, par)
            return c

        turns = rows // DEPTH
        keep_partners(0, partners(0))
        lax.fori_loop(1, turns, dense, 0)
        keep_waves(turns - 1, waves_of(turns - 1))

        def quad(k, c):
            b, c2 = jnp.float32(quads[0][0]), jnp.float32(quads[0][1])
            for m in range(1, len(quads)):
                b = jnp.where(k == m, jnp.float32(quads[m][0]), b)
                c2 = jnp.where(k == m, jnp.float32(quads[m][1]), c2)
            mu_b = mu + b

            def first(t, r, cur, near):
                two[t + 1, pl.ds(8 + r, STRIP), :] = near + mu_b * cur

            def second(t, r, cur, near):
                at = pl.ds(8 + r, STRIP)
                one[t + 1, at, :] = (near + mu * cur) + c2 * one[t + 1, at, :]

            count = h + EDGE - 1 - 2 * k
            sweep(one, count, first)
            sweep(two, count - 1, second)
            return c

        lax.fori_loop(0, len(quads), quad, 0)
        mu_line = mu + line

        def finish(g, c):
            values = [[] for _ in range(UNROLL)]
            for r in range(0, y, STRIP):
                at = pl.ds(8 + r, STRIP)
                col = [one[g * UNROLL + q, at, :] for q in range(UNROLL + 2)]
                for q in range(UNROLL):
                    t = g * UNROLL + q
                    sides = one[t + 1, pl.ds(7 + r, STRIP), :] + one[t + 1, pl.ds(9 + r, STRIP), :]
                    values[q].append((col[q] + col[q + 2]) + sides + mu_line * col[q + 1])
            both = turn_z(jnp.concatenate(sum(values, []), axis=0), basis_back)
            for q in range(UNROLL):
                t = g * UNROLL + q
                pot = both[q * y : (q + 1) * y]
                gains[t] = pot * par2[t]
                prod[t + 1, 0:y, :] = pot * own2[t]
            return c

        lax.fori_loop(0, h // UNROLL, finish, 0)

        back = pos + jnp.where(low, bp, bq)
        good = (back >= 0) & (back < z)
        turn_p, turn_q = lax.rem(w - bp, w), lax.rem(w - bq, w)

        def plane(t):
            at = (t + 1) * tall
            moved_p = pltpu.roll(flat_prod[pl.ds(at + ap, y), :], turn_p, axis=1)
            moved_q = pltpu.roll(flat_prod[pl.ds(at + aq, y), :], turn_q, axis=1)
            backs[t] = jnp.where(good, jnp.where(low, moved_p, moved_q), 0.0)

        repeat(h, 4, plane)

    return run


def solver_scratch(fields, h, y, w, rows):
    planes = 2 * rows
    return [
        pltpu.VMEM((fields + 1, rows, y + PAD, w), F32),
        pltpu.VMEM((planes + 6, y + 16, w), F32),
        pltpu.VMEM((planes + 6, y + 16, w), F32),
        pltpu.VMEM((planes, y, w), F32),
        pltpu.VMEM((planes, y, w), F32),
        pltpu.VMEM((h + 1, y + PAD, w), F32),
        pltpu.VMEM((2 * w, 2 * w), jnp.int32),
        pltpu.VMEM((2 * w, 2 * w), jnp.bfloat16),
    ]


def swap_kernel(
    counts, plan, fields, edges, basis, basis_back, levels, prior, nxt, halos, results,
    room, one, two, own2, par2, prod, wheel, moves, sends, got, trim, hal, parts,
    in_sem, send, recv, edge_send, edge_recv, trim_send, trim_recv, main_sem, rim_sem,
    hal_sem, part_sem,
):
    n, halo, y, w = edges.shape
    rows = fields.shape[1]
    half = rows - halo
    m = sends.shape[1]
    late = hal.shape[0]
    size, width = lax.axis_size(CYCLE), lax.axis_size("orb")
    o = lax.axis_index("orb")
    me = lax.axis_index("grp") * width + o
    slab = lax.axis_index("slab")
    other = {"slab": 1 - slab}

    def peer(s):
        to = lax.rem(me + s, size)
        return {"grp": lax.div(to, width), "orb": lax.rem(to, width)}

    def limit(q):
        return jnp.where(q % 2 == 0, counts[2], jnp.where(q == width - 1, counts[1], counts[0]))

    above, under = limit(o), limit(lax.rem(o + width - 1, width))
    ways = ((0, above, under, prior), (1, under, above, nxt))

    def load(f):
        return pltpu.make_async_copy(fields.at[f], room.at[f + 1, :, pl.ds(0, y)], in_sem.at[f])

    def edge_copy(k):
        return pltpu.make_async_remote_copy(
            src_ref=edges.at[n - 1 - late + k], dst_ref=hal.at[k],
            send_sem=edge_send.at[k], recv_sem=edge_recv.at[k],
            device_id=other, device_id_type=pl.DeviceIdType.MESH,
        )

    def keep_hal(k):
        return pltpu.make_async_copy(hal.at[k], halos.at[k], hal_sem.at[k])

    def copy(way, r):
        return pltpu.make_async_remote_copy(
            src_ref=sends.at[way, r], dst_ref=got.at[way, r, pl.ds(0, half)],
            send_sem=send.at[way, r], recv_sem=recv.at[way, r],
            device_id=peer((1, size - 1)[way]), device_id_type=pl.DeviceIdType.MESH,
        )

    def head(way):
        return pltpu.make_async_copy(
            fields.at[n + 2 + way, pl.ds(0, half)], got.at[way, 0, pl.ds(0, half)],
            recv.at[way, 0],
        )

    def trim_copy(way, r):
        return pltpu.make_async_remote_copy(
            src_ref=trim.at[way, r], dst_ref=got.at[way, r, pl.ds(half, halo)],
            send_sem=trim_send.at[way, r], recv_sem=trim_recv.at[way, r],
            device_id=other, device_id_type=pl.DeviceIdType.MESH,
        )

    def main_out(way, r, dst):
        part = pl.ds(0, half)
        return pltpu.make_async_copy(got.at[way, r, part], dst.at[r, part], main_sem.at[way, r])

    def rim_out(way, r, dst):
        part = pl.ds(half, halo)
        return pltpu.make_async_copy(got.at[way, r, part], dst.at[r, part], rim_sem.at[way, r])

    def part_out(g):
        return pltpu.make_async_copy(parts.at[g % 2], results.at[g], part_sem.at[g % 2])

    def each(start, stop, do):
        def step(k, c):
            do(k)
            return c

        lax.fori_loop(start, stop, step, 0)

    each(0, n + 2, lambda f: load(f).start())
    barrier = pltpu.get_barrier_semaphore()
    for to in (peer(1), peer(size - 1), other):
        pl.semaphore_signal(barrier, inc=1, device_id=to, device_id_type=pl.DeviceIdType.MESH)
    wipe_room(room, y)
    run = solver(
        plan, room, one, two, own2, par2, prod, wheel, moves, basis, basis_back, levels, 2 * half
    )
    pl.semaphore_wait(barrier, 3)
    each(0, late, lambda k: edge_copy(k).start())
    for way in range(2):
        head(way).start()
    each(0, n + 2, lambda f: load(f).wait())

    def launch(r):
        for way, out, _, _ in ways:
            @pl.when(r < out)
            def _(way=way):
                k = plan[LISTS + way * 2 * n + r]

                def row(t):
                    sends[way, r, t] = room[k + 1, t, 0:y, :]

                each(0, half, row)
                copy(way, r).start()

    each(1, m, launch)
    low = lanes((1, w)) < w // 2

    def land(r):
        for way, _, into, dst in ways:
            @pl.when(r < into)
            def _(way=way, dst=dst):
                pl.when(r == 0)(lambda: head(way).wait())
                pl.when(r > 0)(lambda: copy(way, r).wait_recv())
                main_out(way, r, dst).start()
                for e in range(halo):
                    a, b = got[way, r, half - 1 - e], got[way, r, half - 1 - halo - e]
                    trim[way, r, e] = jnp.where(low, pltpu.roll(a, w // 2, axis=1), b)
                trim_copy(way, r).start()

    def work(g):
        pl.when(g >= 2)(lambda: part_out(g - 2).wait())

        @pl.when(g == 2)
        def _():
            for k in range(late):
                edge_copy(k).wait()
                keep_hal(k).start()
                room[n - late + k, half:, 0:y, :] = hal[k]

        run(g, parts.at[g % 2, 0], parts.at[g % 2, 1])
        part_out(g).start()
        pl.when(g < m)(lambda: land(g))

    each(0, AHEAD, work)
    each(min(AHEAD, m), m, land)
    for k in range(late):
        keep_hal(k).wait()
    for g in range(AHEAD - 2, AHEAD):
        part_out(g).wait()

    def settle(r):
        for way, out, into, dst in ways:
            @pl.when(r < into)
            def _(way=way, dst=dst):
                trim_copy(way, r).wait()
                rim_out(way, r, dst).start()

            @pl.when((r > 0) & (r < out))
            def _(way=way):
                copy(way, r).wait_send()

    each(0, m, settle)

    def close(r):
        for way, _, into, dst in ways:
            @pl.when(r < into)
            def _(way=way, dst=dst):
                main_out(way, r, dst).wait()
                rim_out(way, r, dst).wait()

    each(0, m, close)


def swap(counts, plan, fields, edges, waves, cid):
    n, halo, y, w = edges.shape
    rows = fields.shape[1]
    half, m = rows - halo, max(counts)
    late = n - 2 - EARLY
    hbm = pl.BlockSpec(memory_space=pl.ANY)
    smem = pl.BlockSpec(memory_space=pltpu.SMEM)
    vmem = pl.BlockSpec(memory_space=pltpu.VMEM)
    dma = pltpu.SemaphoreType.DMA
    out = jax.ShapeDtypeStruct((n - 1, rows, y, w), F32)
    return pl.pallas_call(
        functools.partial(swap_kernel, counts),
        in_specs=[smem, hbm, hbm, vmem, vmem, vmem],
        out_specs=[hbm, hbm, hbm, hbm],
        out_shape=[
            out,
            out,
            jax.ShapeDtypeStruct((late, halo, y, w), F32),
            jax.ShapeDtypeStruct((AHEAD, 2, 2 * half, y, w), F32),
        ],
        scratch_shapes=solver_scratch(n + 2, 2 * half, y, w, rows)
        + [
            pltpu.VMEM((2, m, half, y, w), F32),
            pltpu.VMEM((2, m, rows, y, w), F32),
            pltpu.VMEM((2, m, halo, y, w), F32),
            pltpu.VMEM((late, halo, y, w), F32),
            pltpu.VMEM((2, 2, 2 * half, y, w), F32),
            dma((n + 2,)), dma((2, m)), dma((2, m)), dma((late,)), dma((late,)),
            dma((2, m)), dma((2, m)), dma((2, m)), dma((2, m)), dma((late,)), dma((2,)),
        ],
        compiler_params=pltpu.CompilerParams(
            collective_id=cid, has_side_effects=True, vmem_limit_bytes=58 * 1024 * 1024
        ),
        name="swap%d%d%d" % counts,
    )(plan, fields, edges, *waves)


def pairs_kernel(
    plan, fields, prior, nxt, halos, results, basis, basis_back, levels, out,
    room, one, two, own2, par2, prod, wheel, moves, acc, stage, parts, sem, rim_sem, out_sem, part_sem,
):
    n, h, y, z = out.shape
    w = 2 * z
    half, rows = h // 2, fields.shape[1]
    halo = rows - half
    most = prior.shape[0]
    late = halos.shape[0]
    slab = lax.axis_index("slab")

    def part(g):
        return pltpu.make_async_copy(results.at[g], parts.at[g % 2], part_sem.at[g % 2])

    def field(src, s, f, first, count, sem):
        return pltpu.make_async_copy(
            src.at[s, pl.ds(first, count)],
            room.at[f + 1, pl.ds(rows - count if src is halos else first, count), pl.ds(0, y)],
            sem.at[f],
        )

    def each_field(do):
        for f in range(n + 2):
            if n - 1 - late <= f < n - 1:
                do(field(fields, f, f, 0, half, sem))
                do(field(halos, f - (n - 1 - late), f, 0, halo, rim_sem))
            else:
                do(field(fields, f, f, 0, rows, sem))
        for src, base, count in ((prior, n + 2, plan[INFO + 3]), (nxt, n + 2 + most, plan[INFO + 4])):
            for s in range(most):
                pl.when(s < count)(
                    lambda src=src, s=s, base=base: do(field(src, s, base + s, 0, rows, sem))
                )

    part(0).start()
    part(1).start()
    each_field(lambda c: c.start())
    acc[...] = jnp.zeros(acc.shape, F32)
    wipe_room(room, y)
    run = solver(plan, room, one, two, own2, par2, prod, wheel, moves, basis, basis_back, levels, h)
    low = lanes((y, w)) < w // 2

    def collect(g, gains, backs):
        p, q = g * 2 * TASK, (g * 2 + 1) * TASK
        for k, src, side in (
            (plan[p + 4], gains, low),
            (plan[q + 4], gains, jnp.logical_not(low)),
            (plan[p + 5], backs, low),
            (plan[q + 5], backs, jnp.logical_not(low)),
        ):
            @pl.when(k < n)
            def _(k=k, src=src, side=side):
                def plane(t):
                    acc[k, t] += jnp.where(side, src[t], 0.0)

                repeat(h, 4, plane)

    def gather(g, c):
        part(g).wait()
        collect(g, parts.at[g % 2, 0], parts.at[g % 2, 1])
        pl.when(g + 2 < AHEAD)(lambda: part(g + 2).start())
        return c

    lax.fori_loop(0, AHEAD, gather, 0)
    each_field(lambda c: c.wait())

    def group(g, c):
        run(g, parts.at[0, 0], parts.at[0, 1])
        collect(g, parts.at[0, 0], parts.at[0, 1])
        return c

    lax.fori_loop(AHEAD, lax.div(plan[INFO + 6] + 1, 2), group, 0)

    def leave(k, slot):
        return pltpu.make_async_copy(stage.at[slot], out.at[k], out_sem.at[slot])

    def write(k, c):
        slot = lax.rem(k, 2)
        pl.when(k >= 2)(lambda: leave(k - 2, slot).wait())

        def plane(t):
            value = acc[k, t]
            value = value + pltpu.roll(value, z, axis=1)
            stage[slot, jnp.where(slab == 0, t, h - 1 - t)] = value[:, :z]

        repeat(h, 4, plane)
        leave(k, slot).start()
        return c

    lax.fori_loop(0, n, write, 0)
    for k in (n - 2, n - 1):
        leave(k, k % 2).wait()


def sines(z):
    k = np.arange(1, z + 1)
    wave = np.sqrt(2.0 / (z + 1)) * np.sin(np.pi * np.outer(k, k) / (z + 1))
    wave = np.kron(np.eye(2), wave).astype(np.float32)
    levels = np.tile(2.0 * np.cos(np.pi * k / (z + 1)), 2).astype(np.float32)[None]

    def parts(values):
        coarse = jnp.asarray(values).astype(jnp.bfloat16)
        fine = (jnp.asarray(values) - coarse.astype(F32)).astype(jnp.bfloat16)
        top = jnp.concatenate([coarse, fine], axis=1)
        bottom = jnp.concatenate([coarse, jnp.zeros_like(fine)], axis=1)
        return jnp.concatenate([top, bottom], axis=0)

    return parts(wave), parts(wave * np.float32(factors()[2])), jnp.asarray(levels)


def solve_pairs(plan, fields, prior, nxt, halos, results, waves, shape):
    n, h, y, z = shape
    w, rows = 2 * z, fields.shape[1]
    most = prior.shape[0]
    hbm = pl.BlockSpec(memory_space=pl.ANY)
    vmem = pl.BlockSpec(memory_space=pltpu.VMEM)
    dma = pltpu.SemaphoreType.DMA
    total = n + 2 + 2 * most
    return pl.pallas_call(
        pairs_kernel,
        grid_spec=pltpu.PrefetchScalarGridSpec(
            num_scalar_prefetch=1,
            grid=(1,),
            in_specs=[hbm] * 5 + [vmem] * 3,
            out_specs=hbm,
            scratch_shapes=solver_scratch(total, h, y, w, rows)
            + [
                pltpu.VMEM((n, h, y, w), F32),
                pltpu.VMEM((2, h, y, z), F32),
                pltpu.VMEM((2, 2, h, y, w), F32),
                dma((total,)), dma((n,)), dma((2,)), dma((2,)),
            ],
        ),
        out_shape=jax.ShapeDtypeStruct(shape, F32),
        compiler_params=pltpu.CompilerParams(vmem_limit_bytes=58 * 1024 * 1024),
        name="pairs",
    )(plan, fields, prior, nxt, halos, results, *waves)


def fast_body(orbitals, offsets, pairs, live):
    n = orbitals.shape[0]
    combos = [(2, 2, 2), (3, 3, 3), (2, 4, 3), (4, 2, 3), (3, 4, 4), (4, 3, 4), (4, 4, 4)]
    combos.append((n - 1,) * 3)
    fields, every, edges = front(orbitals, pairs, live)
    plan, which = make_plan(every, offsets, n, combos)
    waves = sines(orbitals.shape[-1])

    def branch(counts, cid):
        return lambda _: swap(counts, plan, fields, edges, waves, cid)

    prior, nxt, halos, results = lax.switch(
        which[0], [branch(c, 2 + i) for i, c in enumerate(combos)], 0
    )
    return solve_pairs(plan, fields, prior, nxt, halos, results, waves, orbitals.shape)


def body(orbitals, offsets, pairs, live):
    n = orbitals.shape[0]
    slots = pairs.shape[0]
    total = offsets.shape[0]
    blocks = total // n
    slabs = lax.axis_size("slab")
    me = lax.axis_index(CYCLE)
    packed = pack(orbitals)

    mine = jnp.concatenate([pairs, live[:, None]], axis=1)
    every = share(jnp.pad(mine, ((0, 0), (0, 128 - mine.shape[1]))))
    ids = jnp.arange(blocks, dtype=jnp.int32)
    second = every[:, :, 1]
    alive = every[:, :, 2] > 0
    orb = jnp.arange(n, dtype=jnp.int32)
    sides = jnp.stack([(ids - 1) % blocks, (ids + 1) % blocks])
    hit = alive[None] & (second[None] // n == sides[:, :, None])
    need = jnp.any(
        hit[..., None] & (second[None, :, :, None] % n == orb), axis=2
    )
    count = jnp.sum(need.astype(jnp.int32), axis=2)
    most = jnp.max(count)

    after, before = (me + 1) % blocks, (me - 1) % blocks
    flags = jnp.stack(
        [need[0, me], need[1, me], need[0, after], need[1, before]]
    ).astype(jnp.int32)
    spot = jnp.sum(
        flags[:, None, :] * (orb[None, :] < orb[:, None]).astype(jnp.int32)[None], axis=2
    )
    lists = jnp.sum(
        (flags[:, None, :] * (spot[:, None, :] == orb[None, :, None])) * orb, axis=2
    )
    back = jnp.stack(
        [spot[2] * flags[2], flags[2], spot[3] * flags[3], flags[3]]
    )

    i, j, on = pairs[:, 0], pairs[:, 1], live > 0
    owner, local = j // n, j % n
    pick_j = (local[:, None] == orb[None, :]).astype(jnp.int32)
    from_prior = (owner == before) & on
    from_next = (owner == after) & on
    kind = jnp.where(from_prior, 1, jnp.where(from_next, 2, 0))
    where_prior = jnp.sum(pick_j * spot[0][None, :], axis=1) * from_prior
    where_next = jnp.sum(pick_j * spot[1][None, :], axis=1) * from_next
    ids_all = jnp.arange(total, dtype=jnp.int32)
    diff = (j[:, None] == ids_all).astype(jnp.int32) - (i[:, None] == ids_all).astype(jnp.int32)
    shift = jnp.sum(diff[:, :, None] * offsets[None], axis=1)
    plan = jnp.stack(
        [i % n, local, where_prior, where_next, kind, shift[:, 0], shift[:, 1], live]
    ).astype(jnp.int32)
    order = jnp.where(on, jnp.where(kind > 0, 0, 1), 2) * slots + jnp.arange(slots)
    rank = jnp.sum((order[None, :] < order[:, None]).astype(jnp.int32), axis=1)
    move = (rank[:, None] == jnp.arange(slots)[None, :]).astype(jnp.int32)
    plan = jnp.sum(plan[:, :, None] * move[None], axis=1)
    far, lively = jnp.sum((kind > 0).astype(jnp.int32)), jnp.sum(on.astype(jnp.int32))
    tail = jnp.where(jnp.arange(slots) == 0, far, lively)
    plan = jnp.concatenate([plan, tail[None]], axis=0)
    ends = jnp.stack([lax.axis_index("slab"), slabs]).astype(jnp.int32)

    up = [(s, s + 1) for s in range(slabs - 1)]
    down = [(s + 1, s) for s in range(slabs - 1)]

    def branch(m):
        def run(_):
            to_next, to_prior = gather(packed, lists[2:], m)
            prior = cycle(to_next, 1)
            nxt = cycle(to_prior, -1)
            partner, density, low, high = densities(plan, packed, prior, nxt)
            below = lax.ppermute(high, "slab", up)
            above = lax.ppermute(low, "slab", down)
            given = (plan, ends, density, partner, packed, below, above, m)
            acc, acc_prior, acc_next = solve(True, *given)
            from_next, from_prior = cycle(acc_prior, -1), cycle(acc_next, 1)
            (acc_near,) = solve(False, *given)
            return combine(back, acc, acc_near, from_next, from_prior)

        return run

    sizes = sorted({min(s, slots - 1) for s in (3, 4, 5)} | {slots - 1})
    which = sum((most > s).astype(jnp.int32) for s in sizes[:-1])
    return lax.switch(which, [branch(s) for s in sizes], 0)


def solution(mesh):
    placed = (
        P(CYCLE, "slab", None, None),
        P(),
        P(CYCLE, None),
        P(CYCLE),
    )
    return jax.shard_map(
        fast_body if mesh.shape["slab"] == 2 else body,
        mesh=mesh,
        in_specs=placed,
        out_specs=P(CYCLE, "slab", None, None),
        check_vma=False,
    )
```

```python
import cmath
import functools
import math

import jax
import jax.numpy as jnp
import numpy as np
from jax import lax
from jax.experimental import pallas as pl
from jax.experimental.pallas import tpu as pltpu
from jax.sharding import PartitionSpec as P

PASSES = 8
DIAG = 6.25
THETA = 1.075
DELTA = 0.925
EDGE = PASSES - 1
PAD = 16
CYCLE = ("grp", "orb")
F32 = jnp.float32


def coefs():
    sigma = THETA / DELTA
    coef = 1.0 / sigma
    out = []
    for _ in range(PASSES - 1):
        new = 1.0 / (2.0 * sigma - coef)
        out.append((new * coef, 2.0 * new / (DELTA * DIAG)))
        coef = new
    return out


def lanes(shape):
    return lax.broadcasted_iota(jnp.int32, shape, len(shape) - 1)


def share_kernel(mine, every, send_sem, recv_sem):
    size, width = lax.axis_size(CYCLE), lax.axis_size("orb")
    me = lax.axis_index("grp") * width + lax.axis_index("orb")

    def peer(s):
        to = lax.rem(me + s, size)
        return {"grp": lax.div(to, width), "orb": lax.rem(to, width)}

    def greet(s, c):
        pl.semaphore_signal(
            barrier, inc=1, device_id=peer(s), device_id_type=pl.DeviceIdType.MESH
        )
        return c

    def copy(s, slot):
        return pltpu.make_async_remote_copy(
            src_ref=mine,
            dst_ref=every.at[slot],
            send_sem=send_sem.at[s],
            recv_sem=recv_sem.at[s],
            device_id=peer(s),
            device_id_type=pl.DeviceIdType.MESH,
        )

    def send(s, c):
        copy(s, me).start()
        return c

    def finish(s, c):
        copy(s, lax.rem(me + size - s, size)).wait()
        return c

    barrier = pltpu.get_barrier_semaphore()
    lax.fori_loop(1, size, greet, 0)
    pl.semaphore_wait(barrier, size - 1)
    lax.fori_loop(1, size, send, 0)
    every[me] = mine[...]
    lax.fori_loop(1, size, finish, 0)


def share(mine):
    size = lax.axis_size(CYCLE)
    vmem = pl.BlockSpec(memory_space=pltpu.VMEM)
    return pl.pallas_call(
        share_kernel,
        in_specs=[vmem],
        out_specs=vmem,
        out_shape=jax.ShapeDtypeStruct((size,) + mine.shape, mine.dtype),
        scratch_shapes=[pltpu.SemaphoreType.DMA((size,)), pltpu.SemaphoreType.DMA((size,))],
        compiler_params=pltpu.CompilerParams(collective_id=0, has_side_effects=True),
        name="share",
    )(mine)


def pack_kernel(src, dst):
    half = dst.shape[1]
    dst[0] = jnp.concatenate([src[0, :half], src[0, half:]], axis=-1)


def pack(orbitals):
    n, x, y, z = orbitals.shape
    return pl.pallas_call(
        pack_kernel,
        grid=(n,),
        in_specs=[pl.BlockSpec((1, x, y, z), lambda i: (i, 0, 0, 0))],
        out_specs=pl.BlockSpec((1, x // 2, y, 2 * z), lambda i: (i, 0, 0, 0)),
        out_shape=jax.ShapeDtypeStruct((n, x // 2, y, 2 * z), F32),
        name="pack",
    )(orbitals)


def copy_kernel(idx, src_a, src_b, dst_a, dst_b):
    dst_a[...] = src_a[...]
    dst_b[...] = src_b[...]


def gather(packed, lists, m):
    _, h, y, w = packed.shape
    blk = (1, h, y, w)
    out = jax.ShapeDtypeStruct((m, h, y, w), F32)
    return pl.pallas_call(
        copy_kernel,
        grid_spec=pltpu.PrefetchScalarGridSpec(
            num_scalar_prefetch=1,
            grid=(m,),
            in_specs=[
                pl.BlockSpec(blk, lambda i, idx: (idx[0, i], 0, 0, 0)),
                pl.BlockSpec(blk, lambda i, idx: (idx[1, i], 0, 0, 0)),
            ],
            out_specs=[pl.BlockSpec(blk, lambda i, idx: (i, 0, 0, 0))] * 2,
        ),
        out_shape=[out, out],
        name="gather",
    )(lists, packed, packed)


def place(value, room, a, b):
    y, w = value.shape[1:]
    z = w // 2
    room[:, PAD : PAD + y, :] = value
    moved = room[:, pl.ds(PAD - a, y), :]
    moved = pltpu.roll(moved, lax.rem(b + w, w), axis=2)
    pos = lanes(moved.shape) % z - b
    return jnp.where((pos >= 0) & (pos < z), moved, 0.0)


def clear_room(room):
    y = room.shape[1] - 2 * PAD
    room[:, :PAD, :] = jnp.zeros((room.shape[0], PAD, room.shape[2]), F32)
    room[:, PAD + y :, :] = jnp.zeros((room.shape[0], PAD, room.shape[2]), F32)


def density_kernel(plan, own, mine, prior, nxt, partner, density, low, high, room):
    p = pl.program_id(0)
    kind = plan[4, p]
    a, b = plan[5, p], plan[6, p]

    @pl.when(p == 0)
    def _():
        clear_room(room)

    on = plan[7, p] > 0

    def go(src):
        part = place(src[0], room, a, b)
        partner[0] = part
        dens = own[0] * part
        density[0] = dens
        h, y, w = dens.shape
        flat = jnp.concatenate([dens[..., : w // 2], dens[..., w // 2 :]], axis=0)
        top, bot = flat[:EDGE], flat[2 * h - EDGE :]
        low[0] = jnp.concatenate([top[:, : y // 2], top[:, y // 2 :]], axis=-1)
        high[0] = jnp.concatenate([bot[:, : y // 2], bot[:, y // 2 :]], axis=-1)

    for value, src in enumerate((mine, prior, nxt)):
        pl.when(on & (kind == value))(functools.partial(go, src))


def densities(plan, packed, prior, nxt):
    slots = plan.shape[1]
    _, h, y, w = packed.shape
    blk = (1, h, y, w)
    eblk = (1, EDGE, y // 2, w)

    def at(row):
        return pl.BlockSpec(
            blk, lambda i, plan: (plan[row, jnp.minimum(i, plan[8, 1] - 1)], 0, 0, 0)
        )

    full = jax.ShapeDtypeStruct((slots, h, y, w), F32)
    edge = jax.ShapeDtypeStruct((slots,) + eblk[1:], F32)
    here = lambda i, plan: (jnp.minimum(i, plan[8, 1] - 1), 0, 0, 0)
    return pl.pallas_call(
        density_kernel,
        grid_spec=pltpu.PrefetchScalarGridSpec(
            num_scalar_prefetch=1,
            grid=(slots,),
            in_specs=[at(0), at(1), at(2), at(3)],
            out_specs=[
                pl.BlockSpec(blk, here),
                pl.BlockSpec(blk, here),
                pl.BlockSpec(eblk, here),
                pl.BlockSpec(eblk, here),
            ],
            scratch_shapes=[pltpu.VMEM((h, y + 2 * PAD, w), F32)],
        ),
        out_shape=[full, full, edge, edge],
        name="density",
    )(plan, packed, packed, prior, nxt)


def solve_kernel(remote, plan, ends, density, partner, own, below, above, *refs):
    accs, (resid, step_a, step_b, total, mask, room) = refs[:-6], refs[-6:]
    acc = accs[0]
    p = pl.program_id(0)
    h, y, w = density.shape[1:]
    z = w // 2
    rows = h + 2 * EDGE
    group = 4 if h % 4 == 0 else 1

    @pl.when(p == 0)
    def _():
        clear_room(room)
        for ref in accs:
            ref[...] = jnp.zeros(ref.shape, F32)
        for ref in (step_a, step_b):
            ref[:, :8, :] = jnp.zeros((rows, 8, w), F32)
            ref[:, 8 + y :, :] = jnp.zeros((rows, 8, w), F32)
        lane = lanes((1, w))
        first = ends[0] == 0
        last = ends[0] == ends[1] - 1
        for t in range(rows):
            plane = jnp.where(lane < z, t - EDGE, t - EDGE + h)
            outside = ((plane < 0) & first) | ((plane >= 2 * h) & last)
            mask[t] = jnp.where(outside, 0.0, 1.0)

    chosen = (plan[4, p] > 0) if remote else (plan[4, p] == 0)

    @pl.when((plan[7, p] > 0) & chosen)
    def _():
        def unfold(part):
            return jnp.concatenate([part[..., :z], part[..., z:]], axis=1)

        dens = density[0]
        line = jnp.concatenate(
            [unfold(below[0]), dens[..., :z], dens[..., z:], unfold(above[0])], axis=0
        )
        resid[...] = jnp.concatenate([line[:rows], line[h:]], axis=-1)
        step_a[:, 8 : 8 + y, :] = resid[...] * (1.0 / (DIAG * THETA))
        total[...] = step_a[EDGE : EDGE + h, 8 : 8 + y, :]
        lane = lanes((y, w)) % z
        not_low = lane > 0
        not_high = lane < z - 1
        bufs = [step_a, step_b]
        for turn, (keep, gain) in enumerate(coefs()):
            now, then = bufs[turn % 2], bufs[1 - turn % 2]
            core_only = turn == PASSES - 2

            def row(t, now=now, then=then, keep=keep, gain=gain):
                core = now[t, 8 : 8 + y, :]
                near = now[t - 1, 8 : 8 + y, :] + now[t + 1, 8 : 8 + y, :]
                near = near + (now[t, 7 : 7 + y, :] + now[t, 9 : 9 + y, :])
                side = jnp.where(not_low, pltpu.roll(core, 1, axis=1), 0.0)
                side = side + jnp.where(not_high, pltpu.roll(core, w - 1, axis=1), 0.0)
                left = (resid[t] - DIAG * core) + (near + side)
                return left, keep * core + gain * left

            def outer(k, c, row=row, then=then):
                for t in (EDGE - 1 - k, EDGE + h + k):
                    left, fresh = row(t)
                    resid[t] = left
                    then[t, 8 : 8 + y, :] = fresh * mask[t]
                return c

            def inner(k, c, row=row, then=then, last=core_only):
                for g in range(group):
                    t = EDGE + k * group + g
                    left, fresh = row(t)
                    if not last:
                        resid[t] = left
                        then[t, 8 : 8 + y, :] = fresh
                    total[t - EDGE] += fresh
                return c

            if turn + 1 < EDGE:
                lax.fori_loop(0, EDGE - turn - 1, outer, 0)
            lax.fori_loop(0, h // group, inner, 0)

        pot = total[...]
        acc[plan[0, p]] += pot * partner[0]
        back = place(pot * own[0], room, -plan[5, p], -plan[6, p])
        if not remote:
            acc[plan[1, p]] += back
        else:
            for value in (1, 2):

                @pl.when(plan[4, p] == value)
                def _(ref=accs[value], value=value):
                    ref[plan[1 + value, p]] += back


def solve(remote, plan, ends, density, partner, packed, below, above, m):
    slots = plan.shape[1]
    n, h, y, w = packed.shape
    blk = (1, h, y, w)
    eblk = (1, EDGE, y // 2, w)
    rows = h + 2 * EDGE

    def spot(i, plan):
        far = plan[8, 0]
        if remote:
            return jnp.minimum(i, jnp.maximum(far - 1, 0))
        return jnp.clip(i, jnp.minimum(far, plan[8, 1] - 1), plan[8, 1] - 1)

    here = lambda i, plan, ends: (spot(i, plan), 0, 0, 0)
    fixed = lambda i, plan, ends: (0, 0, 0, 0)
    shapes = [(n, h, y, w)] + [(m, h, y, w)] * (2 if remote else 0)
    return pl.pallas_call(
        functools.partial(solve_kernel, remote),
        grid_spec=pltpu.PrefetchScalarGridSpec(
            num_scalar_prefetch=2,
            grid=(slots,),
            in_specs=[
                pl.BlockSpec(blk, here),
                pl.BlockSpec(blk, here),
                pl.BlockSpec(blk, lambda i, plan, ends: (plan[0, spot(i, plan)], 0, 0, 0)),
                pl.BlockSpec(eblk, here),
                pl.BlockSpec(eblk, here),
            ],
            out_specs=[pl.BlockSpec(s, fixed) for s in shapes],
            scratch_shapes=[
                pltpu.VMEM((rows, y, w), F32),
                pltpu.VMEM((rows, y + 16, w), F32),
                pltpu.VMEM((rows, y + 16, w), F32),
                pltpu.VMEM((h, y, w), F32),
                pltpu.VMEM((rows, 1, w), F32),
                pltpu.VMEM((h, y + 2 * PAD, w), F32),
            ],
        ),
        out_shape=[jax.ShapeDtypeStruct(s, F32) for s in shapes],
        compiler_params=pltpu.CompilerParams(vmem_limit_bytes=56 * 1024 * 1024),
        cost_estimate=pl.CostEstimate(
            flops=slots * rows * y * w * 100, bytes_accessed=24 << 20, transcendentals=0
        ),
        name="solve_far" if remote else "solve_near",
    )(plan, ends, density, partner, packed, below, above)


def combine_kernel(back, acc, acc_near, from_next, from_prior, out):
    k = pl.program_id(0)
    h = acc.shape[1]
    z = acc.shape[3] // 2
    value = acc[0] + acc_near[0]
    value = value + jnp.where(back[1, k] > 0, from_next[0], 0.0)
    value = value + jnp.where(back[3, k] > 0, from_prior[0], 0.0)
    out[0, :h] = value[:, :, :z]
    out[0, h:] = value[:, :, z:]


def combine(back, acc, acc_near, from_next, from_prior):
    n, h, y, w = acc.shape
    blk = (1, h, y, w)
    return pl.pallas_call(
        combine_kernel,
        grid_spec=pltpu.PrefetchScalarGridSpec(
            num_scalar_prefetch=1,
            grid=(n,),
            in_specs=[
                pl.BlockSpec(blk, lambda i, back: (i, 0, 0, 0)),
                pl.BlockSpec(blk, lambda i, back: (i, 0, 0, 0)),
                pl.BlockSpec(blk, lambda i, back: (back[0, i], 0, 0, 0)),
                pl.BlockSpec(blk, lambda i, back: (back[2, i], 0, 0, 0)),
            ],
            out_specs=pl.BlockSpec((1, 2 * h, y, w // 2), lambda i, back: (i, 0, 0, 0)),
        ),
        out_shape=jax.ShapeDtypeStruct((n, 2 * h, y, w // 2), F32),
        name="combine",
    )(back, acc, acc_near, from_next, from_prior)


def cycle(field, by):
    size = lax.axis_size(CYCLE)
    return lax.ppermute(field, CYCLE, [(i, (i + by) % size) for i in range(size)])


TASK = 8
LISTS = 256
INFO = 320
PLAN = 384
AHEAD = 4
UNROLL = 4
DEPTH = 5
STRIP = 8


def factors():
    ratio = THETA / DELTA
    tall = math.acosh(ratio)
    points = [cmath.cosh(complex(tall, k * math.pi / 4)) for k in range(8)]
    marks = [DIAG * (1.0 - (THETA - DELTA * x)) for x in points]
    quads = [(-2.0 * marks[k].real, abs(marks[k]) ** 2) for k in (1, 2, 3)]
    line = -marks[4].real
    coef, resid, value, step = 1.0 / ratio, 1.0, 0.0, 1.0 / (DIAG * THETA)
    value += step
    for keep, gain in coefs():
        resid -= DIAG * step
        step = keep * step + gain * resid
        value += step
    product = line
    for _, c in quads:
        product *= c
    return quads, line, value / product


def front_kernel(
    orbs, pairs, live, offsets, basis, basis_back, levels, fields, every, statics,
    room, one, two, own2, par2, prod, wheel, moves,
    stage, own, rims, far, edge, table, first, tasks, parts,
    in_sem, out_sem, rim_sem, tab_send, tab_recv, edge_send, edge_recv, far_send, far_recv,
    part_sem,
):
    n, h = orbs.shape[0], orbs.shape[1]
    half = h // 2
    halo = edge.shape[1]
    size, width = lax.axis_size(CYCLE), lax.axis_size("orb")
    me = lax.axis_index("grp") * width + lax.axis_index("orb")
    slab = lax.axis_index("slab")

    def peer(s):
        to = lax.rem(me + s, size)
        return {"grp": lax.div(to, width), "orb": lax.rem(to, width)}

    def load(k):
        return pltpu.make_async_copy(orbs.at[k], stage.at[k], in_sem.at[k])

    def order(q):
        return jnp.where(q == 0, 0, jnp.where(q == 1, n - 1, q - 1))

    def begin(q, c):
        load(order(q)).start()
        return c

    lax.fori_loop(0, n, begin, 0)

    barrier = pltpu.get_barrier_semaphore()

    def greet(s, c):
        pl.semaphore_signal(
            barrier, inc=1, device_id=peer(s), device_id_type=pl.DeviceIdType.MESH
        )
        return c

    lax.fori_loop(1, size, greet, 0)
    pl.semaphore_signal(
        barrier, inc=1, device_id={"slab": 1 - slab}, device_id_type=pl.DeviceIdType.MESH
    )
    table[...] = jnp.zeros(table.shape, jnp.int32)
    table[0:2, 0:n] = pairs[...]
    table[2:3, 0:n] = live[...]
    run = solver(
        tasks, room, one, two, own2, par2, prod, wheel, moves, basis, basis_back, levels, h
    )
    before, after = lax.rem(me + size - 1, size), lax.rem(me + 1, size)
    last, head, above_head, under_last = me * n + n - 1, me * n, after * n, before * n + n - 1
    for t, (i, j, ri, rj) in enumerate((
        (last, above_head, 0, 3), (above_head, last, 3, 0),
        (head, under_last, 1, 2), (under_last, head, 2, 1),
    )):
        tasks[t * TASK], tasks[t * TASK + 1] = jnp.int32(ri), jnp.int32(rj)
        tasks[t * TASK + 2] = offsets[0, j] - offsets[0, i]
        tasks[t * TASK + 3] = offsets[1, j] - offsets[1, i]
    wipe_room(room, own.shape[2])
    pl.semaphore_wait(barrier, size)

    def share_copy(s, slot):
        return pltpu.make_async_remote_copy(
            src_ref=table, dst_ref=every.at[slot],
            send_sem=tab_send.at[s], recv_sem=tab_recv.at[s],
            device_id=peer(s), device_id_type=pl.DeviceIdType.MESH,
        )

    def share_send(s, c):
        share_copy(s, me).start()
        return c

    lax.fori_loop(1, size, share_send, 0)
    every[me] = table[...]

    def edge_copy(e, f, dst):
        return pltpu.make_async_remote_copy(
            src_ref=edge.at[f], dst_ref=dst,
            send_sem=edge_send.at[e], recv_sem=edge_recv.at[e],
            device_id={"slab": 1 - slab}, device_id_type=pl.DeviceIdType.MESH,
        )

    def own_edge(k, e):
        return edge_copy(e, k, rims.at[k])

    def far_copy(src, f, s):
        return pltpu.make_async_remote_copy(
            src_ref=src, dst_ref=far.at[f, pl.ds(0, half)],
            send_sem=far_send.at[f], recv_sem=far_recv.at[f],
            device_id=peer(s), device_id_type=pl.DeviceIdType.MESH,
        )

    def spot(t):
        return jnp.where(slab == 0, t, h - 1 - t)

    def pack(k):
        def row(r, c):
            own[k, r] = jnp.concatenate(
                [stage[k, spot(r)], stage[k, spot(r + half)]], axis=-1
            )
            return c

        lax.fori_loop(0, half, row, 0)

    def make_edge(k):
        for m in range(halo):
            edge[k, m] = jnp.concatenate(
                [stage[k, spot(h - 1 - m)], stage[k, spot(h - 1 - halo - m)]], axis=-1
            )

    def save(k):
        return pltpu.make_async_copy(
            own.at[k], fields.at[k, pl.ds(0, half)], out_sem.at[k]
        )

    def save_far(f):
        return pltpu.make_async_copy(
            far.at[f, pl.ds(0, half)], fields.at[n + f, pl.ds(0, half)], out_sem.at[n + f]
        )

    def rim(f, src):
        return pltpu.make_async_copy(src, fields.at[f, pl.ds(half, halo)], rim_sem.at[f])


    up, down = far_copy(own.at[n - 1], 0, 1), far_copy(own.at[0], 1, size - 1)
    for k, send, e in ((0, down, 0), (n - 1, up, 1)):
        load(k).wait()
        pack(k)
        send.start()
        make_edge(k)
        own_edge(k, e).start()
        save(k).start()

    def rest(k, c):
        load(k).wait()
        pack(k)
        save(k).start()
        make_edge(k)
        pl.when(k < n // 2 - 1)(lambda: own_edge(k, 3 + k).start())
        return c

    lax.fori_loop(1, n - 1, rest, 0)

    def share_done(s, c):
        share_copy(s, lax.rem(me + size - s, size)).wait()
        return c

    lax.fori_loop(1, size, share_done, 0)

    bits = n.bit_length() - 1
    here, under, above = every[me], every[lax.rem(me + size - 1, size)], every[lax.rem(me + 1, size)]
    slot = lanes((1, here.shape[1])) < n

    def lowest(tile, source, target, row, free):
        to = lax.shift_right_logical(tile[1:2], bits)
        value = tile[row : row + 1] & (n - 1)
        fit = slot & (tile[2:3] > 0) & (to == target) & (value != free)
        return jnp.min(jnp.where(fit, value, n))

    up_first = jnp.minimum(
        lowest(here, me, after, 0, n - 1), lowest(above, after, me, 1, n - 1)
    )
    down_first = jnp.minimum(lowest(here, me, before, 0, 0), lowest(under, before, me, 1, 0))
    more = []
    for f, (k, s) in enumerate(((up_first, 1), (down_first, size - 1))):
        k = jnp.where(k == n, 0, k)

        def row(r, c, f=f, k=k):
            first[f, r] = own[k, r]
            return c

        lax.fori_loop(0, half, row, 0)
        more.append(far_copy(first.at[f], 2 + f, s))
        more[f].start()

    w = own.shape[-1]
    y = own.shape[2]
    low = lanes((1, w)) < w // 2
    for f, copy in ((1, down), (0, up)):
        copy.wait()
        for m in range(halo):
            a, b = far[f, half - 1 - m], far[f, half - 1 - halo - m]
            edge[n + f, m] = jnp.where(low, pltpu.roll(a, w // 2, axis=1), b)
        edge_copy(2 + f, n + f, far.at[f, pl.ds(half, halo)]).start()
        save_far(f).start()

    def later(k, c):
        own_edge(k, 3 + k).start()
        return c

    lax.fori_loop(n // 2 - 1, n - 1, later, 0)

    def fill(slot, src, dst, count):
        def row(r, c):
            room[slot + 1, dst + r, 0:y, :] = src[r]
            return c

        lax.fori_loop(0, count, row, 0)

    def out_part(g):
        return pltpu.make_async_copy(parts.at[g, 0], statics.at[g], part_sem.at[g])

    for g, (k, e, f, here_at, far_at) in enumerate(((n - 1, 1, 1, 0, 3), (0, 0, 0, 1, 2))):
        own_edge(k, e).wait()
        rim(k, rims.at[k]).start()
        fill(here_at, own.at[k], 0, half)
        fill(here_at, rims.at[k], half, halo)
        edge_copy(2 + f, n + f, far.at[f, pl.ds(half, halo)]).wait()
        rim(n + f, far.at[f, pl.ds(half, halo)]).start()
        fill(far_at, far.at[f], 0, half + halo)

    def solve(g, c):
        run(g, parts.at[g, 0], parts.at[g, 1])

        def merge(t):
            parts[g, 0, t] = jnp.where(low, parts[g, 0, t], parts[g, 1, t])

        repeat(h, 4, merge)
        out_part(g).start()
        return c

    lax.fori_loop(0, 2, solve, 0)

    def own_done(k, c):
        own_edge(k, 3 + k).wait()
        rim(k, rims.at[k]).start()
        return c

    lax.fori_loop(1, n - 1, own_done, 0)
    for f in range(2):
        more[f].wait()
        save_far(2 + f).start()

    def out_done(k, c):
        save(k).wait()
        rim(k, rims.at[k]).wait()
        return c

    lax.fori_loop(0, n, out_done, 0)
    for f in (1, 0):
        rim(n + f, far.at[f, pl.ds(half, halo)]).wait()
    for f in range(4):
        save_far(f).wait()
    for g in range(2):
        out_part(g).wait()


def front(orbitals, pairs, live, offsets, waves):
    n, h, y, z = orbitals.shape
    half, halo, w = h // 2, (EDGE + 1) // 2, 2 * z
    rows = half + halo
    size = lax.axis_size(CYCLE)
    vmem = pl.BlockSpec(memory_space=pltpu.VMEM)
    smem = pl.BlockSpec(memory_space=pltpu.SMEM)
    hbm = pl.BlockSpec(memory_space=pl.ANY)
    dma = pltpu.SemaphoreType.DMA
    return pl.pallas_call(
        front_kernel,
        in_specs=[hbm, vmem, vmem, smem, vmem, vmem, vmem],
        out_specs=[hbm, vmem, hbm],
        out_shape=[
            jax.ShapeDtypeStruct((n + 4, rows, y, w), F32),
            jax.ShapeDtypeStruct((size, 8, 128), jnp.int32),
            jax.ShapeDtypeStruct((2, h, y, w), F32),
        ],
        scratch_shapes=solver_scratch(4, h, y, w, rows)
        + [
            pltpu.VMEM((n, h, y, z), F32),
            pltpu.VMEM((n, half, y, w), F32),
            pltpu.VMEM((n, halo, y, w), F32),
            pltpu.VMEM((4, rows, y, w), F32),
            pltpu.VMEM((n + 2, halo, y, w), F32),
            pltpu.VMEM((8, 128), jnp.int32),
            pltpu.VMEM((2, half, y, w), F32),
            pltpu.SMEM((4 * TASK,), jnp.int32),
            pltpu.VMEM((2, 2, h, y, w), F32),
            dma((n,)), dma((n + 4,)), dma((n + 2,)), dma((size,)), dma((size,)),
            dma((n + 2,)), dma((n + 2,)), dma((4,)), dma((4,)), dma((2,)),
        ],
        compiler_params=pltpu.CompilerParams(
            collective_id=1, has_side_effects=True, vmem_limit_bytes=58 * 1024 * 1024
        ),
        name="front",
    )(orbitals, pairs.T, live[None], offsets.T, *waves)


def plan_kernel(n, combos, every, offsets, plan, which, ups, downs, nups, ndowns, alive):
    size = every.shape[0]
    width = lax.axis_size("orb")
    me = lax.axis_index("grp") * width + lax.axis_index("orb")
    before, after = lax.rem(me + size - 1, size), lax.rem(me + 1, size)
    block = lambda x: lax.shift_right_logical(x, n.bit_length() - 1)

    def clear(e, c):
        ups[e] = 0
        downs[e] = 0
        nups[e] = 0
        ndowns[e] = 0
        alive[e] = sum(every[e, 2, r] for r in range(n))
        return c

    lax.fori_loop(0, size, clear, 0)

    def read(blk, r):
        i, j = every[blk, 0, r], every[blk, 1, r]
        bj = block(j)
        is_up = bj == jnp.where(blk + 1 == size, 0, blk + 1)
        li, lj = i & (n - 1), j & (n - 1)
        u, v = jnp.where(is_up, li, lj), jnp.where(is_up, lj, li)
        return i, j, bj, u, v, jnp.where(is_up, blk, bj)

    def mark(blk, c):
        def row(r, c):
            i, j, bj, u, v, edge = read(blk, r)

            @pl.when(bj != blk)
            def _():
                for bits, counts, x, free in ((ups, nups, u, n - 1), (downs, ndowns, v, 0)):
                    bit = jnp.where(x == free, 0, lax.shift_left(1, x))
                    had = bits[edge]
                    bits[edge] = had | bit
                    counts[edge] = counts[edge] + jnp.where((had | bit) != had, 1, 0)

            return c

        return lax.fori_loop(2, alive[blk], row, c)

    lax.fori_loop(0, size, mark, 0)

    def widest(e, most):
        o = lax.rem(e, width)
        mine = jnp.where(o % 2 == 0, 2, jnp.where(o == width - 1, 1, 0))
        here = jnp.maximum(nups[e], ndowns[e])
        return tuple(jnp.maximum(m, jnp.where(mine == c, here, 0)) for c, m in enumerate(most))

    most = lax.fori_loop(0, size, widest, (jnp.int32(0),) * 3)
    pick = jnp.int32(len(combos) - 1)
    for c in range(len(combos) - 2, -1, -1):
        fit = functools.reduce(lambda p, q: p & q, [m <= k for m, k in zip(most, combos[c])])
        pick = jnp.where(fit, c, pick)
    which[0] = pick

    def listing(bits, base):
        def step(q, s):
            plan[base + s] = q
            return s + (lax.shift_right_logical(bits, q) & 1)

        for q in range(n):
            plan[base + q] = 0
        return lax.fori_loop(0, n, step, jnp.int32(0))

    listing(ups[me], LISTS)
    listing(downs[before], LISTS + 2 * n)
    plan[INFO + 3] = nups[before]
    plan[INFO + 4] = ndowns[me]

    def rank(bits, x):
        return sum(
            jnp.where(q < x, lax.shift_right_logical(bits, q) & 1, 0) for q in range(n)
        )

    def place_of(x):
        blk, loc = block(x), x & (n - 1)
        low_rank, high_rank = rank(ups[before], loc), rank(downs[me], loc)
        low_at = jnp.where(low_rank == 0, n + 2, n + 3 + low_rank)
        high_at = jnp.where(high_rank == 0, n + 3, 2 * n + 1 + high_rank)
        from_before = jnp.where(loc == n - 1, n, low_at)
        from_after = jnp.where(loc == 0, n + 1, high_at)
        return jnp.where(blk == me, loc, jnp.where(blk == before, from_before, from_after))

    def sweep(level, blk, start, skip, count):
        def step(r, s):
            i, j, bj, u, v, edge = read(blk, r)
            above = edge == me
            free = (bj == blk) | jnp.where(above, v == 0, u == n - 1)
            late = jnp.where(above, rank(downs[me], v), rank(ups[before], u))
            mine = jnp.where(free, 0, jnp.where(late == 0, 1, 2))
            want = ((blk == me) | (bj == me)) & (mine == level) & (r != skip)

            @pl.when(want)
            def _():
                write(s * TASK, i, j)

            return s + jnp.where(want, 1, 0)

        return lax.fori_loop(start, alive[blk], step, count)

    def write(at, i, j):
        plan[at] = place_of(i)
        plan[at + 1] = place_of(j)
        plan[at + 2] = offsets[0, j] - offsets[0, i]
        plan[at + 3] = offsets[1, j] - offsets[1, i]
        plan[at + 4] = jnp.where(block(i) == me, i & (n - 1), n)
        plan[at + 5] = jnp.where(block(j) == me, j & (n - 1), n)

    def blank(s):
        for c, value in enumerate((0, 0, 0, 0, n, n)):
            plan[s * TASK + c] = value

    for s in range(2 * AHEAD):
        blank(s)
    count = jnp.int32(0)
    for level in range(3):
        count = sweep(level, me, 2, n, count)
        count = sweep(level, before, 0, 1, count)
        count = sweep(level, after, 1, n, count)
        if level < 2:
            count = jnp.maximum(count, (2, 2 * AHEAD)[level])
    plan[INFO + 6] = count
    blank(count)


def make_plan(every, offsets, n, combos):
    size = every.shape[0]
    smem = pl.BlockSpec(memory_space=pltpu.SMEM)
    return pl.pallas_call(
        functools.partial(plan_kernel, n, combos),
        in_specs=[smem, smem],
        out_specs=[smem, smem],
        out_shape=[
            jax.ShapeDtypeStruct((PLAN,), jnp.int32),
            jax.ShapeDtypeStruct((1,), jnp.int32),
        ],
        scratch_shapes=[pltpu.SMEM((size,), jnp.int32)] * 5,
        name="plan",
    )(every, offsets.T)


def wipe_room(room, y):
    def step(f, c):
        room[f, :, y:, :] = jnp.zeros((room.shape[1], PAD, room.shape[3]), F32)
        return c

    lax.fori_loop(0, room.shape[0], step, 0)


def repeat(count, unroll, do):
    def step(g, c):
        for q in range(unroll):
            do(g * unroll + q)
        return c

    lax.fori_loop(0, count // unroll, step, 0)


def solver(plan, room, one, two, own2, par2, prod, wheel, moves, basis, basis_back, levels, h):
    rows, tall, w = room.shape[1:]
    y, z = tall - PAD, w // 2
    half = h // 2
    halo = rows - half
    each = rows * tall
    quads, line, _ = factors()

    prod[0] = jnp.zeros((tall, w), F32)
    prod[:, y:, :] = jnp.zeros((h + 1, PAD, w), F32)
    for ref in (one, two):
        planes = ref.shape[0]
        ref[0] = jnp.zeros(ref.shape[1:], F32)
        ref[:, 0:8, :] = jnp.zeros((planes, 8, w), F32)
        ref[:, 8 + y :, :] = jnp.zeros((planes, 8, w), F32)
    flat_room = room.reshape(room.shape[0] * each, w)
    flat_prod = prod.reshape((h + 1) * tall, w)

    k_at = lax.broadcasted_iota(jnp.int32, (2 * w, 2 * w), 0)
    c_at = lax.broadcasted_iota(jnp.int32, (2 * w, 2 * w), 1)
    task_k, half_k, task_c, half_c = k_at // w, k_at % w // z, c_at % w // z, c_at // w
    gap = k_at % z - c_at % z
    wheel[...] = jnp.where((task_k == task_c) & (half_k == half_c), gap, 4 * z)

    lane = lanes((y, w))
    low = lane < z
    pos = lane % z
    mu = jnp.broadcast_to(levels[...], (STRIP, w))

    def sweep(src, count, emit):
        def step(g, c):
            for r in range(0, y, STRIP):
                at = pl.ds(8 + r, STRIP)
                col = [src[g * UNROLL + q, at, :] for q in range(UNROLL + 2)]
                for q in range(UNROLL):
                    t = g * UNROLL + q
                    sides = src[t + 1, pl.ds(7 + r, STRIP), :] + src[t + 1, pl.ds(9 + r, STRIP), :]
                    emit(t, r, col[q + 1], (col[q] + col[q + 2]) + sides)
            return c

        lax.fori_loop(0, (count + UNROLL - 1) // UNROLL, step, 0)

    def split(values):
        coarse = values.astype(jnp.bfloat16)
        return coarse, (values - coarse.astype(F32)).astype(jnp.bfloat16)

    def turn_z(values, wave):
        both = jnp.dot(
            jnp.concatenate(split(values), axis=1), wave[...], preferred_element_type=F32
        )
        return both[:, :w] + both[:, w:]

    def planes(r):
        return jnp.where(r < half, r, r + half), jnp.where(r < half, r + half, r + half + halo)

    def run(g, gains, backs):
        p, q = g * 2 * TASK, (g * 2 + 1) * TASK
        rp, rq = (plan[p] + 1) * each, (plan[q] + 1) * each
        ap, aq, bp, bq = plan[p + 2], plan[q + 2], plan[p + 3], plan[q + 3]
        sp, sq = (plan[p + 1] + 1) * each - ap, (plan[q + 1] + 1) * each - aq
        col = lanes((1, 2 * w)) % w < z
        moves[...] = jnp.where(wheel[...] == jnp.where(col, -bp, -bq), 1.0, 0.0).astype(jnp.bfloat16)

        def waves_of(g):
            raw = []
            for q in range(DEPTH):
                for t in planes(g * DEPTH + q):
                    raw.append(two[t + 1, 8 : 8 + y, :])
            return turn_z(jnp.concatenate(raw, axis=0), basis)

        def keep_waves(g, waves):
            for q in range(DEPTH):
                for side, t in enumerate(planes(g * DEPTH + q)):
                    at = (2 * q + side) * y
                    one[t + 1, 8 : 8 + y, :] = waves[at : at + y]

        def partners(g):
            par = [
                jnp.concatenate(
                    [flat_room[pl.ds(sp + r * tall, y), :], flat_room[pl.ds(sq + r * tall, y), :]],
                    axis=1,
                )
                for r in [g * DEPTH + q for q in range(DEPTH)]
            ]
            par = jnp.concatenate(split(jnp.concatenate(par, axis=0)), axis=0)
            par = jnp.dot(par, moves[...], preferred_element_type=F32)
            return par[: DEPTH * y] + par[DEPTH * y :]

        def keep_partners(g, par):
            for q in range(DEPTH):
                r = g * DEPTH + q
                own_p = flat_room[pl.ds(rp + r * tall, y), :]
                own_q = flat_room[pl.ds(rq + r * tall, y), :]
                own_a = jnp.where(low, own_p, pltpu.roll(own_q, z, axis=1))
                own_b = jnp.where(low, pltpu.roll(own_p, z, axis=1), own_q)
                for t, own, half_par in zip(
                    planes(r), (own_a, own_b), jnp.split(par[q * y : (q + 1) * y], 2, axis=1)
                ):
                    two[t + 1, 8 : 8 + y, :] = own * half_par
                    own2[t] = own
                    par2[t] = half_par

        def dense(g, c):
            waves, par = waves_of(g - 1), partners(g)
            keep_waves(g - 1, waves)
            keep_partners(g, par)
            return c

        turns = rows // DEPTH
        keep_partners(0, partners(0))
        lax.fori_loop(1, turns, dense, 0)
        keep_waves(turns - 1, waves_of(turns - 1))

        def quad(k, c):
            b, c2 = jnp.float32(quads[0][0]), jnp.float32(quads[0][1])
            for m in range(1, len(quads)):
                b = jnp.where(k == m, jnp.float32(quads[m][0]), b)
                c2 = jnp.where(k == m, jnp.float32(quads[m][1]), c2)
            mu_b = mu + b

            def first(t, r, cur, near):
                two[t + 1, pl.ds(8 + r, STRIP), :] = near + mu_b * cur

            def second(t, r, cur, near):
                at = pl.ds(8 + r, STRIP)
                one[t + 1, at, :] = (near + mu * cur) + c2 * one[t + 1, at, :]

            count = h + EDGE - 1 - 2 * k
            sweep(one, count, first)
            sweep(two, count - 1, second)
            return c

        lax.fori_loop(0, len(quads), quad, 0)
        mu_line = mu + line

        def finish(g, c):
            values = [[] for _ in range(UNROLL)]
            for r in range(0, y, STRIP):
                at = pl.ds(8 + r, STRIP)
                col = [one[g * UNROLL + q, at, :] for q in range(UNROLL + 2)]
                for q in range(UNROLL):
                    t = g * UNROLL + q
                    sides = one[t + 1, pl.ds(7 + r, STRIP), :] + one[t + 1, pl.ds(9 + r, STRIP), :]
                    values[q].append((col[q] + col[q + 2]) + sides + mu_line * col[q + 1])
            both = turn_z(jnp.concatenate(sum(values, []), axis=0), basis_back)
            for q in range(UNROLL):
                t = g * UNROLL + q
                pot = both[q * y : (q + 1) * y]
                gains[t] = pot * par2[t]
                prod[t + 1, 0:y, :] = pot * own2[t]
            return c

        lax.fori_loop(0, h // UNROLL, finish, 0)

        back = pos + jnp.where(low, bp, bq)
        good = (back >= 0) & (back < z)
        turn_p, turn_q = lax.rem(w - bp, w), lax.rem(w - bq, w)

        def plane(t):
            at = (t + 1) * tall
            moved_p = pltpu.roll(flat_prod[pl.ds(at + ap, y), :], turn_p, axis=1)
            moved_q = pltpu.roll(flat_prod[pl.ds(at + aq, y), :], turn_q, axis=1)
            backs[t] = jnp.where(good, jnp.where(low, moved_p, moved_q), 0.0)

        repeat(h, 4, plane)

    return run


def solver_scratch(fields, h, y, w, rows):
    planes = 2 * rows
    return [
        pltpu.VMEM((fields + 1, rows, y + PAD, w), F32),
        pltpu.VMEM((planes + 6, y + 16, w), F32),
        pltpu.VMEM((planes + 6, y + 16, w), F32),
        pltpu.VMEM((planes, y, w), F32),
        pltpu.VMEM((planes, y, w), F32),
        pltpu.VMEM((h + 1, y + PAD, w), F32),
        pltpu.VMEM((2 * w, 2 * w), jnp.int32),
        pltpu.VMEM((2 * w, 2 * w), jnp.bfloat16),
    ]


def swap_kernel(
    counts, plan, fields, basis, basis_back, levels, prior, nxt, results,
    room, one, two, own2, par2, prod, wheel, moves, sends, got, trim, parts,
    in_sem, send, recv, trim_send, trim_recv, main_sem, rim_sem, part_sem,
):
    n, (rows, y, w) = fields.shape[0] - 4, fields.shape[1:]
    halo = trim.shape[2]
    half = rows - halo
    m = sends.shape[1]
    size, width = lax.axis_size(CYCLE), lax.axis_size("orb")
    o = lax.axis_index("orb")
    me = lax.axis_index("grp") * width + o
    slab = lax.axis_index("slab")
    other = {"slab": 1 - slab}

    def peer(s):
        to = lax.rem(me + s, size)
        return {"grp": lax.div(to, width), "orb": lax.rem(to, width)}

    def limit(q):
        return jnp.where(q % 2 == 0, counts[2], jnp.where(q == width - 1, counts[1], counts[0]))

    above, under = limit(o), limit(lax.rem(o + width - 1, width))
    ways = ((0, above, under, prior), (1, under, above, nxt))

    def load(f):
        return pltpu.make_async_copy(fields.at[f], room.at[f + 1, :, pl.ds(0, y)], in_sem.at[f])

    def copy(way, r):
        return pltpu.make_async_remote_copy(
            src_ref=sends.at[way, r], dst_ref=got.at[way, r, pl.ds(0, half)],
            send_sem=send.at[way, r], recv_sem=recv.at[way, r],
            device_id=peer((1, size - 1)[way]), device_id_type=pl.DeviceIdType.MESH,
        )

    def head(way):
        return pltpu.make_async_copy(
            fields.at[n + 2 + way, pl.ds(0, half)], got.at[way, 0, pl.ds(0, half)],
            recv.at[way, 0],
        )

    def trim_copy(way, r):
        return pltpu.make_async_remote_copy(
            src_ref=trim.at[way, r], dst_ref=got.at[way, r, pl.ds(half, halo)],
            send_sem=trim_send.at[way, r], recv_sem=trim_recv.at[way, r],
            device_id=other, device_id_type=pl.DeviceIdType.MESH,
        )

    def main_out(way, r, dst):
        part = pl.ds(0, half)
        return pltpu.make_async_copy(got.at[way, r, part], dst.at[r, part], main_sem.at[way, r])

    def rim_out(way, r, dst):
        part = pl.ds(half, halo)
        return pltpu.make_async_copy(got.at[way, r, part], dst.at[r, part], rim_sem.at[way, r])

    def part_out(g):
        return pltpu.make_async_copy(parts.at[g % 2], results.at[g], part_sem.at[g % 2])

    def each(start, stop, do):
        def step(k, c):
            do(k)
            return c

        lax.fori_loop(start, stop, step, 0)

    each(0, n + 2, lambda f: load(f).start())
    barrier = pltpu.get_barrier_semaphore()
    for to in (peer(1), peer(size - 1), other):
        pl.semaphore_signal(barrier, inc=1, device_id=to, device_id_type=pl.DeviceIdType.MESH)
    wipe_room(room, y)
    run = solver(
        plan, room, one, two, own2, par2, prod, wheel, moves, basis, basis_back, levels, 2 * half
    )
    pl.semaphore_wait(barrier, 3)
    for way in range(2):
        head(way).start()
    each(0, n + 2, lambda f: load(f).wait())

    def launch(r):
        for way, out, _, _ in ways:
            @pl.when(r < out)
            def _(way=way):
                k = plan[LISTS + way * 2 * n + r]

                def row(t):
                    sends[way, r, t] = room[k + 1, t, 0:y, :]

                each(0, half, row)
                copy(way, r).start()

    each(1, m, launch)
    low = lanes((1, w)) < w // 2

    def land(r):
        for way, _, into, dst in ways:
            @pl.when(r < into)
            def _(way=way, dst=dst):
                pl.when(r == 0)(lambda: head(way).wait())
                pl.when(r > 0)(lambda: copy(way, r).wait_recv())
                main_out(way, r, dst).start()
                for e in range(halo):
                    a, b = got[way, r, half - 1 - e], got[way, r, half - 1 - halo - e]
                    trim[way, r, e] = jnp.where(low, pltpu.roll(a, w // 2, axis=1), b)
                trim_copy(way, r).start()

    def work(g):
        pl.when(g >= 2)(lambda: part_out(g - 2).wait())

        @pl.when(g == 1)
        def _():
            for way, _, _, dst in ways:
                trim_copy(way, 0).wait()
                rim_out(way, 0, dst).start()

                def row(t):
                    room[n + 3 + way, t, 0:y, :] = got[way, 0, t]

                each(0, rows, row)

        run(g, parts.at[g % 2, 0], parts.at[g % 2, 1])
        part_out(g).start()
        pl.when(g + 1 < m)(lambda: land(g + 1))

    land(0)
    each(0, AHEAD, work)
    each(min(AHEAD + 1, m), m, land)
    for g in range(AHEAD - 2, AHEAD):
        part_out(g).wait()

    def settle(r):
        for way, out, into, dst in ways:
            @pl.when(r < into)
            def _(way=way, dst=dst):
                trim_copy(way, r).wait()
                rim_out(way, r, dst).start()

            @pl.when(r < out)
            def _(way=way):
                copy(way, r).wait_send()

    each(1, m, settle)

    def close(r):
        for way, _, into, dst in ways:
            @pl.when(r < into)
            def _(way=way, dst=dst):
                main_out(way, r, dst).wait()
                rim_out(way, r, dst).wait()

    each(0, m, close)


def swap(counts, plan, fields, waves, cid):
    n, (rows, y, w) = fields.shape[0] - 4, fields.shape[1:]
    halo = (EDGE + 1) // 2
    half, m = rows - halo, max(counts)
    hbm = pl.BlockSpec(memory_space=pl.ANY)
    smem = pl.BlockSpec(memory_space=pltpu.SMEM)
    vmem = pl.BlockSpec(memory_space=pltpu.VMEM)
    dma = pltpu.SemaphoreType.DMA
    out = jax.ShapeDtypeStruct((n - 1, rows, y, w), F32)
    return pl.pallas_call(
        functools.partial(swap_kernel, counts),
        in_specs=[smem, hbm, vmem, vmem, vmem],
        out_specs=[hbm, hbm, hbm],
        out_shape=[
            out,
            out,
            jax.ShapeDtypeStruct((AHEAD, 2, 2 * half, y, w), F32),
        ],
        scratch_shapes=solver_scratch(n + 4, 2 * half, y, w, rows)
        + [
            pltpu.VMEM((2, m, half, y, w), F32),
            pltpu.VMEM((2, m, rows, y, w), F32),
            pltpu.VMEM((2, m, halo, y, w), F32),
            pltpu.VMEM((2, 2, 2 * half, y, w), F32),
            dma((n + 2,)), dma((2, m)), dma((2, m)), dma((2, m)), dma((2, m)), dma((2, m)),
            dma((2, m)), dma((2,)),
        ],
        compiler_params=pltpu.CompilerParams(
            collective_id=cid, has_side_effects=True, vmem_limit_bytes=58 * 1024 * 1024
        ),
        name="swap%d%d%d" % counts,
    )(plan, fields, *waves)


def pairs_kernel(
    plan, fields, prior, nxt, statics, results, basis, basis_back, levels, out,
    room, one, two, own2, par2, prod, wheel, moves, acc, stage, parts, sem, acc_sem, out_sem, part_sem,
):
    n, h, y, z = out.shape
    w = 2 * z
    most = prior.shape[0]
    slab = lax.axis_index("slab")

    def part(g):
        return pltpu.make_async_copy(results.at[g], parts.at[g % 2], part_sem.at[g % 2])

    tasks = plan[INFO + 6]

    def field(src, s, f):
        return pltpu.make_async_copy(src.at[s], room.at[f + 1, :, pl.ds(0, y)], sem.at[f])

    def each_field(do):
        @pl.when(tasks > 2 * AHEAD)
        def _():
            for f in range(n + 2):
                do(field(fields, f, f))
            for way, (src, count) in enumerate(((prior, plan[INFO + 3]), (nxt, plan[INFO + 4]))):
                for s in range(most):
                    f = n + 2 + way if s == 0 else n + 3 + way * (n - 2) + s
                    pl.when(s < count)(lambda src=src, s=s, f=f: do(field(src, s, f)))

    def static(g, k):
        return pltpu.make_async_copy(statics.at[g], acc.at[k], acc_sem.at[g])

    part(0).start()
    part(1).start()
    static(0, n - 1).start()
    static(1, 0).start()
    each_field(lambda c: c.start())
    acc[1 : n - 1] = jnp.zeros((n - 2,) + acc.shape[1:], F32)
    wipe_room(room, y)
    run = solver(plan, room, one, two, own2, par2, prod, wheel, moves, basis, basis_back, levels, h)
    low = lanes((y, w)) < w // 2

    def collect(g, gains, backs):
        p, q = g * 2 * TASK, (g * 2 + 1) * TASK
        for k, src, side in (
            (plan[p + 4], gains, low),
            (plan[q + 4], gains, jnp.logical_not(low)),
            (plan[p + 5], backs, low),
            (plan[q + 5], backs, jnp.logical_not(low)),
        ):
            @pl.when(k < n)
            def _(k=k, src=src, side=side):
                def plane(t):
                    acc[k, t] += jnp.where(side, src[t], 0.0)

                repeat(h, 4, plane)

    def gather(g, c):
        part(g).wait()
        collect(g, parts.at[g % 2, 0], parts.at[g % 2, 1])
        pl.when(g + 2 < AHEAD)(lambda: part(g + 2).start())
        return c

    static(0, n - 1).wait()
    static(1, 0).wait()
    lax.fori_loop(0, AHEAD, gather, 0)
    each_field(lambda c: c.wait())

    def group(g, c):
        run(g, parts.at[0, 0], parts.at[0, 1])
        collect(g, parts.at[0, 0], parts.at[0, 1])
        return c

    lax.fori_loop(AHEAD, lax.div(tasks + 1, 2), group, 0)

    def leave(k, slot):
        return pltpu.make_async_copy(stage.at[slot], out.at[k], out_sem.at[slot])

    def write(k, c):
        slot = lax.rem(k, 2)
        pl.when(k >= 2)(lambda: leave(k - 2, slot).wait())

        def plane(t):
            value = acc[k, t]
            value = value + pltpu.roll(value, z, axis=1)
            stage[slot, jnp.where(slab == 0, t, h - 1 - t)] = value[:, :z]

        repeat(h, 4, plane)
        leave(k, slot).start()
        return c

    lax.fori_loop(0, n, write, 0)
    for k in (n - 2, n - 1):
        leave(k, k % 2).wait()


def sines(z):
    k = np.arange(1, z + 1)
    wave = np.sqrt(2.0 / (z + 1)) * np.sin(np.pi * np.outer(k, k) / (z + 1))
    wave = np.kron(np.eye(2), wave).astype(np.float32)
    levels = np.tile(2.0 * np.cos(np.pi * k / (z + 1)), 2).astype(np.float32)[None]

    def parts(values):
        coarse = jnp.asarray(values).astype(jnp.bfloat16)
        fine = (jnp.asarray(values) - coarse.astype(F32)).astype(jnp.bfloat16)
        top = jnp.concatenate([coarse, fine], axis=1)
        bottom = jnp.concatenate([coarse, jnp.zeros_like(fine)], axis=1)
        return jnp.concatenate([top, bottom], axis=0)

    return parts(wave), parts(wave * np.float32(factors()[2])), jnp.asarray(levels)


def solve_pairs(plan, fields, prior, nxt, statics, results, waves, shape):
    n, h, y, z = shape
    w, rows = 2 * z, fields.shape[1]
    most = prior.shape[0]
    hbm = pl.BlockSpec(memory_space=pl.ANY)
    vmem = pl.BlockSpec(memory_space=pltpu.VMEM)
    dma = pltpu.SemaphoreType.DMA
    total = n + 2 + 2 * most
    return pl.pallas_call(
        pairs_kernel,
        grid_spec=pltpu.PrefetchScalarGridSpec(
            num_scalar_prefetch=1,
            grid=(1,),
            in_specs=[hbm] * 5 + [vmem] * 3,
            out_specs=hbm,
            scratch_shapes=solver_scratch(total, h, y, w, rows)
            + [
                pltpu.VMEM((n, h, y, w), F32),
                pltpu.VMEM((2, h, y, z), F32),
                pltpu.VMEM((2, 2, h, y, w), F32),
                dma((total,)), dma((2,)), dma((2,)), dma((2,)),
            ],
        ),
        out_shape=jax.ShapeDtypeStruct(shape, F32),
        compiler_params=pltpu.CompilerParams(vmem_limit_bytes=58 * 1024 * 1024),
        name="pairs",
    )(plan, fields, prior, nxt, statics, results, *waves)


def fast_body(orbitals, offsets, pairs, live):
    n = orbitals.shape[0]
    combos = [(2, 2, 2), (3, 3, 3), (2, 4, 3), (4, 2, 3), (3, 4, 4), (4, 3, 4), (4, 4, 4)]
    combos.append((n - 1,) * 3)
    waves = sines(orbitals.shape[-1])
    fields, every, statics = front(orbitals, pairs, live, offsets, waves)
    plan, which = make_plan(every, offsets, n, combos)

    def branch(counts, cid):
        return lambda _: swap(counts, plan, fields, waves, cid)

    prior, nxt, results = lax.switch(
        which[0], [branch(c, 2 + i) for i, c in enumerate(combos)], 0
    )
    return solve_pairs(plan, fields, prior, nxt, statics, results, waves, orbitals.shape)


def body(orbitals, offsets, pairs, live):
    n = orbitals.shape[0]
    slots = pairs.shape[0]
    total = offsets.shape[0]
    blocks = total // n
    slabs = lax.axis_size("slab")
    me = lax.axis_index(CYCLE)
    packed = pack(orbitals)

    mine = jnp.concatenate([pairs, live[:, None]], axis=1)
    every = share(jnp.pad(mine, ((0, 0), (0, 128 - mine.shape[1]))))
    ids = jnp.arange(blocks, dtype=jnp.int32)
    second = every[:, :, 1]
    alive = every[:, :, 2] > 0
    orb = jnp.arange(n, dtype=jnp.int32)
    sides = jnp.stack([(ids - 1) % blocks, (ids + 1) % blocks])
    hit = alive[None] & (second[None] // n == sides[:, :, None])
    need = jnp.any(
        hit[..., None] & (second[None, :, :, None] % n == orb), axis=2
    )
    count = jnp.sum(need.astype(jnp.int32), axis=2)
    most = jnp.max(count)

    after, before = (me + 1) % blocks, (me - 1) % blocks
    flags = jnp.stack(
        [need[0, me], need[1, me], need[0, after], need[1, before]]
    ).astype(jnp.int32)
    spot = jnp.sum(
        flags[:, None, :] * (orb[None, :] < orb[:, None]).astype(jnp.int32)[None], axis=2
    )
    lists = jnp.sum(
        (flags[:, None, :] * (spot[:, None, :] == orb[None, :, None])) * orb, axis=2
    )
    back = jnp.stack(
        [spot[2] * flags[2], flags[2], spot[3] * flags[3], flags[3]]
    )

    i, j, on = pairs[:, 0], pairs[:, 1], live > 0
    owner, local = j // n, j % n
    pick_j = (local[:, None] == orb[None, :]).astype(jnp.int32)
    from_prior = (owner == before) & on
    from_next = (owner == after) & on
    kind = jnp.where(from_prior, 1, jnp.where(from_next, 2, 0))
    where_prior = jnp.sum(pick_j * spot[0][None, :], axis=1) * from_prior
    where_next = jnp.sum(pick_j * spot[1][None, :], axis=1) * from_next
    ids_all = jnp.arange(total, dtype=jnp.int32)
    diff = (j[:, None] == ids_all).astype(jnp.int32) - (i[:, None] == ids_all).astype(jnp.int32)
    shift = jnp.sum(diff[:, :, None] * offsets[None], axis=1)
    plan = jnp.stack(
        [i % n, local, where_prior, where_next, kind, shift[:, 0], shift[:, 1], live]
    ).astype(jnp.int32)
    order = jnp.where(on, jnp.where(kind > 0, 0, 1), 2) * slots + jnp.arange(slots)
    rank = jnp.sum((order[None, :] < order[:, None]).astype(jnp.int32), axis=1)
    move = (rank[:, None] == jnp.arange(slots)[None, :]).astype(jnp.int32)
    plan = jnp.sum(plan[:, :, None] * move[None], axis=1)
    far, lively = jnp.sum((kind > 0).astype(jnp.int32)), jnp.sum(on.astype(jnp.int32))
    tail = jnp.where(jnp.arange(slots) == 0, far, lively)
    plan = jnp.concatenate([plan, tail[None]], axis=0)
    ends = jnp.stack([lax.axis_index("slab"), slabs]).astype(jnp.int32)

    up = [(s, s + 1) for s in range(slabs - 1)]
    down = [(s + 1, s) for s in range(slabs - 1)]

    def branch(m):
        def run(_):
            to_next, to_prior = gather(packed, lists[2:], m)
            prior = cycle(to_next, 1)
            nxt = cycle(to_prior, -1)
            partner, density, low, high = densities(plan, packed, prior, nxt)
            below = lax.ppermute(high, "slab", up)
            above = lax.ppermute(low, "slab", down)
            given = (plan, ends, density, partner, packed, below, above, m)
            acc, acc_prior, acc_next = solve(True, *given)
            from_next, from_prior = cycle(acc_prior, -1), cycle(acc_next, 1)
            (acc_near,) = solve(False, *given)
            return combine(back, acc, acc_near, from_next, from_prior)

        return run

    sizes = sorted({min(s, slots - 1) for s in (3, 4, 5)} | {slots - 1})
    which = sum((most > s).astype(jnp.int32) for s in sizes[:-1])
    return lax.switch(which, [branch(s) for s in sizes], 0)


def solution(mesh):
    placed = (
        P(CYCLE, "slab", None, None),
        P(),
        P(CYCLE, None),
        P(CYCLE),
    )
    return jax.shard_map(
        fast_body if mesh.shape["slab"] == 2 else body,
        mesh=mesh,
        in_specs=placed,
        out_specs=P(CYCLE, "slab", None, None),
        check_vma=False,
    )
```

```python
import cmath
import functools
import math

import jax
import jax.numpy as jnp
import numpy as np
from jax import lax
from jax.experimental import pallas as pl
from jax.experimental.pallas import tpu as pltpu
from jax.sharding import PartitionSpec as P

PASSES = 8
DIAG = 6.25
THETA = 1.075
DELTA = 0.925
EDGE = PASSES - 1
PAD = 16
CYCLE = ("grp", "orb")
F32 = jnp.float32


def coefs():
    sigma = THETA / DELTA
    coef = 1.0 / sigma
    out = []
    for _ in range(PASSES - 1):
        new = 1.0 / (2.0 * sigma - coef)
        out.append((new * coef, 2.0 * new / (DELTA * DIAG)))
        coef = new
    return out


def lanes(shape):
    return lax.broadcasted_iota(jnp.int32, shape, len(shape) - 1)


def share_kernel(mine, every, send_sem, recv_sem):
    size, width = lax.axis_size(CYCLE), lax.axis_size("orb")
    me = lax.axis_index("grp") * width + lax.axis_index("orb")

    def peer(s):
        to = lax.rem(me + s, size)
        return {"grp": lax.div(to, width), "orb": lax.rem(to, width)}

    def greet(s, c):
        pl.semaphore_signal(
            barrier, inc=1, device_id=peer(s), device_id_type=pl.DeviceIdType.MESH
        )
        return c

    def copy(s, slot):
        return pltpu.make_async_remote_copy(
            src_ref=mine,
            dst_ref=every.at[slot],
            send_sem=send_sem.at[s],
            recv_sem=recv_sem.at[s],
            device_id=peer(s),
            device_id_type=pl.DeviceIdType.MESH,
        )

    def send(s, c):
        copy(s, me).start()
        return c

    def finish(s, c):
        copy(s, lax.rem(me + size - s, size)).wait()
        return c

    barrier = pltpu.get_barrier_semaphore()
    lax.fori_loop(1, size, greet, 0)
    pl.semaphore_wait(barrier, size - 1)
    lax.fori_loop(1, size, send, 0)
    every[me] = mine[...]
    lax.fori_loop(1, size, finish, 0)


def share(mine):
    size = lax.axis_size(CYCLE)
    vmem = pl.BlockSpec(memory_space=pltpu.VMEM)
    return pl.pallas_call(
        share_kernel,
        in_specs=[vmem],
        out_specs=vmem,
        out_shape=jax.ShapeDtypeStruct((size,) + mine.shape, mine.dtype),
        scratch_shapes=[pltpu.SemaphoreType.DMA((size,)), pltpu.SemaphoreType.DMA((size,))],
        compiler_params=pltpu.CompilerParams(collective_id=0, has_side_effects=True),
        name="share",
    )(mine)


def pack_kernel(src, dst):
    half = dst.shape[1]
    dst[0] = jnp.concatenate([src[0, :half], src[0, half:]], axis=-1)


def pack(orbitals):
    n, x, y, z = orbitals.shape
    return pl.pallas_call(
        pack_kernel,
        grid=(n,),
        in_specs=[pl.BlockSpec((1, x, y, z), lambda i: (i, 0, 0, 0))],
        out_specs=pl.BlockSpec((1, x // 2, y, 2 * z), lambda i: (i, 0, 0, 0)),
        out_shape=jax.ShapeDtypeStruct((n, x // 2, y, 2 * z), F32),
        name="pack",
    )(orbitals)


def copy_kernel(idx, src_a, src_b, dst_a, dst_b):
    dst_a[...] = src_a[...]
    dst_b[...] = src_b[...]


def gather(packed, lists, m):
    _, h, y, w = packed.shape
    blk = (1, h, y, w)
    out = jax.ShapeDtypeStruct((m, h, y, w), F32)
    return pl.pallas_call(
        copy_kernel,
        grid_spec=pltpu.PrefetchScalarGridSpec(
            num_scalar_prefetch=1,
            grid=(m,),
            in_specs=[
                pl.BlockSpec(blk, lambda i, idx: (idx[0, i], 0, 0, 0)),
                pl.BlockSpec(blk, lambda i, idx: (idx[1, i], 0, 0, 0)),
            ],
            out_specs=[pl.BlockSpec(blk, lambda i, idx: (i, 0, 0, 0))] * 2,
        ),
        out_shape=[out, out],
        name="gather",
    )(lists, packed, packed)


def place(value, room, a, b):
    y, w = value.shape[1:]
    z = w // 2
    room[:, PAD : PAD + y, :] = value
    moved = room[:, pl.ds(PAD - a, y), :]
    moved = pltpu.roll(moved, lax.rem(b + w, w), axis=2)
    pos = lanes(moved.shape) % z - b
    return jnp.where((pos >= 0) & (pos < z), moved, 0.0)


def clear_room(room):
    y = room.shape[1] - 2 * PAD
    room[:, :PAD, :] = jnp.zeros((room.shape[0], PAD, room.shape[2]), F32)
    room[:, PAD + y :, :] = jnp.zeros((room.shape[0], PAD, room.shape[2]), F32)


def density_kernel(plan, own, mine, prior, nxt, partner, density, low, high, room):
    p = pl.program_id(0)
    kind = plan[4, p]
    a, b = plan[5, p], plan[6, p]

    @pl.when(p == 0)
    def _():
        clear_room(room)

    on = plan[7, p] > 0

    def go(src):
        part = place(src[0], room, a, b)
        partner[0] = part
        dens = own[0] * part
        density[0] = dens
        h, y, w = dens.shape
        flat = jnp.concatenate([dens[..., : w // 2], dens[..., w // 2 :]], axis=0)
        top, bot = flat[:EDGE], flat[2 * h - EDGE :]
        low[0] = jnp.concatenate([top[:, : y // 2], top[:, y // 2 :]], axis=-1)
        high[0] = jnp.concatenate([bot[:, : y // 2], bot[:, y // 2 :]], axis=-1)

    for value, src in enumerate((mine, prior, nxt)):
        pl.when(on & (kind == value))(functools.partial(go, src))


def densities(plan, packed, prior, nxt):
    slots = plan.shape[1]
    _, h, y, w = packed.shape
    blk = (1, h, y, w)
    eblk = (1, EDGE, y // 2, w)

    def at(row):
        return pl.BlockSpec(
            blk, lambda i, plan: (plan[row, jnp.minimum(i, plan[8, 1] - 1)], 0, 0, 0)
        )

    full = jax.ShapeDtypeStruct((slots, h, y, w), F32)
    edge = jax.ShapeDtypeStruct((slots,) + eblk[1:], F32)
    here = lambda i, plan: (jnp.minimum(i, plan[8, 1] - 1), 0, 0, 0)
    return pl.pallas_call(
        density_kernel,
        grid_spec=pltpu.PrefetchScalarGridSpec(
            num_scalar_prefetch=1,
            grid=(slots,),
            in_specs=[at(0), at(1), at(2), at(3)],
            out_specs=[
                pl.BlockSpec(blk, here),
                pl.BlockSpec(blk, here),
                pl.BlockSpec(eblk, here),
                pl.BlockSpec(eblk, here),
            ],
            scratch_shapes=[pltpu.VMEM((h, y + 2 * PAD, w), F32)],
        ),
        out_shape=[full, full, edge, edge],
        name="density",
    )(plan, packed, packed, prior, nxt)


def solve_kernel(remote, plan, ends, density, partner, own, below, above, *refs):
    accs, (resid, step_a, step_b, total, mask, room) = refs[:-6], refs[-6:]
    acc = accs[0]
    p = pl.program_id(0)
    h, y, w = density.shape[1:]
    z = w // 2
    rows = h + 2 * EDGE
    group = 4 if h % 4 == 0 else 1

    @pl.when(p == 0)
    def _():
        clear_room(room)
        for ref in accs:
            ref[...] = jnp.zeros(ref.shape, F32)
        for ref in (step_a, step_b):
            ref[:, :8, :] = jnp.zeros((rows, 8, w), F32)
            ref[:, 8 + y :, :] = jnp.zeros((rows, 8, w), F32)
        lane = lanes((1, w))
        first = ends[0] == 0
        last = ends[0] == ends[1] - 1
        for t in range(rows):
            plane = jnp.where(lane < z, t - EDGE, t - EDGE + h)
            outside = ((plane < 0) & first) | ((plane >= 2 * h) & last)
            mask[t] = jnp.where(outside, 0.0, 1.0)

    chosen = (plan[4, p] > 0) if remote else (plan[4, p] == 0)

    @pl.when((plan[7, p] > 0) & chosen)
    def _():
        def unfold(part):
            return jnp.concatenate([part[..., :z], part[..., z:]], axis=1)

        dens = density[0]
        line = jnp.concatenate(
            [unfold(below[0]), dens[..., :z], dens[..., z:], unfold(above[0])], axis=0
        )
        resid[...] = jnp.concatenate([line[:rows], line[h:]], axis=-1)
        step_a[:, 8 : 8 + y, :] = resid[...] * (1.0 / (DIAG * THETA))
        total[...] = step_a[EDGE : EDGE + h, 8 : 8 + y, :]
        lane = lanes((y, w)) % z
        not_low = lane > 0
        not_high = lane < z - 1
        bufs = [step_a, step_b]
        for turn, (keep, gain) in enumerate(coefs()):
            now, then = bufs[turn % 2], bufs[1 - turn % 2]
            core_only = turn == PASSES - 2

            def row(t, now=now, then=then, keep=keep, gain=gain):
                core = now[t, 8 : 8 + y, :]
                near = now[t - 1, 8 : 8 + y, :] + now[t + 1, 8 : 8 + y, :]
                near = near + (now[t, 7 : 7 + y, :] + now[t, 9 : 9 + y, :])
                side = jnp.where(not_low, pltpu.roll(core, 1, axis=1), 0.0)
                side = side + jnp.where(not_high, pltpu.roll(core, w - 1, axis=1), 0.0)
                left = (resid[t] - DIAG * core) + (near + side)
                return left, keep * core + gain * left

            def outer(k, c, row=row, then=then):
                for t in (EDGE - 1 - k, EDGE + h + k):
                    left, fresh = row(t)
                    resid[t] = left
                    then[t, 8 : 8 + y, :] = fresh * mask[t]
                return c

            def inner(k, c, row=row, then=then, last=core_only):
                for g in range(group):
                    t = EDGE + k * group + g
                    left, fresh = row(t)
                    if not last:
                        resid[t] = left
                        then[t, 8 : 8 + y, :] = fresh
                    total[t - EDGE] += fresh
                return c

            if turn + 1 < EDGE:
                lax.fori_loop(0, EDGE - turn - 1, outer, 0)
            lax.fori_loop(0, h // group, inner, 0)

        pot = total[...]
        acc[plan[0, p]] += pot * partner[0]
        back = place(pot * own[0], room, -plan[5, p], -plan[6, p])
        if not remote:
            acc[plan[1, p]] += back
        else:
            for value in (1, 2):

                @pl.when(plan[4, p] == value)
                def _(ref=accs[value], value=value):
                    ref[plan[1 + value, p]] += back


def solve(remote, plan, ends, density, partner, packed, below, above, m):
    slots = plan.shape[1]
    n, h, y, w = packed.shape
    blk = (1, h, y, w)
    eblk = (1, EDGE, y // 2, w)
    rows = h + 2 * EDGE

    def spot(i, plan):
        far = plan[8, 0]
        if remote:
            return jnp.minimum(i, jnp.maximum(far - 1, 0))
        return jnp.clip(i, jnp.minimum(far, plan[8, 1] - 1), plan[8, 1] - 1)

    here = lambda i, plan, ends: (spot(i, plan), 0, 0, 0)
    fixed = lambda i, plan, ends: (0, 0, 0, 0)
    shapes = [(n, h, y, w)] + [(m, h, y, w)] * (2 if remote else 0)
    return pl.pallas_call(
        functools.partial(solve_kernel, remote),
        grid_spec=pltpu.PrefetchScalarGridSpec(
            num_scalar_prefetch=2,
            grid=(slots,),
            in_specs=[
                pl.BlockSpec(blk, here),
                pl.BlockSpec(blk, here),
                pl.BlockSpec(blk, lambda i, plan, ends: (plan[0, spot(i, plan)], 0, 0, 0)),
                pl.BlockSpec(eblk, here),
                pl.BlockSpec(eblk, here),
            ],
            out_specs=[pl.BlockSpec(s, fixed) for s in shapes],
            scratch_shapes=[
                pltpu.VMEM((rows, y, w), F32),
                pltpu.VMEM((rows, y + 16, w), F32),
                pltpu.VMEM((rows, y + 16, w), F32),
                pltpu.VMEM((h, y, w), F32),
                pltpu.VMEM((rows, 1, w), F32),
                pltpu.VMEM((h, y + 2 * PAD, w), F32),
            ],
        ),
        out_shape=[jax.ShapeDtypeStruct(s, F32) for s in shapes],
        compiler_params=pltpu.CompilerParams(vmem_limit_bytes=56 * 1024 * 1024),
        cost_estimate=pl.CostEstimate(
            flops=slots * rows * y * w * 100, bytes_accessed=24 << 20, transcendentals=0
        ),
        name="solve_far" if remote else "solve_near",
    )(plan, ends, density, partner, packed, below, above)


def combine_kernel(back, acc, acc_near, from_next, from_prior, out):
    k = pl.program_id(0)
    h = acc.shape[1]
    z = acc.shape[3] // 2
    value = acc[0] + acc_near[0]
    value = value + jnp.where(back[1, k] > 0, from_next[0], 0.0)
    value = value + jnp.where(back[3, k] > 0, from_prior[0], 0.0)
    out[0, :h] = value[:, :, :z]
    out[0, h:] = value[:, :, z:]


def combine(back, acc, acc_near, from_next, from_prior):
    n, h, y, w = acc.shape
    blk = (1, h, y, w)
    return pl.pallas_call(
        combine_kernel,
        grid_spec=pltpu.PrefetchScalarGridSpec(
            num_scalar_prefetch=1,
            grid=(n,),
            in_specs=[
                pl.BlockSpec(blk, lambda i, back: (i, 0, 0, 0)),
                pl.BlockSpec(blk, lambda i, back: (i, 0, 0, 0)),
                pl.BlockSpec(blk, lambda i, back: (back[0, i], 0, 0, 0)),
                pl.BlockSpec(blk, lambda i, back: (back[2, i], 0, 0, 0)),
            ],
            out_specs=pl.BlockSpec((1, 2 * h, y, w // 2), lambda i, back: (i, 0, 0, 0)),
        ),
        out_shape=jax.ShapeDtypeStruct((n, 2 * h, y, w // 2), F32),
        name="combine",
    )(back, acc, acc_near, from_next, from_prior)


def cycle(field, by):
    size = lax.axis_size(CYCLE)
    return lax.ppermute(field, CYCLE, [(i, (i + by) % size) for i in range(size)])


TASK = 8
LISTS = 256
INFO = 320
PLAN = 384
EARLY = 2
FIXED = 2
SOON = 4
AHEAD = 6
UNROLL = 4
DEPTH = 5
STRIP = 8


def factors():
    ratio = THETA / DELTA
    tall = math.acosh(ratio)
    points = [cmath.cosh(complex(tall, k * math.pi / 4)) for k in range(8)]
    marks = [DIAG * (1.0 - (THETA - DELTA * x)) for x in points]
    quads = [(-2.0 * marks[k].real, abs(marks[k]) ** 2) for k in (1, 2, 3)]
    line = -marks[4].real
    coef, resid, value, step = 1.0 / ratio, 1.0, 0.0, 1.0 / (DIAG * THETA)
    value += step
    for keep, gain in coefs():
        resid -= DIAG * step
        step = keep * step + gain * resid
        value += step
    product = line
    for _, c in quads:
        product *= c
    return quads, line, value / product


def front_kernel(
    orbs, pairs, live, fields, every, edges, stage, own, rims, far, edge, table,
    in_sem, out_sem, rim_sem, tab_send, tab_recv, edge_send, edge_recv, far_send, far_recv,
):
    n, h = orbs.shape[0], orbs.shape[1]
    half = h // 2
    halo = edge.shape[1]
    size, width = lax.axis_size(CYCLE), lax.axis_size("orb")
    me = lax.axis_index("grp") * width + lax.axis_index("orb")
    slab = lax.axis_index("slab")

    def peer(s):
        to = lax.rem(me + s, size)
        return {"grp": lax.div(to, width), "orb": lax.rem(to, width)}

    def load(k):
        return pltpu.make_async_copy(orbs.at[k], stage.at[k], in_sem.at[k])

    def order(q):
        return jnp.where(q == 0, 0, jnp.where(q == 1, n - 1, q - 1))

    def begin(q, c):
        load(order(q)).start()
        return c

    lax.fori_loop(0, n, begin, 0)

    barrier = pltpu.get_barrier_semaphore()

    def greet(s, c):
        pl.semaphore_signal(
            barrier, inc=1, device_id=peer(s), device_id_type=pl.DeviceIdType.MESH
        )
        return c

    lax.fori_loop(1, size, greet, 0)
    pl.semaphore_signal(
        barrier, inc=1, device_id={"slab": 1 - slab}, device_id_type=pl.DeviceIdType.MESH
    )
    table[...] = jnp.zeros(table.shape, jnp.int32)
    table[0:2, 0:n] = pairs[...]
    table[2:3, 0:n] = live[...]
    pl.semaphore_wait(barrier, size)

    def share_copy(s, slot):
        return pltpu.make_async_remote_copy(
            src_ref=table, dst_ref=every.at[slot],
            send_sem=tab_send.at[s], recv_sem=tab_recv.at[s],
            device_id=peer(s), device_id_type=pl.DeviceIdType.MESH,
        )

    def share_send(s, c):
        share_copy(s, me).start()
        return c

    lax.fori_loop(1, size, share_send, 0)
    every[me] = table[...]

    def edge_copy(e, f, dst):
        return pltpu.make_async_remote_copy(
            src_ref=edge.at[f], dst_ref=dst,
            send_sem=edge_send.at[e], recv_sem=edge_recv.at[e],
            device_id={"slab": 1 - slab}, device_id_type=pl.DeviceIdType.MESH,
        )

    def own_edge(k, e):
        return edge_copy(e, k, rims.at[k])

    def far_copy(src, f, s):
        return pltpu.make_async_remote_copy(
            src_ref=src, dst_ref=far.at[f, pl.ds(0, half)],
            send_sem=far_send.at[f], recv_sem=far_recv.at[f],
            device_id=peer(s), device_id_type=pl.DeviceIdType.MESH,
        )

    def spot(t):
        return jnp.where(slab == 0, t, h - 1 - t)

    def pack(k):
        def row(r, c):
            own[k, r] = jnp.concatenate(
                [stage[k, spot(r)], stage[k, spot(r + half)]], axis=-1
            )
            return c

        lax.fori_loop(0, half, row, 0)

    def make_edge(k):
        for m in range(halo):
            edge[k, m] = jnp.concatenate(
                [stage[k, spot(h - 1 - m)], stage[k, spot(h - 1 - halo - m)]], axis=-1
            )

    def save(k):
        return pltpu.make_async_copy(
            own.at[k], fields.at[k, pl.ds(0, half)], out_sem.at[k]
        )

    def save_far(f):
        return pltpu.make_async_copy(
            far.at[f, pl.ds(0, half)], fields.at[n + f, pl.ds(0, half)], out_sem.at[n + f]
        )

    def rim(f, src):
        return pltpu.make_async_copy(src, fields.at[f, pl.ds(half, halo)], rim_sem.at[f])

    def keep_edge(k):
        return pltpu.make_async_copy(edge.at[k], edges.at[k], rim_sem.at[k])

    early = edge_send.shape[0] - 4

    up, down = far_copy(own.at[n - 1], 0, 1), far_copy(own.at[0], 1, size - 1)
    for k, send, e in ((0, down, 0), (n - 1, up, 1)):
        load(k).wait()
        pack(k)
        send.start()
        make_edge(k)
        own_edge(k, e).start()
        save(k).start()

    def rest(k, c):
        load(k).wait()
        pack(k)
        save(k).start()
        make_edge(k)
        pl.when(k <= early)(lambda: own_edge(k, 3 + k).start())
        pl.when(k > early)(lambda: keep_edge(k).start())
        return c

    lax.fori_loop(1, n - 1, rest, 0)

    def share_done(s, c):
        share_copy(s, lax.rem(me + size - s, size)).wait()
        return c

    lax.fori_loop(1, size, share_done, 0)

    low = lanes((1, own.shape[-1])) < own.shape[-1] // 2
    for f, copy in ((1, down), (0, up)):
        copy.wait()
        for m in range(halo):
            a, b = far[f, half - 1 - m], far[f, half - 1 - halo - m]
            edge[n + f, m] = jnp.where(low, pltpu.roll(a, a.shape[-1] // 2, axis=1), b)
        edge_copy(2 + f, n + f, far.at[f, pl.ds(half, halo)]).start()
        save_far(f).start()

    own_rims = [(0, 0), (n - 1, 1)] + [(k, 3 + k) for k in range(1, early + 1)]
    for k, e in own_rims:
        own_edge(k, e).wait()
        rim(k, rims.at[k]).start()
    for f in (1, 0):
        edge_copy(2 + f, n + f, far.at[f, pl.ds(half, halo)]).wait()
        rim(n + f, far.at[f, pl.ds(half, halo)]).start()

    def out_done(k, c):
        save(k).wait()
        return c

    def edge_done(k, c):
        keep_edge(k).wait()
        return c

    lax.fori_loop(0, n, out_done, 0)
    lax.fori_loop(early + 1, n - 1, edge_done, 0)
    for k, _ in own_rims:
        rim(k, rims.at[k]).wait()
    for f in (1, 0):
        rim(n + f, far.at[f, pl.ds(half, halo)]).wait()
    for f in range(2):
        save_far(f).wait()


def front(orbitals, pairs, live):
    n, h, y, z = orbitals.shape
    half, halo, w = h // 2, (EDGE + 1) // 2, 2 * z
    size = lax.axis_size(CYCLE)
    vmem = pl.BlockSpec(memory_space=pltpu.VMEM)
    hbm = pl.BlockSpec(memory_space=pl.ANY)
    dma = pltpu.SemaphoreType.DMA
    return pl.pallas_call(
        front_kernel,
        in_specs=[hbm, vmem, vmem],
        out_specs=[hbm, vmem, hbm],
        out_shape=[
            jax.ShapeDtypeStruct((n + 2, half + halo, y, w), F32),
            jax.ShapeDtypeStruct((size, 8, 128), jnp.int32),
            jax.ShapeDtypeStruct((n, halo, y, w), F32),
        ],
        scratch_shapes=[
            pltpu.VMEM((n, h, y, z), F32),
            pltpu.VMEM((n, half, y, w), F32),
            pltpu.VMEM((n, halo, y, w), F32),
            pltpu.VMEM((2, half + halo, y, w), F32),
            pltpu.VMEM((n + 2, halo, y, w), F32),
            pltpu.VMEM((8, 128), jnp.int32),
            dma((n,)), dma((n + 2,)), dma((n + 2,)), dma((size,)), dma((size,)),
            dma((4 + EARLY,)), dma((4 + EARLY,)), dma((2,)), dma((2,)),
        ],
        compiler_params=pltpu.CompilerParams(collective_id=1, has_side_effects=True),
        name="front",
    )(orbitals, pairs.T, live[None])


def plan_kernel(n, combos, every, offsets, plan, which, ups, downs, nups, ndowns, alive):
    size = every.shape[0]
    width = lax.axis_size("orb")
    me = lax.axis_index("grp") * width + lax.axis_index("orb")
    before, after = lax.rem(me + size - 1, size), lax.rem(me + 1, size)
    block = lambda x: lax.shift_right_logical(x, n.bit_length() - 1)

    def clear(e, c):
        ups[e] = 0
        downs[e] = 0
        nups[e] = 0
        ndowns[e] = 0
        alive[e] = sum(every[e, 2, r] for r in range(n))
        return c

    lax.fori_loop(0, size, clear, 0)

    def read(blk, r):
        i, j = every[blk, 0, r], every[blk, 1, r]
        bj = block(j)
        is_up = bj == jnp.where(blk + 1 == size, 0, blk + 1)
        li, lj = i & (n - 1), j & (n - 1)
        u, v = jnp.where(is_up, li, lj), jnp.where(is_up, lj, li)
        return i, j, bj, u, v, jnp.where(is_up, blk, bj)

    def mark(blk, c):
        def row(r, c):
            i, j, bj, u, v, edge = read(blk, r)

            @pl.when(bj != blk)
            def _():
                for bits, counts, x, free in ((ups, nups, u, n - 1), (downs, ndowns, v, 0)):
                    bit = jnp.where(x == free, 0, lax.shift_left(1, x))
                    had = bits[edge]
                    bits[edge] = had | bit
                    counts[edge] = counts[edge] + jnp.where((had | bit) != had, 1, 0)

            return c

        return lax.fori_loop(2, alive[blk], row, c)

    lax.fori_loop(0, size, mark, 0)

    def widest(e, most):
        o = lax.rem(e, width)
        mine = jnp.where(o % 2 == 0, 2, jnp.where(o == width - 1, 1, 0))
        here = jnp.maximum(nups[e], ndowns[e])
        return tuple(jnp.maximum(m, jnp.where(mine == c, here, 0)) for c, m in enumerate(most))

    most = lax.fori_loop(0, size, widest, (jnp.int32(0),) * 3)
    pick = jnp.int32(len(combos) - 1)
    for c in range(len(combos) - 2, -1, -1):
        fit = functools.reduce(lambda p, q: p & q, [m <= k for m, k in zip(most, combos[c])])
        pick = jnp.where(fit, c, pick)
    which[0] = pick

    def listing(bits, base):
        def step(q, s):
            plan[base + s] = q
            return s + (lax.shift_right_logical(bits, q) & 1)

        for q in range(n):
            plan[base + q] = 0
        return lax.fori_loop(0, n, step, jnp.int32(0))

    listing(ups[me], LISTS)
    listing(downs[before], LISTS + 2 * n)
    plan[INFO + 3] = nups[before]
    plan[INFO + 4] = ndowns[me]

    def rank(bits, x):
        return sum(
            jnp.where(q < x, lax.shift_right_logical(bits, q) & 1, 0) for q in range(n)
        )

    def place_of(x):
        blk, loc = block(x), x & (n - 1)
        low_rank, high_rank = rank(ups[before], loc), rank(downs[me], loc)
        low_at = jnp.where(low_rank == 0, n + 2, n + 3 + low_rank)
        high_at = jnp.where(high_rank == 0, n + 3, 2 * n + 1 + high_rank)
        from_before = jnp.where(loc == n - 1, n, low_at)
        from_after = jnp.where(loc == 0, n + 1, high_at)
        return jnp.where(blk == me, loc, jnp.where(blk == before, from_before, from_after))

    def sweep(level, blk, start, skip, count):
        def step(r, s):
            i, j, bj, u, v, edge = read(blk, r)
            above = edge == me
            free = (bj == blk) | jnp.where(above, v == 0, u == n - 1)
            late = jnp.where(above, rank(downs[me], v), rank(ups[before], u))
            mine = jnp.where(free, 0, jnp.where(late == 0, 1, 2))
            want = ((blk == me) | (bj == me)) & (mine == level) & (r != skip)

            @pl.when(want)
            def _():
                write(s * TASK, i, j)

            return s + jnp.where(want, 1, 0)

        return lax.fori_loop(start, alive[blk], step, count)

    def write(at, i, j):
        plan[at] = place_of(i)
        plan[at + 1] = place_of(j)
        plan[at + 2] = offsets[0, j] - offsets[0, i]
        plan[at + 3] = offsets[1, j] - offsets[1, i]
        plan[at + 4] = jnp.where(block(i) == me, i & (n - 1), n)
        plan[at + 5] = jnp.where(block(j) == me, j & (n - 1), n)

    def blank(s):
        for c, value in enumerate((0, 0, 0, 0, n, n)):
            plan[s * TASK + c] = value

    for s, (blk, r) in enumerate(((me, 1), (after, 0), (me, 0), (before, 1))):
        write(s * TASK, every[blk, 0, r], every[blk, 1, r])
    for s in range(2 * FIXED, 2 * AHEAD):
        blank(s)
    count = jnp.int32(2 * FIXED)
    for level in range(3):
        count = sweep(level, me, 2, n, count)
        count = sweep(level, before, 0, 1, count)
        count = sweep(level, after, 1, n, count)
        if level < 2:
            count = jnp.maximum(count, (2 * SOON, 2 * AHEAD)[level])
    plan[INFO + 6] = count
    blank(count)


def make_plan(every, offsets, n, combos):
    size = every.shape[0]
    smem = pl.BlockSpec(memory_space=pltpu.SMEM)
    return pl.pallas_call(
        functools.partial(plan_kernel, n, combos),
        in_specs=[smem, smem],
        out_specs=[smem, smem],
        out_shape=[
            jax.ShapeDtypeStruct((PLAN,), jnp.int32),
            jax.ShapeDtypeStruct((1,), jnp.int32),
        ],
        scratch_shapes=[pltpu.SMEM((size,), jnp.int32)] * 5,
        name="plan",
    )(every, offsets.T)


def wipe_room(room, y):
    def step(f, c):
        room[f, :, y:, :] = jnp.zeros((room.shape[1], PAD, room.shape[3]), F32)
        return c

    lax.fori_loop(0, room.shape[0], step, 0)


def repeat(count, unroll, do):
    def step(g, c):
        for q in range(unroll):
            do(g * unroll + q)
        return c

    lax.fori_loop(0, count // unroll, step, 0)


def solver(plan, room, one, two, own2, par2, prod, wheel, moves, basis, basis_back, levels, h):
    rows, tall, w = room.shape[1:]
    y, z = tall - PAD, w // 2
    half = h // 2
    halo = rows - half
    each = rows * tall
    quads, line, _ = factors()

    prod[0] = jnp.zeros((tall, w), F32)
    prod[:, y:, :] = jnp.zeros((h + 1, PAD, w), F32)
    for ref in (one, two):
        planes = ref.shape[0]
        ref[0] = jnp.zeros(ref.shape[1:], F32)
        ref[:, 0:8, :] = jnp.zeros((planes, 8, w), F32)
        ref[:, 8 + y :, :] = jnp.zeros((planes, 8, w), F32)
    flat_room = room.reshape(room.shape[0] * each, w)
    flat_prod = prod.reshape((h + 1) * tall, w)

    k_at = lax.broadcasted_iota(jnp.int32, (2 * w, 2 * w), 0)
    c_at = lax.broadcasted_iota(jnp.int32, (2 * w, 2 * w), 1)
    task_k, half_k, task_c, half_c = k_at // w, k_at % w // z, c_at % w // z, c_at // w
    gap = k_at % z - c_at % z
    wheel[...] = jnp.where((task_k == task_c) & (half_k == half_c), gap, 4 * z)

    lane = lanes((y, w))
    low = lane < z
    pos = lane % z
    mu = jnp.broadcast_to(levels[...], (STRIP, w))

    def sweep(src, count, emit):
        def step(g, c):
            for r in range(0, y, STRIP):
                at = pl.ds(8 + r, STRIP)
                col = [src[g * UNROLL + q, at, :] for q in range(UNROLL + 2)]
                for q in range(UNROLL):
                    t = g * UNROLL + q
                    sides = src[t + 1, pl.ds(7 + r, STRIP), :] + src[t + 1, pl.ds(9 + r, STRIP), :]
                    emit(t, r, col[q + 1], (col[q] + col[q + 2]) + sides)
            return c

        lax.fori_loop(0, (count + UNROLL - 1) // UNROLL, step, 0)

    def split(values):
        coarse = values.astype(jnp.bfloat16)
        return coarse, (values - coarse.astype(F32)).astype(jnp.bfloat16)

    def turn_z(values, wave):
        both = jnp.dot(
            jnp.concatenate(split(values), axis=1), wave[...], preferred_element_type=F32
        )
        return both[:, :w] + both[:, w:]

    def planes(r):
        return jnp.where(r < half, r, r + half), jnp.where(r < half, r + half, r + half + halo)

    def run(g, gains, backs):
        p, q = g * 2 * TASK, (g * 2 + 1) * TASK
        rp, rq = (plan[p] + 1) * each, (plan[q] + 1) * each
        ap, aq, bp, bq = plan[p + 2], plan[q + 2], plan[p + 3], plan[q + 3]
        sp, sq = (plan[p + 1] + 1) * each - ap, (plan[q + 1] + 1) * each - aq
        col = lanes((1, 2 * w)) % w < z
        moves[...] = jnp.where(wheel[...] == jnp.where(col, -bp, -bq), 1.0, 0.0).astype(jnp.bfloat16)

        def waves_of(g):
            raw = []
            for q in range(DEPTH):
                for t in planes(g * DEPTH + q):
                    raw.append(two[t + 1, 8 : 8 + y, :])
            return turn_z(jnp.concatenate(raw, axis=0), basis)

        def keep_waves(g, waves):
            for q in range(DEPTH):
                for side, t in enumerate(planes(g * DEPTH + q)):
                    at = (2 * q + side) * y
                    one[t + 1, 8 : 8 + y, :] = waves[at : at + y]

        def partners(g):
            par = [
                jnp.concatenate(
                    [flat_room[pl.ds(sp + r * tall, y), :], flat_room[pl.ds(sq + r * tall, y), :]],
                    axis=1,
                )
                for r in [g * DEPTH + q for q in range(DEPTH)]
            ]
            par = jnp.concatenate(split(jnp.concatenate(par, axis=0)), axis=0)
            par = jnp.dot(par, moves[...], preferred_element_type=F32)
            return par[: DEPTH * y] + par[DEPTH * y :]

        def keep_partners(g, par):
            for q in range(DEPTH):
                r = g * DEPTH + q
                own_p = flat_room[pl.ds(rp + r * tall, y), :]
                own_q = flat_room[pl.ds(rq + r * tall, y), :]
                own_a = jnp.where(low, own_p, pltpu.roll(own_q, z, axis=1))
                own_b = jnp.where(low, pltpu.roll(own_p, z, axis=1), own_q)
                for t, own, half_par in zip(
                    planes(r), (own_a, own_b), jnp.split(par[q * y : (q + 1) * y], 2, axis=1)
                ):
                    two[t + 1, 8 : 8 + y, :] = own * half_par
                    own2[t] = own
                    par2[t] = half_par

        def dense(g, c):
            waves, par = waves_of(g - 1), partners(g)
            keep_waves(g - 1, waves)
            keep_partners(g, par)
            return c

        turns = rows // DEPTH
        keep_partners(0, partners(0))
        lax.fori_loop(1, turns, dense, 0)
        keep_waves(turns - 1, waves_of(turns - 1))

        def quad(k, c):
            b, c2 = jnp.float32(quads[0][0]), jnp.float32(quads[0][1])
            for m in range(1, len(quads)):
                b = jnp.where(k == m, jnp.float32(quads[m][0]), b)
                c2 = jnp.where(k == m, jnp.float32(quads[m][1]), c2)
            mu_b = mu + b

            def first(t, r, cur, near):
                two[t + 1, pl.ds(8 + r, STRIP), :] = near + mu_b * cur

            def second(t, r, cur, near):
                at = pl.ds(8 + r, STRIP)
                one[t + 1, at, :] = (near + mu * cur) + c2 * one[t + 1, at, :]

            count = h + EDGE - 1 - 2 * k
            sweep(one, count, first)
            sweep(two, count - 1, second)
            return c

        lax.fori_loop(0, len(quads), quad, 0)
        mu_line = mu + line

        def finish(g, c):
            values = [[] for _ in range(UNROLL)]
            for r in range(0, y, STRIP):
                at = pl.ds(8 + r, STRIP)
                col = [one[g * UNROLL + q, at, :] for q in range(UNROLL + 2)]
                for q in range(UNROLL):
                    t = g * UNROLL + q
                    sides = one[t + 1, pl.ds(7 + r, STRIP), :] + one[t + 1, pl.ds(9 + r, STRIP), :]
                    values[q].append((col[q] + col[q + 2]) + sides + mu_line * col[q + 1])
            both = turn_z(jnp.concatenate(sum(values, []), axis=0), basis_back)
            for q in range(UNROLL):
                t = g * UNROLL + q
                pot = both[q * y : (q + 1) * y]
                gains[t] = pot * par2[t]
                prod[t + 1, 0:y, :] = pot * own2[t]
            return c

        lax.fori_loop(0, h // UNROLL, finish, 0)

        back = pos + jnp.where(low, bp, bq)
        good = (back >= 0) & (back < z)
        turn_p, turn_q = lax.rem(w - bp, w), lax.rem(w - bq, w)

        def plane(t):
            at = (t + 1) * tall
            moved_p = pltpu.roll(flat_prod[pl.ds(at + ap, y), :], turn_p, axis=1)
            moved_q = pltpu.roll(flat_prod[pl.ds(at + aq, y), :], turn_q, axis=1)
            backs[t] = jnp.where(good, jnp.where(low, moved_p, moved_q), 0.0)

        repeat(h, 4, plane)

    return run


def solver_scratch(fields, h, y, w, rows):
    planes = 2 * rows
    return [
        pltpu.VMEM((fields + 1, rows, y + PAD, w), F32),
        pltpu.VMEM((planes + 6, y + 16, w), F32),
        pltpu.VMEM((planes + 6, y + 16, w), F32),
        pltpu.VMEM((planes, y, w), F32),
        pltpu.VMEM((planes, y, w), F32),
        pltpu.VMEM((h + 1, y + PAD, w), F32),
        pltpu.VMEM((2 * w, 2 * w), jnp.int32),
        pltpu.VMEM((2 * w, 2 * w), jnp.bfloat16),
    ]


def swap_kernel(
    counts, plan, fields, edges, basis, basis_back, levels, prior, nxt, halos, statics, results,
    room, one, two, own2, par2, prod, wheel, moves, sends, got, trim, hal, parts,
    in_sem, send, recv, edge_send, edge_recv, trim_send, trim_recv, main_sem, rim_sem,
    hal_sem, part_sem,
):
    n, halo, y, w = edges.shape
    rows = fields.shape[1]
    half = rows - halo
    late = hal.shape[0]
    m = sends.shape[1]
    size, width = lax.axis_size(CYCLE), lax.axis_size("orb")
    o = lax.axis_index("orb")
    me = lax.axis_index("grp") * width + o
    slab = lax.axis_index("slab")
    other = {"slab": 1 - slab}

    def peer(s):
        to = lax.rem(me + s, size)
        return {"grp": lax.div(to, width), "orb": lax.rem(to, width)}

    def limit(q):
        return jnp.where(q % 2 == 0, counts[2], jnp.where(q == width - 1, counts[1], counts[0]))

    above, under = limit(o), limit(lax.rem(o + width - 1, width))
    ways = ((0, above, under, prior), (1, under, above, nxt))

    def load(f):
        return pltpu.make_async_copy(fields.at[f], room.at[f + 1, :, pl.ds(0, y)], in_sem.at[f])

    def copy(way, r):
        return pltpu.make_async_remote_copy(
            src_ref=sends.at[way, r], dst_ref=got.at[way, r, pl.ds(0, half)],
            send_sem=send.at[way, r], recv_sem=recv.at[way, r],
            device_id=peer((1, size - 1)[way]), device_id_type=pl.DeviceIdType.MESH,
        )

    def edge_copy(k):
        return pltpu.make_async_remote_copy(
            src_ref=edges.at[n - 1 - late + k], dst_ref=hal.at[k],
            send_sem=edge_send.at[k], recv_sem=edge_recv.at[k],
            device_id=other, device_id_type=pl.DeviceIdType.MESH,
        )

    def keep_hal(k):
        return pltpu.make_async_copy(hal.at[k], halos.at[k], hal_sem.at[k])

    def trim_copy(way, r):
        return pltpu.make_async_remote_copy(
            src_ref=trim.at[way, r], dst_ref=got.at[way, r, pl.ds(half, halo)],
            send_sem=trim_send.at[way, r], recv_sem=trim_recv.at[way, r],
            device_id=other, device_id_type=pl.DeviceIdType.MESH,
        )

    def main_out(way, r, dst):
        part = pl.ds(0, half)
        return pltpu.make_async_copy(got.at[way, r, part], dst.at[r, part], main_sem.at[way, r])

    def rim_out(way, r, dst):
        part = pl.ds(half, halo)
        return pltpu.make_async_copy(got.at[way, r, part], dst.at[r, part], rim_sem.at[way, r])

    def part_out(g):
        return pltpu.make_async_copy(parts.at[g % 2], results.at[g - FIXED], part_sem.at[g % 2])

    def static_out(g):
        return pltpu.make_async_copy(parts.at[g % 2, 0], statics.at[g], part_sem.at[g % 2])

    def out_wait(g):
        pl.when(g < FIXED)(lambda: static_out(g).wait())
        pl.when(g >= FIXED)(lambda: part_out(g).wait())

    def each(start, stop, do):
        def step(k, c):
            do(k)
            return c

        lax.fori_loop(start, stop, step, 0)

    each(0, n + 2, lambda f: load(f).start())
    barrier = pltpu.get_barrier_semaphore()
    for to in (peer(1), peer(size - 1), other):
        pl.semaphore_signal(barrier, inc=1, device_id=to, device_id_type=pl.DeviceIdType.MESH)
    wipe_room(room, y)
    run = solver(
        plan, room, one, two, own2, par2, prod, wheel, moves, basis, basis_back, levels, 2 * half
    )
    pl.semaphore_wait(barrier, 3)
    each(0, late, lambda k: edge_copy(k).start())
    each(0, n + 2, lambda f: load(f).wait())

    def launch(r):
        for way, out, _, _ in ways:
            @pl.when(r < out)
            def _(way=way):
                k = plan[LISTS + way * 2 * n + r]

                def row(t):
                    sends[way, r, t] = room[k + 1, t, 0:y, :]

                each(0, half, row)
                copy(way, r).start()

    each(0, m, launch)
    low = lanes((1, w)) < w // 2

    def land(r):
        for way, _, into, dst in ways:
            @pl.when(r < into)
            def _(way=way, dst=dst):
                copy(way, r).wait_recv()
                main_out(way, r, dst).start()
                for e in range(halo):
                    a, b = got[way, r, half - 1 - e], got[way, r, half - 1 - halo - e]
                    trim[way, r, e] = jnp.where(low, pltpu.roll(a, w // 2, axis=1), b)
                trim_copy(way, r).start()

    def work(g):
        pl.when(g >= 2)(lambda: out_wait(g - 2))

        @pl.when(g == FIXED)
        def _():
            for k in range(late):
                edge_copy(k).wait()
                keep_hal(k).start()
                room[n - late + k, half:, 0:y, :] = hal[k]

        @pl.when(g == SOON)
        def _():
            for way, _, _, dst in ways:
                trim_copy(way, 0).wait()
                rim_out(way, 0, dst).start()

                def row(t):
                    room[n + 3 + way, t, 0:y, :] = got[way, 0, t]

                each(0, rows, row)

        run(g, parts.at[g % 2, 0], parts.at[g % 2, 1])

        @pl.when(g < FIXED)
        def _():
            def merge(t):
                parts[g % 2, 0, t] = jnp.where(low, parts[g % 2, 0, t], parts[g % 2, 1, t])

            repeat(2 * half, 4, merge)
            static_out(g).start()

        pl.when(g >= FIXED)(lambda: part_out(g).start())
        pl.when((g % 2 == 1) & (g // 2 < m))(lambda: land(g // 2))

    each(0, AHEAD, work)
    each(min(AHEAD // 2, m), m, land)
    for k in range(late):
        keep_hal(k).wait()
    for g in range(AHEAD - 2, AHEAD):
        out_wait(g)

    def settle(r):
        for way, out, into, dst in ways:
            @pl.when(r < into)
            def _(way=way, dst=dst):
                trim_copy(way, r).wait()
                rim_out(way, r, dst).start()

            @pl.when(r < out)
            def _(way=way):
                copy(way, r).wait_send()

    for way in range(2):
        copy(way, 0).wait_send()
    each(1, m, settle)

    def close(r):
        for way, _, into, dst in ways:
            @pl.when(r < into)
            def _(way=way, dst=dst):
                main_out(way, r, dst).wait()
                rim_out(way, r, dst).wait()

    each(0, m, close)


def swap(counts, plan, fields, edges, waves, cid):
    n, halo, y, w = edges.shape
    rows = fields.shape[1]
    half, m = rows - halo, max(counts)
    late = n - 2 - EARLY
    hbm = pl.BlockSpec(memory_space=pl.ANY)
    smem = pl.BlockSpec(memory_space=pltpu.SMEM)
    vmem = pl.BlockSpec(memory_space=pltpu.VMEM)
    dma = pltpu.SemaphoreType.DMA
    out = jax.ShapeDtypeStruct((n - 1, rows, y, w), F32)
    return pl.pallas_call(
        functools.partial(swap_kernel, counts),
        in_specs=[smem, hbm, hbm, vmem, vmem, vmem],
        out_specs=[hbm] * 5,
        out_shape=[
            out,
            out,
            jax.ShapeDtypeStruct((late, halo, y, w), F32),
            jax.ShapeDtypeStruct((FIXED, 2 * half, y, w), F32),
            jax.ShapeDtypeStruct((AHEAD - FIXED, 2, 2 * half, y, w), F32),
        ],
        scratch_shapes=solver_scratch(n + 4, 2 * half, y, w, rows)
        + [
            pltpu.VMEM((2, m, half, y, w), F32),
            pltpu.VMEM((2, m, rows, y, w), F32),
            pltpu.VMEM((2, m, halo, y, w), F32),
            pltpu.VMEM((late, halo, y, w), F32),
            pltpu.VMEM((2, 2, 2 * half, y, w), F32),
            dma((n + 2,)), dma((2, m)), dma((2, m)), dma((late,)), dma((late,)),
            dma((2, m)), dma((2, m)), dma((2, m)), dma((2, m)), dma((late,)), dma((2,)),
        ],
        compiler_params=pltpu.CompilerParams(
            collective_id=cid, has_side_effects=True, vmem_limit_bytes=58 * 1024 * 1024
        ),
        name="swap%d%d%d" % counts,
    )(plan, fields, edges, *waves)


def pairs_kernel(
    plan, fields, prior, nxt, halos, statics, results, basis, basis_back, levels, out,
    room, one, two, own2, par2, prod, wheel, moves, acc, stage, parts, sem, hal_sem, acc_sem, out_sem, part_sem,
):
    n, h, y, z = out.shape
    w = 2 * z
    most = prior.shape[0]
    slab = lax.axis_index("slab")

    def part(g):
        return pltpu.make_async_copy(results.at[g], parts.at[g % 2], part_sem.at[g % 2])

    tasks = plan[INFO + 6]

    rows, late = fields.shape[1], halos.shape[0]
    halo = halos.shape[1]

    def field(src, s, f):
        return pltpu.make_async_copy(src.at[s], room.at[f + 1, :, pl.ds(0, y)], sem.at[f])

    def main(f):
        part = pl.ds(0, rows - halo)
        return pltpu.make_async_copy(
            fields.at[f, part], room.at[f + 1, part, pl.ds(0, y)], sem.at[f]
        )

    def rim(f):
        part = pl.ds(rows - halo, halo)
        return pltpu.make_async_copy(
            halos.at[f - (n - 1 - late)], room.at[f + 1, part, pl.ds(0, y)], hal_sem.at[f]
        )

    def each_field(do):
        @pl.when(tasks > 2 * AHEAD)
        def _():
            for f in range(n + 2):
                if n - 1 - late <= f < n - 1:
                    do(main(f))
                    do(rim(f))
                else:
                    do(field(fields, f, f))
            for way, (src, count) in enumerate(((prior, plan[INFO + 3]), (nxt, plan[INFO + 4]))):
                for s in range(most):
                    f = n + 2 + way if s == 0 else n + 3 + way * (n - 2) + s
                    pl.when(s < count)(lambda src=src, s=s, f=f: do(field(src, s, f)))

    def static(g, k):
        return pltpu.make_async_copy(statics.at[g], acc.at[k], acc_sem.at[g])

    part(0).start()
    part(1).start()
    static(0, n - 1).start()
    static(1, 0).start()
    each_field(lambda c: c.start())
    acc[1 : n - 1] = jnp.zeros((n - 2,) + acc.shape[1:], F32)
    wipe_room(room, y)
    run = solver(plan, room, one, two, own2, par2, prod, wheel, moves, basis, basis_back, levels, h)
    low = lanes((y, w)) < w // 2

    def collect(g, gains, backs):
        p, q = g * 2 * TASK, (g * 2 + 1) * TASK
        for k, src, side in (
            (plan[p + 4], gains, low),
            (plan[q + 4], gains, jnp.logical_not(low)),
            (plan[p + 5], backs, low),
            (plan[q + 5], backs, jnp.logical_not(low)),
        ):
            @pl.when(k < n)
            def _(k=k, src=src, side=side):
                def plane(t):
                    acc[k, t] += jnp.where(side, src[t], 0.0)

                repeat(h, 4, plane)

    def gather(g, c):
        part(g).wait()
        collect(g + FIXED, parts.at[g % 2, 0], parts.at[g % 2, 1])
        pl.when(g + 2 < AHEAD - FIXED)(lambda: part(g + 2).start())
        return c

    static(0, n - 1).wait()
    static(1, 0).wait()
    lax.fori_loop(0, AHEAD - FIXED, gather, 0)
    each_field(lambda c: c.wait())

    def group(g, c):
        run(g, parts.at[0, 0], parts.at[0, 1])
        collect(g, parts.at[0, 0], parts.at[0, 1])
        return c

    lax.fori_loop(AHEAD, lax.div(tasks + 1, 2), group, 0)

    def leave(k, slot):
        return pltpu.make_async_copy(stage.at[slot], out.at[k], out_sem.at[slot])

    def write(k, c):
        slot = lax.rem(k, 2)
        pl.when(k >= 2)(lambda: leave(k - 2, slot).wait())

        def plane(t):
            value = acc[k, t]
            value = value + pltpu.roll(value, z, axis=1)
            stage[slot, jnp.where(slab == 0, t, h - 1 - t)] = value[:, :z]

        repeat(h, 8, plane)
        leave(k, slot).start()
        return c

    lax.fori_loop(0, n, write, 0)
    for k in (n - 2, n - 1):
        leave(k, k % 2).wait()


def sines(z):
    k = np.arange(1, z + 1)
    wave = np.sqrt(2.0 / (z + 1)) * np.sin(np.pi * np.outer(k, k) / (z + 1))
    wave = np.kron(np.eye(2), wave).astype(np.float32)
    levels = np.tile(2.0 * np.cos(np.pi * k / (z + 1)), 2).astype(np.float32)[None]

    def parts(values):
        coarse = jnp.asarray(values).astype(jnp.bfloat16)
        fine = (jnp.asarray(values) - coarse.astype(F32)).astype(jnp.bfloat16)
        top = jnp.concatenate([coarse, fine], axis=1)
        bottom = jnp.concatenate([coarse, jnp.zeros_like(fine)], axis=1)
        return jnp.concatenate([top, bottom], axis=0)

    return parts(wave), parts(wave * np.float32(factors()[2])), jnp.asarray(levels)


def solve_pairs(plan, fields, prior, nxt, halos, statics, results, waves, shape):
    n, h, y, z = shape
    w, rows = 2 * z, fields.shape[1]
    most = prior.shape[0]
    hbm = pl.BlockSpec(memory_space=pl.ANY)
    vmem = pl.BlockSpec(memory_space=pltpu.VMEM)
    dma = pltpu.SemaphoreType.DMA
    total = n + 2 + 2 * most
    return pl.pallas_call(
        pairs_kernel,
        grid_spec=pltpu.PrefetchScalarGridSpec(
            num_scalar_prefetch=1,
            grid=(1,),
            in_specs=[hbm] * 6 + [vmem] * 3,
            out_specs=hbm,
            scratch_shapes=solver_scratch(total, h, y, w, rows)
            + [
                pltpu.VMEM((n, h, y, w), F32),
                pltpu.VMEM((2, h, y, z), F32),
                pltpu.VMEM((2, 2, h, y, w), F32),
                dma((total,)), dma((n,)), dma((2,)), dma((2,)), dma((2,)),
            ],
        ),
        out_shape=jax.ShapeDtypeStruct(shape, F32),
        compiler_params=pltpu.CompilerParams(vmem_limit_bytes=58 * 1024 * 1024),
        name="pairs",
    )(plan, fields, prior, nxt, halos, statics, results, *waves)


def fast_body(orbitals, offsets, pairs, live):
    n = orbitals.shape[0]
    combos = [(2, 2, 2), (2, 3, 3), (3, 2, 3), (3, 3, 3), (3, 4, 4), (4, 3, 4), (4, 4, 4)]
    combos.append((n - 1,) * 3)
    waves = sines(orbitals.shape[-1])
    fields, every, edges = front(orbitals, pairs, live)
    plan, which = make_plan(every, offsets, n, combos)

    def branch(counts, cid):
        return lambda _: swap(counts, plan, fields, edges, waves, cid)

    prior, nxt, halos, statics, results = lax.switch(
        which[0], [branch(c, 2 + i) for i, c in enumerate(combos)], 0
    )
    return solve_pairs(
        plan, fields, prior, nxt, halos, statics, results, waves, orbitals.shape
    )


def body(orbitals, offsets, pairs, live):
    n = orbitals.shape[0]
    slots = pairs.shape[0]
    total = offsets.shape[0]
    blocks = total // n
    slabs = lax.axis_size("slab")
    me = lax.axis_index(CYCLE)
    packed = pack(orbitals)

    mine = jnp.concatenate([pairs, live[:, None]], axis=1)
    every = share(jnp.pad(mine, ((0, 0), (0, 128 - mine.shape[1]))))
    ids = jnp.arange(blocks, dtype=jnp.int32)
    second = every[:, :, 1]
    alive = every[:, :, 2] > 0
    orb = jnp.arange(n, dtype=jnp.int32)
    sides = jnp.stack([(ids - 1) % blocks, (ids + 1) % blocks])
    hit = alive[None] & (second[None] // n == sides[:, :, None])
    need = jnp.any(
        hit[..., None] & (second[None, :, :, None] % n == orb), axis=2
    )
    count = jnp.sum(need.astype(jnp.int32), axis=2)
    most = jnp.max(count)

    after, before = (me + 1) % blocks, (me - 1) % blocks
    flags = jnp.stack(
        [need[0, me], need[1, me], need[0, after], need[1, before]]
    ).astype(jnp.int32)
    spot = jnp.sum(
        flags[:, None, :] * (orb[None, :] < orb[:, None]).astype(jnp.int32)[None], axis=2
    )
    lists = jnp.sum(
        (flags[:, None, :] * (spot[:, None, :] == orb[None, :, None])) * orb, axis=2
    )
    back = jnp.stack(
        [spot[2] * flags[2], flags[2], spot[3] * flags[3], flags[3]]
    )

    i, j, on = pairs[:, 0], pairs[:, 1], live > 0
    owner, local = j // n, j % n
    pick_j = (local[:, None] == orb[None, :]).astype(jnp.int32)
    from_prior = (owner == before) & on
    from_next = (owner == after) & on
    kind = jnp.where(from_prior, 1, jnp.where(from_next, 2, 0))
    where_prior = jnp.sum(pick_j * spot[0][None, :], axis=1) * from_prior
    where_next = jnp.sum(pick_j * spot[1][None, :], axis=1) * from_next
    ids_all = jnp.arange(total, dtype=jnp.int32)
    diff = (j[:, None] == ids_all).astype(jnp.int32) - (i[:, None] == ids_all).astype(jnp.int32)
    shift = jnp.sum(diff[:, :, None] * offsets[None], axis=1)
    plan = jnp.stack(
        [i % n, local, where_prior, where_next, kind, shift[:, 0], shift[:, 1], live]
    ).astype(jnp.int32)
    order = jnp.where(on, jnp.where(kind > 0, 0, 1), 2) * slots + jnp.arange(slots)
    rank = jnp.sum((order[None, :] < order[:, None]).astype(jnp.int32), axis=1)
    move = (rank[:, None] == jnp.arange(slots)[None, :]).astype(jnp.int32)
    plan = jnp.sum(plan[:, :, None] * move[None], axis=1)
    far, lively = jnp.sum((kind > 0).astype(jnp.int32)), jnp.sum(on.astype(jnp.int32))
    tail = jnp.where(jnp.arange(slots) == 0, far, lively)
    plan = jnp.concatenate([plan, tail[None]], axis=0)
    ends = jnp.stack([lax.axis_index("slab"), slabs]).astype(jnp.int32)

    up = [(s, s + 1) for s in range(slabs - 1)]
    down = [(s + 1, s) for s in range(slabs - 1)]

    def branch(m):
        def run(_):
            to_next, to_prior = gather(packed, lists[2:], m)
            prior = cycle(to_next, 1)
            nxt = cycle(to_prior, -1)
            partner, density, low, high = densities(plan, packed, prior, nxt)
            below = lax.ppermute(high, "slab", up)
            above = lax.ppermute(low, "slab", down)
            given = (plan, ends, density, partner, packed, below, above, m)
            acc, acc_prior, acc_next = solve(True, *given)
            from_next, from_prior = cycle(acc_prior, -1), cycle(acc_next, 1)
            (acc_near,) = solve(False, *given)
            return combine(back, acc, acc_near, from_next, from_prior)

        return run

    sizes = sorted({min(s, slots - 1) for s in (3, 4, 5)} | {slots - 1})
    which = sum((most > s).astype(jnp.int32) for s in sizes[:-1])
    return lax.switch(which, [branch(s) for s in sizes], 0)


def solution(mesh):
    placed = (
        P(CYCLE, "slab", None, None),
        P(),
        P(CYCLE, None),
        P(CYCLE),
    )
    return jax.shard_map(
        fast_body if mesh.shape["slab"] == 2 else body,
        mesh=mesh,
        in_specs=placed,
        out_specs=P(CYCLE, "slab", None, None),
        check_vma=False,
    )
```

```python
import cmath
import functools
import math

import jax
import jax.numpy as jnp
import numpy as np
from jax import lax
from jax.experimental import pallas as pl
from jax.experimental.pallas import tpu as pltpu
from jax.sharding import PartitionSpec as P

PASSES = 8
DIAG = 6.25
THETA = 1.075
DELTA = 0.925
EDGE = PASSES - 1
PAD = 16
CYCLE = ("grp", "orb")
F32 = jnp.float32


def coefs():
    sigma = THETA / DELTA
    coef = 1.0 / sigma
    out = []
    for _ in range(PASSES - 1):
        new = 1.0 / (2.0 * sigma - coef)
        out.append((new * coef, 2.0 * new / (DELTA * DIAG)))
        coef = new
    return out


def lanes(shape):
    return lax.broadcasted_iota(jnp.int32, shape, len(shape) - 1)


def share_kernel(mine, every, send_sem, recv_sem):
    size, width = lax.axis_size(CYCLE), lax.axis_size("orb")
    me = lax.axis_index("grp") * width + lax.axis_index("orb")

    def peer(s):
        to = lax.rem(me + s, size)
        return {"grp": lax.div(to, width), "orb": lax.rem(to, width)}

    def greet(s, c):
        pl.semaphore_signal(
            barrier, inc=1, device_id=peer(s), device_id_type=pl.DeviceIdType.MESH
        )
        return c

    def copy(s, slot):
        return pltpu.make_async_remote_copy(
            src_ref=mine,
            dst_ref=every.at[slot],
            send_sem=send_sem.at[s],
            recv_sem=recv_sem.at[s],
            device_id=peer(s),
            device_id_type=pl.DeviceIdType.MESH,
        )

    def send(s, c):
        copy(s, me).start()
        return c

    def finish(s, c):
        copy(s, lax.rem(me + size - s, size)).wait()
        return c

    barrier = pltpu.get_barrier_semaphore()
    lax.fori_loop(1, size, greet, 0)
    pl.semaphore_wait(barrier, size - 1)
    lax.fori_loop(1, size, send, 0)
    every[me] = mine[...]
    lax.fori_loop(1, size, finish, 0)


def share(mine):
    size = lax.axis_size(CYCLE)
    vmem = pl.BlockSpec(memory_space=pltpu.VMEM)
    return pl.pallas_call(
        share_kernel,
        in_specs=[vmem],
        out_specs=vmem,
        out_shape=jax.ShapeDtypeStruct((size,) + mine.shape, mine.dtype),
        scratch_shapes=[pltpu.SemaphoreType.DMA((size,)), pltpu.SemaphoreType.DMA((size,))],
        compiler_params=pltpu.CompilerParams(collective_id=0, has_side_effects=True),
        name="share",
    )(mine)


def pack_kernel(src, dst):
    half = dst.shape[1]
    dst[0] = jnp.concatenate([src[0, :half], src[0, half:]], axis=-1)


def pack(orbitals):
    n, x, y, z = orbitals.shape
    return pl.pallas_call(
        pack_kernel,
        grid=(n,),
        in_specs=[pl.BlockSpec((1, x, y, z), lambda i: (i, 0, 0, 0))],
        out_specs=pl.BlockSpec((1, x // 2, y, 2 * z), lambda i: (i, 0, 0, 0)),
        out_shape=jax.ShapeDtypeStruct((n, x // 2, y, 2 * z), F32),
        name="pack",
    )(orbitals)


def copy_kernel(idx, src_a, src_b, dst_a, dst_b):
    dst_a[...] = src_a[...]
    dst_b[...] = src_b[...]


def gather(packed, lists, m):
    _, h, y, w = packed.shape
    blk = (1, h, y, w)
    out = jax.ShapeDtypeStruct((m, h, y, w), F32)
    return pl.pallas_call(
        copy_kernel,
        grid_spec=pltpu.PrefetchScalarGridSpec(
            num_scalar_prefetch=1,
            grid=(m,),
            in_specs=[
                pl.BlockSpec(blk, lambda i, idx: (idx[0, i], 0, 0, 0)),
                pl.BlockSpec(blk, lambda i, idx: (idx[1, i], 0, 0, 0)),
            ],
            out_specs=[pl.BlockSpec(blk, lambda i, idx: (i, 0, 0, 0))] * 2,
        ),
        out_shape=[out, out],
        name="gather",
    )(lists, packed, packed)


def place(value, room, a, b):
    y, w = value.shape[1:]
    z = w // 2
    room[:, PAD : PAD + y, :] = value
    moved = room[:, pl.ds(PAD - a, y), :]
    moved = pltpu.roll(moved, lax.rem(b + w, w), axis=2)
    pos = lanes(moved.shape) % z - b
    return jnp.where((pos >= 0) & (pos < z), moved, 0.0)


def clear_room(room):
    y = room.shape[1] - 2 * PAD
    room[:, :PAD, :] = jnp.zeros((room.shape[0], PAD, room.shape[2]), F32)
    room[:, PAD + y :, :] = jnp.zeros((room.shape[0], PAD, room.shape[2]), F32)


def density_kernel(plan, own, mine, prior, nxt, partner, density, low, high, room):
    p = pl.program_id(0)
    kind = plan[4, p]
    a, b = plan[5, p], plan[6, p]

    @pl.when(p == 0)
    def _():
        clear_room(room)

    on = plan[7, p] > 0

    def go(src):
        part = place(src[0], room, a, b)
        partner[0] = part
        dens = own[0] * part
        density[0] = dens
        h, y, w = dens.shape
        flat = jnp.concatenate([dens[..., : w // 2], dens[..., w // 2 :]], axis=0)
        top, bot = flat[:EDGE], flat[2 * h - EDGE :]
        low[0] = jnp.concatenate([top[:, : y // 2], top[:, y // 2 :]], axis=-1)
        high[0] = jnp.concatenate([bot[:, : y // 2], bot[:, y // 2 :]], axis=-1)

    for value, src in enumerate((mine, prior, nxt)):
        pl.when(on & (kind == value))(functools.partial(go, src))


def densities(plan, packed, prior, nxt):
    slots = plan.shape[1]
    _, h, y, w = packed.shape
    blk = (1, h, y, w)
    eblk = (1, EDGE, y // 2, w)

    def at(row):
        return pl.BlockSpec(
            blk, lambda i, plan: (plan[row, jnp.minimum(i, plan[8, 1] - 1)], 0, 0, 0)
        )

    full = jax.ShapeDtypeStruct((slots, h, y, w), F32)
    edge = jax.ShapeDtypeStruct((slots,) + eblk[1:], F32)
    here = lambda i, plan: (jnp.minimum(i, plan[8, 1] - 1), 0, 0, 0)
    return pl.pallas_call(
        density_kernel,
        grid_spec=pltpu.PrefetchScalarGridSpec(
            num_scalar_prefetch=1,
            grid=(slots,),
            in_specs=[at(0), at(1), at(2), at(3)],
            out_specs=[
                pl.BlockSpec(blk, here),
                pl.BlockSpec(blk, here),
                pl.BlockSpec(eblk, here),
                pl.BlockSpec(eblk, here),
            ],
            scratch_shapes=[pltpu.VMEM((h, y + 2 * PAD, w), F32)],
        ),
        out_shape=[full, full, edge, edge],
        name="density",
    )(plan, packed, packed, prior, nxt)


def solve_kernel(remote, plan, ends, density, partner, own, below, above, *refs):
    accs, (resid, step_a, step_b, total, mask, room) = refs[:-6], refs[-6:]
    acc = accs[0]
    p = pl.program_id(0)
    h, y, w = density.shape[1:]
    z = w // 2
    rows = h + 2 * EDGE
    group = 4 if h % 4 == 0 else 1

    @pl.when(p == 0)
    def _():
        clear_room(room)
        for ref in accs:
            ref[...] = jnp.zeros(ref.shape, F32)
        for ref in (step_a, step_b):
            ref[:, :8, :] = jnp.zeros((rows, 8, w), F32)
            ref[:, 8 + y :, :] = jnp.zeros((rows, 8, w), F32)
        lane = lanes((1, w))
        first = ends[0] == 0
        last = ends[0] == ends[1] - 1
        for t in range(rows):
            plane = jnp.where(lane < z, t - EDGE, t - EDGE + h)
            outside = ((plane < 0) & first) | ((plane >= 2 * h) & last)
            mask[t] = jnp.where(outside, 0.0, 1.0)

    chosen = (plan[4, p] > 0) if remote else (plan[4, p] == 0)

    @pl.when((plan[7, p] > 0) & chosen)
    def _():
        def unfold(part):
            return jnp.concatenate([part[..., :z], part[..., z:]], axis=1)

        dens = density[0]
        line = jnp.concatenate(
            [unfold(below[0]), dens[..., :z], dens[..., z:], unfold(above[0])], axis=0
        )
        resid[...] = jnp.concatenate([line[:rows], line[h:]], axis=-1)
        step_a[:, 8 : 8 + y, :] = resid[...] * (1.0 / (DIAG * THETA))
        total[...] = step_a[EDGE : EDGE + h, 8 : 8 + y, :]
        lane = lanes((y, w)) % z
        not_low = lane > 0
        not_high = lane < z - 1
        bufs = [step_a, step_b]
        for turn, (keep, gain) in enumerate(coefs()):
            now, then = bufs[turn % 2], bufs[1 - turn % 2]
            core_only = turn == PASSES - 2

            def row(t, now=now, then=then, keep=keep, gain=gain):
                core = now[t, 8 : 8 + y, :]
                near = now[t - 1, 8 : 8 + y, :] + now[t + 1, 8 : 8 + y, :]
                near = near + (now[t, 7 : 7 + y, :] + now[t, 9 : 9 + y, :])
                side = jnp.where(not_low, pltpu.roll(core, 1, axis=1), 0.0)
                side = side + jnp.where(not_high, pltpu.roll(core, w - 1, axis=1), 0.0)
                left = (resid[t] - DIAG * core) + (near + side)
                return left, keep * core + gain * left

            def outer(k, c, row=row, then=then):
                for t in (EDGE - 1 - k, EDGE + h + k):
                    left, fresh = row(t)
                    resid[t] = left
                    then[t, 8 : 8 + y, :] = fresh * mask[t]
                return c

            def inner(k, c, row=row, then=then, last=core_only):
                for g in range(group):
                    t = EDGE + k * group + g
                    left, fresh = row(t)
                    if not last:
                        resid[t] = left
                        then[t, 8 : 8 + y, :] = fresh
                    total[t - EDGE] += fresh
                return c

            if turn + 1 < EDGE:
                lax.fori_loop(0, EDGE - turn - 1, outer, 0)
            lax.fori_loop(0, h // group, inner, 0)

        pot = total[...]
        acc[plan[0, p]] += pot * partner[0]
        back = place(pot * own[0], room, -plan[5, p], -plan[6, p])
        if not remote:
            acc[plan[1, p]] += back
        else:
            for value in (1, 2):

                @pl.when(plan[4, p] == value)
                def _(ref=accs[value], value=value):
                    ref[plan[1 + value, p]] += back


def solve(remote, plan, ends, density, partner, packed, below, above, m):
    slots = plan.shape[1]
    n, h, y, w = packed.shape
    blk = (1, h, y, w)
    eblk = (1, EDGE, y // 2, w)
    rows = h + 2 * EDGE

    def spot(i, plan):
        far = plan[8, 0]
        if remote:
            return jnp.minimum(i, jnp.maximum(far - 1, 0))
        return jnp.clip(i, jnp.minimum(far, plan[8, 1] - 1), plan[8, 1] - 1)

    here = lambda i, plan, ends: (spot(i, plan), 0, 0, 0)
    fixed = lambda i, plan, ends: (0, 0, 0, 0)
    shapes = [(n, h, y, w)] + [(m, h, y, w)] * (2 if remote else 0)
    return pl.pallas_call(
        functools.partial(solve_kernel, remote),
        grid_spec=pltpu.PrefetchScalarGridSpec(
            num_scalar_prefetch=2,
            grid=(slots,),
            in_specs=[
                pl.BlockSpec(blk, here),
                pl.BlockSpec(blk, here),
                pl.BlockSpec(blk, lambda i, plan, ends: (plan[0, spot(i, plan)], 0, 0, 0)),
                pl.BlockSpec(eblk, here),
                pl.BlockSpec(eblk, here),
            ],
            out_specs=[pl.BlockSpec(s, fixed) for s in shapes],
            scratch_shapes=[
                pltpu.VMEM((rows, y, w), F32),
                pltpu.VMEM((rows, y + 16, w), F32),
                pltpu.VMEM((rows, y + 16, w), F32),
                pltpu.VMEM((h, y, w), F32),
                pltpu.VMEM((rows, 1, w), F32),
                pltpu.VMEM((h, y + 2 * PAD, w), F32),
            ],
        ),
        out_shape=[jax.ShapeDtypeStruct(s, F32) for s in shapes],
        compiler_params=pltpu.CompilerParams(vmem_limit_bytes=56 * 1024 * 1024),
        cost_estimate=pl.CostEstimate(
            flops=slots * rows * y * w * 100, bytes_accessed=24 << 20, transcendentals=0
        ),
        name="solve_far" if remote else "solve_near",
    )(plan, ends, density, partner, packed, below, above)


def combine_kernel(back, acc, acc_near, from_next, from_prior, out):
    k = pl.program_id(0)
    h = acc.shape[1]
    z = acc.shape[3] // 2
    value = acc[0] + acc_near[0]
    value = value + jnp.where(back[1, k] > 0, from_next[0], 0.0)
    value = value + jnp.where(back[3, k] > 0, from_prior[0], 0.0)
    out[0, :h] = value[:, :, :z]
    out[0, h:] = value[:, :, z:]


def combine(back, acc, acc_near, from_next, from_prior):
    n, h, y, w = acc.shape
    blk = (1, h, y, w)
    return pl.pallas_call(
        combine_kernel,
        grid_spec=pltpu.PrefetchScalarGridSpec(
            num_scalar_prefetch=1,
            grid=(n,),
            in_specs=[
                pl.BlockSpec(blk, lambda i, back: (i, 0, 0, 0)),
                pl.BlockSpec(blk, lambda i, back: (i, 0, 0, 0)),
                pl.BlockSpec(blk, lambda i, back: (back[0, i], 0, 0, 0)),
                pl.BlockSpec(blk, lambda i, back: (back[2, i], 0, 0, 0)),
            ],
            out_specs=pl.BlockSpec((1, 2 * h, y, w // 2), lambda i, back: (i, 0, 0, 0)),
        ),
        out_shape=jax.ShapeDtypeStruct((n, 2 * h, y, w // 2), F32),
        name="combine",
    )(back, acc, acc_near, from_next, from_prior)


def cycle(field, by):
    size = lax.axis_size(CYCLE)
    return lax.ppermute(field, CYCLE, [(i, (i + by) % size) for i in range(size)])


TASK = 8
LISTS = 256
INFO = 320
PLAN = 384
EARLY = 2
FIXED = 2
SOON = 4
AHEAD = 6
UNROLL = 4
DEPTH = 10
ENDING = 16
STRIP = 8


def factors():
    ratio = THETA / DELTA
    tall = math.acosh(ratio)
    points = [cmath.cosh(complex(tall, k * math.pi / 4)) for k in range(8)]
    marks = [DIAG * (1.0 - (THETA - DELTA * x)) for x in points]
    quads = [(-2.0 * marks[k].real, abs(marks[k]) ** 2) for k in (1, 2, 3)]
    line = -marks[4].real
    coef, resid, value, step = 1.0 / ratio, 1.0, 0.0, 1.0 / (DIAG * THETA)
    value += step
    for keep, gain in coefs():
        resid -= DIAG * step
        step = keep * step + gain * resid
        value += step
    product = line
    for _, c in quads:
        product *= c
    return quads, line, value / product


def front_kernel(
    orbs, pairs, live, fields, every, edges, stage, own, rims, far, edge, table,
    in_sem, out_sem, rim_sem, tab_send, tab_recv, edge_send, edge_recv, far_send, far_recv,
):
    n, h = orbs.shape[0], orbs.shape[1]
    half = h // 2
    halo = edge.shape[1]
    size, width = lax.axis_size(CYCLE), lax.axis_size("orb")
    me = lax.axis_index("grp") * width + lax.axis_index("orb")
    slab = lax.axis_index("slab")

    def peer(s):
        to = lax.rem(me + s, size)
        return {"grp": lax.div(to, width), "orb": lax.rem(to, width)}

    def load(k):
        return pltpu.make_async_copy(orbs.at[k], stage.at[k], in_sem.at[k])

    def order(q):
        return jnp.where(q == 0, 0, jnp.where(q == 1, n - 1, q - 1))

    def begin(q, c):
        load(order(q)).start()
        return c

    lax.fori_loop(0, n, begin, 0)

    barrier = pltpu.get_barrier_semaphore()

    def greet(s, c):
        pl.semaphore_signal(
            barrier, inc=1, device_id=peer(s), device_id_type=pl.DeviceIdType.MESH
        )
        return c

    lax.fori_loop(1, size, greet, 0)
    pl.semaphore_signal(
        barrier, inc=1, device_id={"slab": 1 - slab}, device_id_type=pl.DeviceIdType.MESH
    )
    table[...] = jnp.zeros(table.shape, jnp.int32)
    table[0:2, 0:n] = pairs[...]
    table[2:3, 0:n] = live[...]
    pl.semaphore_wait(barrier, size)

    def share_copy(s, slot):
        return pltpu.make_async_remote_copy(
            src_ref=table, dst_ref=every.at[slot],
            send_sem=tab_send.at[s], recv_sem=tab_recv.at[s],
            device_id=peer(s), device_id_type=pl.DeviceIdType.MESH,
        )

    def share_send(s, c):
        share_copy(s, me).start()
        return c

    lax.fori_loop(1, size, share_send, 0)
    every[me] = table[...]

    def edge_copy(e, f, dst):
        return pltpu.make_async_remote_copy(
            src_ref=edge.at[f], dst_ref=dst,
            send_sem=edge_send.at[e], recv_sem=edge_recv.at[e],
            device_id={"slab": 1 - slab}, device_id_type=pl.DeviceIdType.MESH,
        )

    def own_edge(k, e):
        return edge_copy(e, k, rims.at[k])

    def far_copy(src, f, s):
        return pltpu.make_async_remote_copy(
            src_ref=src, dst_ref=far.at[f, pl.ds(0, half)],
            send_sem=far_send.at[f], recv_sem=far_recv.at[f],
            device_id=peer(s), device_id_type=pl.DeviceIdType.MESH,
        )

    def spot(t):
        return jnp.where(slab == 0, t, h - 1 - t)

    def pack(k):
        def row(r, c):
            own[k, r] = jnp.concatenate(
                [stage[k, spot(r)], stage[k, spot(r + half)]], axis=-1
            )
            return c

        lax.fori_loop(0, half, row, 0)

    def make_edge(k):
        for m in range(halo):
            edge[k, m] = jnp.concatenate(
                [stage[k, spot(h - 1 - m)], stage[k, spot(h - 1 - halo - m)]], axis=-1
            )

    def save(k):
        return pltpu.make_async_copy(
            own.at[k], fields.at[k, pl.ds(0, half)], out_sem.at[k]
        )

    def save_far(f):
        return pltpu.make_async_copy(
            far.at[f, pl.ds(0, half)], fields.at[n + f, pl.ds(0, half)], out_sem.at[n + f]
        )

    def rim(f, src):
        return pltpu.make_async_copy(src, fields.at[f, pl.ds(half, halo)], rim_sem.at[f])

    def keep_edge(k):
        return pltpu.make_async_copy(edge.at[k], edges.at[k], rim_sem.at[k])

    early = edge_send.shape[0] - 4

    up, down = far_copy(own.at[n - 1], 0, 1), far_copy(own.at[0], 1, size - 1)
    for k, send, e in ((0, down, 0), (n - 1, up, 1)):
        load(k).wait()
        pack(k)
        send.start()
        make_edge(k)
        own_edge(k, e).start()
        save(k).start()

    def rest(k, c):
        load(k).wait()
        pack(k)
        save(k).start()
        make_edge(k)
        pl.when(k <= early)(lambda: own_edge(k, 3 + k).start())
        pl.when(k > early)(lambda: keep_edge(k).start())
        return c

    lax.fori_loop(1, n - 1, rest, 0)

    def share_done(s, c):
        share_copy(s, lax.rem(me + size - s, size)).wait()
        return c

    lax.fori_loop(1, size, share_done, 0)

    low = lanes((1, own.shape[-1])) < own.shape[-1] // 2
    for f, copy in ((1, down), (0, up)):
        copy.wait()
        for m in range(halo):
            a, b = far[f, half - 1 - m], far[f, half - 1 - halo - m]
            edge[n + f, m] = jnp.where(low, pltpu.roll(a, a.shape[-1] // 2, axis=1), b)
        edge_copy(2 + f, n + f, far.at[f, pl.ds(half, halo)]).start()
        save_far(f).start()

    own_rims = [(0, 0), (n - 1, 1)] + [(k, 3 + k) for k in range(1, early + 1)]
    for k, e in own_rims:
        own_edge(k, e).wait()
        rim(k, rims.at[k]).start()
    for f in (1, 0):
        edge_copy(2 + f, n + f, far.at[f, pl.ds(half, halo)]).wait()
        rim(n + f, far.at[f, pl.ds(half, halo)]).start()

    def out_done(k, c):
        save(k).wait()
        return c

    def edge_done(k, c):
        keep_edge(k).wait()
        return c

    lax.fori_loop(0, n, out_done, 0)
    lax.fori_loop(early + 1, n - 1, edge_done, 0)
    for k, _ in own_rims:
        rim(k, rims.at[k]).wait()
    for f in (1, 0):
        rim(n + f, far.at[f, pl.ds(half, halo)]).wait()
    for f in range(2):
        save_far(f).wait()


def front(orbitals, pairs, live):
    n, h, y, z = orbitals.shape
    half, halo, w = h // 2, (EDGE + 1) // 2, 2 * z
    size = lax.axis_size(CYCLE)
    vmem = pl.BlockSpec(memory_space=pltpu.VMEM)
    hbm = pl.BlockSpec(memory_space=pl.ANY)
    dma = pltpu.SemaphoreType.DMA
    return pl.pallas_call(
        front_kernel,
        in_specs=[hbm, vmem, vmem],
        out_specs=[hbm, vmem, hbm],
        out_shape=[
            jax.ShapeDtypeStruct((n + 2, half + halo, y, w), F32),
            jax.ShapeDtypeStruct((size, 8, 128), jnp.int32),
            jax.ShapeDtypeStruct((n, halo, y, w), F32),
        ],
        scratch_shapes=[
            pltpu.VMEM((n, h, y, z), F32),
            pltpu.VMEM((n, half, y, w), F32),
            pltpu.VMEM((n, halo, y, w), F32),
            pltpu.VMEM((2, half + halo, y, w), F32),
            pltpu.VMEM((n + 2, halo, y, w), F32),
            pltpu.VMEM((8, 128), jnp.int32),
            dma((n,)), dma((n + 2,)), dma((n + 2,)), dma((size,)), dma((size,)),
            dma((4 + EARLY,)), dma((4 + EARLY,)), dma((2,)), dma((2,)),
        ],
        compiler_params=pltpu.CompilerParams(collective_id=1, has_side_effects=True),
        name="front",
    )(orbitals, pairs.T, live[None])


def plan_kernel(n, combos, every, offsets, plan, which, ups, downs, nups, ndowns, alive, kinds):
    size = every.shape[0]
    width = lax.axis_size("orb")
    me = lax.axis_index("grp") * width + lax.axis_index("orb")
    before, after = lax.rem(me + size - 1, size), lax.rem(me + 1, size)
    block = lambda x: lax.shift_right_logical(x, n.bit_length() - 1)

    def clear(e, c):
        ups[e] = 0
        downs[e] = 0
        nups[e] = 0
        ndowns[e] = 0
        alive[e] = sum(every[e, 2, r] for r in range(n))
        return c

    lax.fori_loop(0, size, clear, 0)

    def read(blk, r):
        i, j = every[blk, 0, r], every[blk, 1, r]
        bj = block(j)
        is_up = bj == jnp.where(blk + 1 == size, 0, blk + 1)
        li, lj = i & (n - 1), j & (n - 1)
        u, v = jnp.where(is_up, li, lj), jnp.where(is_up, lj, li)
        return i, j, bj, u, v, jnp.where(is_up, blk, bj)

    def mark(blk, c):
        def row(r, c):
            i, j, bj, u, v, edge = read(blk, r)

            @pl.when(bj != blk)
            def _():
                for bits, counts, x, free in ((ups, nups, u, n - 1), (downs, ndowns, v, 0)):
                    bit = jnp.where(x == free, 0, lax.shift_left(1, x))
                    had = bits[edge]
                    bits[edge] = had | bit
                    counts[edge] = counts[edge] + jnp.where((had | bit) != had, 1, 0)

            return c

        return lax.fori_loop(2, alive[blk], row, c)

    lax.fori_loop(0, size, mark, 0)

    def widest(e, most):
        o = lax.rem(e, width)
        mine = jnp.where(o % 2 == 0, 2, jnp.where(o == width - 1, 1, 0))
        here = jnp.maximum(nups[e], ndowns[e])
        return tuple(jnp.maximum(m, jnp.where(mine == c, here, 0)) for c, m in enumerate(most))

    most = lax.fori_loop(0, size, widest, (jnp.int32(0),) * 3)
    pick = jnp.int32(len(combos) - 1)
    for c in range(len(combos) - 2, -1, -1):
        fit = functools.reduce(lambda p, q: p & q, [m <= k for m, k in zip(most, combos[c])])
        pick = jnp.where(fit, c, pick)
    which[0] = pick

    def listing(bits, base):
        def step(q, s):
            plan[base + s] = q
            return s + (lax.shift_right_logical(bits, q) & 1)

        for q in range(n):
            plan[base + q] = 0
        return lax.fori_loop(0, n, step, jnp.int32(0))

    listing(ups[me], LISTS)
    listing(downs[before], LISTS + 2 * n)
    plan[INFO + 3] = nups[before]
    plan[INFO + 4] = ndowns[me]

    def rank(bits, x):
        return sum(
            jnp.where(q < x, lax.shift_right_logical(bits, q) & 1, 0) for q in range(n)
        )

    def place_of(x):
        blk, loc = block(x), x & (n - 1)
        low_rank, high_rank = rank(ups[before], loc), rank(downs[me], loc)
        low_at = jnp.where(low_rank == 0, n + 2, n + 3 + low_rank)
        high_at = jnp.where(high_rank == 0, n + 3, 2 * n + 1 + high_rank)
        from_before = jnp.where(loc == n - 1, n, low_at)
        from_after = jnp.where(loc == 0, n + 1, high_at)
        return jnp.where(blk == me, loc, jnp.where(blk == before, from_before, from_after))

    sources = ((me, 2, n), (before, 0, 1), (after, 1, n))

    def survey(b, counts):
        blk, start, skip = sources[b]

        def step(r, counts):
            i, j, bj, u, v, edge = read(blk, r)
            above = edge == me
            free = (bj == blk) | jnp.where(above, v == 0, u == n - 1)
            late = jnp.where(above, rank(downs[me], v), rank(ups[before], u))
            level = jnp.where(free, 0, jnp.where(late == 0, 1, 2))
            level = jnp.where(((blk == me) | (bj == me)) & (r != skip), level, 3)
            kinds[b * n + r] = level
            return tuple(c + jnp.where(level == k, 1, 0) for k, c in enumerate(counts))

        return lax.fori_loop(start, alive[blk], step, counts)

    def settle(b, spots):
        blk, start, _ = sources[b]

        def step(r, spots):
            level = kinds[b * n + r]

            @pl.when(level < 3)
            def _():
                s = jnp.where(level == 0, spots[0], jnp.where(level == 1, spots[1], spots[2]))
                write(s * TASK, every[blk, 0, r], every[blk, 1, r])

            return tuple(c + jnp.where(level == k, 1, 0) for k, c in enumerate(spots))

        return lax.fori_loop(start, alive[blk], step, spots)

    def write(at, i, j):
        plan[at] = place_of(i)
        plan[at + 1] = place_of(j)
        plan[at + 2] = offsets[0, j] - offsets[0, i]
        plan[at + 3] = offsets[1, j] - offsets[1, i]
        plan[at + 4] = jnp.where(block(i) == me, i & (n - 1), n)
        plan[at + 5] = jnp.where(block(j) == me, j & (n - 1), n)

    def blank(s):
        for c, value in enumerate((0, 0, 0, 0, n, n)):
            plan[s * TASK + c] = value

    for s, (blk, r) in enumerate(((me, 1), (after, 0), (me, 0), (before, 1))):
        write(s * TASK, every[blk, 0, r], every[blk, 1, r])
    for s in range(2 * FIXED, 2 * AHEAD):
        blank(s)
    counts = (jnp.int32(0),) * 3
    for b in range(3):
        counts = survey(b, counts)
    first = jnp.int32(2 * FIXED)
    second = jnp.maximum(first + counts[0], 2 * SOON)
    third = jnp.maximum(second + counts[1], 2 * AHEAD)
    spots = (first, second, third)
    for b in range(3):
        spots = settle(b, spots)
    plan[INFO + 6] = third + counts[2]
    blank(third + counts[2])


def make_plan(every, offsets, n, combos):
    size = every.shape[0]
    smem = pl.BlockSpec(memory_space=pltpu.SMEM)
    return pl.pallas_call(
        functools.partial(plan_kernel, n, combos),
        in_specs=[smem, smem],
        out_specs=[smem, smem],
        out_shape=[
            jax.ShapeDtypeStruct((PLAN,), jnp.int32),
            jax.ShapeDtypeStruct((1,), jnp.int32),
        ],
        scratch_shapes=[pltpu.SMEM((size,), jnp.int32)] * 5 + [pltpu.SMEM((3 * n,), jnp.int32)],
        name="plan",
    )(every, offsets.T)


def wipe_room(room, y):
    def step(f, c):
        room[f, :, y:, :] = jnp.zeros((room.shape[1], PAD, room.shape[3]), F32)
        return c

    lax.fori_loop(0, room.shape[0], step, 0)


def repeat(count, unroll, do):
    def step(g, c):
        for q in range(unroll):
            do(g * unroll + q)
        return c

    lax.fori_loop(0, count // unroll, step, 0)


def solver(plan, room, one, two, own2, par2, prod, wheel, moves, basis, basis_back, levels, h):
    rows, tall, w = room.shape[1:]
    y, z = tall - PAD, w // 2
    half = h // 2
    halo = rows - half
    each = rows * tall
    quads, line, _ = factors()

    prod[0] = jnp.zeros((tall, w), F32)
    prod[:, y:, :] = jnp.zeros((h + 1, PAD, w), F32)
    for ref in (one, two):
        planes = ref.shape[0]
        ref[0] = jnp.zeros(ref.shape[1:], F32)
        ref[:, 0:8, :] = jnp.zeros((planes, 8, w), F32)
        ref[:, 8 + y :, :] = jnp.zeros((planes, 8, w), F32)
    flat_room = room.reshape(room.shape[0] * each, w)
    flat_prod = prod.reshape((h + 1) * tall, w)

    k_at = lax.broadcasted_iota(jnp.int32, (2 * w, 2 * w), 0)
    c_at = lax.broadcasted_iota(jnp.int32, (2 * w, 2 * w), 1)
    half_k, task_c, half_c = k_at % w // z, c_at % w // z, c_at // w
    gap = k_at % z - c_at % z
    wheel[...] = jnp.where((task_c == 1) & (half_k == half_c), gap, 4 * z)

    lane = lanes((y, w))
    low = lane < z
    pos = lane % z
    mu = jnp.broadcast_to(levels[...], (STRIP, w))

    def sweep(src, count, emit):
        def step(g, c):
            for r in range(0, y, STRIP):
                at = pl.ds(8 + r, STRIP)
                col = [src[g * UNROLL + q, at, :] for q in range(UNROLL + 2)]
                for q in range(UNROLL):
                    t = g * UNROLL + q
                    sides = src[t + 1, pl.ds(7 + r, STRIP), :] + src[t + 1, pl.ds(9 + r, STRIP), :]
                    emit(t, r, col[q + 1], (col[q] + col[q + 2]) + sides)
            return c

        lax.fori_loop(0, (count + UNROLL - 1) // UNROLL, step, 0)

    def split(values):
        coarse = values.astype(jnp.bfloat16)
        return coarse, (values - coarse.astype(F32)).astype(jnp.bfloat16)

    def turn_z(values, wave):
        both = jnp.dot(
            jnp.concatenate(split(values), axis=1), wave[...], preferred_element_type=F32
        )
        return both[:, :w] + both[:, w:]

    def planes(r):
        return jnp.where(r < half, r, r + half), jnp.where(r < half, r + half, r + half + halo)

    def run(g, gains, backs):
        p, q = g * 2 * TASK, (g * 2 + 1) * TASK
        rp, rq = (plan[p] + 1) * each, (plan[q] + 1) * each
        ap, aq, bp, bq = plan[p + 2], plan[q + 2], plan[p + 3], plan[q + 3]
        sp, sq = (plan[p + 1] + 1) * each - ap, (plan[q + 1] + 1) * each - aq
        moves[...] = jnp.where(wheel[...] == -bq, 1.0, 0.0).astype(jnp.bfloat16)
        fits = low & (pos - bp >= 0) & (pos - bp < z)
        turn_in, flip_in = lax.rem(bp + w, w), lax.rem(bp + w + z, w)

        def waves_of(g):
            raw = []
            for q in range(DEPTH):
                for t in planes(g * DEPTH + q):
                    raw.append(two[t + 1, 8 : 8 + y, :])
            return turn_z(jnp.concatenate(raw, axis=0), basis)

        def keep_waves(g, waves):
            for q in range(DEPTH):
                for side, t in enumerate(planes(g * DEPTH + q)):
                    at = (2 * q + side) * y
                    one[t + 1, 8 : 8 + y, :] = waves[at : at + y]

        def partners(g):
            par = [flat_room[pl.ds(sq + (g * DEPTH + q) * tall, y), :] for q in range(DEPTH)]
            par = jnp.concatenate(split(jnp.concatenate(par, axis=0)), axis=1)
            return jnp.dot(par, moves[...], preferred_element_type=F32)

        def keep_partners(g, par):
            for q in range(DEPTH):
                r = g * DEPTH + q
                own_p = flat_room[pl.ds(rp + r * tall, y), :]
                own_q = flat_room[pl.ds(rq + r * tall, y), :]
                own_a = jnp.where(low, own_p, pltpu.roll(own_q, z, axis=1))
                own_b = jnp.where(low, pltpu.roll(own_p, z, axis=1), own_q)
                par_p = flat_room[pl.ds(sp + r * tall, y), :]
                near_p = jnp.where(fits, pltpu.roll(par_p, turn_in, axis=1), 0.0)
                far_p = jnp.where(fits, pltpu.roll(par_p, flip_in, axis=1), 0.0)
                both_q = par[q * y : (q + 1) * y]
                for t, own, in_p, in_q in (
                    (planes(r)[0], own_a, near_p, both_q[:, :w]),
                    (planes(r)[1], own_b, far_p, both_q[:, w:]),
                ):
                    half_par = in_p + in_q
                    two[t + 1, 8 : 8 + y, :] = own * half_par
                    own2[t] = own
                    par2[t] = half_par

        def dense(g, c):
            waves, par = waves_of(g - 1), partners(g)
            keep_waves(g - 1, waves)
            keep_partners(g, par)
            return c

        turns = rows // DEPTH
        keep_partners(0, partners(0))
        lax.fori_loop(1, turns, dense, 0)
        keep_waves(turns - 1, waves_of(turns - 1))

        def quad(k, c):
            b, c2 = jnp.float32(quads[0][0]), jnp.float32(quads[0][1])
            for m in range(1, len(quads)):
                b = jnp.where(k == m, jnp.float32(quads[m][0]), b)
                c2 = jnp.where(k == m, jnp.float32(quads[m][1]), c2)
            mu_b = mu + b

            def first(t, r, cur, near):
                two[t + 1, pl.ds(8 + r, STRIP), :] = near + mu_b * cur

            def second(t, r, cur, near):
                at = pl.ds(8 + r, STRIP)
                one[t + 1, at, :] = (near + mu * cur) + c2 * one[t + 1, at, :]

            count = h + EDGE - 1 - 2 * k
            sweep(one, count, first)
            sweep(two, count - 1, second)
            return c

        lax.fori_loop(0, len(quads), quad, 0)
        mu_line = mu + line

        def finish(g, c):
            values = [[] for _ in range(ENDING)]
            for r in range(0, y, STRIP):
                at = pl.ds(8 + r, STRIP)
                col = [one[g * ENDING + q, at, :] for q in range(ENDING + 2)]
                for q in range(ENDING):
                    t = g * ENDING + q
                    sides = one[t + 1, pl.ds(7 + r, STRIP), :] + one[t + 1, pl.ds(9 + r, STRIP), :]
                    values[q].append((col[q] + col[q + 2]) + sides + mu_line * col[q + 1])
            both = turn_z(jnp.concatenate(sum(values, []), axis=0), basis_back)
            for q in range(ENDING):
                t = g * ENDING + q
                pot = both[q * y : (q + 1) * y]
                gains[t] = pot * par2[t]
                prod[t + 1, 0:y, :] = pot * own2[t]
            return c

        lax.fori_loop(0, h // ENDING, finish, 0)

        back = pos + jnp.where(low, bp, bq)
        good = (back >= 0) & (back < z)
        spot = jnp.where(good, jnp.where(low, back, back + z), 0)

        def plane(t):
            at = (t + 1) * tall
            value = jnp.where(low, flat_prod[pl.ds(at + ap, y), :], flat_prod[pl.ds(at + aq, y), :])
            backs[t] = jnp.where(good, jnp.take_along_axis(value, spot, axis=1), 0.0)

        repeat(h, 4, plane)

    return run


def solver_scratch(fields, h, y, w, rows):
    planes = 2 * rows
    return [
        pltpu.VMEM((fields + 1, rows, y + PAD, w), F32),
        pltpu.VMEM((planes + 6, y + 16, w), F32),
        pltpu.VMEM((planes + 6, y + 16, w), F32),
        pltpu.VMEM((planes, y, w), F32),
        pltpu.VMEM((planes, y, w), F32),
        pltpu.VMEM((h + 1, y + PAD, w), F32),
        pltpu.VMEM((2 * w, 2 * w), jnp.int32),
        pltpu.VMEM((2 * w, 2 * w), jnp.bfloat16),
    ]


def swap_kernel(
    counts, plan, fields, edges, basis, basis_back, levels, prior, nxt, halos, statics, results,
    room, one, two, own2, par2, prod, wheel, moves, sends, got, trim, hal, parts,
    in_sem, send, recv, edge_send, edge_recv, trim_send, trim_recv, main_sem, rim_sem,
    hal_sem, part_sem,
):
    n, halo, y, w = edges.shape
    rows = fields.shape[1]
    half = rows - halo
    late = hal.shape[0]
    m = sends.shape[1]
    size, width = lax.axis_size(CYCLE), lax.axis_size("orb")
    o = lax.axis_index("orb")
    me = lax.axis_index("grp") * width + o
    slab = lax.axis_index("slab")
    other = {"slab": 1 - slab}

    def peer(s):
        to = lax.rem(me + s, size)
        return {"grp": lax.div(to, width), "orb": lax.rem(to, width)}

    def limit(q):
        return jnp.where(q % 2 == 0, counts[2], jnp.where(q == width - 1, counts[1], counts[0]))

    above, under = limit(o), limit(lax.rem(o + width - 1, width))
    ways = ((0, above, under, prior), (1, under, above, nxt))

    def load(f):
        return pltpu.make_async_copy(fields.at[f], room.at[f + 1, :, pl.ds(0, y)], in_sem.at[f])

    def copy(way, r):
        return pltpu.make_async_remote_copy(
            src_ref=sends.at[way, r], dst_ref=got.at[way, r, pl.ds(0, half)],
            send_sem=send.at[way, r], recv_sem=recv.at[way, r],
            device_id=peer((1, size - 1)[way]), device_id_type=pl.DeviceIdType.MESH,
        )

    def edge_copy(k):
        return pltpu.make_async_remote_copy(
            src_ref=edges.at[n - 1 - late + k], dst_ref=hal.at[k],
            send_sem=edge_send.at[k], recv_sem=edge_recv.at[k],
            device_id=other, device_id_type=pl.DeviceIdType.MESH,
        )

    def keep_hal(k):
        return pltpu.make_async_copy(hal.at[k], halos.at[k], hal_sem.at[k])

    def trim_copy(way, r):
        return pltpu.make_async_remote_copy(
            src_ref=trim.at[way, r], dst_ref=got.at[way, r, pl.ds(half, halo)],
            send_sem=trim_send.at[way, r], recv_sem=trim_recv.at[way, r],
            device_id=other, device_id_type=pl.DeviceIdType.MESH,
        )

    def main_out(way, r, dst):
        part = pl.ds(0, half)
        return pltpu.make_async_copy(got.at[way, r, part], dst.at[r, part], main_sem.at[way, r])

    def rim_out(way, r, dst):
        part = pl.ds(half, halo)
        return pltpu.make_async_copy(got.at[way, r, part], dst.at[r, part], rim_sem.at[way, r])

    def part_out(g):
        return pltpu.make_async_copy(parts.at[g % 2], results.at[g - FIXED], part_sem.at[g % 2])

    def static_out(g):
        return pltpu.make_async_copy(parts.at[g % 2, 0], statics.at[g], part_sem.at[g % 2])

    def out_wait(g):
        pl.when(g < FIXED)(lambda: static_out(g).wait())
        pl.when(g >= FIXED)(lambda: part_out(g).wait())

    def each(start, stop, do):
        def step(k, c):
            do(k)
            return c

        lax.fori_loop(start, stop, step, 0)

    each(0, n + 2, lambda f: load(f).start())
    barrier = pltpu.get_barrier_semaphore()
    for to in (peer(1), peer(size - 1), other):
        pl.semaphore_signal(barrier, inc=1, device_id=to, device_id_type=pl.DeviceIdType.MESH)
    wipe_room(room, y)
    run = solver(
        plan, room, one, two, own2, par2, prod, wheel, moves, basis, basis_back, levels, 2 * half
    )
    pl.semaphore_wait(barrier, 3)
    each(0, late, lambda k: edge_copy(k).start())
    each(0, n + 2, lambda f: load(f).wait())

    def launch(r):
        for way, out, _, _ in ways:
            @pl.when(r < out)
            def _(way=way):
                k = plan[LISTS + way * 2 * n + r]

                def row(t):
                    sends[way, r, t] = room[k + 1, t, 0:y, :]

                each(0, half, row)
                copy(way, r).start()

    each(0, m, launch)
    low = lanes((1, w)) < w // 2

    def land(r):
        for way, _, into, dst in ways:
            @pl.when(r < into)
            def _(way=way, dst=dst):
                copy(way, r).wait_recv()
                main_out(way, r, dst).start()
                for e in range(halo):
                    a, b = got[way, r, half - 1 - e], got[way, r, half - 1 - halo - e]
                    trim[way, r, e] = jnp.where(low, pltpu.roll(a, w // 2, axis=1), b)
                trim_copy(way, r).start()

    def work(g):
        pl.when(g >= 2)(lambda: out_wait(g - 2))

        @pl.when(g == FIXED)
        def _():
            for k in range(late):
                edge_copy(k).wait()
                keep_hal(k).start()
                room[n - late + k, half:, 0:y, :] = hal[k]

        @pl.when(g == SOON)
        def _():
            for way, _, _, dst in ways:
                trim_copy(way, 0).wait()
                rim_out(way, 0, dst).start()

                def row(t):
                    room[n + 3 + way, t, 0:y, :] = got[way, 0, t]

                each(0, rows, row)

        run(g, parts.at[g % 2, 0], parts.at[g % 2, 1])

        @pl.when(g < FIXED)
        def _():
            def merge(t):
                parts[g % 2, 0, t] = jnp.where(low, parts[g % 2, 0, t], parts[g % 2, 1, t])

            repeat(2 * half, 4, merge)
            static_out(g).start()

        pl.when(g >= FIXED)(lambda: part_out(g).start())
        pl.when((g % 2 == 1) & (g // 2 < m))(lambda: land(g // 2))

    each(0, AHEAD, work)
    each(min(AHEAD // 2, m), m, land)
    for k in range(late):
        keep_hal(k).wait()
    for g in range(AHEAD - 2, AHEAD):
        out_wait(g)

    def settle(r):
        for way, out, into, dst in ways:
            @pl.when(r < into)
            def _(way=way, dst=dst):
                trim_copy(way, r).wait()
                rim_out(way, r, dst).start()

            @pl.when(r < out)
            def _(way=way):
                copy(way, r).wait_send()

    for way in range(2):
        copy(way, 0).wait_send()
    each(1, m, settle)

    def close(r):
        for way, _, into, dst in ways:
            @pl.when(r < into)
            def _(way=way, dst=dst):
                main_out(way, r, dst).wait()
                rim_out(way, r, dst).wait()

    each(0, m, close)


def swap(counts, plan, fields, edges, waves, cid):
    n, halo, y, w = edges.shape
    rows = fields.shape[1]
    half, m = rows - halo, max(counts)
    late = n - 2 - EARLY
    hbm = pl.BlockSpec(memory_space=pl.ANY)
    smem = pl.BlockSpec(memory_space=pltpu.SMEM)
    vmem = pl.BlockSpec(memory_space=pltpu.VMEM)
    dma = pltpu.SemaphoreType.DMA
    out = jax.ShapeDtypeStruct((n - 1, rows, y, w), F32)
    return pl.pallas_call(
        functools.partial(swap_kernel, counts),
        in_specs=[smem, hbm, hbm, vmem, vmem, vmem],
        out_specs=[hbm] * 5,
        out_shape=[
            out,
            out,
            jax.ShapeDtypeStruct((late, halo, y, w), F32),
            jax.ShapeDtypeStruct((FIXED, 2 * half, y, w), F32),
            jax.ShapeDtypeStruct((AHEAD - FIXED, 2, 2 * half, y, w), F32),
        ],
        scratch_shapes=solver_scratch(n + 4, 2 * half, y, w, rows)
        + [
            pltpu.VMEM((2, m, half, y, w), F32),
            pltpu.VMEM((2, m, rows, y, w), F32),
            pltpu.VMEM((2, m, halo, y, w), F32),
            pltpu.VMEM((late, halo, y, w), F32),
            pltpu.VMEM((2, 2, 2 * half, y, w), F32),
            dma((n + 2,)), dma((2, m)), dma((2, m)), dma((late,)), dma((late,)),
            dma((2, m)), dma((2, m)), dma((2, m)), dma((2, m)), dma((late,)), dma((2,)),
        ],
        compiler_params=pltpu.CompilerParams(
            collective_id=cid, has_side_effects=True, vmem_limit_bytes=58 * 1024 * 1024
        ),
        name="swap%d%d%d" % counts,
    )(plan, fields, edges, *waves)


def pairs_kernel(
    plan, fields, prior, nxt, halos, statics, results, basis, basis_back, levels, out,
    room, one, two, own2, par2, prod, wheel, moves, acc, stage, parts, sem, hal_sem, acc_sem, out_sem, part_sem,
):
    n, h, y, z = out.shape
    w = 2 * z
    most = prior.shape[0]
    slab = lax.axis_index("slab")

    def part(g):
        return pltpu.make_async_copy(results.at[g], parts.at[g % 2], part_sem.at[g % 2])

    tasks = plan[INFO + 6]

    rows, late = fields.shape[1], halos.shape[0]
    halo = halos.shape[1]

    def field(src, s, f):
        return pltpu.make_async_copy(src.at[s], room.at[f + 1, :, pl.ds(0, y)], sem.at[f])

    def main(f):
        part = pl.ds(0, rows - halo)
        return pltpu.make_async_copy(
            fields.at[f, part], room.at[f + 1, part, pl.ds(0, y)], sem.at[f]
        )

    def rim(f):
        part = pl.ds(rows - halo, halo)
        return pltpu.make_async_copy(
            halos.at[f - (n - 1 - late)], room.at[f + 1, part, pl.ds(0, y)], hal_sem.at[f]
        )

    def each_field(do):
        @pl.when(tasks > 2 * AHEAD)
        def _():
            for f in range(n + 2):
                if n - 1 - late <= f < n - 1:
                    do(main(f))
                    do(rim(f))
                else:
                    do(field(fields, f, f))
            for way, (src, count) in enumerate(((prior, plan[INFO + 3]), (nxt, plan[INFO + 4]))):
                for s in range(most):
                    f = n + 2 + way if s == 0 else n + 3 + way * (n - 2) + s
                    pl.when(s < count)(lambda src=src, s=s, f=f: do(field(src, s, f)))

    def static(g, k):
        return pltpu.make_async_copy(statics.at[g], acc.at[k], acc_sem.at[g])

    part(0).start()
    part(1).start()
    static(0, n - 1).start()
    static(1, 0).start()
    each_field(lambda c: c.start())
    acc[1 : n - 1] = jnp.zeros((n - 2,) + acc.shape[1:], F32)
    wipe_room(room, y)
    run = solver(plan, room, one, two, own2, par2, prod, wheel, moves, basis, basis_back, levels, h)
    low = lanes((y, w)) < w // 2

    def collect(g, gains, backs):
        p, q = g * 2 * TASK, (g * 2 + 1) * TASK
        for k, src, side in (
            (plan[p + 4], gains, low),
            (plan[q + 4], gains, jnp.logical_not(low)),
            (plan[p + 5], backs, low),
            (plan[q + 5], backs, jnp.logical_not(low)),
        ):
            @pl.when(k < n)
            def _(k=k, src=src, side=side):
                def plane(t):
                    acc[k, t] += jnp.where(side, src[t], 0.0)

                repeat(h, 4, plane)

    def gather(g, c):
        part(g).wait()
        collect(g + FIXED, parts.at[g % 2, 0], parts.at[g % 2, 1])
        pl.when(g + 2 < AHEAD - FIXED)(lambda: part(g + 2).start())
        return c

    static(0, n - 1).wait()
    static(1, 0).wait()
    lax.fori_loop(0, AHEAD - FIXED, gather, 0)
    each_field(lambda c: c.wait())

    def group(g, c):
        run(g, parts.at[0, 0], parts.at[0, 1])
        collect(g, parts.at[0, 0], parts.at[0, 1])
        return c

    lax.fori_loop(AHEAD, lax.div(tasks + 1, 2), group, 0)

    def leave(k, slot):
        return pltpu.make_async_copy(stage.at[slot], out.at[k], out_sem.at[slot])

    def write(k, c):
        slot = lax.rem(k, 2)
        pl.when(k >= 2)(lambda: leave(k - 2, slot).wait())

        def plane(t):
            value = acc[k, t]
            value = value + pltpu.roll(value, z, axis=1)
            stage[slot, jnp.where(slab == 0, t, h - 1 - t)] = value[:, :z]

        repeat(h, 8, plane)
        leave(k, slot).start()
        return c

    lax.fori_loop(0, n, write, 0)
    for k in (n - 2, n - 1):
        leave(k, k % 2).wait()


def sines(z):
    k = np.arange(1, z + 1)
    wave = np.sqrt(2.0 / (z + 1)) * np.sin(np.pi * np.outer(k, k) / (z + 1))
    wave = np.kron(np.eye(2), wave).astype(np.float32)
    levels = np.tile(2.0 * np.cos(np.pi * k / (z + 1)), 2).astype(np.float32)[None]

    def parts(values):
        coarse = jnp.asarray(values).astype(jnp.bfloat16)
        fine = (jnp.asarray(values) - coarse.astype(F32)).astype(jnp.bfloat16)
        top = jnp.concatenate([coarse, fine], axis=1)
        bottom = jnp.concatenate([coarse, jnp.zeros_like(fine)], axis=1)
        return jnp.concatenate([top, bottom], axis=0)

    return parts(wave), parts(wave * np.float32(factors()[2])), jnp.asarray(levels)


def solve_pairs(plan, fields, prior, nxt, halos, statics, results, waves, shape):
    n, h, y, z = shape
    w, rows = 2 * z, fields.shape[1]
    most = prior.shape[0]
    hbm = pl.BlockSpec(memory_space=pl.ANY)
    vmem = pl.BlockSpec(memory_space=pltpu.VMEM)
    dma = pltpu.SemaphoreType.DMA
    total = n + 2 + 2 * most
    return pl.pallas_call(
        pairs_kernel,
        grid_spec=pltpu.PrefetchScalarGridSpec(
            num_scalar_prefetch=1,
            grid=(1,),
            in_specs=[hbm] * 6 + [vmem] * 3,
            out_specs=hbm,
            scratch_shapes=solver_scratch(total, h, y, w, rows)
            + [
                pltpu.VMEM((n, h, y, w), F32),
                pltpu.VMEM((2, h, y, z), F32),
                pltpu.VMEM((2, 2, h, y, w), F32),
                dma((total,)), dma((n,)), dma((2,)), dma((2,)), dma((2,)),
            ],
        ),
        out_shape=jax.ShapeDtypeStruct(shape, F32),
        compiler_params=pltpu.CompilerParams(vmem_limit_bytes=58 * 1024 * 1024),
        name="pairs",
    )(plan, fields, prior, nxt, halos, statics, results, *waves)


def fast_body(orbitals, offsets, pairs, live):
    n = orbitals.shape[0]
    combos = [(2, 2, 2), (2, 3, 3), (3, 2, 3), (3, 3, 3), (3, 4, 4), (4, 3, 4), (4, 4, 4)]
    combos.append((n - 1,) * 3)
    waves = sines(orbitals.shape[-1])
    fields, every, edges = front(orbitals, pairs, live)
    plan, which = make_plan(every, offsets, n, combos)

    def branch(counts, cid):
        return lambda _: swap(counts, plan, fields, edges, waves, cid)

    prior, nxt, halos, statics, results = lax.switch(
        which[0], [branch(c, 2 + i) for i, c in enumerate(combos)], 0
    )
    return solve_pairs(
        plan, fields, prior, nxt, halos, statics, results, waves, orbitals.shape
    )


def body(orbitals, offsets, pairs, live):
    n = orbitals.shape[0]
    slots = pairs.shape[0]
    total = offsets.shape[0]
    blocks = total // n
    slabs = lax.axis_size("slab")
    me = lax.axis_index(CYCLE)
    packed = pack(orbitals)

    mine = jnp.concatenate([pairs, live[:, None]], axis=1)
    every = share(jnp.pad(mine, ((0, 0), (0, 128 - mine.shape[1]))))
    ids = jnp.arange(blocks, dtype=jnp.int32)
    second = every[:, :, 1]
    alive = every[:, :, 2] > 0
    orb = jnp.arange(n, dtype=jnp.int32)
    sides = jnp.stack([(ids - 1) % blocks, (ids + 1) % blocks])
    hit = alive[None] & (second[None] // n == sides[:, :, None])
    need = jnp.any(
        hit[..., None] & (second[None, :, :, None] % n == orb), axis=2
    )
    count = jnp.sum(need.astype(jnp.int32), axis=2)
    most = jnp.max(count)

    after, before = (me + 1) % blocks, (me - 1) % blocks
    flags = jnp.stack(
        [need[0, me], need[1, me], need[0, after], need[1, before]]
    ).astype(jnp.int32)
    spot = jnp.sum(
        flags[:, None, :] * (orb[None, :] < orb[:, None]).astype(jnp.int32)[None], axis=2
    )
    lists = jnp.sum(
        (flags[:, None, :] * (spot[:, None, :] == orb[None, :, None])) * orb, axis=2
    )
    back = jnp.stack(
        [spot[2] * flags[2], flags[2], spot[3] * flags[3], flags[3]]
    )

    i, j, on = pairs[:, 0], pairs[:, 1], live > 0
    owner, local = j // n, j % n
    pick_j = (local[:, None] == orb[None, :]).astype(jnp.int32)
    from_prior = (owner == before) & on
    from_next = (owner == after) & on
    kind = jnp.where(from_prior, 1, jnp.where(from_next, 2, 0))
    where_prior = jnp.sum(pick_j * spot[0][None, :], axis=1) * from_prior
    where_next = jnp.sum(pick_j * spot[1][None, :], axis=1) * from_next
    ids_all = jnp.arange(total, dtype=jnp.int32)
    diff = (j[:, None] == ids_all).astype(jnp.int32) - (i[:, None] == ids_all).astype(jnp.int32)
    shift = jnp.sum(diff[:, :, None] * offsets[None], axis=1)
    plan = jnp.stack(
        [i % n, local, where_prior, where_next, kind, shift[:, 0], shift[:, 1], live]
    ).astype(jnp.int32)
    order = jnp.where(on, jnp.where(kind > 0, 0, 1), 2) * slots + jnp.arange(slots)
    rank = jnp.sum((order[None, :] < order[:, None]).astype(jnp.int32), axis=1)
    move = (rank[:, None] == jnp.arange(slots)[None, :]).astype(jnp.int32)
    plan = jnp.sum(plan[:, :, None] * move[None], axis=1)
    far, lively = jnp.sum((kind > 0).astype(jnp.int32)), jnp.sum(on.astype(jnp.int32))
    tail = jnp.where(jnp.arange(slots) == 0, far, lively)
    plan = jnp.concatenate([plan, tail[None]], axis=0)
    ends = jnp.stack([lax.axis_index("slab"), slabs]).astype(jnp.int32)

    up = [(s, s + 1) for s in range(slabs - 1)]
    down = [(s + 1, s) for s in range(slabs - 1)]

    def branch(m):
        def run(_):
            to_next, to_prior = gather(packed, lists[2:], m)
            prior = cycle(to_next, 1)
            nxt = cycle(to_prior, -1)
            partner, density, low, high = densities(plan, packed, prior, nxt)
            below = lax.ppermute(high, "slab", up)
            above = lax.ppermute(low, "slab", down)
            given = (plan, ends, density, partner, packed, below, above, m)
            acc, acc_prior, acc_next = solve(True, *given)
            from_next, from_prior = cycle(acc_prior, -1), cycle(acc_next, 1)
            (acc_near,) = solve(False, *given)
            return combine(back, acc, acc_near, from_next, from_prior)

        return run

    sizes = sorted({min(s, slots - 1) for s in (3, 4, 5)} | {slots - 1})
    which = sum((most > s).astype(jnp.int32) for s in sizes[:-1])
    return lax.switch(which, [branch(s) for s in sizes], 0)


def solution(mesh):
    placed = (
        P(CYCLE, "slab", None, None),
        P(),
        P(CYCLE, None),
        P(CYCLE),
    )
    return jax.shard_map(
        fast_body if mesh.shape["slab"] == 2 else body,
        mesh=mesh,
        in_specs=placed,
        out_specs=P(CYCLE, "slab", None, None),
        check_vma=False,
    )
```

```python
import cmath
import functools
import math

import jax
import jax.numpy as jnp
import numpy as np
from jax import lax
from jax.experimental import pallas as pl
from jax.experimental.pallas import tpu as pltpu
from jax.sharding import PartitionSpec as P

PASSES = 8
DIAG = 6.25
THETA = 1.075
DELTA = 0.925
EDGE = PASSES - 1
PAD = 16
CYCLE = ("grp", "orb")
F32 = jnp.float32


def coefs():
    sigma = THETA / DELTA
    coef = 1.0 / sigma
    out = []
    for _ in range(PASSES - 1):
        new = 1.0 / (2.0 * sigma - coef)
        out.append((new * coef, 2.0 * new / (DELTA * DIAG)))
        coef = new
    return out


def lanes(shape):
    return lax.broadcasted_iota(jnp.int32, shape, len(shape) - 1)


def share_kernel(mine, every, send_sem, recv_sem):
    size, width = lax.axis_size(CYCLE), lax.axis_size("orb")
    me = lax.axis_index("grp") * width + lax.axis_index("orb")

    def peer(s):
        to = lax.rem(me + s, size)
        return {"grp": lax.div(to, width), "orb": lax.rem(to, width)}

    def greet(s, c):
        pl.semaphore_signal(
            barrier, inc=1, device_id=peer(s), device_id_type=pl.DeviceIdType.MESH
        )
        return c

    def copy(s, slot):
        return pltpu.make_async_remote_copy(
            src_ref=mine,
            dst_ref=every.at[slot],
            send_sem=send_sem.at[s],
            recv_sem=recv_sem.at[s],
            device_id=peer(s),
            device_id_type=pl.DeviceIdType.MESH,
        )

    def send(s, c):
        copy(s, me).start()
        return c

    def finish(s, c):
        copy(s, lax.rem(me + size - s, size)).wait()
        return c

    barrier = pltpu.get_barrier_semaphore()
    lax.fori_loop(1, size, greet, 0)
    pl.semaphore_wait(barrier, size - 1)
    lax.fori_loop(1, size, send, 0)
    every[me] = mine[...]
    lax.fori_loop(1, size, finish, 0)


def share(mine):
    size = lax.axis_size(CYCLE)
    vmem = pl.BlockSpec(memory_space=pltpu.VMEM)
    return pl.pallas_call(
        share_kernel,
        in_specs=[vmem],
        out_specs=vmem,
        out_shape=jax.ShapeDtypeStruct((size,) + mine.shape, mine.dtype),
        scratch_shapes=[pltpu.SemaphoreType.DMA((size,)), pltpu.SemaphoreType.DMA((size,))],
        compiler_params=pltpu.CompilerParams(collective_id=0, has_side_effects=True),
        name="share",
    )(mine)


def pack_kernel(src, dst):
    half = dst.shape[1]
    dst[0] = jnp.concatenate([src[0, :half], src[0, half:]], axis=-1)


def pack(orbitals):
    n, x, y, z = orbitals.shape
    return pl.pallas_call(
        pack_kernel,
        grid=(n,),
        in_specs=[pl.BlockSpec((1, x, y, z), lambda i: (i, 0, 0, 0))],
        out_specs=pl.BlockSpec((1, x // 2, y, 2 * z), lambda i: (i, 0, 0, 0)),
        out_shape=jax.ShapeDtypeStruct((n, x // 2, y, 2 * z), F32),
        name="pack",
    )(orbitals)


def copy_kernel(idx, src_a, src_b, dst_a, dst_b):
    dst_a[...] = src_a[...]
    dst_b[...] = src_b[...]


def gather(packed, lists, m):
    _, h, y, w = packed.shape
    blk = (1, h, y, w)
    out = jax.ShapeDtypeStruct((m, h, y, w), F32)
    return pl.pallas_call(
        copy_kernel,
        grid_spec=pltpu.PrefetchScalarGridSpec(
            num_scalar_prefetch=1,
            grid=(m,),
            in_specs=[
                pl.BlockSpec(blk, lambda i, idx: (idx[0, i], 0, 0, 0)),
                pl.BlockSpec(blk, lambda i, idx: (idx[1, i], 0, 0, 0)),
            ],
            out_specs=[pl.BlockSpec(blk, lambda i, idx: (i, 0, 0, 0))] * 2,
        ),
        out_shape=[out, out],
        name="gather",
    )(lists, packed, packed)


def place(value, room, a, b):
    y, w = value.shape[1:]
    z = w // 2
    room[:, PAD : PAD + y, :] = value
    moved = room[:, pl.ds(PAD - a, y), :]
    moved = pltpu.roll(moved, lax.rem(b + w, w), axis=2)
    pos = lanes(moved.shape) % z - b
    return jnp.where((pos >= 0) & (pos < z), moved, 0.0)


def clear_room(room):
    y = room.shape[1] - 2 * PAD
    room[:, :PAD, :] = jnp.zeros((room.shape[0], PAD, room.shape[2]), F32)
    room[:, PAD + y :, :] = jnp.zeros((room.shape[0], PAD, room.shape[2]), F32)


def density_kernel(plan, own, mine, prior, nxt, partner, density, low, high, room):
    p = pl.program_id(0)
    kind = plan[4, p]
    a, b = plan[5, p], plan[6, p]

    @pl.when(p == 0)
    def _():
        clear_room(room)

    on = plan[7, p] > 0

    def go(src):
        part = place(src[0], room, a, b)
        partner[0] = part
        dens = own[0] * part
        density[0] = dens
        h, y, w = dens.shape
        flat = jnp.concatenate([dens[..., : w // 2], dens[..., w // 2 :]], axis=0)
        top, bot = flat[:EDGE], flat[2 * h - EDGE :]
        low[0] = jnp.concatenate([top[:, : y // 2], top[:, y // 2 :]], axis=-1)
        high[0] = jnp.concatenate([bot[:, : y // 2], bot[:, y // 2 :]], axis=-1)

    for value, src in enumerate((mine, prior, nxt)):
        pl.when(on & (kind == value))(functools.partial(go, src))


def densities(plan, packed, prior, nxt):
    slots = plan.shape[1]
    _, h, y, w = packed.shape
    blk = (1, h, y, w)
    eblk = (1, EDGE, y // 2, w)

    def at(row):
        return pl.BlockSpec(
            blk, lambda i, plan: (plan[row, jnp.minimum(i, plan[8, 1] - 1)], 0, 0, 0)
        )

    full = jax.ShapeDtypeStruct((slots, h, y, w), F32)
    edge = jax.ShapeDtypeStruct((slots,) + eblk[1:], F32)
    here = lambda i, plan: (jnp.minimum(i, plan[8, 1] - 1), 0, 0, 0)
    return pl.pallas_call(
        density_kernel,
        grid_spec=pltpu.PrefetchScalarGridSpec(
            num_scalar_prefetch=1,
            grid=(slots,),
            in_specs=[at(0), at(1), at(2), at(3)],
            out_specs=[
                pl.BlockSpec(blk, here),
                pl.BlockSpec(blk, here),
                pl.BlockSpec(eblk, here),
                pl.BlockSpec(eblk, here),
            ],
            scratch_shapes=[pltpu.VMEM((h, y + 2 * PAD, w), F32)],
        ),
        out_shape=[full, full, edge, edge],
        name="density",
    )(plan, packed, packed, prior, nxt)


def solve_kernel(remote, plan, ends, density, partner, own, below, above, *refs):
    accs, (resid, step_a, step_b, total, mask, room) = refs[:-6], refs[-6:]
    acc = accs[0]
    p = pl.program_id(0)
    h, y, w = density.shape[1:]
    z = w // 2
    rows = h + 2 * EDGE
    group = 4 if h % 4 == 0 else 1

    @pl.when(p == 0)
    def _():
        clear_room(room)
        for ref in accs:
            ref[...] = jnp.zeros(ref.shape, F32)
        for ref in (step_a, step_b):
            ref[:, :8, :] = jnp.zeros((rows, 8, w), F32)
            ref[:, 8 + y :, :] = jnp.zeros((rows, 8, w), F32)
        lane = lanes((1, w))
        first = ends[0] == 0
        last = ends[0] == ends[1] - 1
        for t in range(rows):
            plane = jnp.where(lane < z, t - EDGE, t - EDGE + h)
            outside = ((plane < 0) & first) | ((plane >= 2 * h) & last)
            mask[t] = jnp.where(outside, 0.0, 1.0)

    chosen = (plan[4, p] > 0) if remote else (plan[4, p] == 0)

    @pl.when((plan[7, p] > 0) & chosen)
    def _():
        def unfold(part):
            return jnp.concatenate([part[..., :z], part[..., z:]], axis=1)

        dens = density[0]
        line = jnp.concatenate(
            [unfold(below[0]), dens[..., :z], dens[..., z:], unfold(above[0])], axis=0
        )
        resid[...] = jnp.concatenate([line[:rows], line[h:]], axis=-1)
        step_a[:, 8 : 8 + y, :] = resid[...] * (1.0 / (DIAG * THETA))
        total[...] = step_a[EDGE : EDGE + h, 8 : 8 + y, :]
        lane = lanes((y, w)) % z
        not_low = lane > 0
        not_high = lane < z - 1
        bufs = [step_a, step_b]
        for turn, (keep, gain) in enumerate(coefs()):
            now, then = bufs[turn % 2], bufs[1 - turn % 2]
            core_only = turn == PASSES - 2

            def row(t, now=now, then=then, keep=keep, gain=gain):
                core = now[t, 8 : 8 + y, :]
                near = now[t - 1, 8 : 8 + y, :] + now[t + 1, 8 : 8 + y, :]
                near = near + (now[t, 7 : 7 + y, :] + now[t, 9 : 9 + y, :])
                side = jnp.where(not_low, pltpu.roll(core, 1, axis=1), 0.0)
                side = side + jnp.where(not_high, pltpu.roll(core, w - 1, axis=1), 0.0)
                left = (resid[t] - DIAG * core) + (near + side)
                return left, keep * core + gain * left

            def outer(k, c, row=row, then=then):
                for t in (EDGE - 1 - k, EDGE + h + k):
                    left, fresh = row(t)
                    resid[t] = left
                    then[t, 8 : 8 + y, :] = fresh * mask[t]
                return c

            def inner(k, c, row=row, then=then, last=core_only):
                for g in range(group):
                    t = EDGE + k * group + g
                    left, fresh = row(t)
                    if not last:
                        resid[t] = left
                        then[t, 8 : 8 + y, :] = fresh
                    total[t - EDGE] += fresh
                return c

            if turn + 1 < EDGE:
                lax.fori_loop(0, EDGE - turn - 1, outer, 0)
            lax.fori_loop(0, h // group, inner, 0)

        pot = total[...]
        acc[plan[0, p]] += pot * partner[0]
        back = place(pot * own[0], room, -plan[5, p], -plan[6, p])
        if not remote:
            acc[plan[1, p]] += back
        else:
            for value in (1, 2):

                @pl.when(plan[4, p] == value)
                def _(ref=accs[value], value=value):
                    ref[plan[1 + value, p]] += back


def solve(remote, plan, ends, density, partner, packed, below, above, m):
    slots = plan.shape[1]
    n, h, y, w = packed.shape
    blk = (1, h, y, w)
    eblk = (1, EDGE, y // 2, w)
    rows = h + 2 * EDGE

    def spot(i, plan):
        far = plan[8, 0]
        if remote:
            return jnp.minimum(i, jnp.maximum(far - 1, 0))
        return jnp.clip(i, jnp.minimum(far, plan[8, 1] - 1), plan[8, 1] - 1)

    here = lambda i, plan, ends: (spot(i, plan), 0, 0, 0)
    fixed = lambda i, plan, ends: (0, 0, 0, 0)
    shapes = [(n, h, y, w)] + [(m, h, y, w)] * (2 if remote else 0)
    return pl.pallas_call(
        functools.partial(solve_kernel, remote),
        grid_spec=pltpu.PrefetchScalarGridSpec(
            num_scalar_prefetch=2,
            grid=(slots,),
            in_specs=[
                pl.BlockSpec(blk, here),
                pl.BlockSpec(blk, here),
                pl.BlockSpec(blk, lambda i, plan, ends: (plan[0, spot(i, plan)], 0, 0, 0)),
                pl.BlockSpec(eblk, here),
                pl.BlockSpec(eblk, here),
            ],
            out_specs=[pl.BlockSpec(s, fixed) for s in shapes],
            scratch_shapes=[
                pltpu.VMEM((rows, y, w), F32),
                pltpu.VMEM((rows, y + 16, w), F32),
                pltpu.VMEM((rows, y + 16, w), F32),
                pltpu.VMEM((h, y, w), F32),
                pltpu.VMEM((rows, 1, w), F32),
                pltpu.VMEM((h, y + 2 * PAD, w), F32),
            ],
        ),
        out_shape=[jax.ShapeDtypeStruct(s, F32) for s in shapes],
        compiler_params=pltpu.CompilerParams(vmem_limit_bytes=56 * 1024 * 1024),
        cost_estimate=pl.CostEstimate(
            flops=slots * rows * y * w * 100, bytes_accessed=24 << 20, transcendentals=0
        ),
        name="solve_far" if remote else "solve_near",
    )(plan, ends, density, partner, packed, below, above)


def combine_kernel(back, acc, acc_near, from_next, from_prior, out):
    k = pl.program_id(0)
    h = acc.shape[1]
    z = acc.shape[3] // 2
    value = acc[0] + acc_near[0]
    value = value + jnp.where(back[1, k] > 0, from_next[0], 0.0)
    value = value + jnp.where(back[3, k] > 0, from_prior[0], 0.0)
    out[0, :h] = value[:, :, :z]
    out[0, h:] = value[:, :, z:]


def combine(back, acc, acc_near, from_next, from_prior):
    n, h, y, w = acc.shape
    blk = (1, h, y, w)
    return pl.pallas_call(
        combine_kernel,
        grid_spec=pltpu.PrefetchScalarGridSpec(
            num_scalar_prefetch=1,
            grid=(n,),
            in_specs=[
                pl.BlockSpec(blk, lambda i, back: (i, 0, 0, 0)),
                pl.BlockSpec(blk, lambda i, back: (i, 0, 0, 0)),
                pl.BlockSpec(blk, lambda i, back: (back[0, i], 0, 0, 0)),
                pl.BlockSpec(blk, lambda i, back: (back[2, i], 0, 0, 0)),
            ],
            out_specs=pl.BlockSpec((1, 2 * h, y, w // 2), lambda i, back: (i, 0, 0, 0)),
        ),
        out_shape=jax.ShapeDtypeStruct((n, 2 * h, y, w // 2), F32),
        name="combine",
    )(back, acc, acc_near, from_next, from_prior)


def cycle(field, by):
    size = lax.axis_size(CYCLE)
    return lax.ppermute(field, CYCLE, [(i, (i + by) % size) for i in range(size)])


TASK = 8
LISTS = 288
INFO = 320
PLAN = 384
EARLY = 2
FIXED = 2
SOON = 4
AHEAD = 7
UNROLL = 4
DEPTH = 10
ENDING = 16
STRIP = 8


def factors():
    ratio = THETA / DELTA
    tall = math.acosh(ratio)
    points = [cmath.cosh(complex(tall, k * math.pi / 4)) for k in range(8)]
    marks = [DIAG * (1.0 - (THETA - DELTA * x)) for x in points]
    quads = [(-2.0 * marks[k].real, abs(marks[k]) ** 2) for k in (1, 2, 3)]
    line = -marks[4].real
    coef, resid, value, step = 1.0 / ratio, 1.0, 0.0, 1.0 / (DIAG * THETA)
    value += step
    for keep, gain in coefs():
        resid -= DIAG * step
        step = keep * step + gain * resid
        value += step
    product = line
    for _, c in quads:
        product *= c
    return quads, line, value / product


def front_kernel(
    orbs, pairs, live, fields, every, edges, stage, own, rims, far, edge, table,
    in_sem, out_sem, rim_sem, tab_send, tab_recv, edge_send, edge_recv, far_send, far_recv,
):
    n, h = orbs.shape[0], orbs.shape[1]
    half = h // 2
    halo = edge.shape[1]
    size, width = lax.axis_size(CYCLE), lax.axis_size("orb")
    me = lax.axis_index("grp") * width + lax.axis_index("orb")
    slab = lax.axis_index("slab")

    def peer(s):
        to = lax.rem(me + s, size)
        return {"grp": lax.div(to, width), "orb": lax.rem(to, width)}

    def load(k):
        return pltpu.make_async_copy(orbs.at[k], stage.at[k], in_sem.at[k])

    def order(q):
        return jnp.where(q == 0, 0, jnp.where(q == 1, n - 1, q - 1))

    def begin(q, c):
        load(order(q)).start()
        return c

    lax.fori_loop(0, n, begin, 0)

    barrier = pltpu.get_barrier_semaphore()

    def greet(s, c):
        pl.semaphore_signal(
            barrier, inc=1, device_id=peer(s), device_id_type=pl.DeviceIdType.MESH
        )
        return c

    lax.fori_loop(1, size, greet, 0)
    pl.semaphore_signal(
        barrier, inc=1, device_id={"slab": 1 - slab}, device_id_type=pl.DeviceIdType.MESH
    )
    table[...] = jnp.zeros(table.shape, jnp.int32)
    table[0:2, 0:n] = pairs[...]
    table[2:3, 0:n] = live[...]
    pl.semaphore_wait(barrier, size)

    def share_copy(s, slot):
        return pltpu.make_async_remote_copy(
            src_ref=table, dst_ref=every.at[slot],
            send_sem=tab_send.at[s], recv_sem=tab_recv.at[s],
            device_id=peer(s), device_id_type=pl.DeviceIdType.MESH,
        )

    def share_send(s, c):
        share_copy(s, me).start()
        return c

    lax.fori_loop(1, size, share_send, 0)
    every[me] = table[...]

    def edge_copy(e, f, dst):
        return pltpu.make_async_remote_copy(
            src_ref=edge.at[f], dst_ref=dst,
            send_sem=edge_send.at[e], recv_sem=edge_recv.at[e],
            device_id={"slab": 1 - slab}, device_id_type=pl.DeviceIdType.MESH,
        )

    def own_edge(k, e):
        return edge_copy(e, k, rims.at[k])

    def far_copy(src, f, s):
        return pltpu.make_async_remote_copy(
            src_ref=src, dst_ref=far.at[f, pl.ds(0, half)],
            send_sem=far_send.at[f], recv_sem=far_recv.at[f],
            device_id=peer(s), device_id_type=pl.DeviceIdType.MESH,
        )

    def spot(t):
        return jnp.where(slab == 0, t, h - 1 - t)

    def pack(k):
        def row(r, c):
            own[k, r] = jnp.concatenate(
                [stage[k, spot(r)], stage[k, spot(r + half)]], axis=-1
            )
            return c

        lax.fori_loop(0, half, row, 0)

    def make_edge(k):
        for m in range(halo):
            edge[k, m] = jnp.concatenate(
                [stage[k, spot(h - 1 - m)], stage[k, spot(h - 1 - halo - m)]], axis=-1
            )

    def save(k):
        return pltpu.make_async_copy(
            own.at[k], fields.at[k, pl.ds(0, half)], out_sem.at[k]
        )

    def save_far(f):
        return pltpu.make_async_copy(
            far.at[f, pl.ds(0, half)], fields.at[n + f, pl.ds(0, half)], out_sem.at[n + f]
        )

    def rim(f, src):
        return pltpu.make_async_copy(src, fields.at[f, pl.ds(half, halo)], rim_sem.at[f])

    def keep_edge(k):
        return pltpu.make_async_copy(edge.at[k], edges.at[k], rim_sem.at[k])

    early = edge_send.shape[0] - 4

    up, down = far_copy(own.at[n - 1], 0, 1), far_copy(own.at[0], 1, size - 1)
    for k, send, e in ((0, down, 0), (n - 1, up, 1)):
        load(k).wait()
        pack(k)
        send.start()
        make_edge(k)
        own_edge(k, e).start()
        save(k).start()

    def rest(k, c):
        load(k).wait()
        pack(k)
        save(k).start()
        make_edge(k)
        pl.when(k <= early)(lambda: own_edge(k, 3 + k).start())
        pl.when(k > early)(lambda: keep_edge(k).start())
        return c

    lax.fori_loop(1, n - 1, rest, 0)

    def share_done(s, c):
        share_copy(s, lax.rem(me + size - s, size)).wait()
        return c

    lax.fori_loop(1, size, share_done, 0)

    low = lanes((1, own.shape[-1])) < own.shape[-1] // 2
    for f, copy in ((1, down), (0, up)):
        copy.wait()
        for m in range(halo):
            a, b = far[f, half - 1 - m], far[f, half - 1 - halo - m]
            edge[n + f, m] = jnp.where(low, pltpu.roll(a, a.shape[-1] // 2, axis=1), b)
        edge_copy(2 + f, n + f, far.at[f, pl.ds(half, halo)]).start()
        save_far(f).start()

    own_rims = [(0, 0), (n - 1, 1)] + [(k, 3 + k) for k in range(1, early + 1)]
    for k, e in own_rims:
        own_edge(k, e).wait()
        rim(k, rims.at[k]).start()
    for f in (1, 0):
        edge_copy(2 + f, n + f, far.at[f, pl.ds(half, halo)]).wait()
        rim(n + f, far.at[f, pl.ds(half, halo)]).start()

    def out_done(k, c):
        save(k).wait()
        return c

    def edge_done(k, c):
        keep_edge(k).wait()
        return c

    lax.fori_loop(0, n, out_done, 0)
    lax.fori_loop(early + 1, n - 1, edge_done, 0)
    for k, _ in own_rims:
        rim(k, rims.at[k]).wait()
    for f in (1, 0):
        rim(n + f, far.at[f, pl.ds(half, halo)]).wait()
    for f in range(2):
        save_far(f).wait()


def front(orbitals, pairs, live):
    n, h, y, z = orbitals.shape
    half, halo, w = h // 2, (EDGE + 1) // 2, 2 * z
    size = lax.axis_size(CYCLE)
    vmem = pl.BlockSpec(memory_space=pltpu.VMEM)
    hbm = pl.BlockSpec(memory_space=pl.ANY)
    dma = pltpu.SemaphoreType.DMA
    return pl.pallas_call(
        front_kernel,
        in_specs=[hbm, vmem, vmem],
        out_specs=[hbm, vmem, hbm],
        out_shape=[
            jax.ShapeDtypeStruct((n + 2, half + halo, y, w), F32),
            jax.ShapeDtypeStruct((size, 8, 128), jnp.int32),
            jax.ShapeDtypeStruct((n, halo, y, w), F32),
        ],
        scratch_shapes=[
            pltpu.VMEM((n, h, y, z), F32),
            pltpu.VMEM((n, half, y, w), F32),
            pltpu.VMEM((n, halo, y, w), F32),
            pltpu.VMEM((2, half + halo, y, w), F32),
            pltpu.VMEM((n + 2, halo, y, w), F32),
            pltpu.VMEM((8, 128), jnp.int32),
            dma((n,)), dma((n + 2,)), dma((n + 2,)), dma((size,)), dma((size,)),
            dma((4 + EARLY,)), dma((4 + EARLY,)), dma((2,)), dma((2,)),
        ],
        compiler_params=pltpu.CompilerParams(collective_id=1, has_side_effects=True),
        name="front",
    )(orbitals, pairs.T, live[None])


def plan_kernel(n, combos, every, offsets, plan, which, ups, downs, nups, ndowns, alive, kinds):
    size = every.shape[0]
    width = lax.axis_size("orb")
    me = lax.axis_index("grp") * width + lax.axis_index("orb")
    before, after = lax.rem(me + size - 1, size), lax.rem(me + 1, size)
    block = lambda x: lax.shift_right_logical(x, n.bit_length() - 1)

    def clear(e, c):
        ups[e] = 0
        downs[e] = 0
        nups[e] = 0
        ndowns[e] = 0
        alive[e] = sum(every[e, 2, r] for r in range(n))
        return c

    lax.fori_loop(0, size, clear, 0)

    def read(blk, r):
        i, j = every[blk, 0, r], every[blk, 1, r]
        bj = block(j)
        is_up = bj == jnp.where(blk + 1 == size, 0, blk + 1)
        li, lj = i & (n - 1), j & (n - 1)
        u, v = jnp.where(is_up, li, lj), jnp.where(is_up, lj, li)
        return i, j, bj, u, v, jnp.where(is_up, blk, bj)

    def mark(blk, c):
        def row(r, c):
            i, j, bj, u, v, edge = read(blk, r)

            @pl.when(bj != blk)
            def _():
                for bits, counts, x, free in ((ups, nups, u, n - 1), (downs, ndowns, v, 0)):
                    bit = jnp.where(x == free, 0, lax.shift_left(1, x))
                    had = bits[edge]
                    bits[edge] = had | bit
                    counts[edge] = counts[edge] + jnp.where((had | bit) != had, 1, 0)

            return c

        return lax.fori_loop(2, alive[blk], row, c)

    lax.fori_loop(0, size, mark, 0)

    def widest(e, most):
        o = lax.rem(e, width)
        mine = jnp.where(o % 2 == 0, 2, jnp.where(o == width - 1, 1, 0))
        here = jnp.maximum(nups[e], ndowns[e])
        return tuple(jnp.maximum(m, jnp.where(mine == c, here, 0)) for c, m in enumerate(most))

    most = lax.fori_loop(0, size, widest, (jnp.int32(0),) * 3)
    pick = jnp.int32(len(combos) - 1)
    for c in range(len(combos) - 2, -1, -1):
        fit = functools.reduce(lambda p, q: p & q, [m <= k for m, k in zip(most, combos[c])])
        pick = jnp.where(fit, c, pick)
    which[0] = pick

    def listing(bits, base):
        def step(q, s):
            plan[base + s] = q
            return s + (lax.shift_right_logical(bits, q) & 1)

        for q in range(n):
            plan[base + q] = 0
        return lax.fori_loop(0, n, step, jnp.int32(0))

    listing(ups[me], LISTS)
    listing(downs[before], LISTS + 2 * n)
    plan[INFO + 3] = nups[before]
    plan[INFO + 4] = ndowns[me]

    def rank(bits, x):
        return sum(
            jnp.where(q < x, lax.shift_right_logical(bits, q) & 1, 0) for q in range(n)
        )

    def place_of(x):
        blk, loc = block(x), x & (n - 1)
        low_rank, high_rank = rank(ups[before], loc), rank(downs[me], loc)
        low_at = jnp.where(low_rank == 0, n + 2, n + 3 + low_rank)
        high_at = jnp.where(high_rank == 0, n + 3, 2 * n + 1 + high_rank)
        from_before = jnp.where(loc == n - 1, n, low_at)
        from_after = jnp.where(loc == 0, n + 1, high_at)
        return jnp.where(blk == me, loc, jnp.where(blk == before, from_before, from_after))

    sources = ((me, 2, n), (before, 0, 1), (after, 1, n))

    def survey(b, counts):
        blk, start, skip = sources[b]

        def step(r, counts):
            i, j, bj, u, v, edge = read(blk, r)
            above = edge == me
            free = (bj == blk) | jnp.where(above, v == 0, u == n - 1)
            late = jnp.where(above, rank(downs[me], v), rank(ups[before], u))
            level = jnp.where(free, 0, jnp.where(late == 0, 1, 2))
            level = jnp.where(((blk == me) | (bj == me)) & (r != skip), level, 3)
            kinds[b * n + r] = level
            return tuple(c + jnp.where(level == k, 1, 0) for k, c in enumerate(counts))

        return lax.fori_loop(start, alive[blk], step, counts)

    def settle(b, spots):
        blk, start, _ = sources[b]

        def step(r, spots):
            level = kinds[b * n + r]

            @pl.when(level < 3)
            def _():
                s = jnp.where(level == 0, spots[0], jnp.where(level == 1, spots[1], spots[2]))
                write(s * TASK, every[blk, 0, r], every[blk, 1, r])

            return tuple(c + jnp.where(level == k, 1, 0) for k, c in enumerate(spots))

        return lax.fori_loop(start, alive[blk], step, spots)

    def write(at, i, j):
        plan[at] = place_of(i)
        plan[at + 1] = place_of(j)
        plan[at + 2] = offsets[0, j] - offsets[0, i]
        plan[at + 3] = offsets[1, j] - offsets[1, i]
        plan[at + 4] = jnp.where(block(i) == me, i & (n - 1), n)
        plan[at + 5] = jnp.where(block(j) == me, j & (n - 1), n)

    def blank(s):
        for c, value in enumerate((0, 0, 0, 0, n, n)):
            plan[s * TASK + c] = value

    for s, (blk, r) in enumerate(((me, 1), (after, 0), (me, 0), (before, 1))):
        write(s * TASK, every[blk, 0, r], every[blk, 1, r])
    for s in range(2 * FIXED, 2 * AHEAD):
        blank(s)
    counts = (jnp.int32(0),) * 3
    for b in range(3):
        counts = survey(b, counts)
    first = jnp.int32(2 * FIXED)
    second = jnp.maximum(first + counts[0], 2 * SOON)
    third = jnp.maximum(second + counts[1], 2 * AHEAD)
    spots = (first, second, third)
    for b in range(3):
        spots = settle(b, spots)
    plan[INFO + 6] = third + counts[2]
    blank(third + counts[2])


def make_plan(every, offsets, n, combos):
    size = every.shape[0]
    smem = pl.BlockSpec(memory_space=pltpu.SMEM)
    return pl.pallas_call(
        functools.partial(plan_kernel, n, combos),
        in_specs=[smem, smem],
        out_specs=[smem, smem],
        out_shape=[
            jax.ShapeDtypeStruct((PLAN,), jnp.int32),
            jax.ShapeDtypeStruct((1,), jnp.int32),
        ],
        scratch_shapes=[pltpu.SMEM((size,), jnp.int32)] * 5 + [pltpu.SMEM((3 * n,), jnp.int32)],
        name="plan",
    )(every, offsets.T)


def wipe_room(room, y):
    def step(f, c):
        room[f, :, y:, :] = jnp.zeros((room.shape[1], PAD, room.shape[3]), F32)
        return c

    lax.fori_loop(0, room.shape[0], step, 0)


def repeat(count, unroll, do):
    def step(g, c):
        for q in range(unroll):
            do(g * unroll + q)
        return c

    lax.fori_loop(0, count // unroll, step, 0)


def solver(plan, room, one, two, own2, par2, prod, wheel, moves, basis, basis_back, levels, h):
    rows, tall, w = room.shape[1:]
    y, z = tall - PAD, w // 2
    half = h // 2
    halo = rows - half
    each = rows * tall
    quads, line, _ = factors()

    prod[0] = jnp.zeros((tall, w), F32)
    prod[:, y:, :] = jnp.zeros((h + 1, PAD, w), F32)
    for ref in (one, two):
        planes = ref.shape[0]
        ref[0] = jnp.zeros(ref.shape[1:], F32)
        ref[:, 0:8, :] = jnp.zeros((planes, 8, w), F32)
        ref[:, 8 + y :, :] = jnp.zeros((planes, 8, w), F32)
    flat_room = room.reshape(room.shape[0] * each, w)
    flat_prod = prod.reshape((h + 1) * tall, w)

    k_at = lax.broadcasted_iota(jnp.int32, (2 * w, 2 * w), 0)
    c_at = lax.broadcasted_iota(jnp.int32, (2 * w, 2 * w), 1)
    half_k, task_c, half_c = k_at % w // z, c_at % w // z, c_at // w
    gap = k_at % z - c_at % z
    wheel[...] = jnp.where((task_c == 1) & (half_k == half_c), gap, 4 * z)

    lane = lanes((y, w))
    low = lane < z
    pos = lane % z
    mu = jnp.broadcast_to(levels[...], (STRIP, w))

    def sweep(src, count, emit):
        def step(g, c):
            for r in range(0, y, STRIP):
                at = pl.ds(8 + r, STRIP)
                col = [src[g * UNROLL + q, at, :] for q in range(UNROLL + 2)]
                for q in range(UNROLL):
                    t = g * UNROLL + q
                    sides = src[t + 1, pl.ds(7 + r, STRIP), :] + src[t + 1, pl.ds(9 + r, STRIP), :]
                    emit(t, r, col[q + 1], (col[q] + col[q + 2]) + sides)
            return c

        lax.fori_loop(0, (count + UNROLL - 1) // UNROLL, step, 0)

    def split(values):
        coarse = values.astype(jnp.bfloat16)
        return coarse, (values - coarse.astype(F32)).astype(jnp.bfloat16)

    def turn_z(values, wave):
        both = jnp.dot(
            jnp.concatenate(split(values), axis=1), wave[...], preferred_element_type=F32
        )
        return both[:, :w] + both[:, w:]

    def planes(r):
        return jnp.where(r < half, r, r + half), jnp.where(r < half, r + half, r + half + halo)

    def run(g, gains, backs):
        p, q = g * 2 * TASK, (g * 2 + 1) * TASK
        rp, rq = (plan[p] + 1) * each, (plan[q] + 1) * each
        ap, aq, bp, bq = plan[p + 2], plan[q + 2], plan[p + 3], plan[q + 3]
        sp, sq = (plan[p + 1] + 1) * each - ap, (plan[q + 1] + 1) * each - aq
        moves[...] = jnp.where(wheel[...] == -bq, 1.0, 0.0).astype(jnp.bfloat16)
        fits = low & (pos - bp >= 0) & (pos - bp < z)
        turn_in, flip_in = lax.rem(bp + w, w), lax.rem(bp + w + z, w)

        def waves_of(g):
            raw = []
            for q in range(DEPTH):
                for t in planes(g * DEPTH + q):
                    raw.append(two[t + 1, 8 : 8 + y, :])
            return turn_z(jnp.concatenate(raw, axis=0), basis)

        def keep_waves(g, waves):
            for q in range(DEPTH):
                for side, t in enumerate(planes(g * DEPTH + q)):
                    at = (2 * q + side) * y
                    one[t + 1, 8 : 8 + y, :] = waves[at : at + y]

        def partners(g):
            par = [flat_room[pl.ds(sq + (g * DEPTH + q) * tall, y), :] for q in range(DEPTH)]
            par = jnp.concatenate(split(jnp.concatenate(par, axis=0)), axis=1)
            return jnp.dot(par, moves[...], preferred_element_type=F32)

        def keep_partners(g, par):
            for q in range(DEPTH):
                r = g * DEPTH + q
                own_p = flat_room[pl.ds(rp + r * tall, y), :]
                own_q = flat_room[pl.ds(rq + r * tall, y), :]
                own_a = jnp.where(low, own_p, pltpu.roll(own_q, z, axis=1))
                own_b = jnp.where(low, pltpu.roll(own_p, z, axis=1), own_q)
                par_p = flat_room[pl.ds(sp + r * tall, y), :]
                near_p = jnp.where(fits, pltpu.roll(par_p, turn_in, axis=1), 0.0)
                far_p = jnp.where(fits, pltpu.roll(par_p, flip_in, axis=1), 0.0)
                both_q = par[q * y : (q + 1) * y]
                for t, own, in_p, in_q in (
                    (planes(r)[0], own_a, near_p, both_q[:, :w]),
                    (planes(r)[1], own_b, far_p, both_q[:, w:]),
                ):
                    half_par = in_p + in_q
                    two[t + 1, 8 : 8 + y, :] = own * half_par
                    own2[t] = own
                    par2[t] = half_par

        def dense(g, c):
            waves, par = waves_of(g - 1), partners(g)
            keep_waves(g - 1, waves)
            keep_partners(g, par)
            return c

        turns = rows // DEPTH
        keep_partners(0, partners(0))
        lax.fori_loop(1, turns, dense, 0)
        keep_waves(turns - 1, waves_of(turns - 1))

        def quad(k, c):
            b, c2 = jnp.float32(quads[0][0]), jnp.float32(quads[0][1])
            for m in range(1, len(quads)):
                b = jnp.where(k == m, jnp.float32(quads[m][0]), b)
                c2 = jnp.where(k == m, jnp.float32(quads[m][1]), c2)
            mu_b = mu + b

            def first(t, r, cur, near):
                two[t + 1, pl.ds(8 + r, STRIP), :] = near + mu_b * cur

            def second(t, r, cur, near):
                at = pl.ds(8 + r, STRIP)
                one[t + 1, at, :] = (near + mu * cur) + c2 * one[t + 1, at, :]

            count = h + EDGE - 1 - 2 * k
            sweep(one, count, first)
            sweep(two, count - 1, second)
            return c

        lax.fori_loop(0, len(quads), quad, 0)
        mu_line = mu + line

        def finish(g, c):
            values = [[] for _ in range(ENDING)]
            for r in range(0, y, STRIP):
                at = pl.ds(8 + r, STRIP)
                col = [one[g * ENDING + q, at, :] for q in range(ENDING + 2)]
                for q in range(ENDING):
                    t = g * ENDING + q
                    sides = one[t + 1, pl.ds(7 + r, STRIP), :] + one[t + 1, pl.ds(9 + r, STRIP), :]
                    values[q].append((col[q] + col[q + 2]) + sides + mu_line * col[q + 1])
            both = turn_z(jnp.concatenate(sum(values, []), axis=0), basis_back)
            for q in range(ENDING):
                t = g * ENDING + q
                pot = both[q * y : (q + 1) * y]
                gains[t] = pot * par2[t]
                prod[t + 1, 0:y, :] = pot * own2[t]
            return c

        lax.fori_loop(0, h // ENDING, finish, 0)

        back = pos + jnp.where(low, bp, bq)
        good = (back >= 0) & (back < z)
        spot = jnp.where(good, jnp.where(low, back, back + z), 0)

        def plane(t):
            at = (t + 1) * tall
            value = jnp.where(low, flat_prod[pl.ds(at + ap, y), :], flat_prod[pl.ds(at + aq, y), :])
            backs[t] = jnp.where(good, jnp.take_along_axis(value, spot, axis=1), 0.0)

        repeat(h, 4, plane)

    return run


def solver_scratch(fields, h, y, w, rows):
    planes = 2 * rows
    return [
        pltpu.VMEM((fields + 1, rows, y + PAD, w), F32),
        pltpu.VMEM((planes + 6, y + 16, w), F32),
        pltpu.VMEM((planes + 6, y + 16, w), F32),
        pltpu.VMEM((planes, y, w), F32),
        pltpu.VMEM((planes, y, w), F32),
        pltpu.VMEM((h + 1, y + PAD, w), F32),
        pltpu.VMEM((2 * w, 2 * w), jnp.int32),
        pltpu.VMEM((2 * w, 2 * w), jnp.bfloat16),
    ]


def swap_kernel(
    counts, plan, fields, edges, basis, basis_back, levels, prior, nxt, halos, statics, results,
    room, one, two, own2, par2, prod, wheel, moves, sends, got, trim, hal, parts,
    in_sem, send, recv, edge_send, edge_recv, trim_send, trim_recv, main_sem, rim_sem,
    hal_sem, part_sem,
):
    n, halo, y, w = edges.shape
    rows = fields.shape[1]
    half = rows - halo
    late = hal.shape[0]
    m = sends.shape[1]
    size, width = lax.axis_size(CYCLE), lax.axis_size("orb")
    o = lax.axis_index("orb")
    me = lax.axis_index("grp") * width + o
    slab = lax.axis_index("slab")
    other = {"slab": 1 - slab}

    def peer(s):
        to = lax.rem(me + s, size)
        return {"grp": lax.div(to, width), "orb": lax.rem(to, width)}

    def limit(q):
        return jnp.where(q % 2 == 0, counts[2], jnp.where(q == width - 1, counts[1], counts[0]))

    above, under = limit(o), limit(lax.rem(o + width - 1, width))
    ways = ((0, above, under, prior), (1, under, above, nxt))

    def load(f):
        return pltpu.make_async_copy(fields.at[f], room.at[f + 1, :, pl.ds(0, y)], in_sem.at[f])

    def copy(way, r):
        return pltpu.make_async_remote_copy(
            src_ref=sends.at[way, r], dst_ref=got.at[way, r, pl.ds(0, half)],
            send_sem=send.at[way, r], recv_sem=recv.at[way, r],
            device_id=peer((1, size - 1)[way]), device_id_type=pl.DeviceIdType.MESH,
        )

    def edge_copy(k):
        return pltpu.make_async_remote_copy(
            src_ref=edges.at[n - 1 - late + k], dst_ref=hal.at[k],
            send_sem=edge_send.at[k], recv_sem=edge_recv.at[k],
            device_id=other, device_id_type=pl.DeviceIdType.MESH,
        )

    def keep_hal(k):
        return pltpu.make_async_copy(hal.at[k], halos.at[k], hal_sem.at[k])

    def trim_copy(way, r):
        return pltpu.make_async_remote_copy(
            src_ref=trim.at[way, r], dst_ref=got.at[way, r, pl.ds(half, halo)],
            send_sem=trim_send.at[way, r], recv_sem=trim_recv.at[way, r],
            device_id=other, device_id_type=pl.DeviceIdType.MESH,
        )

    def main_out(way, r, dst):
        part = pl.ds(0, half)
        return pltpu.make_async_copy(got.at[way, r, part], dst.at[r, part], main_sem.at[way, r])

    def rim_out(way, r, dst):
        part = pl.ds(half, halo)
        return pltpu.make_async_copy(got.at[way, r, part], dst.at[r, part], rim_sem.at[way, r])

    def part_out(g):
        return pltpu.make_async_copy(parts.at[g % 2], results.at[g - FIXED], part_sem.at[g % 2])

    def static_out(g):
        return pltpu.make_async_copy(parts.at[g % 2, 0], statics.at[g], part_sem.at[g % 2])

    def out_wait(g):
        pl.when(g < FIXED)(lambda: static_out(g).wait())
        pl.when(g >= FIXED)(lambda: part_out(g).wait())

    def each(start, stop, do):
        def step(k, c):
            do(k)
            return c

        lax.fori_loop(start, stop, step, 0)

    each(0, n + 2, lambda f: load(f).start())
    barrier = pltpu.get_barrier_semaphore()
    for to in (peer(1), peer(size - 1), other):
        pl.semaphore_signal(barrier, inc=1, device_id=to, device_id_type=pl.DeviceIdType.MESH)
    wipe_room(room, y)
    run = solver(
        plan, room, one, two, own2, par2, prod, wheel, moves, basis, basis_back, levels, 2 * half
    )
    pl.semaphore_wait(barrier, 3)
    each(0, late, lambda k: edge_copy(k).start())
    each(0, n + 2, lambda f: load(f).wait())

    def launch(r):
        for way, out, _, _ in ways:
            @pl.when(r < out)
            def _(way=way):
                k = plan[LISTS + way * 2 * n + r]

                def row(t):
                    sends[way, r, t] = room[k + 1, t, 0:y, :]

                each(0, half, row)
                copy(way, r).start()

    each(0, m, launch)
    low = lanes((1, w)) < w // 2

    def land(r):
        for way, _, into, dst in ways:
            @pl.when(r < into)
            def _(way=way, dst=dst):
                copy(way, r).wait_recv()
                main_out(way, r, dst).start()
                for e in range(halo):
                    a, b = got[way, r, half - 1 - e], got[way, r, half - 1 - halo - e]
                    trim[way, r, e] = jnp.where(low, pltpu.roll(a, w // 2, axis=1), b)
                trim_copy(way, r).start()

    def work(g):
        pl.when(g >= 2)(lambda: out_wait(g - 2))

        @pl.when(g == FIXED)
        def _():
            for k in range(late):
                edge_copy(k).wait()
                keep_hal(k).start()
                room[n - late + k, half:, 0:y, :] = hal[k]

        @pl.when(g == SOON)
        def _():
            for way, _, _, dst in ways:
                trim_copy(way, 0).wait()
                rim_out(way, 0, dst).start()

                def row(t):
                    room[n + 3 + way, t, 0:y, :] = got[way, 0, t]

                each(0, rows, row)

        run(g, parts.at[g % 2, 0], parts.at[g % 2, 1])

        @pl.when(g < FIXED)
        def _():
            def merge(t):
                parts[g % 2, 0, t] = jnp.where(low, parts[g % 2, 0, t], parts[g % 2, 1, t])

            repeat(2 * half, 4, merge)
            static_out(g).start()

        pl.when(g >= FIXED)(lambda: part_out(g).start())
        r = g // 2 - 1
        pl.when((g % 2 == 0) & (r >= 0) & (r < m))(lambda: land(r))

    each(0, AHEAD, work)
    each(min((AHEAD - 1) // 2, m), m, land)
    for k in range(late):
        keep_hal(k).wait()
    for g in range(AHEAD - 2, AHEAD):
        out_wait(g)

    def settle(r):
        for way, out, into, dst in ways:
            @pl.when(r < into)
            def _(way=way, dst=dst):
                trim_copy(way, r).wait()
                rim_out(way, r, dst).start()

            @pl.when(r < out)
            def _(way=way):
                copy(way, r).wait_send()

    for way in range(2):
        copy(way, 0).wait_send()
    each(1, m, settle)

    def close(r):
        for way, _, into, dst in ways:
            @pl.when(r < into)
            def _(way=way, dst=dst):
                main_out(way, r, dst).wait()
                rim_out(way, r, dst).wait()

    each(0, m, close)


def swap(counts, plan, fields, edges, waves, cid):
    n, halo, y, w = edges.shape
    rows = fields.shape[1]
    half, m = rows - halo, max(counts)
    late = n - 2 - EARLY
    hbm = pl.BlockSpec(memory_space=pl.ANY)
    smem = pl.BlockSpec(memory_space=pltpu.SMEM)
    vmem = pl.BlockSpec(memory_space=pltpu.VMEM)
    dma = pltpu.SemaphoreType.DMA
    out = jax.ShapeDtypeStruct((n - 1, rows, y, w), F32)
    return pl.pallas_call(
        functools.partial(swap_kernel, counts),
        in_specs=[smem, hbm, hbm, vmem, vmem, vmem],
        out_specs=[hbm] * 5,
        out_shape=[
            out,
            out,
            jax.ShapeDtypeStruct((late, halo, y, w), F32),
            jax.ShapeDtypeStruct((FIXED, 2 * half, y, w), F32),
            jax.ShapeDtypeStruct((AHEAD - FIXED, 2, 2 * half, y, w), F32),
        ],
        scratch_shapes=solver_scratch(n + 4, 2 * half, y, w, rows)
        + [
            pltpu.VMEM((2, m, half, y, w), F32),
            pltpu.VMEM((2, m, rows, y, w), F32),
            pltpu.VMEM((2, m, halo, y, w), F32),
            pltpu.VMEM((late, halo, y, w), F32),
            pltpu.VMEM((2, 2, 2 * half, y, w), F32),
            dma((n + 2,)), dma((2, m)), dma((2, m)), dma((late,)), dma((late,)),
            dma((2, m)), dma((2, m)), dma((2, m)), dma((2, m)), dma((late,)), dma((2,)),
        ],
        compiler_params=pltpu.CompilerParams(
            collective_id=cid, has_side_effects=True, vmem_limit_bytes=58 * 1024 * 1024
        ),
        name="swap%d%d%d" % counts,
    )(plan, fields, edges, *waves)


def pairs_kernel(
    plan, fields, prior, nxt, halos, statics, results, basis, basis_back, levels, out,
    room, one, two, own2, par2, prod, wheel, moves, acc, stage, parts, sem, hal_sem, acc_sem, out_sem, part_sem,
):
    n, h, y, z = out.shape
    w = 2 * z
    most = prior.shape[0]
    slab = lax.axis_index("slab")

    def part(g):
        return pltpu.make_async_copy(results.at[g], parts.at[g % 2], part_sem.at[g % 2])

    tasks = plan[INFO + 6]

    rows, late = fields.shape[1], halos.shape[0]
    halo = halos.shape[1]

    def field(src, s, f):
        return pltpu.make_async_copy(src.at[s], room.at[f + 1, :, pl.ds(0, y)], sem.at[f])

    def main(f):
        part = pl.ds(0, rows - halo)
        return pltpu.make_async_copy(
            fields.at[f, part], room.at[f + 1, part, pl.ds(0, y)], sem.at[f]
        )

    def rim(f):
        part = pl.ds(rows - halo, halo)
        return pltpu.make_async_copy(
            halos.at[f - (n - 1 - late)], room.at[f + 1, part, pl.ds(0, y)], hal_sem.at[f]
        )

    def each_field(do):
        @pl.when(tasks > 2 * AHEAD)
        def _():
            for f in range(n + 2):
                if n - 1 - late <= f < n - 1:
                    do(main(f))
                    do(rim(f))
                else:
                    do(field(fields, f, f))
            for way, (src, count) in enumerate(((prior, plan[INFO + 3]), (nxt, plan[INFO + 4]))):
                for s in range(most):
                    f = n + 2 + way if s == 0 else n + 3 + way * (n - 2) + s
                    pl.when(s < count)(lambda src=src, s=s, f=f: do(field(src, s, f)))

    def static(g, k):
        return pltpu.make_async_copy(statics.at[g], acc.at[k], acc_sem.at[g])

    part(0).start()
    part(1).start()
    static(0, n - 1).start()
    static(1, 0).start()
    each_field(lambda c: c.start())
    acc[1 : n - 1] = jnp.zeros((n - 2,) + acc.shape[1:], F32)
    wipe_room(room, y)
    run = solver(plan, room, one, two, own2, par2, prod, wheel, moves, basis, basis_back, levels, h)
    low = lanes((y, w)) < w // 2

    def collect(g, gains, backs):
        p, q = g * 2 * TASK, (g * 2 + 1) * TASK
        for k, src, side in (
            (plan[p + 4], gains, low),
            (plan[q + 4], gains, jnp.logical_not(low)),
            (plan[p + 5], backs, low),
            (plan[q + 5], backs, jnp.logical_not(low)),
        ):
            @pl.when(k < n)
            def _(k=k, src=src, side=side):
                def plane(t):
                    acc[k, t] += jnp.where(side, src[t], 0.0)

                repeat(h, 4, plane)

    def gather(g, c):
        part(g).wait()
        collect(g + FIXED, parts.at[g % 2, 0], parts.at[g % 2, 1])
        pl.when(g + 2 < AHEAD - FIXED)(lambda: part(g + 2).start())
        return c

    static(0, n - 1).wait()
    static(1, 0).wait()
    lax.fori_loop(0, AHEAD - FIXED, gather, 0)
    each_field(lambda c: c.wait())

    def group(g, c):
        run(g, parts.at[0, 0], parts.at[0, 1])
        collect(g, parts.at[0, 0], parts.at[0, 1])
        return c

    lax.fori_loop(AHEAD, lax.div(tasks + 1, 2), group, 0)

    def leave(k, slot):
        return pltpu.make_async_copy(stage.at[slot], out.at[k], out_sem.at[slot])

    def write(k, c):
        slot = lax.rem(k, 2)
        pl.when(k >= 2)(lambda: leave(k - 2, slot).wait())

        def plane(t):
            value = acc[k, t]
            value = value + pltpu.roll(value, z, axis=1)
            stage[slot, jnp.where(slab == 0, t, h - 1 - t)] = value[:, :z]

        repeat(h, 8, plane)
        leave(k, slot).start()
        return c

    lax.fori_loop(0, n, write, 0)
    for k in (n - 2, n - 1):
        leave(k, k % 2).wait()


def sines(z):
    k = np.arange(1, z + 1)
    wave = np.sqrt(2.0 / (z + 1)) * np.sin(np.pi * np.outer(k, k) / (z + 1))
    wave = np.kron(np.eye(2), wave).astype(np.float32)
    levels = np.tile(2.0 * np.cos(np.pi * k / (z + 1)), 2).astype(np.float32)[None]

    def parts(values):
        coarse = jnp.asarray(values).astype(jnp.bfloat16)
        fine = (jnp.asarray(values) - coarse.astype(F32)).astype(jnp.bfloat16)
        top = jnp.concatenate([coarse, fine], axis=1)
        bottom = jnp.concatenate([coarse, jnp.zeros_like(fine)], axis=1)
        return jnp.concatenate([top, bottom], axis=0)

    return parts(wave), parts(wave * np.float32(factors()[2])), jnp.asarray(levels)


def solve_pairs(plan, fields, prior, nxt, halos, statics, results, waves, shape):
    n, h, y, z = shape
    w, rows = 2 * z, fields.shape[1]
    most = prior.shape[0]
    hbm = pl.BlockSpec(memory_space=pl.ANY)
    vmem = pl.BlockSpec(memory_space=pltpu.VMEM)
    dma = pltpu.SemaphoreType.DMA
    total = n + 2 + 2 * most
    return pl.pallas_call(
        pairs_kernel,
        grid_spec=pltpu.PrefetchScalarGridSpec(
            num_scalar_prefetch=1,
            grid=(1,),
            in_specs=[hbm] * 6 + [vmem] * 3,
            out_specs=hbm,
            scratch_shapes=solver_scratch(total, h, y, w, rows)
            + [
                pltpu.VMEM((n, h, y, w), F32),
                pltpu.VMEM((2, h, y, z), F32),
                pltpu.VMEM((2, 2, h, y, w), F32),
                dma((total,)), dma((n,)), dma((2,)), dma((2,)), dma((2,)),
            ],
        ),
        out_shape=jax.ShapeDtypeStruct(shape, F32),
        compiler_params=pltpu.CompilerParams(vmem_limit_bytes=58 * 1024 * 1024),
        name="pairs",
    )(plan, fields, prior, nxt, halos, statics, results, *waves)


def fast_body(orbitals, offsets, pairs, live):
    n = orbitals.shape[0]
    combos = [(2, 2, 2), (2, 3, 3), (3, 2, 3), (3, 3, 3), (3, 4, 4), (4, 3, 4), (4, 4, 4)]
    combos.append((n - 1,) * 3)
    waves = sines(orbitals.shape[-1])
    fields, every, edges = front(orbitals, pairs, live)
    plan, which = make_plan(every, offsets, n, combos)

    def branch(counts, cid):
        return lambda _: swap(counts, plan, fields, edges, waves, cid)

    prior, nxt, halos, statics, results = lax.switch(
        which[0], [branch(c, 2 + i) for i, c in enumerate(combos)], 0
    )
    return solve_pairs(
        plan, fields, prior, nxt, halos, statics, results, waves, orbitals.shape
    )


def body(orbitals, offsets, pairs, live):
    n = orbitals.shape[0]
    slots = pairs.shape[0]
    total = offsets.shape[0]
    blocks = total // n
    slabs = lax.axis_size("slab")
    me = lax.axis_index(CYCLE)
    packed = pack(orbitals)

    mine = jnp.concatenate([pairs, live[:, None]], axis=1)
    every = share(jnp.pad(mine, ((0, 0), (0, 128 - mine.shape[1]))))
    ids = jnp.arange(blocks, dtype=jnp.int32)
    second = every[:, :, 1]
    alive = every[:, :, 2] > 0
    orb = jnp.arange(n, dtype=jnp.int32)
    sides = jnp.stack([(ids - 1) % blocks, (ids + 1) % blocks])
    hit = alive[None] & (second[None] // n == sides[:, :, None])
    need = jnp.any(
        hit[..., None] & (second[None, :, :, None] % n == orb), axis=2
    )
    count = jnp.sum(need.astype(jnp.int32), axis=2)
    most = jnp.max(count)

    after, before = (me + 1) % blocks, (me - 1) % blocks
    flags = jnp.stack(
        [need[0, me], need[1, me], need[0, after], need[1, before]]
    ).astype(jnp.int32)
    spot = jnp.sum(
        flags[:, None, :] * (orb[None, :] < orb[:, None]).astype(jnp.int32)[None], axis=2
    )
    lists = jnp.sum(
        (flags[:, None, :] * (spot[:, None, :] == orb[None, :, None])) * orb, axis=2
    )
    back = jnp.stack(
        [spot[2] * flags[2], flags[2], spot[3] * flags[3], flags[3]]
    )

    i, j, on = pairs[:, 0], pairs[:, 1], live > 0
    owner, local = j // n, j % n
    pick_j = (local[:, None] == orb[None, :]).astype(jnp.int32)
    from_prior = (owner == before) & on
    from_next = (owner == after) & on
    kind = jnp.where(from_prior, 1, jnp.where(from_next, 2, 0))
    where_prior = jnp.sum(pick_j * spot[0][None, :], axis=1) * from_prior
    where_next = jnp.sum(pick_j * spot[1][None, :], axis=1) * from_next
    ids_all = jnp.arange(total, dtype=jnp.int32)
    diff = (j[:, None] == ids_all).astype(jnp.int32) - (i[:, None] == ids_all).astype(jnp.int32)
    shift = jnp.sum(diff[:, :, None] * offsets[None], axis=1)
    plan = jnp.stack(
        [i % n, local, where_prior, where_next, kind, shift[:, 0], shift[:, 1], live]
    ).astype(jnp.int32)
    order = jnp.where(on, jnp.where(kind > 0, 0, 1), 2) * slots + jnp.arange(slots)
    rank = jnp.sum((order[None, :] < order[:, None]).astype(jnp.int32), axis=1)
    move = (rank[:, None] == jnp.arange(slots)[None, :]).astype(jnp.int32)
    plan = jnp.sum(plan[:, :, None] * move[None], axis=1)
    far, lively = jnp.sum((kind > 0).astype(jnp.int32)), jnp.sum(on.astype(jnp.int32))
    tail = jnp.where(jnp.arange(slots) == 0, far, lively)
    plan = jnp.concatenate([plan, tail[None]], axis=0)
    ends = jnp.stack([lax.axis_index("slab"), slabs]).astype(jnp.int32)

    up = [(s, s + 1) for s in range(slabs - 1)]
    down = [(s + 1, s) for s in range(slabs - 1)]

    def branch(m):
        def run(_):
            to_next, to_prior = gather(packed, lists[2:], m)
            prior = cycle(to_next, 1)
            nxt = cycle(to_prior, -1)
            partner, density, low, high = densities(plan, packed, prior, nxt)
            below = lax.ppermute(high, "slab", up)
            above = lax.ppermute(low, "slab", down)
            given = (plan, ends, density, partner, packed, below, above, m)
            acc, acc_prior, acc_next = solve(True, *given)
            from_next, from_prior = cycle(acc_prior, -1), cycle(acc_next, 1)
            (acc_near,) = solve(False, *given)
            return combine(back, acc, acc_near, from_next, from_prior)

        return run

    sizes = sorted({min(s, slots - 1) for s in (3, 4, 5)} | {slots - 1})
    which = sum((most > s).astype(jnp.int32) for s in sizes[:-1])
    return lax.switch(which, [branch(s) for s in sizes], 0)


def solution(mesh):
    placed = (
        P(CYCLE, "slab", None, None),
        P(),
        P(CYCLE, None),
        P(CYCLE),
    )
    return jax.shard_map(
        fast_body if mesh.shape["slab"] == 2 else body,
        mesh=mesh,
        in_specs=placed,
        out_specs=P(CYCLE, "slab", None, None),
        check_vma=False,
    )
```

```python
import cmath
import functools
import math

import jax
import jax.numpy as jnp
import numpy as np
from jax import lax
from jax.experimental import pallas as pl
from jax.experimental.pallas import tpu as pltpu
from jax.sharding import PartitionSpec as P

PASSES = 8
DIAG = 6.25
THETA = 1.075
DELTA = 0.925
EDGE = PASSES - 1
PAD = 16
CYCLE = ("grp", "orb")
F32 = jnp.float32


def coefs():
    sigma = THETA / DELTA
    coef = 1.0 / sigma
    out = []
    for _ in range(PASSES - 1):
        new = 1.0 / (2.0 * sigma - coef)
        out.append((new * coef, 2.0 * new / (DELTA * DIAG)))
        coef = new
    return out


def lanes(shape):
    return lax.broadcasted_iota(jnp.int32, shape, len(shape) - 1)


def share_kernel(mine, every, send_sem, recv_sem):
    size, width = lax.axis_size(CYCLE), lax.axis_size("orb")
    me = lax.axis_index("grp") * width + lax.axis_index("orb")

    def peer(s):
        to = lax.rem(me + s, size)
        return {"grp": lax.div(to, width), "orb": lax.rem(to, width)}

    def greet(s, c):
        pl.semaphore_signal(
            barrier, inc=1, device_id=peer(s), device_id_type=pl.DeviceIdType.MESH
        )
        return c

    def copy(s, slot):
        return pltpu.make_async_remote_copy(
            src_ref=mine,
            dst_ref=every.at[slot],
            send_sem=send_sem.at[s],
            recv_sem=recv_sem.at[s],
            device_id=peer(s),
            device_id_type=pl.DeviceIdType.MESH,
        )

    def send(s, c):
        copy(s, me).start()
        return c

    def finish(s, c):
        copy(s, lax.rem(me + size - s, size)).wait()
        return c

    barrier = pltpu.get_barrier_semaphore()
    lax.fori_loop(1, size, greet, 0)
    pl.semaphore_wait(barrier, size - 1)
    lax.fori_loop(1, size, send, 0)
    every[me] = mine[...]
    lax.fori_loop(1, size, finish, 0)


def share(mine):
    size = lax.axis_size(CYCLE)
    vmem = pl.BlockSpec(memory_space=pltpu.VMEM)
    return pl.pallas_call(
        share_kernel,
        in_specs=[vmem],
        out_specs=vmem,
        out_shape=jax.ShapeDtypeStruct((size,) + mine.shape, mine.dtype),
        scratch_shapes=[pltpu.SemaphoreType.DMA((size,)), pltpu.SemaphoreType.DMA((size,))],
        compiler_params=pltpu.CompilerParams(collective_id=0, has_side_effects=True),
        name="share",
    )(mine)


def pack_kernel(src, dst):
    half = dst.shape[1]
    dst[0] = jnp.concatenate([src[0, :half], src[0, half:]], axis=-1)


def pack(orbitals):
    n, x, y, z = orbitals.shape
    return pl.pallas_call(
        pack_kernel,
        grid=(n,),
        in_specs=[pl.BlockSpec((1, x, y, z), lambda i: (i, 0, 0, 0))],
        out_specs=pl.BlockSpec((1, x // 2, y, 2 * z), lambda i: (i, 0, 0, 0)),
        out_shape=jax.ShapeDtypeStruct((n, x // 2, y, 2 * z), F32),
        name="pack",
    )(orbitals)


def copy_kernel(idx, src_a, src_b, dst_a, dst_b):
    dst_a[...] = src_a[...]
    dst_b[...] = src_b[...]


def gather(packed, lists, m):
    _, h, y, w = packed.shape
    blk = (1, h, y, w)
    out = jax.ShapeDtypeStruct((m, h, y, w), F32)
    return pl.pallas_call(
        copy_kernel,
        grid_spec=pltpu.PrefetchScalarGridSpec(
            num_scalar_prefetch=1,
            grid=(m,),
            in_specs=[
                pl.BlockSpec(blk, lambda i, idx: (idx[0, i], 0, 0, 0)),
                pl.BlockSpec(blk, lambda i, idx: (idx[1, i], 0, 0, 0)),
            ],
            out_specs=[pl.BlockSpec(blk, lambda i, idx: (i, 0, 0, 0))] * 2,
        ),
        out_shape=[out, out],
        name="gather",
    )(lists, packed, packed)


def place(value, room, a, b):
    y, w = value.shape[1:]
    z = w // 2
    room[:, PAD : PAD + y, :] = value
    moved = room[:, pl.ds(PAD - a, y), :]
    moved = pltpu.roll(moved, lax.rem(b + w, w), axis=2)
    pos = lanes(moved.shape) % z - b
    return jnp.where((pos >= 0) & (pos < z), moved, 0.0)


def clear_room(room):
    y = room.shape[1] - 2 * PAD
    room[:, :PAD, :] = jnp.zeros((room.shape[0], PAD, room.shape[2]), F32)
    room[:, PAD + y :, :] = jnp.zeros((room.shape[0], PAD, room.shape[2]), F32)


def density_kernel(plan, own, mine, prior, nxt, partner, density, low, high, room):
    p = pl.program_id(0)
    kind = plan[4, p]
    a, b = plan[5, p], plan[6, p]

    @pl.when(p == 0)
    def _():
        clear_room(room)

    on = plan[7, p] > 0

    def go(src):
        part = place(src[0], room, a, b)
        partner[0] = part
        dens = own[0] * part
        density[0] = dens
        h, y, w = dens.shape
        flat = jnp.concatenate([dens[..., : w // 2], dens[..., w // 2 :]], axis=0)
        top, bot = flat[:EDGE], flat[2 * h - EDGE :]
        low[0] = jnp.concatenate([top[:, : y // 2], top[:, y // 2 :]], axis=-1)
        high[0] = jnp.concatenate([bot[:, : y // 2], bot[:, y // 2 :]], axis=-1)

    for value, src in enumerate((mine, prior, nxt)):
        pl.when(on & (kind == value))(functools.partial(go, src))


def densities(plan, packed, prior, nxt):
    slots = plan.shape[1]
    _, h, y, w = packed.shape
    blk = (1, h, y, w)
    eblk = (1, EDGE, y // 2, w)

    def at(row):
        return pl.BlockSpec(
            blk, lambda i, plan: (plan[row, jnp.minimum(i, plan[8, 1] - 1)], 0, 0, 0)
        )

    full = jax.ShapeDtypeStruct((slots, h, y, w), F32)
    edge = jax.ShapeDtypeStruct((slots,) + eblk[1:], F32)
    here = lambda i, plan: (jnp.minimum(i, plan[8, 1] - 1), 0, 0, 0)
    return pl.pallas_call(
        density_kernel,
        grid_spec=pltpu.PrefetchScalarGridSpec(
            num_scalar_prefetch=1,
            grid=(slots,),
            in_specs=[at(0), at(1), at(2), at(3)],
            out_specs=[
                pl.BlockSpec(blk, here),
                pl.BlockSpec(blk, here),
                pl.BlockSpec(eblk, here),
                pl.BlockSpec(eblk, here),
            ],
            scratch_shapes=[pltpu.VMEM((h, y + 2 * PAD, w), F32)],
        ),
        out_shape=[full, full, edge, edge],
        name="density",
    )(plan, packed, packed, prior, nxt)


def solve_kernel(remote, plan, ends, density, partner, own, below, above, *refs):
    accs, (resid, step_a, step_b, total, mask, room) = refs[:-6], refs[-6:]
    acc = accs[0]
    p = pl.program_id(0)
    h, y, w = density.shape[1:]
    z = w // 2
    rows = h + 2 * EDGE
    group = 4 if h % 4 == 0 else 1

    @pl.when(p == 0)
    def _():
        clear_room(room)
        for ref in accs:
            ref[...] = jnp.zeros(ref.shape, F32)
        for ref in (step_a, step_b):
            ref[:, :8, :] = jnp.zeros((rows, 8, w), F32)
            ref[:, 8 + y :, :] = jnp.zeros((rows, 8, w), F32)
        lane = lanes((1, w))
        first = ends[0] == 0
        last = ends[0] == ends[1] - 1
        for t in range(rows):
            plane = jnp.where(lane < z, t - EDGE, t - EDGE + h)
            outside = ((plane < 0) & first) | ((plane >= 2 * h) & last)
            mask[t] = jnp.where(outside, 0.0, 1.0)

    chosen = (plan[4, p] > 0) if remote else (plan[4, p] == 0)

    @pl.when((plan[7, p] > 0) & chosen)
    def _():
        def unfold(part):
            return jnp.concatenate([part[..., :z], part[..., z:]], axis=1)

        dens = density[0]
        line = jnp.concatenate(
            [unfold(below[0]), dens[..., :z], dens[..., z:], unfold(above[0])], axis=0
        )
        resid[...] = jnp.concatenate([line[:rows], line[h:]], axis=-1)
        step_a[:, 8 : 8 + y, :] = resid[...] * (1.0 / (DIAG * THETA))
        total[...] = step_a[EDGE : EDGE + h, 8 : 8 + y, :]
        lane = lanes((y, w)) % z
        not_low = lane > 0
        not_high = lane < z - 1
        bufs = [step_a, step_b]
        for turn, (keep, gain) in enumerate(coefs()):
            now, then = bufs[turn % 2], bufs[1 - turn % 2]
            core_only = turn == PASSES - 2

            def row(t, now=now, then=then, keep=keep, gain=gain):
                core = now[t, 8 : 8 + y, :]
                near = now[t - 1, 8 : 8 + y, :] + now[t + 1, 8 : 8 + y, :]
                near = near + (now[t, 7 : 7 + y, :] + now[t, 9 : 9 + y, :])
                side = jnp.where(not_low, pltpu.roll(core, 1, axis=1), 0.0)
                side = side + jnp.where(not_high, pltpu.roll(core, w - 1, axis=1), 0.0)
                left = (resid[t] - DIAG * core) + (near + side)
                return left, keep * core + gain * left

            def outer(k, c, row=row, then=then):
                for t in (EDGE - 1 - k, EDGE + h + k):
                    left, fresh = row(t)
                    resid[t] = left
                    then[t, 8 : 8 + y, :] = fresh * mask[t]
                return c

            def inner(k, c, row=row, then=then, last=core_only):
                for g in range(group):
                    t = EDGE + k * group + g
                    left, fresh = row(t)
                    if not last:
                        resid[t] = left
                        then[t, 8 : 8 + y, :] = fresh
                    total[t - EDGE] += fresh
                return c

            if turn + 1 < EDGE:
                lax.fori_loop(0, EDGE - turn - 1, outer, 0)
            lax.fori_loop(0, h // group, inner, 0)

        pot = total[...]
        acc[plan[0, p]] += pot * partner[0]
        back = place(pot * own[0], room, -plan[5, p], -plan[6, p])
        if not remote:
            acc[plan[1, p]] += back
        else:
            for value in (1, 2):

                @pl.when(plan[4, p] == value)
                def _(ref=accs[value], value=value):
                    ref[plan[1 + value, p]] += back


def solve(remote, plan, ends, density, partner, packed, below, above, m):
    slots = plan.shape[1]
    n, h, y, w = packed.shape
    blk = (1, h, y, w)
    eblk = (1, EDGE, y // 2, w)
    rows = h + 2 * EDGE

    def spot(i, plan):
        far = plan[8, 0]
        if remote:
            return jnp.minimum(i, jnp.maximum(far - 1, 0))
        return jnp.clip(i, jnp.minimum(far, plan[8, 1] - 1), plan[8, 1] - 1)

    here = lambda i, plan, ends: (spot(i, plan), 0, 0, 0)
    fixed = lambda i, plan, ends: (0, 0, 0, 0)
    shapes = [(n, h, y, w)] + [(m, h, y, w)] * (2 if remote else 0)
    return pl.pallas_call(
        functools.partial(solve_kernel, remote),
        grid_spec=pltpu.PrefetchScalarGridSpec(
            num_scalar_prefetch=2,
            grid=(slots,),
            in_specs=[
                pl.BlockSpec(blk, here),
                pl.BlockSpec(blk, here),
                pl.BlockSpec(blk, lambda i, plan, ends: (plan[0, spot(i, plan)], 0, 0, 0)),
                pl.BlockSpec(eblk, here),
                pl.BlockSpec(eblk, here),
            ],
            out_specs=[pl.BlockSpec(s, fixed) for s in shapes],
            scratch_shapes=[
                pltpu.VMEM((rows, y, w), F32),
                pltpu.VMEM((rows, y + 16, w), F32),
                pltpu.VMEM((rows, y + 16, w), F32),
                pltpu.VMEM((h, y, w), F32),
                pltpu.VMEM((rows, 1, w), F32),
                pltpu.VMEM((h, y + 2 * PAD, w), F32),
            ],
        ),
        out_shape=[jax.ShapeDtypeStruct(s, F32) for s in shapes],
        compiler_params=pltpu.CompilerParams(vmem_limit_bytes=56 * 1024 * 1024),
        cost_estimate=pl.CostEstimate(
            flops=slots * rows * y * w * 100, bytes_accessed=24 << 20, transcendentals=0
        ),
        name="solve_far" if remote else "solve_near",
    )(plan, ends, density, partner, packed, below, above)


def combine_kernel(back, acc, acc_near, from_next, from_prior, out):
    k = pl.program_id(0)
    h = acc.shape[1]
    z = acc.shape[3] // 2
    value = acc[0] + acc_near[0]
    value = value + jnp.where(back[1, k] > 0, from_next[0], 0.0)
    value = value + jnp.where(back[3, k] > 0, from_prior[0], 0.0)
    out[0, :h] = value[:, :, :z]
    out[0, h:] = value[:, :, z:]


def combine(back, acc, acc_near, from_next, from_prior):
    n, h, y, w = acc.shape
    blk = (1, h, y, w)
    return pl.pallas_call(
        combine_kernel,
        grid_spec=pltpu.PrefetchScalarGridSpec(
            num_scalar_prefetch=1,
            grid=(n,),
            in_specs=[
                pl.BlockSpec(blk, lambda i, back: (i, 0, 0, 0)),
                pl.BlockSpec(blk, lambda i, back: (i, 0, 0, 0)),
                pl.BlockSpec(blk, lambda i, back: (back[0, i], 0, 0, 0)),
                pl.BlockSpec(blk, lambda i, back: (back[2, i], 0, 0, 0)),
            ],
            out_specs=pl.BlockSpec((1, 2 * h, y, w // 2), lambda i, back: (i, 0, 0, 0)),
        ),
        out_shape=jax.ShapeDtypeStruct((n, 2 * h, y, w // 2), F32),
        name="combine",
    )(back, acc, acc_near, from_next, from_prior)


def cycle(field, by):
    size = lax.axis_size(CYCLE)
    return lax.ppermute(field, CYCLE, [(i, (i + by) % size) for i in range(size)])


TASK = 8
LISTS = 288
INFO = 320
PLAN = 384
EARLY = 1
FIXED = 2
SOON = 4
AHEAD = 7
UNROLL = 4
DEPTH = 10
ENDING = 16
STRIP = 8


def factors():
    ratio = THETA / DELTA
    tall = math.acosh(ratio)
    points = [cmath.cosh(complex(tall, k * math.pi / 4)) for k in range(8)]
    marks = [DIAG * (1.0 - (THETA - DELTA * x)) for x in points]
    quads = [(-2.0 * marks[k].real, abs(marks[k]) ** 2) for k in (1, 2, 3)]
    line = -marks[4].real
    coef, resid, value, step = 1.0 / ratio, 1.0, 0.0, 1.0 / (DIAG * THETA)
    value += step
    for keep, gain in coefs():
        resid -= DIAG * step
        step = keep * step + gain * resid
        value += step
    product = line
    for _, c in quads:
        product *= c
    return quads, line, value / product


def front_kernel(
    orbs, pairs, live, fields, every, edges, stage, own, rims, far, edge, table,
    in_sem, out_sem, rim_sem, tab_send, tab_recv, edge_send, edge_recv, far_send, far_recv,
):
    n, h = orbs.shape[0], orbs.shape[1]
    half = h // 2
    halo = edge.shape[1]
    size, width = lax.axis_size(CYCLE), lax.axis_size("orb")
    me = lax.axis_index("grp") * width + lax.axis_index("orb")
    slab = lax.axis_index("slab")

    def peer(s):
        to = lax.rem(me + s, size)
        return {"grp": lax.div(to, width), "orb": lax.rem(to, width)}

    def load(k):
        return pltpu.make_async_copy(orbs.at[k], stage.at[k], in_sem.at[k])

    def order(q):
        return jnp.where(q == 0, 0, jnp.where(q == 1, n - 1, q - 1))

    def begin(q, c):
        load(order(q)).start()
        return c

    lax.fori_loop(0, n, begin, 0)

    barrier = pltpu.get_barrier_semaphore()

    def greet(s, c):
        pl.semaphore_signal(
            barrier, inc=1, device_id=peer(s), device_id_type=pl.DeviceIdType.MESH
        )
        return c

    lax.fori_loop(1, size, greet, 0)
    pl.semaphore_signal(
        barrier, inc=1, device_id={"slab": 1 - slab}, device_id_type=pl.DeviceIdType.MESH
    )
    table[...] = jnp.zeros(table.shape, jnp.int32)
    table[0:2, 0:n] = pairs[...]
    table[2:3, 0:n] = live[...]
    pl.semaphore_wait(barrier, size)

    def share_copy(s, slot):
        return pltpu.make_async_remote_copy(
            src_ref=table, dst_ref=every.at[slot],
            send_sem=tab_send.at[s], recv_sem=tab_recv.at[s],
            device_id=peer(s), device_id_type=pl.DeviceIdType.MESH,
        )

    def share_send(s, c):
        share_copy(s, me).start()
        return c

    lax.fori_loop(1, size, share_send, 0)
    every[me] = table[...]

    def edge_copy(e, f, dst):
        return pltpu.make_async_remote_copy(
            src_ref=edge.at[f], dst_ref=dst,
            send_sem=edge_send.at[e], recv_sem=edge_recv.at[e],
            device_id={"slab": 1 - slab}, device_id_type=pl.DeviceIdType.MESH,
        )

    def own_edge(k, e):
        return edge_copy(e, k, rims.at[k])

    def far_copy(k, f, s, part):
        some = pl.ds((1 - part) * (half // 2), half // 2)
        return pltpu.make_async_remote_copy(
            src_ref=own.at[k, some], dst_ref=far.at[f, some],
            send_sem=far_send.at[2 * f + part], recv_sem=far_recv.at[2 * f + part],
            device_id=peer(s), device_id_type=pl.DeviceIdType.MESH,
        )

    def spot(t):
        return jnp.where(slab == 0, t, h - 1 - t)

    def pack(k):
        def row(r, c):
            own[k, r] = jnp.concatenate(
                [stage[k, spot(r)], stage[k, spot(r + half)]], axis=-1
            )
            return c

        lax.fori_loop(0, half, row, 0)

    def make_edge(k):
        for m in range(halo):
            edge[k, m] = jnp.concatenate(
                [stage[k, spot(h - 1 - m)], stage[k, spot(h - 1 - halo - m)]], axis=-1
            )

    def save(k):
        return pltpu.make_async_copy(
            own.at[k], fields.at[k, pl.ds(0, half)], out_sem.at[k]
        )

    def save_far(f):
        return pltpu.make_async_copy(
            far.at[f, pl.ds(0, half)], fields.at[n + f, pl.ds(0, half)], out_sem.at[n + f]
        )

    def rim(f, src):
        return pltpu.make_async_copy(src, fields.at[f, pl.ds(half, halo)], rim_sem.at[f])

    def keep_edge(k):
        return pltpu.make_async_copy(edge.at[k], edges.at[k], rim_sem.at[k])

    early = edge_send.shape[0] - 4

    up = [far_copy(n - 1, 0, 1, part) for part in range(2)]
    down = [far_copy(0, 1, size - 1, part) for part in range(2)]
    for k, send, e in ((0, down, 0), (n - 1, up, 1)):
        load(k).wait()
        pack(k)
        for part in send:
            part.start()
        make_edge(k)
        own_edge(k, e).start()
        save(k).start()

    def rest(k, c):
        load(k).wait()
        pack(k)
        save(k).start()
        make_edge(k)
        pl.when(k <= early)(lambda: own_edge(k, 3 + k).start())
        pl.when(k > early)(lambda: keep_edge(k).start())
        return c

    lax.fori_loop(1, n - 1, rest, 0)

    low = lanes((1, own.shape[-1])) < own.shape[-1] // 2
    for f, copy in ((1, down), (0, up)):
        copy[0].wait()
        for m in range(halo):
            a, b = far[f, half - 1 - m], far[f, half - 1 - halo - m]
            edge[n + f, m] = jnp.where(low, pltpu.roll(a, a.shape[-1] // 2, axis=1), b)
        edge_copy(2 + f, n + f, far.at[f, pl.ds(half, halo)]).start()

    for f, copy in ((1, down), (0, up)):
        copy[1].wait()
        save_far(f).start()

    def share_done(s, c):
        share_copy(s, lax.rem(me + size - s, size)).wait()
        return c

    lax.fori_loop(1, size, share_done, 0)

    own_rims = [(0, 0), (n - 1, 1)] + [(k, 3 + k) for k in range(1, early + 1)]
    for k, e in own_rims:
        own_edge(k, e).wait()
        rim(k, rims.at[k]).start()
    for f in (1, 0):
        edge_copy(2 + f, n + f, far.at[f, pl.ds(half, halo)]).wait()
        rim(n + f, far.at[f, pl.ds(half, halo)]).start()

    def out_done(k, c):
        save(k).wait()
        return c

    def edge_done(k, c):
        keep_edge(k).wait()
        return c

    lax.fori_loop(0, n, out_done, 0)
    lax.fori_loop(early + 1, n - 1, edge_done, 0)
    for k, _ in own_rims:
        rim(k, rims.at[k]).wait()
    for f in (1, 0):
        rim(n + f, far.at[f, pl.ds(half, halo)]).wait()
    for f in range(2):
        save_far(f).wait()


def front(orbitals, pairs, live):
    n, h, y, z = orbitals.shape
    half, halo, w = h // 2, (EDGE + 1) // 2, 2 * z
    size = lax.axis_size(CYCLE)
    vmem = pl.BlockSpec(memory_space=pltpu.VMEM)
    hbm = pl.BlockSpec(memory_space=pl.ANY)
    dma = pltpu.SemaphoreType.DMA
    return pl.pallas_call(
        front_kernel,
        in_specs=[hbm, vmem, vmem],
        out_specs=[hbm, vmem, hbm],
        out_shape=[
            jax.ShapeDtypeStruct((n + 2, half + halo, y, w), F32),
            jax.ShapeDtypeStruct((size, 8, 128), jnp.int32),
            jax.ShapeDtypeStruct((n, halo, y, w), F32),
        ],
        scratch_shapes=[
            pltpu.VMEM((n, h, y, z), F32),
            pltpu.VMEM((n, half, y, w), F32),
            pltpu.VMEM((n, halo, y, w), F32),
            pltpu.VMEM((2, half + halo, y, w), F32),
            pltpu.VMEM((n + 2, halo, y, w), F32),
            pltpu.VMEM((8, 128), jnp.int32),
            dma((n,)), dma((n + 2,)), dma((n + 2,)), dma((size,)), dma((size,)),
            dma((4 + EARLY,)), dma((4 + EARLY,)), dma((4,)), dma((4,)),
        ],
        compiler_params=pltpu.CompilerParams(collective_id=1, has_side_effects=True),
        name="front",
    )(orbitals, pairs.T, live[None])


def plan_kernel(n, combos, every, offsets, plan, which, ups, downs, nups, ndowns, alive, kinds):
    size = every.shape[0]
    width = lax.axis_size("orb")
    me = lax.axis_index("grp") * width + lax.axis_index("orb")
    before, after = lax.rem(me + size - 1, size), lax.rem(me + 1, size)
    block = lambda x: lax.shift_right_logical(x, n.bit_length() - 1)

    def clear(e, c):
        ups[e] = 0
        downs[e] = 0
        nups[e] = 0
        ndowns[e] = 0
        alive[e] = sum(every[e, 2, r] for r in range(n))
        return c

    lax.fori_loop(0, size, clear, 0)

    def read(blk, r):
        i, j = every[blk, 0, r], every[blk, 1, r]
        bj = block(j)
        is_up = bj == jnp.where(blk + 1 == size, 0, blk + 1)
        li, lj = i & (n - 1), j & (n - 1)
        u, v = jnp.where(is_up, li, lj), jnp.where(is_up, lj, li)
        return i, j, bj, u, v, jnp.where(is_up, blk, bj)

    def mark(blk, c):
        def row(r, c):
            i, j, bj, u, v, edge = read(blk, r)

            @pl.when(bj != blk)
            def _():
                for bits, counts, x, free in ((ups, nups, u, n - 1), (downs, ndowns, v, 0)):
                    bit = jnp.where(x == free, 0, lax.shift_left(1, x))
                    had = bits[edge]
                    bits[edge] = had | bit
                    counts[edge] = counts[edge] + jnp.where((had | bit) != had, 1, 0)

            return c

        return lax.fori_loop(2, alive[blk], row, c)

    lax.fori_loop(0, size, mark, 0)

    def widest(e, most):
        o = lax.rem(e, width)
        mine = jnp.where(o % 2 == 0, 2, jnp.where(o == width - 1, 1, 0))
        here = jnp.maximum(nups[e], ndowns[e])
        return tuple(jnp.maximum(m, jnp.where(mine == c, here, 0)) for c, m in enumerate(most))

    most = lax.fori_loop(0, size, widest, (jnp.int32(0),) * 3)
    pick = jnp.int32(len(combos) - 1)
    for c in range(len(combos) - 2, -1, -1):
        fit = functools.reduce(lambda p, q: p & q, [m <= k for m, k in zip(most, combos[c])])
        pick = jnp.where(fit, c, pick)
    which[0] = pick

    def listing(bits, base):
        def step(q, s):
            plan[base + s] = q
            return s + (lax.shift_right_logical(bits, q) & 1)

        for q in range(n):
            plan[base + q] = 0
        return lax.fori_loop(0, n, step, jnp.int32(0))

    listing(ups[me], LISTS)
    listing(downs[before], LISTS + 2 * n)
    plan[INFO + 3] = nups[before]
    plan[INFO + 4] = ndowns[me]

    def rank(bits, x):
        return sum(
            jnp.where(q < x, lax.shift_right_logical(bits, q) & 1, 0) for q in range(n)
        )

    def place_of(x):
        blk, loc = block(x), x & (n - 1)
        low_rank, high_rank = rank(ups[before], loc), rank(downs[me], loc)
        low_at = jnp.where(low_rank == 0, n + 2, n + 3 + low_rank)
        high_at = jnp.where(high_rank == 0, n + 3, 2 * n + 1 + high_rank)
        from_before = jnp.where(loc == n - 1, n, low_at)
        from_after = jnp.where(loc == 0, n + 1, high_at)
        return jnp.where(blk == me, loc, jnp.where(blk == before, from_before, from_after))

    sources = ((me, 2, n), (before, 0, 1), (after, 1, n))

    def survey(b, counts):
        blk, start, skip = sources[b]

        def step(r, counts):
            i, j, bj, u, v, edge = read(blk, r)
            above = edge == me
            free = (bj == blk) | jnp.where(above, v == 0, u == n - 1)
            late = jnp.where(above, rank(downs[me], v), rank(ups[before], u))
            level = jnp.where(free, 0, jnp.where(late == 0, 1, 2))
            level = jnp.where(((blk == me) | (bj == me)) & (r != skip), level, 3)
            kinds[b * n + r] = level
            return tuple(c + jnp.where(level == k, 1, 0) for k, c in enumerate(counts))

        return lax.fori_loop(start, alive[blk], step, counts)

    def settle(b, spots):
        blk, start, _ = sources[b]

        def step(r, spots):
            level = kinds[b * n + r]

            @pl.when(level < 3)
            def _():
                s = jnp.where(level == 0, spots[0], jnp.where(level == 1, spots[1], spots[2]))
                write(s * TASK, every[blk, 0, r], every[blk, 1, r])

            return tuple(c + jnp.where(level == k, 1, 0) for k, c in enumerate(spots))

        return lax.fori_loop(start, alive[blk], step, spots)

    def write(at, i, j):
        plan[at] = place_of(i)
        plan[at + 1] = place_of(j)
        plan[at + 2] = offsets[0, j] - offsets[0, i]
        plan[at + 3] = offsets[1, j] - offsets[1, i]
        plan[at + 4] = jnp.where(block(i) == me, i & (n - 1), n)
        plan[at + 5] = jnp.where(block(j) == me, j & (n - 1), n)

    def blank(s):
        for c, value in enumerate((0, 0, 0, 0, n, n)):
            plan[s * TASK + c] = value

    for s, (blk, r) in enumerate(((me, 1), (after, 0), (me, 0), (before, 1))):
        write(s * TASK, every[blk, 0, r], every[blk, 1, r])
    for s in range(2 * FIXED, 2 * AHEAD):
        blank(s)
    counts = (jnp.int32(0),) * 3
    for b in range(3):
        counts = survey(b, counts)
    first = jnp.int32(2 * FIXED)
    second = jnp.maximum(first + counts[0], 2 * SOON)
    third = jnp.maximum(second + counts[1], 2 * AHEAD)
    spots = (first, second, third)
    for b in range(3):
        spots = settle(b, spots)
    plan[INFO + 6] = third + counts[2]
    blank(third + counts[2])


def make_plan(every, offsets, n, combos):
    size = every.shape[0]
    smem = pl.BlockSpec(memory_space=pltpu.SMEM)
    return pl.pallas_call(
        functools.partial(plan_kernel, n, combos),
        in_specs=[smem, smem],
        out_specs=[smem, smem],
        out_shape=[
            jax.ShapeDtypeStruct((PLAN,), jnp.int32),
            jax.ShapeDtypeStruct((1,), jnp.int32),
        ],
        scratch_shapes=[pltpu.SMEM((size,), jnp.int32)] * 5 + [pltpu.SMEM((3 * n,), jnp.int32)],
        name="plan",
    )(every, offsets.T)


def wipe_room(room, y):
    def step(f, c):
        room[f, :, y:, :] = jnp.zeros((room.shape[1], PAD, room.shape[3]), F32)
        return c

    lax.fori_loop(0, room.shape[0], step, 0)


def repeat(count, unroll, do):
    def step(g, c):
        for q in range(unroll):
            do(g * unroll + q)
        return c

    lax.fori_loop(0, count // unroll, step, 0)


def solver(plan, room, one, two, own2, par2, prod, wheel, moves, basis, basis_back, levels, h):
    rows, tall, w = room.shape[1:]
    y, z = tall - PAD, w // 2
    half = h // 2
    halo = rows - half
    each = rows * tall
    quads, line, _ = factors()

    prod[0] = jnp.zeros((tall, w), F32)
    prod[:, y:, :] = jnp.zeros((h + 1, PAD, w), F32)
    for ref in (one, two):
        planes = ref.shape[0]
        ref[0] = jnp.zeros(ref.shape[1:], F32)
        ref[:, 0:8, :] = jnp.zeros((planes, 8, w), F32)
        ref[:, 8 + y :, :] = jnp.zeros((planes, 8, w), F32)
    flat_room = room.reshape(room.shape[0] * each, w)
    flat_prod = prod.reshape((h + 1) * tall, w)

    k_at = lax.broadcasted_iota(jnp.int32, (2 * w, 2 * w), 0)
    c_at = lax.broadcasted_iota(jnp.int32, (2 * w, 2 * w), 1)
    half_k, task_c, half_c = k_at % w // z, c_at % w // z, c_at // w
    gap = k_at % z - c_at % z
    wheel[...] = jnp.where((task_c == 1) & (half_k == half_c), gap, 4 * z)

    lane = lanes((y, w))
    low = lane < z
    pos = lane % z
    mu = jnp.broadcast_to(levels[...], (STRIP, w))

    def sweep(src, count, emit):
        def step(g, c):
            for r in range(0, y, STRIP):
                at = pl.ds(8 + r, STRIP)
                col = [src[g * UNROLL + q, at, :] for q in range(UNROLL + 2)]
                for q in range(UNROLL):
                    t = g * UNROLL + q
                    sides = src[t + 1, pl.ds(7 + r, STRIP), :] + src[t + 1, pl.ds(9 + r, STRIP), :]
                    emit(t, r, col[q + 1], (col[q] + col[q + 2]) + sides)
            return c

        lax.fori_loop(0, (count + UNROLL - 1) // UNROLL, step, 0)

    def split(values):
        coarse = values.astype(jnp.bfloat16)
        return coarse, (values - coarse.astype(F32)).astype(jnp.bfloat16)

    def turn_z(values, wave):
        both = jnp.dot(
            jnp.concatenate(split(values), axis=1), wave[...], preferred_element_type=F32
        )
        return both[:, :w] + both[:, w:]

    def planes(r):
        return jnp.where(r < half, r, r + half), jnp.where(r < half, r + half, r + half + halo)

    def run(g, gains, backs):
        p, q = g * 2 * TASK, (g * 2 + 1) * TASK
        rp, rq = (plan[p] + 1) * each, (plan[q] + 1) * each
        ap, aq, bp, bq = plan[p + 2], plan[q + 2], plan[p + 3], plan[q + 3]
        sp, sq = (plan[p + 1] + 1) * each - ap, (plan[q + 1] + 1) * each - aq
        moves[...] = jnp.where(wheel[...] == -bq, 1.0, 0.0).astype(jnp.bfloat16)
        fits = low & (pos - bp >= 0) & (pos - bp < z)
        turn_in, flip_in = lax.rem(bp + w, w), lax.rem(bp + w + z, w)

        def waves_of(g):
            raw = []
            for q in range(DEPTH):
                for t in planes(g * DEPTH + q):
                    raw.append(two[t + 1, 8 : 8 + y, :])
            return turn_z(jnp.concatenate(raw, axis=0), basis)

        def keep_waves(g, waves):
            for q in range(DEPTH):
                for side, t in enumerate(planes(g * DEPTH + q)):
                    at = (2 * q + side) * y
                    one[t + 1, 8 : 8 + y, :] = waves[at : at + y]

        def partners(g):
            par = [flat_room[pl.ds(sq + (g * DEPTH + q) * tall, y), :] for q in range(DEPTH)]
            par = jnp.concatenate(split(jnp.concatenate(par, axis=0)), axis=1)
            return jnp.dot(par, moves[...], preferred_element_type=F32)

        def keep_partners(g, par):
            for q in range(DEPTH):
                r = g * DEPTH + q
                own_p = flat_room[pl.ds(rp + r * tall, y), :]
                own_q = flat_room[pl.ds(rq + r * tall, y), :]
                own_a = jnp.where(low, own_p, pltpu.roll(own_q, z, axis=1))
                own_b = jnp.where(low, pltpu.roll(own_p, z, axis=1), own_q)
                par_p = flat_room[pl.ds(sp + r * tall, y), :]
                near_p = jnp.where(fits, pltpu.roll(par_p, turn_in, axis=1), 0.0)
                far_p = jnp.where(fits, pltpu.roll(par_p, flip_in, axis=1), 0.0)
                both_q = par[q * y : (q + 1) * y]
                for t, own, in_p, in_q in (
                    (planes(r)[0], own_a, near_p, both_q[:, :w]),
                    (planes(r)[1], own_b, far_p, both_q[:, w:]),
                ):
                    half_par = in_p + in_q
                    two[t + 1, 8 : 8 + y, :] = own * half_par
                    own2[t] = own
                    par2[t] = half_par

        def dense(g, c):
            waves, par = waves_of(g - 1), partners(g)
            keep_waves(g - 1, waves)
            keep_partners(g, par)
            return c

        turns = rows // DEPTH
        keep_partners(0, partners(0))
        lax.fori_loop(1, turns, dense, 0)
        keep_waves(turns - 1, waves_of(turns - 1))

        def quad(k, c):
            b, c2 = jnp.float32(quads[0][0]), jnp.float32(quads[0][1])
            for m in range(1, len(quads)):
                b = jnp.where(k == m, jnp.float32(quads[m][0]), b)
                c2 = jnp.where(k == m, jnp.float32(quads[m][1]), c2)
            mu_b = mu + b

            def first(t, r, cur, near):
                two[t + 1, pl.ds(8 + r, STRIP), :] = near + mu_b * cur

            def second(t, r, cur, near):
                at = pl.ds(8 + r, STRIP)
                one[t + 1, at, :] = (near + mu * cur) + c2 * one[t + 1, at, :]

            count = h + EDGE - 1 - 2 * k
            sweep(one, count, first)
            sweep(two, count - 1, second)
            return c

        lax.fori_loop(0, len(quads), quad, 0)
        mu_line = mu + line

        def finish(g, c):
            values = [[] for _ in range(ENDING)]
            for r in range(0, y, STRIP):
                at = pl.ds(8 + r, STRIP)
                col = [one[g * ENDING + q, at, :] for q in range(ENDING + 2)]
                for q in range(ENDING):
                    t = g * ENDING + q
                    sides = one[t + 1, pl.ds(7 + r, STRIP), :] + one[t + 1, pl.ds(9 + r, STRIP), :]
                    values[q].append((col[q] + col[q + 2]) + sides + mu_line * col[q + 1])
            both = turn_z(jnp.concatenate(sum(values, []), axis=0), basis_back)
            for q in range(ENDING):
                t = g * ENDING + q
                pot = both[q * y : (q + 1) * y]
                gains[t] = pot * par2[t]
                prod[t + 1, 0:y, :] = pot * own2[t]
            return c

        lax.fori_loop(0, h // ENDING, finish, 0)

        back = pos + jnp.where(low, bp, bq)
        good = (back >= 0) & (back < z)
        spot = jnp.where(good, jnp.where(low, back, back + z), 0)

        def plane(t):
            at = (t + 1) * tall
            value = jnp.where(low, flat_prod[pl.ds(at + ap, y), :], flat_prod[pl.ds(at + aq, y), :])
            backs[t] = jnp.where(good, jnp.take_along_axis(value, spot, axis=1), 0.0)

        repeat(h, 4, plane)

    return run


def solver_scratch(fields, h, y, w, rows):
    planes = 2 * rows
    return [
        pltpu.VMEM((fields + 1, rows, y + PAD, w), F32),
        pltpu.VMEM((planes + 6, y + 16, w), F32),
        pltpu.VMEM((planes + 6, y + 16, w), F32),
        pltpu.VMEM((planes, y, w), F32),
        pltpu.VMEM((planes, y, w), F32),
        pltpu.VMEM((h + 1, y + PAD, w), F32),
        pltpu.VMEM((2 * w, 2 * w), jnp.int32),
        pltpu.VMEM((2 * w, 2 * w), jnp.bfloat16),
    ]


def swap_kernel(
    counts, plan, fields, edges, basis, basis_back, levels, prior, nxt, halos, statics, results,
    room, one, two, own2, par2, prod, wheel, moves, sends, got, trim, hal, parts,
    in_sem, send, recv, edge_send, edge_recv, trim_send, trim_recv, main_sem, rim_sem,
    hal_sem, part_sem,
):
    n, halo, y, w = edges.shape
    rows = fields.shape[1]
    half = rows - halo
    late = hal.shape[0]
    m = sends.shape[1]
    size, width = lax.axis_size(CYCLE), lax.axis_size("orb")
    o = lax.axis_index("orb")
    me = lax.axis_index("grp") * width + o
    slab = lax.axis_index("slab")
    other = {"slab": 1 - slab}

    def peer(s):
        to = lax.rem(me + s, size)
        return {"grp": lax.div(to, width), "orb": lax.rem(to, width)}

    def limit(q):
        return jnp.where(q % 2 == 0, counts[2], jnp.where(q == width - 1, counts[1], counts[0]))

    above, under = limit(o), limit(lax.rem(o + width - 1, width))
    ways = ((0, above, under, prior), (1, under, above, nxt))

    def load(f):
        return pltpu.make_async_copy(fields.at[f], room.at[f + 1, :, pl.ds(0, y)], in_sem.at[f])

    def copy(way, r):
        return pltpu.make_async_remote_copy(
            src_ref=sends.at[way, r], dst_ref=got.at[way, r, pl.ds(0, half)],
            send_sem=send.at[way, r], recv_sem=recv.at[way, r],
            device_id=peer((1, size - 1)[way]), device_id_type=pl.DeviceIdType.MESH,
        )

    def edge_copy(k):
        return pltpu.make_async_remote_copy(
            src_ref=edges.at[n - 1 - late + k], dst_ref=hal.at[k],
            send_sem=edge_send.at[k], recv_sem=edge_recv.at[k],
            device_id=other, device_id_type=pl.DeviceIdType.MESH,
        )

    def keep_hal(k):
        return pltpu.make_async_copy(hal.at[k], halos.at[k], hal_sem.at[k])

    def trim_copy(way, r):
        return pltpu.make_async_remote_copy(
            src_ref=trim.at[way, r], dst_ref=got.at[way, r, pl.ds(half, halo)],
            send_sem=trim_send.at[way, r], recv_sem=trim_recv.at[way, r],
            device_id=other, device_id_type=pl.DeviceIdType.MESH,
        )

    def main_out(way, r, dst):
        part = pl.ds(0, half)
        return pltpu.make_async_copy(got.at[way, r, part], dst.at[r, part], main_sem.at[way, r])

    def rim_out(way, r, dst):
        part = pl.ds(half, halo)
        return pltpu.make_async_copy(got.at[way, r, part], dst.at[r, part], rim_sem.at[way, r])

    def part_out(g):
        return pltpu.make_async_copy(parts.at[g % 2], results.at[g - FIXED], part_sem.at[g % 2])

    def static_out(g):
        return pltpu.make_async_copy(parts.at[g % 2, 0], statics.at[g], part_sem.at[g % 2])

    def out_wait(g):
        pl.when(g < FIXED)(lambda: static_out(g).wait())
        pl.when(g >= FIXED)(lambda: part_out(g).wait())

    def each(start, stop, do):
        def step(k, c):
            do(k)
            return c

        lax.fori_loop(start, stop, step, 0)

    each(0, n + 2, lambda f: load(f).start())
    barrier = pltpu.get_barrier_semaphore()
    for to in (peer(1), peer(size - 1), other):
        pl.semaphore_signal(barrier, inc=1, device_id=to, device_id_type=pl.DeviceIdType.MESH)
    wipe_room(room, y)
    run = solver(
        plan, room, one, two, own2, par2, prod, wheel, moves, basis, basis_back, levels, 2 * half
    )
    pl.semaphore_wait(barrier, 3)
    each(0, late, lambda k: edge_copy(k).start())
    each(0, n + 2, lambda f: load(f).wait())

    def launch(r):
        for way, out, _, _ in ways:
            @pl.when(r < out)
            def _(way=way):
                k = plan[LISTS + way * 2 * n + r]

                def row(t):
                    sends[way, r, t] = room[k + 1, t, 0:y, :]

                each(0, half, row)
                copy(way, r).start()

    each(0, m, launch)
    low = lanes((1, w)) < w // 2

    def land(r):
        for way, _, into, dst in ways:
            @pl.when(r < into)
            def _(way=way, dst=dst):
                copy(way, r).wait_recv()
                main_out(way, r, dst).start()
                for e in range(halo):
                    a, b = got[way, r, half - 1 - e], got[way, r, half - 1 - halo - e]
                    trim[way, r, e] = jnp.where(low, pltpu.roll(a, w // 2, axis=1), b)
                trim_copy(way, r).start()

    def work(g):
        pl.when(g >= 2)(lambda: out_wait(g - 2))

        @pl.when(g == FIXED)
        def _():
            for k in range(late):
                edge_copy(k).wait()
                keep_hal(k).start()
                room[n - late + k, half:, 0:y, :] = hal[k]

        @pl.when(g == SOON)
        def _():
            for way, _, _, dst in ways:
                trim_copy(way, 0).wait()
                rim_out(way, 0, dst).start()

                def row(t):
                    room[n + 3 + way, t, 0:y, :] = got[way, 0, t]

                each(0, rows, row)

        run(g, parts.at[g % 2, 0], parts.at[g % 2, 1])

        @pl.when(g < FIXED)
        def _():
            def merge(t):
                parts[g % 2, 0, t] = jnp.where(low, parts[g % 2, 0, t], parts[g % 2, 1, t])

            repeat(2 * half, 4, merge)
            static_out(g).start()

        pl.when(g >= FIXED)(lambda: part_out(g).start())
        r = g // 2 - 1
        pl.when((g % 2 == 0) & (r >= 0) & (r < m))(lambda: land(r))

    each(0, AHEAD, work)
    each(min((AHEAD - 1) // 2, m), m, land)
    for k in range(late):
        keep_hal(k).wait()
    for g in range(AHEAD - 2, AHEAD):
        out_wait(g)

    def settle(r):
        for way, out, into, dst in ways:
            @pl.when(r < into)
            def _(way=way, dst=dst):
                trim_copy(way, r).wait()
                rim_out(way, r, dst).start()

            @pl.when(r < out)
            def _(way=way):
                copy(way, r).wait_send()

    for way in range(2):
        copy(way, 0).wait_send()
    each(1, m, settle)

    def close(r):
        for way, _, into, dst in ways:
            @pl.when(r < into)
            def _(way=way, dst=dst):
                main_out(way, r, dst).wait()
                rim_out(way, r, dst).wait()

    each(0, m, close)


def swap(counts, plan, fields, edges, waves, cid):
    n, halo, y, w = edges.shape
    rows = fields.shape[1]
    half, m = rows - halo, max(counts)
    late = n - 2 - EARLY
    hbm = pl.BlockSpec(memory_space=pl.ANY)
    smem = pl.BlockSpec(memory_space=pltpu.SMEM)
    vmem = pl.BlockSpec(memory_space=pltpu.VMEM)
    dma = pltpu.SemaphoreType.DMA
    out = jax.ShapeDtypeStruct((n - 1, rows, y, w), F32)
    return pl.pallas_call(
        functools.partial(swap_kernel, counts),
        in_specs=[smem, hbm, hbm, vmem, vmem, vmem],
        out_specs=[hbm] * 5,
        out_shape=[
            out,
            out,
            jax.ShapeDtypeStruct((late, halo, y, w), F32),
            jax.ShapeDtypeStruct((FIXED, 2 * half, y, w), F32),
            jax.ShapeDtypeStruct((AHEAD - FIXED, 2, 2 * half, y, w), F32),
        ],
        scratch_shapes=solver_scratch(n + 4, 2 * half, y, w, rows)
        + [
            pltpu.VMEM((2, m, half, y, w), F32),
            pltpu.VMEM((2, m, rows, y, w), F32),
            pltpu.VMEM((2, m, halo, y, w), F32),
            pltpu.VMEM((late, halo, y, w), F32),
            pltpu.VMEM((2, 2, 2 * half, y, w), F32),
            dma((n + 2,)), dma((2, m)), dma((2, m)), dma((late,)), dma((late,)),
            dma((2, m)), dma((2, m)), dma((2, m)), dma((2, m)), dma((late,)), dma((2,)),
        ],
        compiler_params=pltpu.CompilerParams(
            collective_id=cid, has_side_effects=True, vmem_limit_bytes=58 * 1024 * 1024
        ),
        name="swap%d%d%d" % counts,
    )(plan, fields, edges, *waves)


def pairs_kernel(
    plan, fields, prior, nxt, halos, statics, results, basis, basis_back, levels, out,
    room, one, two, own2, par2, prod, wheel, moves, acc, stage, parts, sem, hal_sem, acc_sem, out_sem, part_sem,
):
    n, h, y, z = out.shape
    w = 2 * z
    most = prior.shape[0]
    slab = lax.axis_index("slab")

    def part(g):
        return pltpu.make_async_copy(results.at[g], parts.at[g], part_sem.at[g])

    tasks = plan[INFO + 6]

    rows, late = fields.shape[1], halos.shape[0]
    halo = halos.shape[1]

    def field(src, s, f):
        return pltpu.make_async_copy(src.at[s], room.at[f + 1, :, pl.ds(0, y)], sem.at[f])

    def main(f):
        part = pl.ds(0, rows - halo)
        return pltpu.make_async_copy(
            fields.at[f, part], room.at[f + 1, part, pl.ds(0, y)], sem.at[f]
        )

    def rim(f):
        part = pl.ds(rows - halo, halo)
        return pltpu.make_async_copy(
            halos.at[f - (n - 1 - late)], room.at[f + 1, part, pl.ds(0, y)], hal_sem.at[f]
        )

    def each_field(do):
        @pl.when(tasks > 2 * AHEAD)
        def _():
            for f in range(n + 2):
                if n - 1 - late <= f < n - 1:
                    do(main(f))
                    do(rim(f))
                else:
                    do(field(fields, f, f))
            for way, (src, count) in enumerate(((prior, plan[INFO + 3]), (nxt, plan[INFO + 4]))):
                for s in range(most):
                    f = n + 2 + way if s == 0 else n + 3 + way * (n - 2) + s
                    pl.when(s < count)(lambda src=src, s=s, f=f: do(field(src, s, f)))

    def static(g, k):
        return pltpu.make_async_copy(statics.at[g], acc.at[k], acc_sem.at[g])

    static(0, n - 1).start()
    static(1, 0).start()
    for g in range(AHEAD - FIXED):
        part(g).start()
    each_field(lambda c: c.start())
    acc[1 : n - 1] = jnp.zeros((n - 2,) + acc.shape[1:], F32)
    wipe_room(room, y)
    run = solver(plan, room, one, two, own2, par2, prod, wheel, moves, basis, basis_back, levels, h)
    low = lanes((y, w)) < w // 2

    def collect(g, gains, backs):
        p, q = g * 2 * TASK, (g * 2 + 1) * TASK
        for k, src, side in (
            (plan[p + 4], gains, low),
            (plan[q + 4], gains, jnp.logical_not(low)),
            (plan[p + 5], backs, low),
            (plan[q + 5], backs, jnp.logical_not(low)),
        ):
            @pl.when(k < n)
            def _(k=k, src=src, side=side):
                def plane(t):
                    acc[k, t] += jnp.where(side, src[t], 0.0)

                repeat(h, 8, plane)

    def gather(g, c):
        part(g).wait()
        collect(g + FIXED, parts.at[g, 0], parts.at[g, 1])
        return c

    static(0, n - 1).wait()
    static(1, 0).wait()
    lax.fori_loop(0, AHEAD - FIXED, gather, 0)
    each_field(lambda c: c.wait())

    def group(g, c):
        run(g, parts.at[0, 0], parts.at[0, 1])
        collect(g, parts.at[0, 0], parts.at[0, 1])
        return c

    lax.fori_loop(AHEAD, lax.div(tasks + 1, 2), group, 0)

    def leave(k, slot):
        return pltpu.make_async_copy(stage.at[slot], out.at[k], out_sem.at[slot])

    def write(k, c):
        slot = lax.rem(k, 2)
        pl.when(k >= 2)(lambda: leave(k - 2, slot).wait())

        def plane(t):
            value = acc[k, t]
            value = value + pltpu.roll(value, z, axis=1)
            stage[slot, jnp.where(slab == 0, t, h - 1 - t)] = value[:, :z]

        repeat(h, 8, plane)
        leave(k, slot).start()
        return c

    lax.fori_loop(0, n, write, 0)
    for k in (n - 2, n - 1):
        leave(k, k % 2).wait()


def sines(z):
    k = np.arange(1, z + 1)
    wave = np.sqrt(2.0 / (z + 1)) * np.sin(np.pi * np.outer(k, k) / (z + 1))
    wave = np.kron(np.eye(2), wave).astype(np.float32)
    levels = np.tile(2.0 * np.cos(np.pi * k / (z + 1)), 2).astype(np.float32)[None]

    def parts(values):
        coarse = jnp.asarray(values).astype(jnp.bfloat16)
        fine = (jnp.asarray(values) - coarse.astype(F32)).astype(jnp.bfloat16)
        top = jnp.concatenate([coarse, fine], axis=1)
        bottom = jnp.concatenate([coarse, jnp.zeros_like(fine)], axis=1)
        return jnp.concatenate([top, bottom], axis=0)

    return parts(wave), parts(wave * np.float32(factors()[2])), jnp.asarray(levels)


def solve_pairs(plan, fields, prior, nxt, halos, statics, results, waves, shape):
    n, h, y, z = shape
    w, rows = 2 * z, fields.shape[1]
    most = prior.shape[0]
    hbm = pl.BlockSpec(memory_space=pl.ANY)
    vmem = pl.BlockSpec(memory_space=pltpu.VMEM)
    dma = pltpu.SemaphoreType.DMA
    total = n + 2 + 2 * most
    return pl.pallas_call(
        pairs_kernel,
        grid_spec=pltpu.PrefetchScalarGridSpec(
            num_scalar_prefetch=1,
            grid=(1,),
            in_specs=[hbm] * 6 + [vmem] * 3,
            out_specs=hbm,
            scratch_shapes=solver_scratch(total, h, y, w, rows)
            + [
                pltpu.VMEM((n, h, y, w), F32),
                pltpu.VMEM((2, h, y, z), F32),
                pltpu.VMEM((AHEAD - FIXED, 2, h, y, w), F32),
                dma((total,)), dma((n,)), dma((2,)), dma((2,)), dma((AHEAD,)),
            ],
        ),
        out_shape=jax.ShapeDtypeStruct(shape, F32),
        compiler_params=pltpu.CompilerParams(vmem_limit_bytes=58 * 1024 * 1024),
        name="pairs",
    )(plan, fields, prior, nxt, halos, statics, results, *waves)


def fast_body(orbitals, offsets, pairs, live):
    n = orbitals.shape[0]
    combos = [(2, 2, 2), (2, 3, 3), (3, 2, 3), (3, 3, 3), (3, 4, 4), (4, 3, 4), (4, 4, 4)]
    combos.append((n - 1,) * 3)
    waves = sines(orbitals.shape[-1])
    fields, every, edges = front(orbitals, pairs, live)
    plan, which = make_plan(every, offsets, n, combos)

    def branch(counts, cid):
        return lambda _: swap(counts, plan, fields, edges, waves, cid)

    prior, nxt, halos, statics, results = lax.switch(
        which[0], [branch(c, 2 + i) for i, c in enumerate(combos)], 0
    )
    return solve_pairs(
        plan, fields, prior, nxt, halos, statics, results, waves, orbitals.shape
    )


def body(orbitals, offsets, pairs, live):
    n = orbitals.shape[0]
    slots = pairs.shape[0]
    total = offsets.shape[0]
    blocks = total // n
    slabs = lax.axis_size("slab")
    me = lax.axis_index(CYCLE)
    packed = pack(orbitals)

    mine = jnp.concatenate([pairs, live[:, None]], axis=1)
    every = share(jnp.pad(mine, ((0, 0), (0, 128 - mine.shape[1]))))
    ids = jnp.arange(blocks, dtype=jnp.int32)
    second = every[:, :, 1]
    alive = every[:, :, 2] > 0
    orb = jnp.arange(n, dtype=jnp.int32)
    sides = jnp.stack([(ids - 1) % blocks, (ids + 1) % blocks])
    hit = alive[None] & (second[None] // n == sides[:, :, None])
    need = jnp.any(
        hit[..., None] & (second[None, :, :, None] % n == orb), axis=2
    )
    count = jnp.sum(need.astype(jnp.int32), axis=2)
    most = jnp.max(count)

    after, before = (me + 1) % blocks, (me - 1) % blocks
    flags = jnp.stack(
        [need[0, me], need[1, me], need[0, after], need[1, before]]
    ).astype(jnp.int32)
    spot = jnp.sum(
        flags[:, None, :] * (orb[None, :] < orb[:, None]).astype(jnp.int32)[None], axis=2
    )
    lists = jnp.sum(
        (flags[:, None, :] * (spot[:, None, :] == orb[None, :, None])) * orb, axis=2
    )
    back = jnp.stack(
        [spot[2] * flags[2], flags[2], spot[3] * flags[3], flags[3]]
    )

    i, j, on = pairs[:, 0], pairs[:, 1], live > 0
    owner, local = j // n, j % n
    pick_j = (local[:, None] == orb[None, :]).astype(jnp.int32)
    from_prior = (owner == before) & on
    from_next = (owner == after) & on
    kind = jnp.where(from_prior, 1, jnp.where(from_next, 2, 0))
    where_prior = jnp.sum(pick_j * spot[0][None, :], axis=1) * from_prior
    where_next = jnp.sum(pick_j * spot[1][None, :], axis=1) * from_next
    ids_all = jnp.arange(total, dtype=jnp.int32)
    diff = (j[:, None] == ids_all).astype(jnp.int32) - (i[:, None] == ids_all).astype(jnp.int32)
    shift = jnp.sum(diff[:, :, None] * offsets[None], axis=1)
    plan = jnp.stack(
        [i % n, local, where_prior, where_next, kind, shift[:, 0], shift[:, 1], live]
    ).astype(jnp.int32)
    order = jnp.where(on, jnp.where(kind > 0, 0, 1), 2) * slots + jnp.arange(slots)
    rank = jnp.sum((order[None, :] < order[:, None]).astype(jnp.int32), axis=1)
    move = (rank[:, None] == jnp.arange(slots)[None, :]).astype(jnp.int32)
    plan = jnp.sum(plan[:, :, None] * move[None], axis=1)
    far, lively = jnp.sum((kind > 0).astype(jnp.int32)), jnp.sum(on.astype(jnp.int32))
    tail = jnp.where(jnp.arange(slots) == 0, far, lively)
    plan = jnp.concatenate([plan, tail[None]], axis=0)
    ends = jnp.stack([lax.axis_index("slab"), slabs]).astype(jnp.int32)

    up = [(s, s + 1) for s in range(slabs - 1)]
    down = [(s + 1, s) for s in range(slabs - 1)]

    def branch(m):
        def run(_):
            to_next, to_prior = gather(packed, lists[2:], m)
            prior = cycle(to_next, 1)
            nxt = cycle(to_prior, -1)
            partner, density, low, high = densities(plan, packed, prior, nxt)
            below = lax.ppermute(high, "slab", up)
            above = lax.ppermute(low, "slab", down)
            given = (plan, ends, density, partner, packed, below, above, m)
            acc, acc_prior, acc_next = solve(True, *given)
            from_next, from_prior = cycle(acc_prior, -1), cycle(acc_next, 1)
            (acc_near,) = solve(False, *given)
            return combine(back, acc, acc_near, from_next, from_prior)

        return run

    sizes = sorted({min(s, slots - 1) for s in (3, 4, 5)} | {slots - 1})
    which = sum((most > s).astype(jnp.int32) for s in sizes[:-1])
    return lax.switch(which, [branch(s) for s in sizes], 0)


def solution(mesh):
    placed = (
        P(CYCLE, "slab", None, None),
        P(),
        P(CYCLE, None),
        P(CYCLE),
    )
    return jax.shard_map(
        fast_body if mesh.shape["slab"] == 2 else body,
        mesh=mesh,
        in_specs=placed,
        out_specs=P(CYCLE, "slab", None, None),
        check_vma=False,
    )
```
